32 devices in a mesh: shard: 8 (over y, x, core), rep: 4 (over z).
Axes of the slice: x: 2, y: 2, z: 4, core: 2. Of those that a mesh axis runs over, the one named last changes fastest.
Arguments:
- inputs: bfloat16 [4, 3, 512, 2048], P('rep', None, 'shard'), may hold values from -6 to 6
- ln1_gain: bfloat16 [2048], replicated, may hold values from 0.5 to 1.5
- ln1_bias: bfloat16 [2048], replicated, may hold values from -1.1953125 to 1.1953125
- w_query: bfloat16 [2048, 2048], P('shard'), may hold values from -0.125 to 0.125
- b_query: bfloat16 [2048], replicated, may hold values from -1.1953125 to 1.1953125
- w_key: bfloat16 [2048, 2048], P('shard'), may hold values from -0.125 to 0.125
- w_value: bfloat16 [2048, 2048], P('shard'), may hold values from -0.125 to 0.125
- b_value: bfloat16 [2048], replicated, may hold values from -1.1953125 to 1.1953125
- w_out: bfloat16 [2048, 2048], P('shard'), may hold values from -0.375 to 0.375
- b_out: bfloat16 [2048], replicated, may hold values from -1.1953125 to 1.1953125
- ln2_gain: bfloat16 [2048], replicated, may hold values from 0.5 to 1.5
- ln2_bias: bfloat16 [2048], replicated, may hold values from -1.1953125 to 1.1953125
- w_up: bfloat16 [2048, 8192], P('shard'), may hold values from -0.125 to 0.125
- b_up: bfloat16 [8192], replicated, may hold values from -1.1953125 to 1.1953125
- w_down: bfloat16 [8192, 2048], P('shard'), may hold values from -0.0625 to 0.0625
- b_down: bfloat16 [2048], replicated, may hold values from -1.1953125 to 1.1953125
- in_query: bfloat16 [8, 16, 2048], P(None, None, 'shard'), may hold values from -0.125 to 0.125
- out_query: bfloat16 [8, 16, 2048], P(None, None, 'shard'), may hold values from -0.75 to 0.75
- in_key: bfloat16 [8, 16, 2048], P(None, None, 'shard'), may hold values from -0.125 to 0.125
- out_key: bfloat16 [8, 16, 2048], P(None, None, 'shard'), may hold values from -0.75 to 0.75
- in_value: bfloat16 [8, 16, 2048], P(None, None, 'shard'), may hold values from -0.125 to 0.125
- out_value: bfloat16 [8, 16, 2048], P(None, None, 'shard'), may hold values from -0.75 to 0.75
- in_attn: bfloat16 [8, 16, 2048], P(None, None, 'shard'), may hold values from -0.125 to 0.125
- out_attn: bfloat16 [8, 16, 2048], P(None, None, 'shard'), may hold values from -0.75 to 0.75
- in_expand: bfloat16 [8, 16, 2048], P(None, None, 'shard'), may hold values from -0.125 to 0.125
- out_expand: bfloat16 [8, 16, 8192], P(None, None, 'shard'), may hold values from -0.75 to 0.75
- in_reduce: bfloat16 [8, 16, 8192], P(None, None, 'shard'), may hold values from -0.0625 to 0.0625
- out_reduce: bfloat16 [8, 16, 2048], P(None, None, 'shard'), may hold values from -0.75 to 0.75
- adapter_pick: int32 [4, 3], P('rep'), may hold values from 0 to 7
- piece_start: int32 [4, 3, 1], P('rep'), may hold values from 0 to 256, as said below
- cotangent: bfloat16 [4, 3, 512, 2048], P('rep', None, 'shard'), may hold values from -6 to 6
Outputs:
- layer_out: bfloat16 [4, 3, 512, 2048], P('rep', None, 'shard')
- input_grad: bfloat16 [4, 3, 512, 2048], P('rep', None, 'shard')
- grad_in_query: float32 [8, 16, 2048], P(None, None, 'shard')
- grad_out_query: float32 [8, 16, 2048], P(None, None, 'shard')
- grad_in_key: float32 [8, 16, 2048], P(None, None, 'shard')
- grad_out_key: float32 [8, 16, 2048], P(None, None, 'shard')
- grad_in_value: float32 [8, 16, 2048], P(None, None, 'shard')
- grad_out_value: float32 [8, 16, 2048], P(None, None, 'shard')
- grad_in_attn: float32 [8, 16, 2048], P(None, None, 'shard')
- grad_out_attn: float32 [8, 16, 2048], P(None, None, 'shard')
- grad_in_expand: float32 [8, 16, 2048], P(None, None, 'shard')
- grad_out_expand: float32 [8, 16, 8192], P(None, None, 'shard')
- grad_in_reduce: float32 [8, 16, 8192], P(None, None, 'shard')
- grad_out_reduce: float32 [8, 16, 2048], P(None, None, 'shard')
The draws below stay inside these ranges and needn't reach their ends.
Inputs may be any that keep to these rules, and one draw needn't show every extreme that they name: `piece_start`: piece k (from 0) of a sequence starts within its own region of 512 positions beginning at k * 512, and ends inside that region unless the region is shorter than 256, in which case it runs to the sequence's end; pieces of one sequence never share a position.
All inputs are finite; a program needn't handle non-finite values.
Results may differ from the reference program's by a relative error of at most 0.023.
Values may be sent and summed in bfloat16 or wider, within the bound.
No kernel may reach another device: no remote copies, remote signals or barrier semaphores. Data moves between devices by JAX's collectives and lax.ppermute only.
A program may use at most 448 MiB of HBM per device.

```python
import jax
import jax.numpy as jnp
from jax import lax

D = 2048
HEADS = 16
HEAD = 128
FF = 8192
RANK = 16
ADAPTERS = 8
SEQS = 3
PIECE = 256
LEN = 512
NPIECE = 1
N_REP = 4


def draw_piece_start(key, part):
    region = LEN // NPIECE
    spare_room = max(region - PIECE, 0)
    offsets = jax.random.randint(key, (N_REP, SEQS, NPIECE), 0, spare_room + 1)
    region_base = jnp.arange(NPIECE, dtype=jnp.int32) * region
    starts = (offsets + region_base[None, None, :]).astype(jnp.int32)
    starts = starts.at[0, 0, NPIECE - 1].set((NPIECE - 1) * region + spare_room)
    starts = starts.at[N_REP - 1, SEQS - 1, 0].set(0)
    return starts


def set_ends(values, own_key, low, largest):
    shape = values.shape
    place = [jax.random.randint(jax.random.fold_in(own_key, axis), (), 0, shape[axis]) for axis in range(len(shape))]
    values = values.at[tuple(place)].set(low)
    longest = shape.index(max(shape))
    place[longest] = (place[longest] + 1) % shape[longest]
    return values.at[tuple(place)].set(largest)


def level_of(own_key, dims, pieces, smallest, largest):
    loudness, own = 1.0, jax.random.fold_in(own_key, 6)
    for dim, shards_of in pieces:
        steps = jnp.exp(jax.random.uniform(jax.random.fold_in(own, dim), (shards_of,), jnp.float32, smallest / len(pieces), largest / len(pieces)))
        loudness = loudness * jnp.repeat(steps, dims[dim] // shards_of).reshape([-1 if axis == dim else 1 for axis in range(len(dims))])
    return loudness


def centred(key, extent, scale, bound, pieces=(), held_as=jnp.bfloat16):
    array = scale * jax.random.normal(key, extent, jnp.float32)
    if pieces:
        array = array * level_of(key, extent, pieces, -0.22, 0.18)
    return jnp.clip(array, -bound, bound).astype(held_as)


def setup_inputs(seed: int = 0) -> dict:
    seeds = jax.random.split(jax.random.key(seed), 32)
    return {
        "inputs": centred(seeds[0], (N_REP, SEQS, LEN, D), 1.0, 6.0, ((0, 4), (2, 8))),
        "ln1_gain": jnp.clip(1.0 + 0.1 * jax.random.normal(seeds[1], (D,), jnp.float32), 0.5, 1.5).astype(jnp.bfloat16),
        "ln1_bias": centred(seeds[2], (D,), 0.2, 1.1953125),
        "w_query": centred(seeds[3], (D, D), D ** -0.5, 0.125, ((0, 8),)),
        "b_query": centred(seeds[4], (D,), 0.2, 1.1953125),
        "w_key": centred(seeds[5], (D, D), D ** -0.5, 0.125, ((0, 8),)),
        "w_value": centred(seeds[6], (D, D), D ** -0.5, 0.125, ((0, 8),)),
        "b_value": centred(seeds[7], (D,), 0.2, 1.1953125),
        "w_out": centred(seeds[8], (D, D), (D // 8) ** -0.5, 0.375, ((0, 8),)),
        "b_out": centred(seeds[9], (D,), 0.2, 1.1953125),
        "ln2_gain": jnp.clip(1.0 + 0.1 * jax.random.normal(seeds[10], (D,), jnp.float32), 0.5, 1.5).astype(jnp.bfloat16),
        "ln2_bias": centred(seeds[11], (D,), 0.2, 1.1953125),
        "w_up": centred(seeds[12], (D, FF), D ** -0.5, 0.125, ((0, 8),)),
        "b_up": centred(seeds[13], (FF,), 0.2, 1.1953125),
        "w_down": centred(seeds[14], (FF, D), FF ** -0.5, 0.0625, ((0, 8),)),
        "b_down": centred(seeds[15], (D,), 0.2, 1.1953125),
        "in_query": centred(seeds[16], (ADAPTERS, RANK, D), D ** -0.5, 0.125, ((2, 8),)),
        "out_query": centred(seeds[17], (ADAPTERS, RANK, D), (4 * RANK) ** -0.5, 0.75, ((2, 8),)),
        "in_key": centred(seeds[18], (ADAPTERS, RANK, D), D ** -0.5, 0.125, ((2, 8),)),
        "out_key": centred(seeds[19], (ADAPTERS, RANK, D), (4 * RANK) ** -0.5, 0.75, ((2, 8),)),
        "in_value": centred(seeds[20], (ADAPTERS, RANK, D), D ** -0.5, 0.125, ((2, 8),)),
        "out_value": centred(seeds[21], (ADAPTERS, RANK, D), (4 * RANK) ** -0.5, 0.75, ((2, 8),)),
        "in_attn": centred(seeds[22], (ADAPTERS, RANK, D), D ** -0.5, 0.125, ((2, 8),)),
        "out_attn": centred(seeds[23], (ADAPTERS, RANK, D), (4 * RANK) ** -0.5, 0.75, ((2, 8),)),
        "in_expand": centred(seeds[24], (ADAPTERS, RANK, D), D ** -0.5, 0.125, ((2, 8),)),
        "out_expand": centred(seeds[25], (ADAPTERS, RANK, FF), (4 * RANK) ** -0.5, 0.75, ((2, 8),)),
        "in_reduce": centred(seeds[26], (ADAPTERS, RANK, FF), FF ** -0.5, 0.0625, ((2, 8),)),
        "out_reduce": centred(seeds[27], (ADAPTERS, RANK, D), (4 * RANK) ** -0.5, 0.75, ((2, 8),)),
        "adapter_pick": set_ends(jax.random.randint(seeds[28], (N_REP, SEQS), 0, ADAPTERS), jax.random.fold_in(seeds[28], 1), 0, ADAPTERS - 1).astype(jnp.int32),
        "piece_start": draw_piece_start(jax.random.fold_in(seeds[31], 71), 0),
        "cotangent": centred(seeds[30], (N_REP, SEQS, LEN, D), 1.0, 6.0, ((0, 4), (2, 8))),
    }


EPSILON = 1e-05
FULL_PRECISION = lax.Precision.HIGHEST
MASKED = -1e+30

@jax.custom_vjp
def low_rank_product(v):
    return lax.optimization_barrier(v.astype(jnp.bfloat16)).astype(jnp.float32)

@jax.custom_vjp
def low_rank_backward(v):
    return v

def low_keep(v):
    return (low_rank_product(v), None)

def low_pass(kept, grad):
    return (grad,)

def back_keep(v):
    return (v, None)

def back_low(kept, grad):
    return (low_rank_product(grad),)
low_rank_product.defvjp(low_keep, low_pass)
low_rank_backward.defvjp(back_keep, back_low)

def layer_norm(values, gain_vec, shift_vec):
    centre = lax.optimization_barrier(jnp.mean(values, axis=-1, keepdims=True))
    offset = values - centre
    spread = lax.optimization_barrier(jnp.mean(offset * offset, axis=-1, keepdims=True))
    return offset * lax.rsqrt(spread + EPSILON) * gain_vec + shift_vec

def piece_labels(starts, positions):
    inside = (positions[:, None] >= starts[None, :]) & (positions[:, None] < starts[None, :] + PIECE)
    labels = jnp.arange(1, starts.shape[0] + 1, dtype=jnp.int32)
    return lax.optimization_barrier(jnp.sum(jnp.where(inside, labels[None, :], 0), axis=1)).astype(jnp.int32)

def visible(query_pos, key_pos, query_label, key_label):
    causal = key_pos[None, :] <= query_pos[:, None]
    shared = (query_label[:, None] == key_label[None, :]) & (query_label[:, None] > 0)
    return causal | shared

def project(hidden_states, weight_matrix):
    return jnp.einsum('gtx,xh->gth', hidden_states, weight_matrix, precision=FULL_PRECISION)

def adapter(hidden_states, entry_projection, leave_map):
    adapter_rank_size = low_rank_backward(low_rank_product(jnp.einsum('pag,pvg->pav', hidden_states, entry_projection, precision=FULL_PRECISION)))
    return jnp.einsum('slr,sre->sle', adapter_rank_size, leave_map, precision=FULL_PRECISION)

def attend(queries, keys_all, values_all, starts):
    block_rows = min(512, LEN)
    block_count = LEN // block_rows
    positions = jnp.arange(LEN, dtype=jnp.int32)
    labels = piece_labels(starts, positions)
    factor = HEAD ** (-0.5)

    def one_block(packed):
        query_block, query_pos, query_label = packed
        scores = jnp.einsum('qhd,khd->hqk', query_block, keys_all, precision=FULL_PRECISION) * factor
        scores = low_rank_backward(scores)
        allowed = visible(query_pos, positions, query_label, labels)
        scores = jnp.where(allowed[None], scores, MASKED)
        probs = low_rank_product(jax.nn.softmax(scores, axis=-1))
        return jnp.einsum('hqk,khd->qhd', probs, values_all, precision=FULL_PRECISION)
    blocks = lax.map(jax.checkpoint(one_block), (queries.reshape(block_count, block_rows, HEADS, HEAD), positions.reshape(block_count, block_rows), labels.reshape(block_count, block_rows)))
    return blocks.reshape(LEN, HEADS * HEAD)

def layer(features, adapt_maps, frozen, picks, starts_all):
    gain_one, shift_one, w_query, b_query, w_key, w_value, b_value, w_out, b_out, gain_two, shift_two, w_up, b_up, w_down, b_down = frozen
    chosen = [jnp.take(table, picks, axis=0) for table in adapt_maps]
    hidden_one = low_rank_product(layer_norm(features, gain_one, shift_one))
    queries = low_rank_backward(low_rank_product(project(hidden_one, w_query) + b_query + adapter(hidden_one, chosen[0], chosen[1])))
    keys_made = low_rank_backward(low_rank_product(project(hidden_one, w_key) + adapter(hidden_one, chosen[2], chosen[3])))
    values_made = low_rank_backward(low_rank_product(project(hidden_one, w_value) + b_value + adapter(hidden_one, chosen[4], chosen[5])))
    rows_list = []
    for which in range(SEQS):
        rows_list.append(attend(queries[which].reshape(LEN, HEADS, HEAD), keys_made[which].reshape(LEN, HEADS, HEAD), values_made[which].reshape(LEN, HEADS, HEAD), starts_all[which]))
    attended = low_rank_backward(low_rank_product(jnp.stack(rows_list)))
    branch = low_rank_backward(project(attended, w_out) + b_out + adapter(attended, chosen[6], chosen[7]))
    residual = features + branch
    hidden_two = low_rank_product(layer_norm(residual, gain_two, shift_two))
    pre_act = low_rank_backward(project(hidden_two, w_up) + b_up + adapter(hidden_two, chosen[8], chosen[9]))
    activated = low_rank_product(jax.nn.gelu(pre_act, approximate=False))
    mlp_out = low_rank_backward(project(activated, w_down) + b_down + adapter(activated, chosen[10], chosen[11]))
    return residual + mlp_out

def reference(inputs, ln1_gain, ln1_bias, w_query, b_query, w_key, w_value, b_value, w_out, b_out, ln2_gain, ln2_bias, w_up, b_up, w_down, b_down, in_query, out_query, in_key, out_key, in_value, out_value, in_attn, out_attn, in_expand, out_expand, in_reduce, out_reduce, adapter_pick, piece_start, cotangent):
    frozen = tuple((item.astype(jnp.float32) for item in (ln1_gain, ln1_bias, w_query, b_query, w_key, w_value, b_value, w_out, b_out, ln2_gain, ln2_bias, w_up, b_up, w_down, b_down)))
    adapt_maps = tuple((item.astype(jnp.float32) for item in (in_query, out_query, in_key, out_key, in_value, out_value, in_attn, out_attn, in_expand, out_expand, in_reduce, out_reduce)))

    def one_group(totals, packed):
        features, cot_rows, picks, starts_all = packed
        result, pull = jax.vjp(lambda feat, maps: layer(feat, maps, frozen, picks, starts_all), features.astype(jnp.float32), adapt_maps)
        grad_feat, grad_maps = pull(cot_rows.astype(jnp.float32))
        totals = tuple((total + grad for total, grad in zip(totals, grad_maps)))
        return (totals, (result.astype(jnp.bfloat16), grad_feat.astype(jnp.bfloat16)))
    zeros = tuple((jnp.zeros(item.shape, jnp.float32) for item in adapt_maps))
    totals, (outputs, grads) = lax.scan(one_group, zeros, (inputs, cotangent, adapter_pick, piece_start))
    return (outputs, grads, totals[0], totals[1], totals[2], totals[3], totals[4], totals[5], totals[6], totals[7], totals[8], totals[9], totals[10], totals[11])
```

```python
import functools

import jax
import jax.numpy as jnp
import numpy as np
from jax import lax
from jax.experimental import pallas as pl
from jax.experimental.pallas import tpu as pltpu
from jax.sharding import PartitionSpec as P

HEADS = 16
HEAD = 128
ADAPTERS = 8
PIECE = 256

EPSILON = 1e-05
MASKED = -1e30
F32 = jnp.float32
BF16 = jnp.bfloat16


def layer_norm(values, gain_vec, shift_vec):
    centre = jnp.mean(values, axis=-1, keepdims=True)
    offset = values - centre
    spread = jnp.mean(offset * offset, axis=-1, keepdims=True)
    return offset * lax.rsqrt(spread + EPSILON) * gain_vec + shift_vec


def piece_labels(starts, positions):
    inside = (positions[:, None] >= starts[None, :]) & (
        positions[:, None] < starts[None, :] + PIECE
    )
    labels = jnp.arange(1, starts.shape[0] + 1, dtype=jnp.int32)
    return jnp.sum(jnp.where(inside, labels[None, :], 0), axis=1)


def mm(a, b):
    return lax.dot_general(a, b, (((1,), (0,)), ((), ())), preferred_element_type=F32)


def mm_t(a, b):
    return lax.dot_general(a, b, (((1,), (1,)), ((), ())), preferred_element_type=F32)


def t_mm(a, b):
    return lax.dot_general(a, b, (((0,), (0,)), ((), ())), preferred_element_type=F32)


def swap(value, axis, mask):
    size = lax.axis_size(axis)
    return lax.ppermute(value, axis, [(i, i ^ mask) for i in range(size)])


def bits_of(size):
    bits = []
    while (1 << len(bits)) < size:
        bits.append(1 << len(bits))
    return bits


def row_plan(size, rows, parts):
    masks, locs = [], []
    for core in (0, 1):
        for low, high, order in parts:
            group = [0]
            for bit in order:
                group = group + [m | bit for m in group]
            for mask in group:
                masks += [mask | core] * (high - low)
                locs += list(range(low, high))
    return np.array(masks, np.int32), np.array(locs, np.int32)


def spread_rows(value, parts):
    pieces = []
    for low, high, order in parts:
        current = value[low:high]
        for bit in order:
            current = jnp.concatenate([current, swap(current, "shard", bit)], 0)
        pieces.append(current)
    current = jnp.concatenate(pieces, 0) if len(pieces) > 1 else pieces[0]
    return jnp.concatenate([current, swap(current, "shard", 1)], 0)


def sum_rows(value, parts):
    def fold(current, bit):
        half = current.shape[0] // 2
        other = swap(current[half:].astype(BF16), "shard", bit)
        return current[:half].astype(F32) + other.astype(F32)

    current = fold(value, 1)
    done, start = [], 0
    for low, high, order in parts:
        count = (high - low) << len(order)
        piece = current[start : start + count]
        start += count
        for bit in reversed(order):
            piece = fold(piece.astype(BF16), bit)
        done.append(piece)
    return jnp.concatenate(done, 0) if len(done) > 1 else done[0]


def gather_blocks(value, axis):
    current = value[None]
    for bit in bits_of(lax.axis_size(axis)):
        current = jnp.concatenate([current, swap(current, axis, bit)], 0)
    return current


def place_kernel(me_ref, *refs, rows):
    pieces, out_ref, sems = refs[:-2], refs[-2], refs[-1]
    me = me_ref[0]
    copies = []
    for mask, piece in enumerate(pieces):
        copies.append(
            pltpu.make_async_copy(
                piece, out_ref.at[pl.ds(pl.multiple_of((me ^ mask) * rows, rows), rows)], sems.at[mask]
            )
        )
    for copy in copies:
        copy.start()
    for copy in copies:
        copy.wait()


def place_rows(me, pieces):
    rows, width = pieces[0].shape
    count = len(pieces)
    return pl.pallas_call(
        functools.partial(place_kernel, rows=rows),
        out_shape=jax.ShapeDtypeStruct((rows * count, width), pieces[0].dtype),
        in_specs=[pl.BlockSpec(memory_space=pltpu.SMEM)]
        + [pl.BlockSpec(memory_space=pl.ANY)] * count,
        out_specs=pl.BlockSpec(memory_space=pltpu.VMEM),
        scratch_shapes=[pltpu.SemaphoreType.DMA((count,))],
        cost_estimate=pl.CostEstimate(
            flops=0, bytes_accessed=4 * rows * count * width, transcendentals=0
        ),
        name="place_rows",
    )(me, *pieces)


def cols_kernel(me_ref, in_ref, out_ref):
    out_ref[...] = in_ref[0]


def place_columns(me, stacked):
    count, rows, width = stacked.shape
    return pl.pallas_call(
        cols_kernel,
        out_shape=jax.ShapeDtypeStruct((rows, count * width), stacked.dtype),
        grid_spec=pltpu.PrefetchScalarGridSpec(
            num_scalar_prefetch=1,
            grid=(count,),
            in_specs=[pl.BlockSpec((1, rows, width), lambda k, me: (me[0] ^ k, 0, 0))],
            out_specs=pl.BlockSpec((rows, width), lambda k, me: (0, k)),
        ),
        name="place_columns",
    )(me, stacked)


def seen(pos_q, pos_k, lab_q, lab_k):
    return (pos_k <= pos_q) | ((lab_q == lab_k) & (lab_q > 0))


def attend_kernel(pq, pk, lq, lk, qkv_ref, out_ref, lse_ref, *, heads, factor):
    allowed = seen(pq[...], pk[...], lq[...], lk[...])
    span = heads * HEAD
    for h in range(heads):
        q = qkv_ref[:, h * HEAD : (h + 1) * HEAD]
        k = qkv_ref[:, span + h * HEAD : span + (h + 1) * HEAD]
        v = qkv_ref[:, 2 * span + h * HEAD : 2 * span + (h + 1) * HEAD]
        scores = jnp.where(allowed, mm_t(q, k) * factor, MASKED)
        top = jnp.max(scores, axis=-1, keepdims=True)
        expo = jnp.exp(scores - top)
        total = jnp.sum(expo, axis=-1, keepdims=True)
        probs = (expo * (1.0 / total)).astype(BF16)
        out_ref[:, h * HEAD : (h + 1) * HEAD] = mm(probs, v).astype(BF16)
        lse_ref[:, h : h + 1] = top + jnp.log(total)


def attend(where, qkv, heads):
    length = qkv.shape[0]
    vmem = pl.BlockSpec(memory_space=pltpu.VMEM)
    return pl.pallas_call(
        functools.partial(attend_kernel, heads=heads, factor=HEAD ** (-0.5)),
        out_shape=(
            jax.ShapeDtypeStruct((length, heads * HEAD), BF16),
            jax.ShapeDtypeStruct((length, heads), F32),
        ),
        in_specs=[vmem] * 5,
        out_specs=(vmem, vmem),
        cost_estimate=pl.CostEstimate(
            flops=heads * length * length * HEAD * 4,
            bytes_accessed=length * heads * HEAD * 8,
            transcendentals=heads * length * length,
        ),
        name="attend",
    )(*where, qkv)


def attend_back_kernel(pq, pk, lq, lk, qkv_ref, lse_ref, ga_ref, out_ref, *, heads, factor):
    allowed = seen(pq[...], pk[...], lq[...], lk[...])
    span = heads * HEAD
    for h in range(heads):
        q = qkv_ref[:, h * HEAD : (h + 1) * HEAD]
        k = qkv_ref[:, span + h * HEAD : span + (h + 1) * HEAD]
        v = qkv_ref[:, 2 * span + h * HEAD : 2 * span + (h + 1) * HEAD]
        ga = ga_ref[:, h * HEAD : (h + 1) * HEAD]
        scores = jnp.where(allowed, mm_t(q, k) * factor, MASKED)
        probs = jnp.exp(scores - lse_ref[:, h : h + 1])
        grad_probs = mm_t(ga, v)
        inner = jnp.sum(probs * grad_probs, axis=-1, keepdims=True)
        grad_scores = (probs * (grad_probs - inner)).astype(BF16)
        low = probs.astype(BF16)
        out_ref[:, h * HEAD : (h + 1) * HEAD] = (mm(grad_scores, k) * factor).astype(BF16)
        out_ref[:, span + h * HEAD : span + (h + 1) * HEAD] = (
            t_mm(grad_scores, q) * factor
        ).astype(BF16)
        out_ref[:, 2 * span + h * HEAD : 2 * span + (h + 1) * HEAD] = t_mm(low, ga).astype(BF16)


def attend_back(where, qkv, lse, grad_attended, heads):
    length = qkv.shape[0]
    vmem = pl.BlockSpec(memory_space=pltpu.VMEM)
    return pl.pallas_call(
        functools.partial(attend_back_kernel, heads=heads, factor=HEAD ** (-0.5)),
        out_shape=jax.ShapeDtypeStruct((length, 3 * heads * HEAD), BF16),
        in_specs=[vmem] * 7,
        out_specs=vmem,
        cost_estimate=pl.CostEstimate(
            flops=heads * length * length * HEAD * 10,
            bytes_accessed=length * heads * HEAD * 14,
            transcendentals=heads * length * length,
        ),
        name="attend_back",
    )(*where, qkv, lse, grad_attended)


def on_device(
    inputs,
    ln1_gain,
    ln1_bias,
    w_query,
    b_query,
    w_key,
    w_value,
    b_value,
    w_out,
    b_out,
    ln2_gain,
    ln2_bias,
    w_up,
    b_up,
    w_down,
    b_down,
    in_query,
    out_query,
    in_key,
    out_key,
    in_value,
    out_value,
    in_attn,
    out_attn,
    in_expand,
    out_expand,
    in_reduce,
    out_reduce,
    adapter_pick,
    piece_start,
    cotangent,
):
    count = inputs.shape[1]
    rows = inputs.shape[2]
    size = lax.axis_size("shard")
    me = lax.axis_index("shard").astype(jnp.int32)
    me_arr = me[None]
    heads = HEADS // size
    span = heads * HEAD
    ff_part = w_up.shape[1] // size
    rank = in_query.shape[1]
    chosen = adapter_pick[0]
    starts = piece_start[0]

    def pick(table, which):
        return lax.dynamic_index_in_dim(table, chosen[which], 0, keepdims=False)

    upper = tuple(bits_of(size)[1:])
    half = rows // 2
    parts = [(0, half, upper), (half, rows, tuple(reversed(upper)))]
    masks, locs = row_plan(size, rows, parts)
    positions = (me ^ jnp.asarray(masks)) * rows + jnp.asarray(locs)
    wheres = []
    for s in range(count):
        labels = piece_labels(starts[s], positions)
        wheres.append((positions[:, None], positions[None, :], labels[:, None], labels[None, :]))

    def block(table, mask, width):
        return lax.dynamic_slice_in_dim(table, (me ^ mask) * width, width, 1)

    def turn(tables, width):
        pieces = []
        for mask in range(size):
            piece = [block(t, mask, width) for t in tables]
            piece = jnp.concatenate(piece, 1) if len(piece) > 1 else piece[0]
            pieces.append(swap(piece, "shard", mask) if mask else piece)
        return place_rows(me_arr, pieces)

    gain_one, shift_one = ln1_gain.astype(F32), ln1_bias.astype(F32)
    gain_two, shift_two = ln2_gain.astype(F32), ln2_bias.astype(F32)

    features = [inputs[0, s].astype(F32) for s in range(count)]
    hidden_one, norm_one_back = [], []
    for s in range(count):
        normed, back = jax.vjp(lambda v: layer_norm(v, gain_one, shift_one), features[s])
        norm_one_back.append(back)
        hidden_one.append(spread_rows(normed.astype(BF16), parts))

    mine = jnp.concatenate(
        [
            pick(t, s)
            for s in range(count)
            for t in (in_query, in_key, in_value, in_expand, out_attn, out_reduce)
        ],
        0,
    )
    whole = place_columns(me_arr, gather_blocks(mine, "shard"))
    whole = whole.reshape(count, 6 * rank, -1)
    in_qkv = [whole[s, : 3 * rank] for s in range(count)]
    in_exp = [whole[s, 3 * rank : 4 * rank] for s in range(count)]
    out_att = [whole[s, 4 * rank : 5 * rank] for s in range(count)]
    out_red = [whole[s, 5 * rank :] for s in range(count)]
    none = jnp.zeros((rank, span), BF16)
    out_qkv = [
        jnp.concatenate(
            [
                jnp.concatenate([pick(out_query, s), none, none], 1),
                jnp.concatenate([none, pick(out_key, s), none], 1),
                jnp.concatenate([none, none, pick(out_value, s)], 1),
            ],
            0,
        )
        for s in range(count)
    ]
    in_att = [pick(in_attn, s) for s in range(count)]
    out_exp = [pick(out_expand, s) for s in range(count)]
    in_red = [pick(in_reduce, s) for s in range(count)]

    w_qkv = turn([w_query, w_key, w_value], span)
    b_qkv = jnp.concatenate(
        [
            lax.dynamic_slice_in_dim(b_query, me * span, span).astype(F32),
            jnp.zeros((span,), F32),
            lax.dynamic_slice_in_dim(b_value, me * span, span).astype(F32),
        ]
    )
    b_up_mine = lax.dynamic_slice_in_dim(b_up, me * ff_part, ff_part).astype(F32)

    low_qkv, qkv, lses, attended, low_att, residual, norm_two_back, hidden_two = (
        [],
        [],
        [],
        [],
        [],
        [],
        [],
        [],
    )
    for s in range(count):
        low = mm_t(hidden_one[s], in_qkv[s]).astype(BF16)
        made = (mm(hidden_one[s], w_qkv) + mm(low, out_qkv[s]) + b_qkv).astype(BF16)
        att, lse = attend(wheres[s], made, heads)
        low_a = mm_t(att, in_att[s]).astype(BF16)
        part = (mm(att, w_out) + mm(low_a, out_att[s])).astype(BF16)
        branch = sum_rows(part, parts) + b_out.astype(F32)
        res = features[s] + branch
        normed, back = jax.vjp(lambda v: layer_norm(v, gain_two, shift_two), res)
        low_qkv.append(low)
        qkv.append(made)
        lses.append(lse)
        attended.append(att)
        low_att.append(low_a)
        residual.append(res)
        norm_two_back.append(back)
        hidden_two.append(spread_rows(normed.astype(BF16), parts))

    w_up_mine = turn([w_up], ff_part)
    grad_out = [spread_rows(cotangent[0, s], parts) for s in range(count)]
    grad_act, glow_red = [], []
    for s in range(count):
        glow = mm_t(grad_out[s], out_red[s]).astype(BF16)
        glow_red.append(glow)
        grad_act.append((mm_t(grad_out[s], w_down) + mm(glow, in_red[s])).astype(BF16))

    layer_rows, grad_residual, grad_branch = [], [], []
    g_in_red, g_out_red, g_in_exp, g_out_exp = [], [], [], []
    for s in range(count):
        low_e = mm_t(hidden_two[s], in_exp[s]).astype(BF16)
        pre = mm(hidden_two[s], w_up_mine) + mm(low_e, out_exp[s]) + b_up_mine
        act, gelu_back = jax.vjp(lambda v: jax.nn.gelu(v, approximate=False), pre)
        act = act.astype(BF16)
        grad_pre = gelu_back(grad_act[s].astype(F32))[0].astype(BF16)
        glow_e = mm_t(grad_pre, out_exp[s]).astype(BF16)
        part = (mm_t(grad_pre, w_up_mine) + mm(glow_e, in_exp[s])).astype(BF16)
        grad_two = sum_rows(part, parts)
        g_res = cotangent[0, s].astype(F32) + norm_two_back[s](grad_two)[0]
        grad_residual.append(g_res)
        grad_branch.append(spread_rows(g_res.astype(BF16), parts))
        low_r = mm_t(act, in_red[s]).astype(BF16)
        part = (mm(act, w_down) + mm(low_r, out_red[s])).astype(BF16)
        layer_rows.append(residual[s] + sum_rows(part, parts) + b_down.astype(F32))
        g_in_red.append(t_mm(glow_red[s], act))
        g_out_exp.append(t_mm(low_e, grad_pre))
        g_out_red.append(t_mm(low_r, grad_out[s]))
        g_in_exp.append(t_mm(glow_e, hidden_two[s]))

    input_rows = []
    g_out_att, g_in_att, g_in_qkv, g_out_qkv = [], [], [], []
    for s in range(count):
        glow_a = mm_t(grad_branch[s], out_att[s]).astype(BF16)
        grad_att = (mm_t(grad_branch[s], w_out) + mm(glow_a, in_att[s])).astype(BF16)
        grad_qkv = attend_back(wheres[s], qkv[s], lses[s], grad_att, heads)
        glow = mm_t(grad_qkv, out_qkv[s]).astype(BF16)
        part = (mm_t(grad_qkv, w_qkv) + mm(glow, in_qkv[s])).astype(BF16)
        grad_one = sum_rows(part, parts)
        input_rows.append(grad_residual[s] + norm_one_back[s](grad_one)[0])
        g_in_att.append(t_mm(glow_a, attended[s]))
        g_out_att.append(t_mm(low_att[s], grad_branch[s]))
        g_in_qkv.append(t_mm(glow, hidden_one[s]))
        full = t_mm(low_qkv[s], grad_qkv)
        g_out_qkv.append([full[t * rank : (t + 1) * rank, t * span : (t + 1) * span] for t in range(3)])

    def sum_columns(value):
        width = value.shape[1] // size

        def side(which):
            return jnp.stack(
                [
                    lax.dynamic_slice_in_dim(value, (2 * k + which) * width, width, 1)
                    for k in range(size // 2)
                ]
            )

        core = me & 1
        current = side(core).astype(F32) + swap(side(1 - core).astype(BF16), "shard", 1).astype(F32)
        for bit in reversed(upper):
            current = current.reshape((2, current.shape[0] // 2) + current.shape[1:])
            own = (me // bit) & 1
            current = lax.dynamic_index_in_dim(current, own, 0, False) + swap(
                lax.dynamic_index_in_dim(current, 1 - own, 0, False).astype(BF16), "shard", bit
            ).astype(F32)
        return current[0]

    table = (chosen[:, None] == jnp.arange(ADAPTERS, dtype=jnp.int32)[None, :]).astype(BF16)

    def over_groups(wide):
        flat = [w.reshape(-1, span).astype(BF16) for w in wide]
        mark = jnp.zeros((16, span), BF16).at[:count, :ADAPTERS].set(table)
        payload = jnp.concatenate(flat + [mark], 0)
        every = gather_blocks(payload, "rep")
        groups = every.shape[0]
        marks = every[:, -16:][:, :count, :ADAPTERS].reshape(groups * count, ADAPTERS)
        outs, start = [], 0
        for w, f in zip(wide, flat):
            taken = every[:, start : start + f.shape[0]]
            start += f.shape[0]
            taken = taken.reshape(groups * count, -1)
            out = lax.dot_general(
                marks, taken, (((0,), (0,)), ((), ())), preferred_element_type=F32
            )
            outs.append(out.reshape((ADAPTERS,) + w.shape[1:]))
        return outs

    first = sum_columns(jnp.concatenate(g_out_att + g_in_exp + g_out_red, 0))
    first = first.reshape(3, count, rank, span)
    s_in_att, s_in_red, s_out_exp, s_out_att, s_in_exp, s_out_red = over_groups(
        [
            jnp.stack(g_in_att),
            jnp.stack(g_in_red),
            jnp.stack(g_out_exp),
            first[0],
            first[1],
            first[2],
        ]
    )
    second = sum_columns(jnp.concatenate(g_in_qkv, 0)).reshape(count, 3, rank, span)
    late = over_groups(
        [second[:, t] for t in range(3)]
        + [jnp.stack([g_out_qkv[s][t] for s in range(count)]) for t in range(3)]
    )
    return (
        jnp.stack(layer_rows).astype(BF16)[None],
        jnp.stack(input_rows).astype(BF16)[None],
        late[0],
        late[3],
        late[1],
        late[4],
        late[2],
        late[5],
        s_in_att,
        s_out_att,
        s_in_exp,
        s_out_exp,
        s_in_red,
        s_out_red,
    )


def solution(mesh):
    row = P("shard", None)
    wide = P(None, None, "shard")
    acts = P("rep", None, "shard", None)
    in_specs = (
        (acts, P(), P(), row, P(), row, row, P(), row, P(), P(), P(), row, P(), row, P())
        + (wide,) * 12
        + (P("rep", None), P("rep", None, None), acts)
    )
    out_specs = (acts, acts) + (wide,) * 12
    return jax.shard_map(
        on_device, mesh=mesh, in_specs=in_specs, out_specs=out_specs, check_vma=False
    )
```

```python
import functools

import jax
import jax.numpy as jnp
import numpy as np
from jax import lax
from jax.experimental import pallas as pl
from jax.experimental.pallas import tpu as pltpu
from jax.sharding import PartitionSpec as P

HEADS = 16
HEAD = 128
ADAPTERS = 8
PIECE = 256

EPSILON = 1e-05
MASKED = -1e30
F32 = jnp.float32
BF16 = jnp.bfloat16


def layer_norm(values, gain_vec, shift_vec):
    centre = jnp.mean(values, axis=-1, keepdims=True)
    offset = values - centre
    spread = jnp.mean(offset * offset, axis=-1, keepdims=True)
    return offset * lax.rsqrt(spread + EPSILON) * gain_vec + shift_vec


def piece_labels(starts, positions):
    inside = (positions[:, None] >= starts[None, :]) & (
        positions[:, None] < starts[None, :] + PIECE
    )
    labels = jnp.arange(1, starts.shape[0] + 1, dtype=jnp.int32)
    return jnp.sum(jnp.where(inside, labels[None, :], 0), axis=1)


def mm(a, b):
    return lax.dot_general(a, b, (((1,), (0,)), ((), ())), preferred_element_type=F32)


def mm_t(a, b):
    return lax.dot_general(a, b, (((1,), (1,)), ((), ())), preferred_element_type=F32)


def t_mm(a, b):
    return lax.dot_general(a, b, (((0,), (0,)), ((), ())), preferred_element_type=F32)


def swap(value, axis, mask):
    size = lax.axis_size(axis)
    return lax.ppermute(value, axis, [(i, i ^ mask) for i in range(size)])


def bits_of(size):
    bits = []
    while (1 << len(bits)) < size:
        bits.append(1 << len(bits))
    return bits


def subsets(bits):
    masks = [0]
    for bit in bits:
        masks = masks + [m | bit for m in masks]
    return masks


def gather_rows(block, bits):
    half = block.shape[0] // 2
    got = {0: [block]}
    upper, lower = {}, {}
    for bit in bits:
        there = swap(block, "shard", bit)
        got[bit] = [there]
        upper[bit], lower[bit] = there[:half], there[half:]
    for which, order in ((upper, bits), (lower, bits[::-1])):
        for k, bit in enumerate(order):
            for sub in subsets(order[:k])[1:]:
                which[sub | bit] = swap(which[sub], "shard", bit)
    pieces = []
    for mask in subsets(bits):
        pieces += got[mask] if mask in got else [upper[mask], lower[mask]]
    return jnp.concatenate(pieces, 0)


def scatter_rows(parts, bits):
    half = parts[0].shape[0] // 2
    upper = {m: p[:half] for m, p in parts.items()}
    lower = {m: p[half:] for m, p in parts.items()}
    for which, order in ((upper, bits), (lower, bits[::-1])):
        for k in reversed(range(len(order))):
            for sub in subsets(order[:k])[1:]:
                other = swap(which[sub | order[k]], "shard", order[k])
                which[sub] = (which[sub].astype(F32) + other.astype(F32)).astype(BF16)
    total = parts[0].astype(F32)
    for bit in bits:
        total = total + swap(jnp.concatenate([upper[bit], lower[bit]], 0), "shard", bit).astype(F32)
    return total


def gather_blocks(value, axis):
    current = value[None]
    for bit in bits_of(lax.axis_size(axis)):
        current = jnp.concatenate([current, swap(current, axis, bit)], 0)
    return current


def run_copies(copies):
    for copy in copies:
        copy.start()
    for copy in copies:
        copy.wait()


def place_kernel(me_ref, *refs, count, terms, width, rows, joined):
    pieces, outs, sems = refs[: 2 * count], refs[2 * count : -1], refs[-1]
    me = me_ref[0]

    def copies(core):
        made = []
        for side in range(2):
            for i in range(count):
                row = pl.multiple_of((me ^ (2 * i) ^ side) * rows, rows)
                piece = pieces[side * count + i]
                for term in range(terms):
                    for k in range(2):
                        own = k ^ core
                        source = piece.at[:, pl.ds((2 * term + k) * width, width)]
                        if joined:
                            target = outs[0].at[pl.ds(row, rows), pl.ds(own * width, width)]
                        else:
                            target = outs[own].at[pl.ds(row, rows), pl.ds(term * width, width)]
                        made.append(pltpu.make_async_copy(source, target, sems.at[len(made)]))
        return made

    @pl.when((me & 1) == 0)
    def _():
        run_copies(copies(0))

    @pl.when((me & 1) == 1)
    def _():
        run_copies(copies(1))


def place_weights(me, pieces, terms, width, joined):
    count = len(pieces) // 2
    rows = pieces[0].shape[0]
    if joined:
        shapes = [jax.ShapeDtypeStruct((rows * count * 2, 2 * width), BF16)]
    else:
        shapes = [jax.ShapeDtypeStruct((rows * count * 2, terms * width), BF16)] * 2
    return pl.pallas_call(
        functools.partial(
            place_kernel, count=count, terms=terms, width=width, rows=rows, joined=joined
        ),
        out_shape=shapes,
        in_specs=[pl.BlockSpec(memory_space=pltpu.SMEM)]
        + [pl.BlockSpec(memory_space=pl.ANY)] * (2 * count),
        out_specs=[pl.BlockSpec(memory_space=pltpu.VMEM)] * len(shapes),
        scratch_shapes=[pltpu.SemaphoreType.DMA((4 * count * terms,))],
        cost_estimate=pl.CostEstimate(
            flops=0, bytes_accessed=16 * rows * count * width * terms, transcendentals=0
        ),
        name="place_weights",
    )(me, *pieces)


def cols_kernel(me_ref, in_ref, out_ref, sems):
    count, _, width = in_ref.shape
    run_copies(
        [
            pltpu.make_async_copy(
                in_ref.at[mask],
                out_ref.at[:, pl.ds(pl.multiple_of((me_ref[0] ^ mask) * width, width), width)],
                sems.at[mask],
            )
            for mask in range(count)
        ]
    )


def place_columns(me, stacked):
    count, rows, width = stacked.shape
    return pl.pallas_call(
        cols_kernel,
        out_shape=jax.ShapeDtypeStruct((rows, count * width), stacked.dtype),
        in_specs=[pl.BlockSpec(memory_space=pltpu.SMEM), pl.BlockSpec(memory_space=pltpu.VMEM)],
        out_specs=pl.BlockSpec(memory_space=pltpu.VMEM),
        scratch_shapes=[pltpu.SemaphoreType.DMA((count,))],
        cost_estimate=pl.CostEstimate(
            flops=0, bytes_accessed=4 * count * rows * width, transcendentals=0
        ),
        name="place_columns",
    )(me, stacked)


def seen(pos_q, pos_k, lab_q, lab_k):
    return (pos_k <= pos_q) | ((lab_q == lab_k) & (lab_q > 0))


def both(own_ref, other_ref, low, high):
    own, other = own_ref[:, 0, :, low:high], other_ref[:, 0, :, low:high]
    chips, rows, width = own.shape
    return jnp.concatenate([own.reshape(chips * rows, width), other.reshape(chips * rows, width)], 0)


def put(own_ref, other_ref, low, high, value):
    chips, _, rows, _ = own_ref.shape
    half = chips * rows
    own_ref[:, 0, :, low:high] = value[:half].reshape(chips, rows, high - low)
    other_ref[:, 0, :, low:high] = value[half:].reshape(chips, rows, high - low)


def attend_kernel(pq, pk, lq, lk, own, other, out_own, out_other, lse_ref, *, heads, factor):
    allowed = seen(pq[...], pk[...], lq[0], lk[0])
    span = heads * HEAD
    for h in range(heads):
        low, high = h * HEAD, (h + 1) * HEAD
        q = both(own, other, low, high)
        k = both(own, other, span + low, span + high)
        v = both(own, other, 2 * span + low, 2 * span + high)
        scores = jnp.where(allowed, mm_t(q, k) * factor, MASKED)
        top = jnp.max(scores, axis=-1, keepdims=True)
        expo = jnp.exp(scores - top)
        total = jnp.sum(expo, axis=-1, keepdims=True)
        probs = (expo * (1.0 / total)).astype(BF16)
        put(out_own, out_other, low, high, mm(probs, v).astype(BF16))
        lse_ref[0, :, h : h + 1] = top + jnp.log(total)


def attend_specs(chips, count, rows, length):
    whole = pl.BlockSpec(memory_space=pltpu.VMEM)
    where = [
        pl.BlockSpec((length, 1), lambda s: (0, 0)),
        pl.BlockSpec((1, length), lambda s: (0, 0)),
        pl.BlockSpec((1, length, 1), lambda s: (s, 0, 0)),
        pl.BlockSpec((1, 1, length), lambda s: (s, 0, 0)),
    ]

    def of(width):
        return pl.BlockSpec((chips, 1, rows, width), lambda s: (0, s, 0, 0))

    return where, of


def attend(where, own, other, heads):
    chips, count, rows, _ = own.shape
    length = 2 * chips * rows
    span = heads * HEAD
    places, of = attend_specs(chips, count, rows, length)
    return pl.pallas_call(
        functools.partial(attend_kernel, heads=heads, factor=HEAD ** (-0.5)),
        out_shape=(
            jax.ShapeDtypeStruct((chips, count, rows, span), BF16),
            jax.ShapeDtypeStruct((chips, count, rows, span), BF16),
            jax.ShapeDtypeStruct((count, length, heads), F32),
        ),
        grid=(count,),
        in_specs=places + [of(3 * span), of(3 * span)],
        out_specs=(of(span), of(span), pl.BlockSpec((1, length, heads), lambda s: (s, 0, 0))),
        cost_estimate=pl.CostEstimate(
            flops=count * heads * length * length * HEAD * 4,
            bytes_accessed=count * length * heads * HEAD * 8,
            transcendentals=count * heads * length * length,
        ),
        name="attend",
    )(*where, own, other)


def attend_back_kernel(
    pq, pk, lq, lk, own, other, lse_ref, ga_own, ga_other, out_own, out_other, *, heads, factor
):
    allowed = seen(pq[...], pk[...], lq[0], lk[0])
    span = heads * HEAD
    for h in range(heads):
        low, high = h * HEAD, (h + 1) * HEAD
        q = both(own, other, low, high)
        k = both(own, other, span + low, span + high)
        v = both(own, other, 2 * span + low, 2 * span + high)
        ga = both(ga_own, ga_other, low, high)
        scores = jnp.where(allowed, mm_t(q, k) * factor, MASKED)
        probs = jnp.exp(scores - lse_ref[0, :, h : h + 1])
        grad_probs = mm_t(ga, v)
        inner = jnp.sum(probs * grad_probs, axis=-1, keepdims=True)
        grad_scores = (probs * (grad_probs - inner)).astype(BF16)
        put(out_own, out_other, low, high, (mm(grad_scores, k) * factor).astype(BF16))
        put(
            out_own,
            out_other,
            span + low,
            span + high,
            (t_mm(grad_scores, q) * factor).astype(BF16),
        )
        put(
            out_own,
            out_other,
            2 * span + low,
            2 * span + high,
            t_mm(probs.astype(BF16), ga).astype(BF16),
        )


def attend_back(where, own, other, lse, ga_own, ga_other, heads):
    chips, count, rows, _ = own.shape
    length = 2 * chips * rows
    span = heads * HEAD
    places, of = attend_specs(chips, count, rows, length)
    return pl.pallas_call(
        functools.partial(attend_back_kernel, heads=heads, factor=HEAD ** (-0.5)),
        out_shape=(jax.ShapeDtypeStruct((chips, count, rows, 3 * span), BF16),) * 2,
        grid=(count,),
        in_specs=places
        + [of(3 * span), of(3 * span)]
        + [pl.BlockSpec((1, length, heads), lambda s: (s, 0, 0)), of(span), of(span)],
        out_specs=(of(3 * span), of(3 * span)),
        cost_estimate=pl.CostEstimate(
            flops=count * heads * length * length * HEAD * 10,
            bytes_accessed=count * length * heads * HEAD * 14,
            transcendentals=count * heads * length * length,
        ),
        name="attend_back",
    )(*where, own, other, lse, ga_own, ga_other)


def on_device(
    inputs,
    ln1_gain,
    ln1_bias,
    w_query,
    b_query,
    w_key,
    w_value,
    b_value,
    w_out,
    b_out,
    ln2_gain,
    ln2_bias,
    w_up,
    b_up,
    w_down,
    b_down,
    in_query,
    out_query,
    in_key,
    out_key,
    in_value,
    out_value,
    in_attn,
    out_attn,
    in_expand,
    out_expand,
    in_reduce,
    out_reduce,
    adapter_pick,
    piece_start,
    cotangent,
):
    count, rows, wide = inputs.shape[1:]
    size = lax.axis_size("shard")
    chips = size // 2
    bits = bits_of(size)[1:]
    me = lax.axis_index("shard").astype(jnp.int32)
    me_arr = me[None]
    heads = HEADS // size
    span = heads * HEAD
    slice_wide = wide // size
    ff_part = w_up.shape[1] // size
    rank = in_query.shape[1]
    block = count * rows
    chosen = adapter_pick[0]
    starts = piece_start[0]

    def pick(table):
        return jnp.concatenate(
            [lax.dynamic_index_in_dim(table, chosen[s], 0, keepdims=False) for s in range(count)], 0
        )

    owners = np.concatenate([np.arange(chips) * 2, np.arange(chips) * 2 + 1]).astype(np.int32)
    locs = np.tile(np.arange(rows, dtype=np.int32), 2 * chips)
    positions = (me ^ jnp.asarray(np.repeat(owners, rows))) * rows + jnp.asarray(locs)
    labels = jnp.stack([piece_labels(starts[s], positions) for s in range(count)])
    where = (positions[:, None], positions[None, :], labels[:, :, None], labels[:, None, :])

    row_seq = np.tile(np.repeat(np.arange(count), rows), chips)

    def keep_own(value, terms=1):
        of_row = lax.broadcasted_iota(jnp.int32, value.shape, 0) // rows % count
        of_col = lax.broadcasted_iota(jnp.int32, value.shape, 1) // (terms * rank)
        return jnp.where(of_row == of_col, value, 0.0).astype(BF16)

    def with_other(value, axis=-1):
        return jnp.concatenate([value, swap(value, "shard", 1)], axis)

    gain_one, shift_one = ln1_gain.astype(F32), ln1_bias.astype(F32)
    gain_two, shift_two = ln2_gain.astype(F32), ln2_bias.astype(F32)

    features = inputs[0].reshape(block, wide).astype(F32)
    cot_mine = cotangent[0].reshape(block, wide)
    normed, norm_one_back = jax.vjp(lambda v: layer_norm(v, gain_one, shift_one), features)
    hidden_one = gather_rows(normed.astype(BF16), bits)

    chip = me // 2

    def turn(tables, width):
        own, other = [], []
        for i in range(chips):
            piece = [
                lax.dynamic_slice_in_dim(t, (chip ^ i) * 2 * width, 2 * width, 1) for t in tables
            ]
            piece = jnp.concatenate(piece, 1) if len(piece) > 1 else piece[0]
            own.append(swap(piece, "shard", 2 * i) if i else piece)
        for piece in own:
            other.append(swap(piece, "shard", 1))
        return own + other

    w_qkv_mine, w_qkv_other = place_weights(
        me_arr, turn([w_query, w_key, w_value], span), 3, span, False
    )

    mine = jnp.concatenate(
        [pick(t) for t in (in_query, in_key, in_value, in_expand, out_attn, out_reduce)], 0
    )
    whole = place_columns(me_arr, gather_blocks(mine, "shard")).reshape(6, count, rank, wide)
    in_qkv = jnp.swapaxes(whole[:3], 0, 1).reshape(count * 3 * rank, wide)
    in_exp, out_att, out_red = (whole[3 + i].reshape(count * rank, wide) for i in range(3))
    narrow = [pick(t) for t in (out_query, out_key, out_value, in_attn, out_expand, in_reduce)]
    packed = jnp.concatenate(narrow, 1)
    packed_other = swap(packed, "shard", 1)
    edges = np.cumsum([0] + [n.shape[1] for n in narrow])

    def unpack(table, i):
        return table[:, edges[i] : edges[i + 1]]

    def out_qkv_of(table):
        stacked = jnp.stack([unpack(table, t).reshape(count, rank, span) for t in range(3)], 1)
        spread = stacked[:, :, :, None, :] * jnp.eye(3, dtype=BF16)[None, :, None, :, None]
        return spread.reshape(count * 3 * rank, 3 * span)

    out_qkv_mine, out_qkv_other = out_qkv_of(packed), out_qkv_of(packed_other)
    in_att, out_exp, in_red = (
        jnp.concatenate([unpack(packed, i), unpack(packed_other, i)], 1) for i in (3, 4, 5)
    )

    def slice_of(bias, index, width):
        return lax.dynamic_slice_in_dim(bias, index * width, width).astype(F32)

    def b_qkv_of(index):
        return jnp.concatenate(
            [slice_of(b_query, index, span), jnp.zeros((span,), F32), slice_of(b_value, index, span)]
        )

    b_up_chip = jnp.concatenate([slice_of(b_up, me, ff_part), slice_of(b_up, me ^ 1, ff_part)])
    w_out_chip = with_other(w_out, 0)
    w_down_chip = with_other(w_down, 0)

    def by_chip(value):
        return value.reshape((chips, count, rows) + value.shape[1:])

    def flat(value):
        return value.reshape(chips * block, value.shape[-1])

    def project_back(value, low, weight, table, transposed):
        main = mm_t if transposed else mm
        parts = {}
        for i in reversed(range(chips)):
            at = slice(i * block, (i + 1) * block)
            parts[2 * i] = (main(value[at], weight) + mm(low[at], table)).astype(BF16)
        return scatter_rows(parts, bits)

    low_qkv = keep_own(mm_t(hidden_one, in_qkv), 3)
    qkv_away = (
        mm(hidden_one, w_qkv_other) + mm(low_qkv, out_qkv_other) + b_qkv_of(me ^ 1)
    ).astype(BF16)
    qkv_other = by_chip(swap(qkv_away, "shard", 1))
    qkv_own = by_chip(
        (mm(hidden_one, w_qkv_mine) + mm(low_qkv, out_qkv_mine) + b_qkv_of(me)).astype(BF16)
    )
    att_own, att_away, lse = attend(where, qkv_own, qkv_other, heads)
    attended = jnp.concatenate([flat(att_own), swap(flat(att_away), "shard", 1)], 1)
    low_att = keep_own(mm_t(attended, in_att))
    branch = project_back(attended, low_att, w_out_chip, out_att, False) + b_out.astype(F32)
    residual = features + branch
    normed, norm_two_back = jax.vjp(lambda v: layer_norm(v, gain_two, shift_two), residual)
    hidden_two = gather_rows(normed.astype(BF16), bits)

    (w_up_chip,) = place_weights(me_arr, turn([w_up], ff_part), 1, ff_part, True)
    cot = gather_rows(cot_mine, bits)
    glow_red = keep_own(mm_t(cot, out_red))
    grad_act = mm_t(cot, w_down_chip) + mm(glow_red, in_red)
    low_exp = keep_own(mm_t(hidden_two, in_exp))
    pre = mm(hidden_two, w_up_chip) + mm(low_exp, out_exp) + b_up_chip
    share = 0.5 * (1.0 + lax.erf(pre * np.float32(0.5**0.5)))
    act = (pre * share).astype(BF16)
    slope = share + pre * (jnp.exp(-0.5 * pre * pre) * np.float32((2 * np.pi) ** -0.5))
    grad_pre = (slope * grad_act).astype(BF16)
    glow_exp = keep_own(mm_t(grad_pre, out_exp))
    grad_two = project_back(grad_pre, glow_exp, w_up_chip, in_exp, True)
    grad_residual = cot_mine.astype(F32) + norm_two_back(grad_two)[0]
    grad_branch = gather_rows(grad_residual.astype(BF16), bits)

    low_red = keep_own(mm_t(act, in_red))
    down = project_back(act, low_red, w_down_chip, out_red, False)
    layer_rows = residual + down + b_down.astype(F32)

    glow_att = keep_own(mm_t(grad_branch, out_att))
    grad_att = (mm_t(grad_branch, w_out_chip) + mm(glow_att, in_att)).astype(BF16)
    ga_own = by_chip(grad_att[:, :span])
    ga_other = by_chip(swap(grad_att[:, span:], "shard", 1))
    grad_own, grad_away = attend_back(where, qkv_own, qkv_other, lse, ga_own, ga_other, heads)
    grad_own = flat(grad_own)
    grad_other = swap(flat(grad_away), "shard", 1)
    glow_qkv = keep_own(mm_t(grad_own, out_qkv_mine) + mm_t(grad_other, out_qkv_other), 3)
    parts = {}
    for i in reversed(range(chips)):
        at = slice(i * block, (i + 1) * block)
        parts[2 * i] = (
            mm_t(grad_own[at], w_qkv_mine)
            + mm_t(grad_other[at], w_qkv_other)
            + mm(glow_qkv[at], in_qkv)
        ).astype(BF16)
    grad_one = scatter_rows(parts, bits)
    input_rows = grad_residual + norm_one_back(grad_one)[0]

    def sum_columns(value):
        width = value.shape[1] // size

        def side(which):
            return jnp.stack(
                [
                    lax.dynamic_slice_in_dim(value, (2 * k + which) * width, width, 1)
                    for k in range(chips)
                ]
            )

        core = me & 1
        current = side(core).astype(F32) + swap(side(1 - core).astype(BF16), "shard", 1).astype(F32)
        for bit in bits[::-1]:
            current = current.reshape((2, current.shape[0] // 2) + current.shape[1:])
            own = (me // bit) & 1
            current = lax.dynamic_index_in_dim(current, own, 0, False) + swap(
                lax.dynamic_index_in_dim(current, 1 - own, 0, False).astype(BF16), "shard", bit
            ).astype(F32)
        return current[0]

    def sum_cores(own, away):
        return own + swap(away.astype(BF16), "shard", 1).astype(F32)

    def over_groups(terms):
        widths = [t.shape[1] for t in terms]
        data = jnp.concatenate([t.astype(BF16) for t in terms], 1)
        mark = (chosen[:, None] == jnp.arange(ADAPTERS, dtype=jnp.int32)[None, :]).astype(BF16)
        mark = jnp.pad(mark, ((0, 16 - count), (0, data.shape[1] - ADAPTERS)))
        every = gather_blocks(jnp.concatenate([data, mark], 0), "rep")
        groups = every.shape[0]
        marks = every[:, count * rank : count * rank + count, :ADAPTERS]
        marks = marks.reshape(groups * count, 1, ADAPTERS, 1)
        place = marks * jnp.eye(rank, dtype=BF16)[None, :, None, :]
        place = place.reshape(groups * count * rank, ADAPTERS * rank)
        taken = every[:, : count * rank].reshape(groups * count * rank, -1)
        outs, start = [], 0
        for width in widths:
            out = t_mm(place, taken[:, start : start + width])
            outs.append(out.reshape(ADAPTERS, rank, width))
            start += width
        return outs

    first = sum_columns(
        jnp.concatenate(
            [t_mm(low_att, grad_branch), t_mm(glow_exp, hidden_two), t_mm(low_red, cot)], 0
        )
    ).reshape(3, count * rank, slice_wide)
    chip_wide = jnp.concatenate(
        [t_mm(glow_att, attended), t_mm(glow_red, act), t_mm(low_exp, grad_pre)], 1
    )
    cut = [0, span, 2 * span, 2 * span + ff_part, 2 * span + 2 * ff_part, 2 * span + 3 * ff_part]
    cut.append(chip_wide.shape[1])
    side = [chip_wide[:, cut[i] : cut[i + 1]] for i in range(6)]
    local = sum_cores(jnp.concatenate(side[::2], 1), jnp.concatenate(side[1::2], 1))
    s_in_att, s_in_red, s_out_exp, s_out_att, s_in_exp, s_out_red = over_groups(
        [
            local[:, :span],
            local[:, span : span + ff_part],
            local[:, span + ff_part :],
            first[0],
            first[1],
            first[2],
        ]
    )

    second = sum_columns(t_mm(glow_qkv, hidden_one)).reshape(count, 3, rank, slice_wide)

    def own_terms(full):
        full = full.reshape(count, 3, rank, 3, span)
        return jnp.concatenate(
            [full[:, t, :, t].reshape(count * rank, span) for t in range(3)], 1
        )

    outer = sum_cores(own_terms(t_mm(low_qkv, grad_own)), own_terms(t_mm(low_qkv, grad_other)))
    late = over_groups(
        [second[:, t].reshape(count * rank, slice_wide) for t in range(3)]
        + [outer[:, t * span : (t + 1) * span] for t in range(3)]
    )
    shape = (1, count, rows, wide)
    return (
        layer_rows.astype(BF16).reshape(shape),
        input_rows.astype(BF16).reshape(shape),
        late[0],
        late[3],
        late[1],
        late[4],
        late[2],
        late[5],
        s_in_att,
        s_out_att,
        s_in_exp,
        s_out_exp,
        s_in_red,
        s_out_red,
    )


def solution(mesh):
    row = P("shard", None)
    wide = P(None, None, "shard")
    acts = P("rep", None, "shard", None)
    in_specs = (
        (acts, P(), P(), row, P(), row, row, P(), row, P(), P(), P(), row, P(), row, P())
        + (wide,) * 12
        + (P("rep", None), P("rep", None, None), acts)
    )
    out_specs = (acts, acts) + (wide,) * 12
    return jax.shard_map(
        on_device, mesh=mesh, in_specs=in_specs, out_specs=out_specs, check_vma=False
    )
```

```python
import functools

import jax
import jax.numpy as jnp
import numpy as np
from jax import lax
from jax.experimental import pallas as pl
from jax.experimental.pallas import tpu as pltpu
from jax.sharding import PartitionSpec as P

HEADS = 16
HEAD = 128
ADAPTERS = 8
PIECE = 256

EPSILON = 1e-05
MASKED = -1e30
F32 = jnp.float32
BF16 = jnp.bfloat16


def layer_norm(values, gain_vec, shift_vec):
    centre = jnp.mean(values, axis=-1, keepdims=True)
    offset = values - centre
    spread = jnp.mean(offset * offset, axis=-1, keepdims=True)
    return offset * lax.rsqrt(spread + EPSILON) * gain_vec + shift_vec


def piece_labels(starts, positions):
    inside = (positions[:, None] >= starts[None, :]) & (
        positions[:, None] < starts[None, :] + PIECE
    )
    labels = jnp.arange(1, starts.shape[0] + 1, dtype=jnp.int32)
    return jnp.sum(jnp.where(inside, labels[None, :], 0), axis=1)


def mm(a, b):
    return lax.dot_general(a, b, (((1,), (0,)), ((), ())), preferred_element_type=F32)


def mm_t(a, b):
    return lax.dot_general(a, b, (((1,), (1,)), ((), ())), preferred_element_type=F32)


def t_mm(a, b):
    return lax.dot_general(a, b, (((0,), (0,)), ((), ())), preferred_element_type=F32)


def swap(value, axis, mask):
    size = lax.axis_size(axis)
    return lax.ppermute(value, axis, [(i, i ^ mask) for i in range(size)])


def after(value, *others):
    return lax.optimization_barrier((value,) + others)[0]


def bits_of(size):
    bits = []
    while (1 << len(bits)) < size:
        bits.append(1 << len(bits))
    return bits


def subsets(bits):
    masks = [0]
    for bit in bits:
        masks = masks + [m | bit for m in masks]
    return masks


def gather_rows(block, bits):
    half = block.shape[0] // 2
    got = {0: [block]}
    upper, lower = {}, {}
    for bit in bits:
        there = swap(block, "shard", bit)
        got[bit] = [there]
        upper[bit], lower[bit] = there[:half], there[half:]
    for which, order in ((upper, bits), (lower, bits[::-1])):
        for k, bit in enumerate(order):
            for sub in subsets(order[:k])[1:]:
                which[sub | bit] = swap(which[sub], "shard", bit)
    pieces = []
    for mask in subsets(bits):
        pieces += got[mask] if mask in got else [upper[mask], lower[mask]]
    return jnp.concatenate(pieces, 0), pieces[1], pieces[-1]


def scatter_rows(parts, bits, gate=()):
    half = parts[0].shape[0] // 2
    upper = {m: p[:half] for m, p in parts.items()}
    lower = {m: p[half:] for m, p in parts.items()}
    for which, order in ((upper, bits), (lower, bits[::-1])):
        for k in reversed(range(len(order))):
            for sub in subsets(order[:k])[1:]:
                other = swap(which[sub | order[k]], "shard", order[k])
                other = after(other, *gate) if gate else other
                which[sub] = (which[sub].astype(F32) + other.astype(F32)).astype(BF16)
    total = parts[0].astype(F32)
    for bit in bits:
        total = total + swap(jnp.concatenate([upper[bit], lower[bit]], 0), "shard", bit).astype(F32)
    return total


def gather_blocks(value, axis, bits, gates=None):
    current = value[None]
    for bit in bits:
        there = swap(current, axis, bit)
        if gates:
            there = after(there, *gates[bit])
        current = jnp.concatenate([current, there], 0)
    return current


def run_copies(copies):
    for copy in copies:
        copy.start()
    for copy in copies:
        copy.wait()


def place_kernel(me_ref, *refs, count, width, rows, joined):
    pieces, outs, sems = refs[: 2 * count], refs[2 * count : -1], refs[-1]
    me = me_ref[0]

    def copies(core):
        made = []
        for side in range(2):
            for i in range(count):
                row = pl.multiple_of((me ^ (2 * i) ^ side) * rows, rows)
                piece = pieces[side * count + i]
                for k in range(2):
                    own = k ^ core
                    source = piece.at[:, pl.ds(k * width, width)]
                    if joined:
                        target = outs[0].at[pl.ds(row, rows), pl.ds(own * width, width)]
                    else:
                        target = outs[own].at[pl.ds(row, rows)]
                    made.append(pltpu.make_async_copy(source, target, sems.at[len(made)]))
        return made

    @pl.when((me & 1) == 0)
    def _():
        run_copies(copies(0))

    @pl.when((me & 1) == 1)
    def _():
        run_copies(copies(1))


def place_weights(me, pieces, width, joined):
    count = len(pieces) // 2
    rows = pieces[0].shape[0]
    if joined:
        shapes = [jax.ShapeDtypeStruct((rows * count * 2, 2 * width), BF16)]
    else:
        shapes = [jax.ShapeDtypeStruct((rows * count * 2, width), BF16)] * 2
    return pl.pallas_call(
        functools.partial(
            place_kernel, count=count, width=width, rows=rows, joined=joined
        ),
        out_shape=shapes,
        in_specs=[pl.BlockSpec(memory_space=pltpu.SMEM)]
        + [pl.BlockSpec(memory_space=pl.ANY)] * (2 * count),
        out_specs=[pl.BlockSpec(memory_space=pltpu.VMEM)] * len(shapes),
        scratch_shapes=[pltpu.SemaphoreType.DMA((4 * count,))],
        cost_estimate=pl.CostEstimate(
            flops=0, bytes_accessed=16 * rows * count * width, transcendentals=0
        ),
        name="place_weights",
    )(me, *pieces)


def pick_kernel(chosen_ref, *refs, tall, rank):
    tables, (tall_ref, flat_ref, sems) = refs[:-3], refs[-3:]
    count = chosen_ref.shape[0]
    copies = []
    for s in range(count):
        column = 0
        for i, table in enumerate(tables):
            if i < tall:
                target = tall_ref.at[pl.ds((i * count + s) * rank, rank)]
            else:
                width = table.shape[2]
                target = flat_ref.at[pl.ds(s * rank, rank), pl.ds(column, width)]
                column += width
            copies.append(
                pltpu.make_async_copy(table.at[chosen_ref[s]], target, sems.at[len(copies)])
            )
    run_copies(copies)


def pick_maps(chosen, upright, flat):
    count, rank = chosen.shape[0], upright[0].shape[1]
    total = sum(t.shape[2] for t in flat)
    shapes = (
        jax.ShapeDtypeStruct((len(upright) * count * rank, upright[0].shape[2]), BF16),
        jax.ShapeDtypeStruct((count * rank, total), BF16),
    )
    tables = upright + flat
    return pl.pallas_call(
        functools.partial(pick_kernel, tall=len(upright), rank=rank),
        out_shape=shapes,
        in_specs=[pl.BlockSpec(memory_space=pltpu.SMEM)]
        + [pl.BlockSpec(memory_space=pl.ANY)] * len(tables),
        out_specs=[pl.BlockSpec(memory_space=pltpu.VMEM)] * 2,
        scratch_shapes=[pltpu.SemaphoreType.DMA((count * len(tables),))],
        cost_estimate=pl.CostEstimate(
            flops=0, bytes_accessed=8 * count * rank * total, transcendentals=0
        ),
        name="pick_maps",
    )(chosen, *tables)


def cols_kernel(me_ref, in_ref, out_ref, sems, *, masks):
    width = in_ref.shape[2]
    run_copies(
        [
            pltpu.make_async_copy(
                in_ref.at[i],
                out_ref.at[:, pl.ds(pl.multiple_of((me_ref[0] ^ mask) * width, width), width)],
                sems.at[i],
            )
            for i, mask in enumerate(masks)
        ]
    )


def place_columns(me, stacked, masks):
    count, rows, width = stacked.shape
    return pl.pallas_call(
        functools.partial(cols_kernel, masks=masks),
        out_shape=jax.ShapeDtypeStruct((rows, count * width), stacked.dtype),
        in_specs=[pl.BlockSpec(memory_space=pltpu.SMEM), pl.BlockSpec(memory_space=pltpu.VMEM)],
        out_specs=pl.BlockSpec(memory_space=pltpu.VMEM),
        scratch_shapes=[pltpu.SemaphoreType.DMA((count,))],
        cost_estimate=pl.CostEstimate(
            flops=0, bytes_accessed=4 * count * rows * width, transcendentals=0
        ),
        name="place_columns",
    )(me, stacked)


def seen(pos_q, pos_k, lab_q, lab_k):
    return (pos_k <= pos_q) | ((lab_q == lab_k) & (lab_q > 0))


def both(own_ref, other_ref, low, high):
    own, other = own_ref[:, 0, :, low:high], other_ref[:, 0, :, low:high]
    chips, rows, width = own.shape
    return jnp.concatenate([own.reshape(chips * rows, width), other.reshape(chips * rows, width)], 0)


def put(own_ref, other_ref, low, high, value):
    chips, _, rows, _ = own_ref.shape
    half = chips * rows
    own_ref[:, 0, :, low:high] = value[:half].reshape(chips, rows, high - low)
    other_ref[:, 0, :, low:high] = value[half:].reshape(chips, rows, high - low)


def attend_kernel(pq, pk, lq, lk, own, other, out_own, out_other, lse_ref, *, heads, factor):
    allowed = seen(pq[...], pk[...], lq[0], lk[0])
    span = heads * HEAD
    for h in range(heads):
        low, high = h * HEAD, (h + 1) * HEAD
        q = both(own, other, low, high)
        k = both(own, other, span + low, span + high)
        v = both(own, other, 2 * span + low, 2 * span + high)
        scores = jnp.where(allowed, mm_t(q, k) * factor, MASKED)
        top = jnp.max(scores, axis=-1, keepdims=True)
        expo = jnp.exp(scores - top)
        total = jnp.sum(expo, axis=-1, keepdims=True)
        probs = (expo * (1.0 / total)).astype(BF16)
        put(out_own, out_other, low, high, mm(probs, v).astype(BF16))
        lse_ref[0, :, h : h + 1] = top + jnp.log(total)


def attend_specs(chips, count, rows, length):
    whole = pl.BlockSpec(memory_space=pltpu.VMEM)
    where = [
        pl.BlockSpec((length, 1), lambda s: (0, 0)),
        pl.BlockSpec((1, length), lambda s: (0, 0)),
        pl.BlockSpec((1, length, 1), lambda s: (s, 0, 0)),
        pl.BlockSpec((1, 1, length), lambda s: (s, 0, 0)),
    ]

    def of(width):
        return pl.BlockSpec((chips, 1, rows, width), lambda s: (0, s, 0, 0))

    return where, of


def attend(where, own, other, heads):
    chips, count, rows, _ = own.shape
    length = 2 * chips * rows
    span = heads * HEAD
    places, of = attend_specs(chips, count, rows, length)
    return pl.pallas_call(
        functools.partial(attend_kernel, heads=heads, factor=HEAD ** (-0.5)),
        out_shape=(
            jax.ShapeDtypeStruct((chips, count, rows, span), BF16),
            jax.ShapeDtypeStruct((chips, count, rows, span), BF16),
            jax.ShapeDtypeStruct((count, length, heads), F32),
        ),
        grid=(count,),
        in_specs=places + [of(3 * span), of(3 * span)],
        out_specs=(of(span), of(span), pl.BlockSpec((1, length, heads), lambda s: (s, 0, 0))),
        cost_estimate=pl.CostEstimate(
            flops=count * heads * length * length * HEAD * 4,
            bytes_accessed=count * length * heads * HEAD * 8,
            transcendentals=count * heads * length * length,
        ),
        name="attend",
    )(*where, own, other)


def attend_back_kernel(
    pq, pk, lq, lk, own, other, lse_ref, ga_own, ga_other, out_own, out_other, *, heads, factor
):
    allowed = seen(pq[...], pk[...], lq[0], lk[0])
    span = heads * HEAD
    for h in range(heads):
        low, high = h * HEAD, (h + 1) * HEAD
        q = both(own, other, low, high)
        k = both(own, other, span + low, span + high)
        v = both(own, other, 2 * span + low, 2 * span + high)
        ga = both(ga_own, ga_other, low, high)
        scores = jnp.where(allowed, mm_t(q, k) * factor, MASKED)
        probs = jnp.exp(scores - lse_ref[0, :, h : h + 1])
        grad_probs = mm_t(ga, v)
        inner = jnp.sum(probs * grad_probs, axis=-1, keepdims=True)
        grad_scores = (probs * (grad_probs - inner)).astype(BF16)
        put(out_own, out_other, low, high, (mm(grad_scores, k) * factor).astype(BF16))
        put(
            out_own,
            out_other,
            span + low,
            span + high,
            (t_mm(grad_scores, q) * factor).astype(BF16),
        )
        put(
            out_own,
            out_other,
            2 * span + low,
            2 * span + high,
            t_mm(probs.astype(BF16), ga).astype(BF16),
        )


def attend_back(where, own, other, lse, ga_own, ga_other, heads):
    chips, count, rows, _ = own.shape
    length = 2 * chips * rows
    span = heads * HEAD
    places, of = attend_specs(chips, count, rows, length)
    return pl.pallas_call(
        functools.partial(attend_back_kernel, heads=heads, factor=HEAD ** (-0.5)),
        out_shape=(jax.ShapeDtypeStruct((chips, count, rows, 3 * span), BF16),) * 2,
        grid=(count,),
        in_specs=places
        + [of(3 * span), of(3 * span)]
        + [pl.BlockSpec((1, length, heads), lambda s: (s, 0, 0)), of(span), of(span)],
        out_specs=(of(3 * span), of(3 * span)),
        cost_estimate=pl.CostEstimate(
            flops=count * heads * length * length * HEAD * 10,
            bytes_accessed=count * length * heads * HEAD * 14,
            transcendentals=count * heads * length * length,
        ),
        name="attend_back",
    )(*where, own, other, lse, ga_own, ga_other)


def on_device(
    inputs,
    ln1_gain,
    ln1_bias,
    w_query,
    b_query,
    w_key,
    w_value,
    b_value,
    w_out,
    b_out,
    ln2_gain,
    ln2_bias,
    w_up,
    b_up,
    w_down,
    b_down,
    in_query,
    out_query,
    in_key,
    out_key,
    in_value,
    out_value,
    in_attn,
    out_attn,
    in_expand,
    out_expand,
    in_reduce,
    out_reduce,
    adapter_pick,
    piece_start,
    cotangent,
):
    count, rows, wide = inputs.shape[1:]
    size = lax.axis_size("shard")
    chips = size // 2
    bits = bits_of(size)[1:]
    me = lax.axis_index("shard").astype(jnp.int32)
    me_arr = me[None]
    heads = HEADS // size
    span = heads * HEAD
    slice_wide = wide // size
    ff_part = w_up.shape[1] // size
    rank = in_query.shape[1]
    block = count * rows
    chosen = adapter_pick[0]
    starts = piece_start[0]

    owners = np.concatenate([np.arange(chips) * 2, np.arange(chips) * 2 + 1]).astype(np.int32)
    locs = np.tile(np.arange(rows, dtype=np.int32), 2 * chips)
    positions = (me ^ jnp.asarray(np.repeat(owners, rows))) * rows + jnp.asarray(locs)
    labels = jnp.stack([piece_labels(starts[s], positions) for s in range(count)])
    where = (positions[:, None], positions[None, :], labels[:, :, None], labels[:, None, :])

    row_seq = np.tile(np.repeat(np.arange(count), rows), chips)

    def keep_own(value, terms=1):
        of_row = lax.broadcasted_iota(jnp.int32, value.shape, 0) // rows % count
        of_col = lax.broadcasted_iota(jnp.int32, value.shape, 1) // (terms * rank)
        return jnp.where(of_row == of_col, value, 0.0).astype(BF16)

    gain_one, shift_one = ln1_gain.astype(F32), ln1_bias.astype(F32)
    gain_two, shift_two = ln2_gain.astype(F32), ln2_bias.astype(F32)

    narrow = [out_query, out_key, out_value, in_attn, out_expand, in_reduce]
    edges = np.cumsum([0] + [n.shape[2] for n in narrow])
    mine, packed = pick_maps(
        chosen, [in_query, in_key, in_value, in_expand, out_attn, out_reduce], narrow
    )
    packed_other = swap(packed, "shard", 1)
    order = bits + [1]
    near = gather_blocks(mine, "shard", bits)
    stacked = jnp.concatenate([near, swap(near, "shard", 1)], 0)
    w_out_other = swap(w_out, "shard", 1)
    w_down_other = swap(w_down, "shard", 1)

    chip = me // 2

    def slices(tables, width):
        pieces = []
        for i in range(chips):
            both = [
                lax.dynamic_slice_in_dim(t, (chip ^ i) * 2 * width, 2 * width, 1) for t in tables
            ]
            if len(both) > 1:
                both = jnp.concatenate(
                    [t[:, k * width : (k + 1) * width] for k in range(2) for t in both], 1
                )
            else:
                both = both[0]
            pieces.append(both)
        return pieces

    def turn(pieces):
        own = [swap(piece, "shard", 2 * i) if i else piece for i, piece in enumerate(pieces)]
        return own + [swap(piece, "shard", 1) for piece in own]

    first_tables = after((w_query, w_key, w_value), mine)
    pieces_qkv = after(
        tuple(slices(first_tables, span)), near, packed_other, w_out_other, w_down_other
    )
    turned = turn(pieces_qkv)
    w_qkv_mine, w_qkv_other = place_weights(me_arr, turned, 3 * span, False)

    features = after(inputs[0].reshape(block, wide), *pieces_qkv).astype(F32)
    normed, norm_one_back = jax.vjp(lambda v: layer_norm(v, gain_one, shift_one), features)
    hidden_block = after(normed.astype(BF16), *[turned[bit // 2] for bit in bits])
    hidden_one, one_first, one_last = gather_rows(hidden_block, bits)

    cot_mine = cotangent[0].reshape(block, wide)
    cot, cot_first, cot_last = gather_rows(after(cot_mine, one_first), bits)
    pieces_up = slices([after(w_up, one_last, cot_first)], ff_part)

    whole = place_columns(me_arr, stacked, subsets(order)).reshape(6, count, rank, wide)
    in_qkv = jnp.swapaxes(whole[:3], 0, 1).reshape(count * 3 * rank, wide)
    in_exp, out_att, out_red = (whole[3 + i].reshape(count * rank, wide) for i in range(3))

    rep_bits = bits_of(lax.axis_size("rep"))
    mark = (chosen[:, None] == jnp.arange(ADAPTERS, dtype=jnp.int32)[None, :]).astype(BF16)
    marks = gather_blocks(jnp.pad(mark, ((0, 16 - count), (0, 128 - ADAPTERS))), "rep", rep_bits)
    groups = marks.shape[0]
    marks = marks[:, :count, :ADAPTERS].reshape(groups * count, 1, ADAPTERS, 1)
    place = (marks * jnp.eye(rank, dtype=BF16)[None, :, None, :]).reshape(
        groups * count * rank, ADAPTERS * rank
    )

    def unpack(table, i):
        return table[:, edges[i] : edges[i + 1]]

    def out_qkv_of(table):
        stacked = jnp.stack([unpack(table, t).reshape(count, rank, span) for t in range(3)], 1)
        spread = stacked[:, :, :, None, :] * jnp.eye(3, dtype=BF16)[None, :, None, :, None]
        return spread.reshape(count * 3 * rank, 3 * span)

    out_qkv_mine, out_qkv_other = out_qkv_of(packed), out_qkv_of(packed_other)
    in_att, out_exp, in_red = (
        jnp.concatenate([unpack(packed, i), unpack(packed_other, i)], 1) for i in (3, 4, 5)
    )

    def slice_of(bias, index, width):
        return lax.dynamic_slice_in_dim(bias, index * width, width).astype(F32)

    def b_qkv_of(index):
        return jnp.concatenate(
            [slice_of(b_query, index, span), jnp.zeros((span,), F32), slice_of(b_value, index, span)]
        )

    b_up_chip = jnp.concatenate([slice_of(b_up, me, ff_part), slice_of(b_up, me ^ 1, ff_part)])
    w_out_chip = jnp.concatenate([w_out, w_out_other], 0)
    w_down_chip = jnp.concatenate([w_down, w_down_other], 0)

    def by_chip(value):
        return value.reshape((chips, count, rows) + value.shape[1:])

    def flat(value):
        return value.reshape(chips * block, value.shape[-1])

    def block_products(products, low, table):
        parts = {}
        for i in reversed(range(chips)):
            at = slice(i * block, (i + 1) * block)
            total = mm(low[at], table)
            for value, weight, main in products:
                total = total + main(value[at], weight)
            parts[2 * i] = total.astype(BF16)
        return parts

    low_qkv = keep_own(mm_t(hidden_one, in_qkv), 3)
    qkv_away = (
        mm(hidden_one, w_qkv_other) + mm(low_qkv, out_qkv_other) + b_qkv_of(me ^ 1)
    ).astype(BF16)
    qkv_other = by_chip(swap(qkv_away, "shard", 1))
    qkv_own = by_chip(
        (mm(hidden_one, w_qkv_mine) + mm(low_qkv, out_qkv_mine) + b_qkv_of(me)).astype(BF16)
    )
    att_own, att_away, lse = attend(where, qkv_own, qkv_other, heads)
    attended = jnp.concatenate([flat(att_own), swap(flat(att_away), "shard", 1)], 1)
    low_att = keep_own(mm_t(attended, in_att))
    glow_red = keep_own(mm_t(cot, out_red))
    grad_act = (mm_t(cot, w_down_chip) + mm(glow_red, in_red)).astype(BF16)
    parts = block_products([(attended, w_out_chip, mm)], low_att, out_att)
    parts[0] = after(parts[0], grad_act)
    branch = scatter_rows(parts, bits) + b_out.astype(F32)
    residual = features + branch
    normed, norm_two_back = jax.vjp(lambda v: layer_norm(v, gain_two, shift_two), residual)
    hidden_two, _, _ = gather_rows(normed.astype(BF16), bits)

    (w_up_chip,) = place_weights(me_arr, turn(pieces_up), ff_part, True)
    low_exp = keep_own(mm_t(hidden_two, in_exp))
    pre = mm(hidden_two, w_up_chip) + mm(low_exp, out_exp) + b_up_chip
    share = 0.5 * (1.0 + lax.erf(pre * np.float32(0.5**0.5)))
    act = (pre * share).astype(BF16)
    slope = share + pre * (jnp.exp(-0.5 * pre * pre) * np.float32((2 * np.pi) ** -0.5))
    grad_pre = (slope * grad_act.astype(F32)).astype(BF16)
    glow_exp = keep_own(mm_t(grad_pre, out_exp))
    grad_two = scatter_rows(block_products([(grad_pre, w_up_chip, mm_t)], glow_exp, in_exp), bits)
    grad_residual = cot_mine.astype(F32) + norm_two_back(grad_two)[0]
    grad_block = grad_residual.astype(BF16)
    grad_branch, _, branch_last = gather_rows(grad_block, bits)

    act_late = after(act, grad_block)
    low_red = keep_own(mm_t(act_late, in_red))
    down_parts = block_products([(act_late, w_down_chip, mm)], low_red, out_red)
    down_parts = {m: after(p, branch_last) for m, p in down_parts.items()}
    glow_att = keep_own(mm_t(grad_branch, out_att))
    grad_att = (mm_t(grad_branch, w_out_chip) + mm(glow_att, in_att)).astype(BF16)
    ga_own = by_chip(grad_att[:, :span])
    ga_other = by_chip(swap(grad_att[:, span:], "shard", 1))
    grad_own, grad_away = attend_back(where, qkv_own, qkv_other, lse, ga_own, ga_other, heads)
    grad_own = flat(grad_own)
    grad_other = swap(flat(grad_away), "shard", 1)
    glow_qkv = keep_own(mm_t(grad_own, out_qkv_mine) + mm_t(grad_other, out_qkv_other), 3)
    def sum_columns(value, gates=None):
        width = value.shape[1] // size

        def side(which):
            return jnp.stack(
                [
                    lax.dynamic_slice_in_dim(value, (2 * k + which) * width, width, 1)
                    for k in range(chips)
                ]
            )

        core = me & 1
        current = side(core).astype(F32) + swap(side(1 - core).astype(BF16), "shard", 1).astype(F32)
        for bit in bits[::-1]:
            current = current.reshape((2, current.shape[0] // 2) + current.shape[1:])
            own = (me // bit) & 1
            there = swap(
                lax.dynamic_index_in_dim(current, 1 - own, 0, False).astype(BF16), "shard", bit
            )
            if gates:
                there = after(there, *gates[bit])
            current = lax.dynamic_index_in_dim(current, own, 0, False) + there.astype(F32)
        return current[0]

    def sum_cores(own, away):
        return own + swap(away.astype(BF16), "shard", 1).astype(F32)

    def over_groups(terms, gates=None):
        widths = [t.shape[1] for t in terms]
        data = jnp.concatenate([t.astype(BF16) for t in terms], 1)
        taken = gather_blocks(data, "rep", rep_bits, gates).reshape(groups * count * rank, -1)
        outs, start = [], 0
        for width in widths:
            out = t_mm(place, taken[:, start : start + width])
            outs.append(out.reshape(ADAPTERS, rank, width))
            start += width
        return outs

    glow_late, low_late = after((glow_exp, low_exp), grad_block)
    arrived = {bit: (grad_away,) for bit in bits}
    first = sum_columns(
        jnp.concatenate(
            [t_mm(low_att, grad_branch), t_mm(glow_late, hidden_two), t_mm(low_red, cot)], 0
        ),
        arrived,
    ).reshape(3, count * rank, slice_wide)
    chip_wide = jnp.concatenate(
        [t_mm(glow_att, attended), t_mm(glow_red, act_late), t_mm(low_late, grad_pre)], 1
    )
    cut = [0, span, 2 * span, 2 * span + ff_part, 2 * span + 2 * ff_part, 2 * span + 3 * ff_part]
    cut.append(chip_wide.shape[1])
    side = [chip_wide[:, cut[i] : cut[i + 1]] for i in range(6)]
    local = sum_cores(jnp.concatenate(side[::2], 1), jnp.concatenate(side[1::2], 1))
    products = [(grad_own, w_qkv_mine, mm_t), (grad_other, w_qkv_other, mm_t)]
    parts = block_products(products, glow_qkv, in_qkv)
    far_part = parts[2 * (chips - 1)]
    early = over_groups(
        [
            local[:, :span],
            local[:, span : span + ff_part],
            local[:, span + ff_part :],
            first[0],
            first[1],
            first[2],
        ],
        {bit: (far_part,) for bit in rep_bits},
    )
    parts[0] = after(parts[0], *early)
    grad_one = scatter_rows(parts, bits)
    input_rows = grad_residual + norm_one_back(grad_one)[0]

    down_parts[0] = after(down_parts[0], far_part)
    down = scatter_rows(down_parts, bits, (grad_away,))
    layer_rows = residual + down + b_down.astype(F32)

    s_in_att, s_in_red, s_out_exp, s_out_att, s_in_exp, s_out_red = early
    glow_last, own_last, other_last = after((glow_qkv, grad_own, grad_other), far_part)
    second = sum_columns(t_mm(glow_last, hidden_one)).reshape(count, 3, rank, slice_wide)

    def own_terms(full):
        full = full.reshape(count, 3, rank, 3, span)
        return jnp.concatenate(
            [full[:, t, :, t].reshape(count * rank, span) for t in range(3)], 1
        )

    outer = sum_cores(own_terms(t_mm(low_qkv, own_last)), own_terms(t_mm(low_qkv, other_last)))
    late = over_groups(
        [second[:, t].reshape(count * rank, slice_wide) for t in range(3)]
        + [outer[:, t * span : (t + 1) * span] for t in range(3)]
    )
    shape = (1, count, rows, wide)
    return (
        layer_rows.astype(BF16).reshape(shape),
        input_rows.astype(BF16).reshape(shape),
        late[0],
        late[3],
        late[1],
        late[4],
        late[2],
        late[5],
        s_in_att,
        s_out_att,
        s_in_exp,
        s_out_exp,
        s_in_red,
        s_out_red,
    )


def solution(mesh):
    row = P("shard", None)
    wide = P(None, None, "shard")
    acts = P("rep", None, "shard", None)
    in_specs = (
        (acts, P(), P(), row, P(), row, row, P(), row, P(), P(), P(), row, P(), row, P())
        + (wide,) * 12
        + (P("rep", None), P("rep", None, None), acts)
    )
    out_specs = (acts, acts) + (wide,) * 12
    return jax.shard_map(
        on_device, mesh=mesh, in_specs=in_specs, out_specs=out_specs, check_vma=False
    )
```

```python
import functools

import jax
import jax.numpy as jnp
import numpy as np
from jax import lax
from jax.experimental import pallas as pl
from jax.experimental.pallas import tpu as pltpu
from jax.sharding import PartitionSpec as P

HEADS = 16
HEAD = 128
ADAPTERS = 8
PIECE = 256

EPSILON = 1e-05
MASKED = -1e30
F32 = jnp.float32
BF16 = jnp.bfloat16


def layer_norm(values, gain_vec, shift_vec):
    centre = jnp.mean(values, axis=-1, keepdims=True)
    offset = values - centre
    spread = jnp.mean(offset * offset, axis=-1, keepdims=True)
    return offset * lax.rsqrt(spread + EPSILON) * gain_vec + shift_vec


def piece_labels(starts, positions):
    inside = (positions[:, None] >= starts[None, :]) & (
        positions[:, None] < starts[None, :] + PIECE
    )
    labels = jnp.arange(1, starts.shape[0] + 1, dtype=jnp.int32)
    return jnp.sum(jnp.where(inside, labels[None, :], 0), axis=1)


def mm(a, b):
    return lax.dot_general(a, b, (((1,), (0,)), ((), ())), preferred_element_type=F32)


def mm_t(a, b):
    return lax.dot_general(a, b, (((1,), (1,)), ((), ())), preferred_element_type=F32)


def t_mm(a, b):
    return lax.dot_general(a, b, (((0,), (0,)), ((), ())), preferred_element_type=F32)


def swap(value, axis, mask):
    size = lax.axis_size(axis)
    return lax.ppermute(value, axis, [(i, i ^ mask) for i in range(size)])


def after(value, *others):
    return lax.optimization_barrier((value,) + others)[0]


def bits_of(size):
    bits = []
    while (1 << len(bits)) < size:
        bits.append(1 << len(bits))
    return bits


def subsets(bits):
    masks = [0]
    for bit in bits:
        masks = masks + [m | bit for m in masks]
    return masks


def gather_rows(block, bits, gate=()):
    half = block.shape[0] // 2
    got = {0: [block]}
    upper, lower = {}, {}
    for bit in bits:
        there = swap(block, "shard", bit)
        there = after(there, *gate) if gate else there
        got[bit] = [there]
        upper[bit], lower[bit] = there[:half], there[half:]
    for which, order in ((upper, bits), (lower, bits[::-1])):
        for k, bit in enumerate(order):
            for sub in subsets(order[:k])[1:]:
                which[sub | bit] = swap(which[sub], "shard", bit)
    pieces = []
    for mask in subsets(bits):
        pieces += got[mask] if mask in got else [upper[mask], lower[mask]]
    return jnp.concatenate(pieces, 0), [got[bit][0] for bit in bits], pieces[-1]


def scatter_rows(parts, bits, gate=()):
    half = parts[0].shape[0] // 2
    upper = {m: p[:half] for m, p in parts.items()}
    lower = {m: p[half:] for m, p in parts.items()}
    for which, order in ((upper, bits), (lower, bits[::-1])):
        for k in reversed(range(len(order))):
            for sub in subsets(order[:k])[1:]:
                other = swap(which[sub | order[k]], "shard", order[k])
                other = after(other, *gate) if gate else other
                which[sub] = (which[sub].astype(F32) + other.astype(F32)).astype(BF16)
    blocks = [jnp.concatenate([upper[bit], lower[bit]], 0) for bit in bits]
    return [parts[0]] + [swap(b, "shard", bit) for b, bit in zip(blocks, bits)], blocks[-1]


def gather_blocks(value, axis, bits, gates=None):
    current = value[None]
    for bit in bits:
        there = swap(current, axis, bit)
        if gates and bit in gates:
            there = after(there, *gates[bit])
        current = jnp.concatenate([current, there], 0)
    return current


def run_copies(copies):
    for copy in copies:
        copy.start()
    for copy in copies:
        copy.wait()


def place_kernel(me_ref, *refs, count, width, rows, joined):
    pieces, outs, sems = refs[: 2 * count], refs[2 * count : -1], refs[-1]
    me = me_ref[0]

    def copies(core):
        made = []
        for side in range(2):
            for i in range(count):
                row = pl.multiple_of((me ^ (2 * i) ^ side) * rows, rows)
                piece = pieces[side * count + i]
                for k in range(2):
                    own = k ^ core
                    source = piece.at[:, pl.ds(k * width, width)]
                    if joined:
                        target = outs[0].at[pl.ds(row, rows), pl.ds(own * width, width)]
                    else:
                        target = outs[own].at[pl.ds(row, rows)]
                    made.append(pltpu.make_async_copy(source, target, sems.at[len(made)]))
        return made

    @pl.when((me & 1) == 0)
    def _():
        run_copies(copies(0))

    @pl.when((me & 1) == 1)
    def _():
        run_copies(copies(1))


def place_weights(me, pieces, width, joined):
    count = len(pieces) // 2
    rows = pieces[0].shape[0]
    if joined:
        shapes = [jax.ShapeDtypeStruct((rows * count * 2, 2 * width), BF16)]
    else:
        shapes = [jax.ShapeDtypeStruct((rows * count * 2, width), BF16)] * 2
    return pl.pallas_call(
        functools.partial(
            place_kernel, count=count, width=width, rows=rows, joined=joined
        ),
        out_shape=shapes,
        in_specs=[pl.BlockSpec(memory_space=pltpu.SMEM)]
        + [pl.BlockSpec(memory_space=pl.ANY)] * (2 * count),
        out_specs=[pl.BlockSpec(memory_space=pltpu.VMEM)] * len(shapes),
        scratch_shapes=[pltpu.SemaphoreType.DMA((4 * count,))],
        cost_estimate=pl.CostEstimate(
            flops=0, bytes_accessed=16 * rows * count * width, transcendentals=0
        ),
        name="place_weights",
    )(me, *pieces)


def pick_kernel(chosen_ref, *refs, tall, rank):
    tables, (tall_ref, flat_ref, sems) = refs[:-3], refs[-3:]
    count = chosen_ref.shape[0]
    copies = []
    for s in range(count):
        column = 0
        for i, table in enumerate(tables):
            if i < tall:
                target = tall_ref.at[pl.ds((i * count + s) * rank, rank)]
            else:
                width = table.shape[2]
                target = flat_ref.at[pl.ds(s * rank, rank), pl.ds(column, width)]
                column += width
            copies.append(
                pltpu.make_async_copy(table.at[chosen_ref[s]], target, sems.at[len(copies)])
            )
    run_copies(copies)


def pick_maps(chosen, upright, flat):
    count, rank = chosen.shape[0], upright[0].shape[1]
    total = sum(t.shape[2] for t in flat)
    shapes = (
        jax.ShapeDtypeStruct((len(upright) * count * rank, upright[0].shape[2]), BF16),
        jax.ShapeDtypeStruct((count * rank, total), BF16),
    )
    tables = upright + flat
    return pl.pallas_call(
        functools.partial(pick_kernel, tall=len(upright), rank=rank),
        out_shape=shapes,
        in_specs=[pl.BlockSpec(memory_space=pltpu.SMEM)]
        + [pl.BlockSpec(memory_space=pl.ANY)] * len(tables),
        out_specs=[pl.BlockSpec(memory_space=pltpu.VMEM)] * 2,
        scratch_shapes=[pltpu.SemaphoreType.DMA((count * len(tables),))],
        cost_estimate=pl.CostEstimate(
            flops=0, bytes_accessed=8 * count * rank * total, transcendentals=0
        ),
        name="pick_maps",
    )(chosen, *tables)


def cols_kernel(me_ref, in_ref, out_ref, sems, *, masks):
    width = in_ref.shape[2]
    run_copies(
        [
            pltpu.make_async_copy(
                in_ref.at[i],
                out_ref.at[:, pl.ds(pl.multiple_of((me_ref[0] ^ mask) * width, width), width)],
                sems.at[i],
            )
            for i, mask in enumerate(masks)
        ]
    )


def place_columns(me, stacked, masks):
    count, rows, width = stacked.shape
    return pl.pallas_call(
        functools.partial(cols_kernel, masks=masks),
        out_shape=jax.ShapeDtypeStruct((rows, count * width), stacked.dtype),
        in_specs=[pl.BlockSpec(memory_space=pltpu.SMEM), pl.BlockSpec(memory_space=pltpu.VMEM)],
        out_specs=pl.BlockSpec(memory_space=pltpu.VMEM),
        scratch_shapes=[pltpu.SemaphoreType.DMA((count,))],
        cost_estimate=pl.CostEstimate(
            flops=0, bytes_accessed=4 * count * rows * width, transcendentals=0
        ),
        name="place_columns",
    )(me, stacked)


def total_of(refs):
    total = refs[0][...].astype(F32)
    for ref in refs[1:]:
        total = total + ref[...].astype(F32)
    return total


def normalised(values):
    centre = jnp.mean(values, axis=-1, keepdims=True)
    offset = values - centre
    scale = lax.rsqrt(jnp.mean(offset * offset, axis=-1, keepdims=True) + EPSILON)
    return offset * scale, scale


def norm_kernel(base, shift, gain, bias, *refs):
    terms, (res_ref, out_ref) = refs[:-2], refs[-2:]
    values = base[...].astype(F32) + (total_of(terms) + shift[...].astype(F32))
    res_ref[...] = values
    unit, _ = normalised(values)
    out_ref[...] = (unit * gain[...].astype(F32) + bias[...].astype(F32)).astype(BF16)


def norm_back_kernel(values, gain, base, *refs, outs):
    terms, outputs = refs[: len(refs) - outs], refs[len(refs) - outs :]
    unit, scale = normalised(values[...].astype(F32))
    grad = total_of(terms) * gain[...].astype(F32)
    mean_one = jnp.mean(grad, axis=-1, keepdims=True)
    mean_two = jnp.mean(grad * unit, axis=-1, keepdims=True)
    total = base[...].astype(F32) + scale * (grad - mean_one - unit * mean_two)
    for out in outputs:
        out[...] = total.astype(out.dtype)


def row_call(kernel, order, rows, wide, dtypes, name):
    tile = 32 if rows % 32 == 0 else rows
    args, specs = [], []
    for value in order:
        if value.ndim == 1:
            args.append(value[None])
            specs.append(pl.BlockSpec((1, wide), lambda i: (0, 0)))
        else:
            args.append(value)
            specs.append(pl.BlockSpec((tile, wide), lambda i: (i, 0)))
    return pl.pallas_call(
        kernel,
        out_shape=[jax.ShapeDtypeStruct((rows, wide), d) for d in dtypes],
        grid=(rows // tile,),
        in_specs=specs,
        out_specs=[pl.BlockSpec((tile, wide), lambda i: (i, 0))] * len(dtypes),
        cost_estimate=pl.CostEstimate(
            flops=20 * rows * wide, bytes_accessed=16 * rows * wide, transcendentals=0
        ),
        name=name,
    )(*args)


def seen(pos_q, pos_k, lab_q, lab_k):
    return (pos_k <= pos_q) | ((lab_q == lab_k) & (lab_q > 0))


def both(own_ref, other_ref, low, high):
    own, other = own_ref[:, 0, :, low:high], other_ref[:, 0, :, low:high]
    chips, rows, width = own.shape
    return jnp.concatenate([own.reshape(chips * rows, width), other.reshape(chips * rows, width)], 0)


def put(own_ref, other_ref, low, high, value):
    chips, _, rows, _ = own_ref.shape
    half = chips * rows
    own_ref[:, 0, :, low:high] = value[:half].reshape(chips, rows, high - low)
    other_ref[:, 0, :, low:high] = value[half:].reshape(chips, rows, high - low)


def attend_kernel(pq, pk, lq, lk, own, other, out_own, out_other, lse_ref, *, heads, factor):
    allowed = seen(pq[...], pk[...], lq[0], lk[0])
    span = heads * HEAD
    for h in range(heads):
        low, high = h * HEAD, (h + 1) * HEAD
        q = both(own, other, low, high)
        k = both(own, other, span + low, span + high)
        v = both(own, other, 2 * span + low, 2 * span + high)
        scores = jnp.where(allowed, mm_t(q, k) * factor, MASKED)
        top = jnp.max(scores, axis=-1, keepdims=True)
        expo = jnp.exp(scores - top)
        total = jnp.sum(expo, axis=-1, keepdims=True)
        probs = (expo * (1.0 / total)).astype(BF16)
        put(out_own, out_other, low, high, mm(probs, v).astype(BF16))
        lse_ref[0, :, h : h + 1] = top + jnp.log(total)


def attend_specs(chips, count, rows, length):
    whole = pl.BlockSpec(memory_space=pltpu.VMEM)
    where = [
        pl.BlockSpec((length, 1), lambda s: (0, 0)),
        pl.BlockSpec((1, length), lambda s: (0, 0)),
        pl.BlockSpec((1, length, 1), lambda s: (s, 0, 0)),
        pl.BlockSpec((1, 1, length), lambda s: (s, 0, 0)),
    ]

    def of(width):
        return pl.BlockSpec((chips, 1, rows, width), lambda s: (0, s, 0, 0))

    return where, of


def attend(where, own, other, heads):
    chips, count, rows, _ = own.shape
    length = 2 * chips * rows
    span = heads * HEAD
    places, of = attend_specs(chips, count, rows, length)
    return pl.pallas_call(
        functools.partial(attend_kernel, heads=heads, factor=HEAD ** (-0.5)),
        out_shape=(
            jax.ShapeDtypeStruct((chips, count, rows, span), BF16),
            jax.ShapeDtypeStruct((chips, count, rows, span), BF16),
            jax.ShapeDtypeStruct((count, length, heads), F32),
        ),
        grid=(count,),
        in_specs=places + [of(3 * span), of(3 * span)],
        out_specs=(of(span), of(span), pl.BlockSpec((1, length, heads), lambda s: (s, 0, 0))),
        cost_estimate=pl.CostEstimate(
            flops=count * heads * length * length * HEAD * 4,
            bytes_accessed=count * length * heads * HEAD * 8,
            transcendentals=count * heads * length * length,
        ),
        name="attend",
    )(*where, own, other)


def attend_back_kernel(
    pq, pk, lq, lk, own, other, lse_ref, ga_own, ga_other, out_own, out_other, *, heads, factor
):
    allowed = seen(pq[...], pk[...], lq[0], lk[0])
    span = heads * HEAD
    for h in range(heads):
        low, high = h * HEAD, (h + 1) * HEAD
        q = both(own, other, low, high)
        k = both(own, other, span + low, span + high)
        v = both(own, other, 2 * span + low, 2 * span + high)
        ga = both(ga_own, ga_other, low, high)
        scores = jnp.where(allowed, mm_t(q, k) * factor, MASKED)
        probs = jnp.exp(scores - lse_ref[0, :, h : h + 1])
        grad_probs = mm_t(ga, v)
        inner = jnp.sum(probs * grad_probs, axis=-1, keepdims=True)
        grad_scores = (probs * (grad_probs - inner)).astype(BF16)
        put(out_own, out_other, low, high, (mm(grad_scores, k) * factor).astype(BF16))
        put(
            out_own,
            out_other,
            span + low,
            span + high,
            (t_mm(grad_scores, q) * factor).astype(BF16),
        )
        put(
            out_own,
            out_other,
            2 * span + low,
            2 * span + high,
            t_mm(probs.astype(BF16), ga).astype(BF16),
        )


def attend_back(where, own, other, lse, ga_own, ga_other, heads):
    chips, count, rows, _ = own.shape
    length = 2 * chips * rows
    span = heads * HEAD
    places, of = attend_specs(chips, count, rows, length)
    return pl.pallas_call(
        functools.partial(attend_back_kernel, heads=heads, factor=HEAD ** (-0.5)),
        out_shape=(jax.ShapeDtypeStruct((chips, count, rows, 3 * span), BF16),) * 2,
        grid=(count,),
        in_specs=places
        + [of(3 * span), of(3 * span)]
        + [pl.BlockSpec((1, length, heads), lambda s: (s, 0, 0)), of(span), of(span)],
        out_specs=(of(3 * span), of(3 * span)),
        cost_estimate=pl.CostEstimate(
            flops=count * heads * length * length * HEAD * 10,
            bytes_accessed=count * length * heads * HEAD * 14,
            transcendentals=count * heads * length * length,
        ),
        name="attend_back",
    )(*where, own, other, lse, ga_own, ga_other)


def on_device(
    inputs,
    ln1_gain,
    ln1_bias,
    w_query,
    b_query,
    w_key,
    w_value,
    b_value,
    w_out,
    b_out,
    ln2_gain,
    ln2_bias,
    w_up,
    b_up,
    w_down,
    b_down,
    in_query,
    out_query,
    in_key,
    out_key,
    in_value,
    out_value,
    in_attn,
    out_attn,
    in_expand,
    out_expand,
    in_reduce,
    out_reduce,
    adapter_pick,
    piece_start,
    cotangent,
):
    count, rows, wide = inputs.shape[1:]
    size = lax.axis_size("shard")
    chips = size // 2
    bits = bits_of(size)[1:]
    me = lax.axis_index("shard").astype(jnp.int32)
    me_arr = me[None]
    heads = HEADS // size
    span = heads * HEAD
    slice_wide = wide // size
    ff_part = w_up.shape[1] // size
    rank = in_query.shape[1]
    block = count * rows
    chosen = adapter_pick[0]
    starts = piece_start[0]

    def keep_own(value, terms=1):
        of_row = lax.broadcasted_iota(jnp.int32, value.shape, 0) // rows % count
        of_col = lax.broadcasted_iota(jnp.int32, value.shape, 1) // (terms * rank)
        return jnp.where(of_row == of_col, value, 0.0).astype(BF16)

    narrow = [out_query, out_key, out_value, in_attn, out_expand, in_reduce]
    edges = np.cumsum([0] + [n.shape[2] for n in narrow])
    mine, packed = pick_maps(
        chosen, [in_query, in_key, in_value, in_expand, out_attn, out_reduce], narrow
    )
    packed_other = swap(packed, "shard", 1)
    order = bits + [1]
    chip = me // 2

    def slices(tables, width):
        pieces = []
        for i in range(chips):
            both = [
                lax.dynamic_slice_in_dim(t, (chip ^ i) * 2 * width, 2 * width, 1) for t in tables
            ]
            if len(both) > 1:
                both = jnp.concatenate(
                    [t[:, k * width : (k + 1) * width] for k in range(2) for t in both], 1
                )
            else:
                both = both[0]
            pieces.append(both)
        return pieces

    def exchange(pieces):
        return [swap(piece, "shard", 2 * i) if i else piece for i, piece in enumerate(pieces)]

    def both_cores(own):
        return own + [swap(piece, "shard", 1) for piece in own]

    first_tables = after((w_query, w_key, w_value), mine)
    pieces_qkv = after(tuple(slices(first_tables, span)), packed_other)
    turned = exchange(pieces_qkv)

    rows_in = after(inputs[0].reshape(block, wide), *pieces_qkv)
    features = rows_in.astype(F32)
    normed = layer_norm(features, ln1_gain.astype(F32), ln1_bias.astype(F32)).astype(BF16)
    starts, b_query, b_value, b_up, me_late, chosen, packed = after(
        (starts, b_query, b_value, b_up, me, chosen, packed), normed
    )
    hidden_block = after(normed, *[turned[bit // 2] for bit in bits])
    hidden_one, one_first, one_last = gather_rows(hidden_block, bits)

    w_out, w_down, turned[0] = after((w_out, w_down, turned[0]), *one_first)
    w_qkv_mine, w_qkv_other = place_weights(me_arr, both_cores(turned), 3 * span, False)
    w_out_other = swap(w_out, "shard", 1)
    w_down_other = swap(w_down, "shard", 1)
    hidden_one = after(hidden_one, w_out_other, w_down_other)
    near = gather_blocks(mine, "shard", bits, {bit: one_first for bit in bits[1:]})
    stacked = jnp.concatenate([near, swap(near, "shard", 1)], 0)

    owners = np.concatenate([np.arange(chips) * 2, np.arange(chips) * 2 + 1]).astype(np.int32)
    locs = np.tile(np.arange(rows, dtype=np.int32), 2 * chips)
    positions = (me_late ^ jnp.asarray(np.repeat(owners, rows))) * rows + jnp.asarray(locs)
    labels = jnp.stack([piece_labels(starts[s], positions) for s in range(count)])
    where = (positions[:, None], positions[None, :], labels[:, :, None], labels[:, None, :])

    whole = place_columns(me_arr, stacked, subsets(order)).reshape(6, count, rank, wide)
    in_qkv = jnp.swapaxes(whole[:3], 0, 1).reshape(count * 3 * rank, wide)
    in_exp, out_att, out_red = (whole[3 + i].reshape(count * rank, wide) for i in range(3))

    rep_bits = bits_of(lax.axis_size("rep"))
    mark = (after(chosen, *one_first)[:, None] == jnp.arange(ADAPTERS, dtype=jnp.int32)[None, :]).astype(BF16)
    marks = gather_blocks(jnp.pad(mark, ((0, 16 - count), (0, 128 - ADAPTERS))), "rep", rep_bits)
    groups = marks.shape[0]
    marks = marks[:, :count, :ADAPTERS].reshape(groups * count, 1, ADAPTERS, 1)
    place = (marks * jnp.eye(rank, dtype=BF16)[None, :, None, :]).reshape(
        groups * count * rank, ADAPTERS * rank
    )

    def unpack(table, i):
        return table[:, edges[i] : edges[i + 1]]

    def out_qkv_of(table):
        stacked = jnp.stack([unpack(table, t).reshape(count, rank, span) for t in range(3)], 1)
        spread = stacked[:, :, :, None, :] * jnp.eye(3, dtype=BF16)[None, :, None, :, None]
        return spread.reshape(count * 3 * rank, 3 * span)

    out_qkv_mine, out_qkv_other = out_qkv_of(packed), out_qkv_of(packed_other)
    in_att, out_exp, in_red = (
        jnp.concatenate([unpack(packed, i), unpack(packed_other, i)], 1) for i in (3, 4, 5)
    )

    def slice_of(bias, index, width):
        return lax.dynamic_slice_in_dim(bias, index * width, width).astype(F32)

    def b_qkv_of(index):
        return jnp.concatenate(
            [slice_of(b_query, index, span), jnp.zeros((span,), F32), slice_of(b_value, index, span)]
        )

    b_up_chip = jnp.concatenate([slice_of(b_up, me, ff_part), slice_of(b_up, me ^ 1, ff_part)])
    w_out_chip = jnp.concatenate([w_out, w_out_other], 0)
    w_down_chip = jnp.concatenate([w_down, w_down_other], 0)

    def by_chip(value):
        return value.reshape((chips, count, rows) + value.shape[1:])

    def flat(value):
        return value.reshape(chips * block, value.shape[-1])

    def block_products(products, low, table):
        parts = {}
        for i in reversed(range(chips)):
            at = slice(i * block, (i + 1) * block)
            total = mm(low[at], table)
            for value, weight, main in products:
                total = total + main(value[at], weight)
            parts[2 * i] = total.astype(BF16)
        return parts

    low_qkv = keep_own(mm_t(hidden_one, in_qkv), 3)
    qkv_away = (
        mm(hidden_one, w_qkv_other) + mm(low_qkv, out_qkv_other) + b_qkv_of(me ^ 1)
    ).astype(BF16)
    qkv_other = by_chip(swap(qkv_away, "shard", 1))
    qkv_own = by_chip(
        (mm(hidden_one, w_qkv_mine) + mm(low_qkv, out_qkv_mine) + b_qkv_of(me)).astype(BF16)
    )
    att_own, att_away, lse = attend(where, qkv_own, qkv_other, heads)
    cot_mine = cotangent[0].reshape(block, wide)
    attended = jnp.concatenate([flat(att_own), swap(flat(att_away), "shard", 1)], 1)
    low_att = keep_own(mm_t(attended, in_att))
    parts = block_products([(attended, w_out_chip, mm)], low_att, out_att)
    terms, relayed = scatter_rows(parts, bits)
    cot, _, _ = gather_rows(after(cot_mine, one_last), bits, (relayed,))
    glow_red = keep_own(mm_t(cot, out_red))
    grad_act = (mm_t(cot, w_down_chip) + mm(glow_red, in_red)).astype(BF16)
    pieces_up = slices([after(w_up, one_last)], ff_part)
    pieces_up = pieces_up[:1] + [after(p, relayed) for p in pieces_up[1:-1]] + pieces_up[-1:]
    residual, hidden_block = row_call(
        norm_kernel, [rows_in, b_out, ln2_gain, ln2_bias] + terms, block, wide, [F32, BF16], "norm"
    )
    hidden_two, _, _ = gather_rows(hidden_block, bits)

    (w_up_chip,) = place_weights(me_arr, both_cores(exchange(pieces_up)), ff_part, True)
    hidden_two = after(hidden_two, grad_act)
    low_exp = keep_own(mm_t(hidden_two, in_exp))
    pre = mm(hidden_two, w_up_chip) + mm(low_exp, out_exp) + b_up_chip
    share = 0.5 * (1.0 + lax.erf(pre * np.float32(0.5**0.5)))
    act = (pre * share).astype(BF16)
    slope = share + pre * (jnp.exp(-0.5 * pre * pre) * np.float32((2 * np.pi) ** -0.5))
    grad_pre = (slope * grad_act.astype(F32)).astype(BF16)
    glow_exp = keep_own(mm_t(grad_pre, out_exp))
    terms, grad_sent = scatter_rows(block_products([(grad_pre, w_up_chip, mm_t)], glow_exp, in_exp), bits)
    grad_residual, grad_block = row_call(
        functools.partial(norm_back_kernel, outs=2),
        [residual, ln2_gain, cot_mine] + terms,
        block,
        wide,
        [F32, BF16],
        "norm_back",
    )
    grad_branch, _, branch_last = gather_rows(grad_block, bits)

    act_late = after(act, grad_block)
    low_red = keep_own(mm_t(act_late, in_red))
    down_parts = block_products([(act_late, w_down_chip, mm)], low_red, out_red)
    glow_att = keep_own(mm_t(grad_branch, out_att))
    grad_att = (mm_t(grad_branch, w_out_chip) + mm(glow_att, in_att)).astype(BF16)
    ga_own = by_chip(grad_att[:, :span])
    ga_other = by_chip(swap(grad_att[:, span:], "shard", 1))
    grad_own, grad_away = attend_back(where, qkv_own, qkv_other, lse, ga_own, ga_other, heads)
    grad_own = flat(grad_own)
    grad_other = swap(flat(grad_away), "shard", 1)
    glow_qkv = keep_own(mm_t(grad_own, out_qkv_mine) + mm_t(grad_other, out_qkv_other), 3)
    def sum_cores(own, away):
        return own + swap(away.astype(BF16), "shard", 1).astype(F32)

    def core_columns(value):
        width = value.shape[1] // size

        def side(which):
            return jnp.stack(
                [
                    lax.dynamic_slice_in_dim(value, (2 * k + which) * width, width, 1)
                    for k in range(chips)
                ]
            )

        core = me & 1
        return sum_cores(side(core), side(1 - core))

    def sum_chips(current):
        sent = None
        for bit in bits[::-1]:
            current = current.reshape((2, current.shape[0] // 2) + current.shape[1:])
            own = (me // bit) & 1
            away = lax.dynamic_index_in_dim(current, 1 - own, 0, False).astype(BF16)
            sent = away if sent is None else sent
            current = lax.dynamic_index_in_dim(current, own, 0, False) + swap(
                away, "shard", bit
            ).astype(F32)
        return current[0], sent

    def over_groups(terms, gates=None):
        widths = [t.shape[1] for t in terms]
        data = jnp.concatenate([t.astype(BF16) for t in terms], 1)
        taken = gather_blocks(data, "rep", rep_bits, gates).reshape(groups * count * rank, -1)
        outs, start = [], 0
        for width in widths:
            out = t_mm(place, taken[:, start : start + width])
            outs.append(out.reshape(ADAPTERS, rank, width))
            start += width
        return outs

    def halves(value):
        middle = value.shape[1] // 2
        return value[:, :middle], value[:, middle:]

    glow_late, low_late = after((glow_exp, low_exp), grad_block)
    act_mid, grad_mid, low_mid, glow_mid = after((act, grad_pre, low_exp, glow_red), grad_sent)
    red_own, red_away = halves(t_mm(glow_mid, act_mid))
    exp_own, exp_away = halves(t_mm(low_mid, grad_mid))
    local = sum_cores(
        jnp.concatenate([red_own, exp_own], 1), jnp.concatenate([red_away, exp_away], 1)
    )
    s_in_red, s_out_exp = over_groups(
        [local[:, :ff_part], local[:, ff_part:]], {rep_bits[-1]: (grad_away,)}
    )

    near_first = core_columns(
        jnp.concatenate(
            [t_mm(low_att, grad_branch), t_mm(glow_late, hidden_two), t_mm(low_red, cot)], 0
        )
    ).astype(BF16)
    tall = near_first.shape[1]
    riders = {}
    for i in range(chips):
        rider = lax.dynamic_index_in_dim(near_first, chip ^ i, 0, False)
        rider = jnp.pad(rider, ((0, block - tall), (0, 0)))
        riders[2 * i] = jnp.concatenate([down_parts[2 * i], rider], 1)
    att_side = sum_cores(*halves(t_mm(glow_att, attended)))

    glow_last = glow_qkv
    in_terms = t_mm(glow_last, hidden_one)

    def own_terms(full):
        full = full.reshape(count, 3, rank, 3, span)
        return jnp.concatenate(
            [full[:, t, :, t].reshape(count * rank, span) for t in range(3)], 1
        )

    near_second = core_columns(in_terms)
    products = [(grad_own, w_qkv_mine, mm_t), (grad_other, w_qkv_other, mm_t)]
    parts = block_products(products, after(glow_qkv, in_terms), in_qkv)
    second, sent = sum_chips(near_second)
    far = 2 * (chips - 1)
    parts[far] = after(parts[far], sent)
    far_part = parts[far]

    terms, relayed = scatter_rows(parts, bits)
    down, _ = scatter_rows(riders, bits, (grad_away,))
    down[0] = after(down[0], relayed)
    first = sum(t[:tall, wide:].astype(F32) for t in down).reshape(3, count * rank, slice_wide)
    layer_rows = residual + b_down.astype(F32) + sum(t[:, :wide].astype(F32) for t in down)

    own_last, other_last = after((grad_own, grad_other), relayed)
    outer = sum_cores(own_terms(t_mm(low_qkv, own_last)), own_terms(t_mm(low_qkv, other_last)))
    second = second.reshape(count, 3, rank, slice_wide)
    s_in_att, s_out_att, s_in_exp, s_out_red = over_groups(
        [att_side, first[0], first[1], first[2]]
    )
    late = over_groups(
        [second[:, t].reshape(count * rank, slice_wide) for t in range(3)]
        + [outer[:, t * span : (t + 1) * span] for t in range(3)]
    )
    (input_rows,) = row_call(
        functools.partial(norm_back_kernel, outs=1),
        [rows_in, ln1_gain, grad_residual] + terms,
        block,
        wide,
        [BF16],
        "norm_back",
    )
    shape = (1, count, rows, wide)
    return (
        layer_rows.astype(BF16).reshape(shape),
        input_rows.reshape(shape),
        late[0],
        late[3],
        late[1],
        late[4],
        late[2],
        late[5],
        s_in_att,
        s_out_att,
        s_in_exp,
        s_out_exp,
        s_in_red,
        s_out_red,
    )


def solution(mesh):
    row = P("shard", None)
    wide = P(None, None, "shard")
    acts = P("rep", None, "shard", None)
    in_specs = (
        (acts, P(), P(), row, P(), row, row, P(), row, P(), P(), P(), row, P(), row, P())
        + (wide,) * 12
        + (P("rep", None), P("rep", None, None), acts)
    )
    out_specs = (acts, acts) + (wide,) * 12
    return jax.shard_map(
        on_device, mesh=mesh, in_specs=in_specs, out_specs=out_specs, check_vma=False
    )
```

```python
import functools

import jax
import jax.numpy as jnp
import numpy as np
from jax import lax
from jax.experimental import pallas as pl
from jax.experimental.pallas import tpu as pltpu
from jax.sharding import PartitionSpec as P

HEADS = 16
HEAD = 128
ADAPTERS = 8
PIECE = 256

EPSILON = 1e-05
MASKED = -1e30
F32 = jnp.float32
BF16 = jnp.bfloat16


def layer_norm(values, gain_vec, shift_vec):
    centre = jnp.mean(values, axis=-1, keepdims=True)
    offset = values - centre
    spread = jnp.mean(offset * offset, axis=-1, keepdims=True)
    return offset * lax.rsqrt(spread + EPSILON) * gain_vec + shift_vec


def piece_labels(starts, positions):
    inside = (positions[:, None] >= starts[None, :]) & (
        positions[:, None] < starts[None, :] + PIECE
    )
    labels = jnp.arange(1, starts.shape[0] + 1, dtype=jnp.int32)
    return jnp.sum(jnp.where(inside, labels[None, :], 0), axis=1)


def mm(a, b):
    return lax.dot_general(a, b, (((1,), (0,)), ((), ())), preferred_element_type=F32)


def mm_t(a, b):
    return lax.dot_general(a, b, (((1,), (1,)), ((), ())), preferred_element_type=F32)


def t_mm(a, b):
    return lax.dot_general(a, b, (((0,), (0,)), ((), ())), preferred_element_type=F32)


def swap(value, axis, mask):
    size = lax.axis_size(axis)
    return lax.ppermute(value, axis, [(i, i ^ mask) for i in range(size)])


def after(value, *others):
    return lax.optimization_barrier((value,) + others)[0]


def bits_of(size):
    bits = []
    while (1 << len(bits)) < size:
        bits.append(1 << len(bits))
    return bits


def subsets(bits):
    masks = [0]
    for bit in bits:
        masks = masks + [m | bit for m in masks]
    return masks


def gather_rows(block, bits, gate=()):
    half = block.shape[0] // 2
    got = {0: [block]}
    upper, lower = {}, {}
    for bit in bits:
        there = swap(block, "shard", bit)
        there = after(there, *gate) if gate else there
        got[bit] = [there]
        upper[bit], lower[bit] = there[:half], there[half:]
    for which, order in ((upper, bits), (lower, bits[::-1])):
        for k, bit in enumerate(order):
            for sub in subsets(order[:k])[1:]:
                which[sub | bit] = swap(which[sub], "shard", bit)
    pieces = []
    for mask in subsets(bits):
        pieces += got[mask] if mask in got else [upper[mask], lower[mask]]
    return jnp.concatenate(pieces, 0), [got[bit][0] for bit in bits], pieces[-1]


def scatter_rows(parts, bits, gate=(), between=None):
    half = parts[0].shape[0] // 2
    upper = {m: p[:half] for m, p in parts.items()}
    lower = {m: p[half:] for m, p in parts.items()}
    for which, order in ((upper, bits), (lower, bits[::-1])):
        for k in reversed(range(len(order))):
            for sub in subsets(order[:k])[1:]:
                other = swap(which[sub | order[k]], "shard", order[k])
                other = after(other, *gate) if gate else other
                which[sub] = (which[sub].astype(F32) + other.astype(F32)).astype(BF16)
    blocks = [jnp.concatenate([upper[bit], lower[bit]], 0) for bit in bits]
    if between:
        blocks = list(after(tuple(blocks), between(blocks[-1])))
    return [parts[0]] + [swap(b, "shard", bit) for b, bit in zip(blocks, bits)], blocks[-1]


def gather_blocks(value, axis, bits, gates=None):
    current = value[None]
    for bit in bits:
        there = swap(current, axis, bit)
        if gates and bit in gates:
            there = after(there, *gates[bit])
        current = jnp.concatenate([current, there], 0)
    return current


def run_copies(copies):
    for copy in copies:
        copy.start()
    for copy in copies:
        copy.wait()


def cut_kernel(at_ref, *refs, count, terms, width):
    tables, outs, sems = refs[:terms], refs[terms:-1], refs[-1]
    me, part = at_ref[0], at_ref[1]
    copies = []
    for i in range(count):
        rows = outs[i].shape[0]
        first = 0 if i == 0 else pl.multiple_of(part * rows, rows)
        for k in range(2):
            column = pl.multiple_of((((me // 2) ^ i) * 2 + k) * width, width)
            for t in range(terms):
                copies.append(
                    pltpu.make_async_copy(
                        tables[t].at[pl.ds(first, rows), pl.ds(column, width)],
                        outs[i].at[:, pl.ds((k * terms + t) * width, width)],
                        sems.at[len(copies)],
                    )
                )
    run_copies(copies)


def cut_pieces(at, tables, width, count):
    rows, terms = tables[0].shape[0], len(tables)
    shapes = [
        jax.ShapeDtypeStruct((rows if i == 0 else rows // 2, 2 * terms * width), BF16)
        for i in range(count)
    ]
    return pl.pallas_call(
        functools.partial(cut_kernel, count=count, terms=terms, width=width),
        out_shape=shapes,
        in_specs=[pl.BlockSpec(memory_space=pltpu.SMEM)]
        + [pl.BlockSpec(memory_space=pl.ANY)] * terms,
        out_specs=[pl.BlockSpec(memory_space=pltpu.VMEM)] * count,
        scratch_shapes=[pltpu.SemaphoreType.DMA((2 * terms * count,))],
        cost_estimate=pl.CostEstimate(
            flops=0, bytes_accessed=4 * rows * count * terms * width, transcendentals=0
        ),
        name="cut_pieces",
    )(at, *tables)


def place_kernel(at_ref, *refs, count, width, rows, joined):
    each = 2 * count - 1
    pieces, outs, sems = refs[: 2 * each], refs[2 * each : -1], refs[-1]
    me, part = at_ref[0], at_ref[1]

    def copies(core):
        made = []
        for side in range(2):
            for j in range(each):
                i, second = (j, 0) if j < count else (j - count + 1, 1)
                piece = pieces[side * each + j]
                height = piece.shape[0]
                row = (me ^ (2 * i) ^ side) * rows
                if i:
                    row = row + (part ^ second) * height
                row = pl.multiple_of(row, height)
                for k in range(2):
                    own = k ^ core
                    source = piece.at[:, pl.ds(k * width, width)]
                    if joined:
                        target = outs[0].at[pl.ds(row, height), pl.ds(own * width, width)]
                    else:
                        target = outs[own].at[pl.ds(row, height)]
                    made.append(pltpu.make_async_copy(source, target, sems.at[len(made)]))
        return made

    @pl.when((me & 1) == 0)
    def _():
        run_copies(copies(0))

    @pl.when((me & 1) == 1)
    def _():
        run_copies(copies(1))


def place_weights(at, pieces, width, joined):
    count = (len(pieces) // 2 + 1) // 2
    rows = pieces[0].shape[0]
    if joined:
        shapes = [jax.ShapeDtypeStruct((rows * count * 2, 2 * width), BF16)]
    else:
        shapes = [jax.ShapeDtypeStruct((rows * count * 2, width), BF16)] * 2
    return pl.pallas_call(
        functools.partial(place_kernel, count=count, width=width, rows=rows, joined=joined),
        out_shape=shapes,
        in_specs=[pl.BlockSpec(memory_space=pltpu.SMEM)]
        + [pl.BlockSpec(memory_space=pl.ANY)] * len(pieces),
        out_specs=[pl.BlockSpec(memory_space=pltpu.VMEM)] * len(shapes),
        scratch_shapes=[pltpu.SemaphoreType.DMA((2 * len(pieces),))],
        cost_estimate=pl.CostEstimate(
            flops=0, bytes_accessed=16 * rows * count * width, transcendentals=0
        ),
        name="place_weights",
    )(at, *pieces)


def pick_kernel(chosen_ref, *refs, tall, rank):
    tables, (tall_ref, flat_ref, sems) = refs[:-3], refs[-3:]
    count = chosen_ref.shape[0]
    copies = []
    for s in range(count):
        column = 0
        for i, table in enumerate(tables):
            if i < tall:
                target = tall_ref.at[pl.ds((i * count + s) * rank, rank)]
            else:
                width = table.shape[2]
                target = flat_ref.at[pl.ds(s * rank, rank), pl.ds(column, width)]
                column += width
            copies.append(
                pltpu.make_async_copy(table.at[chosen_ref[s]], target, sems.at[len(copies)])
            )
    run_copies(copies)


def pick_maps(chosen, upright, flat):
    count, rank = chosen.shape[0], upright[0].shape[1]
    total = sum(t.shape[2] for t in flat)
    shapes = (
        jax.ShapeDtypeStruct((len(upright) * count * rank, upright[0].shape[2]), BF16),
        jax.ShapeDtypeStruct((count * rank, total), BF16),
    )
    tables = upright + flat
    return pl.pallas_call(
        functools.partial(pick_kernel, tall=len(upright), rank=rank),
        out_shape=shapes,
        in_specs=[pl.BlockSpec(memory_space=pltpu.SMEM)]
        + [pl.BlockSpec(memory_space=pl.ANY)] * len(tables),
        out_specs=[pl.BlockSpec(memory_space=pltpu.VMEM)] * 2,
        scratch_shapes=[pltpu.SemaphoreType.DMA((count * len(tables),))],
        cost_estimate=pl.CostEstimate(
            flops=0, bytes_accessed=8 * count * rank * total, transcendentals=0
        ),
        name="pick_maps",
    )(chosen, *tables)


def cols_kernel(me_ref, in_ref, out_ref, sems, *, masks):
    width = in_ref.shape[2]
    run_copies(
        [
            pltpu.make_async_copy(
                in_ref.at[i],
                out_ref.at[:, pl.ds(pl.multiple_of((me_ref[0] ^ mask) * width, width), width)],
                sems.at[i],
            )
            for i, mask in enumerate(masks)
        ]
    )


def place_columns(me, stacked, masks):
    count, rows, width = stacked.shape
    return pl.pallas_call(
        functools.partial(cols_kernel, masks=masks),
        out_shape=jax.ShapeDtypeStruct((rows, count * width), stacked.dtype),
        in_specs=[pl.BlockSpec(memory_space=pltpu.SMEM), pl.BlockSpec(memory_space=pltpu.VMEM)],
        out_specs=pl.BlockSpec(memory_space=pltpu.VMEM),
        scratch_shapes=[pltpu.SemaphoreType.DMA((count,))],
        cost_estimate=pl.CostEstimate(
            flops=0, bytes_accessed=4 * count * rows * width, transcendentals=0
        ),
        name="place_columns",
    )(me, stacked)


def normalised(values):
    centre = jnp.mean(values, axis=-1, keepdims=True)
    offset = values - centre
    scale = lax.rsqrt(jnp.mean(offset * offset, axis=-1, keepdims=True) + EPSILON)
    return offset * scale, scale


def total_of(refs, at):
    total = refs[0][at].astype(F32)
    for ref in refs[1:]:
        total = total + ref[at].astype(F32)
    return total


def tiles_of(rows):
    tile = 32 if rows % 32 == 0 else rows
    return [slice(i, i + tile) for i in range(0, rows, tile)]


def norm_kernel(base, shift, gain, bias, *refs):
    terms, (res_ref, out_ref) = refs[:-2], refs[-2:]
    for at in tiles_of(base.shape[0]):
        values = base[at].astype(F32) + (total_of(terms, at) + shift[...].astype(F32))
        res_ref[at] = values
        unit, _ = normalised(values)
        out_ref[at] = (unit * gain[...].astype(F32) + bias[...].astype(F32)).astype(BF16)


def norm_back_kernel(values, gain, base, *refs, outs):
    terms, outputs = refs[: len(refs) - outs], refs[len(refs) - outs :]
    for at in tiles_of(values.shape[0]):
        unit, scale = normalised(values[at].astype(F32))
        grad = total_of(terms, at) * gain[...].astype(F32)
        mean_one = jnp.mean(grad, axis=-1, keepdims=True)
        mean_two = jnp.mean(grad * unit, axis=-1, keepdims=True)
        total = base[at].astype(F32) + scale * (grad - mean_one - unit * mean_two)
        for out in outputs:
            out[at] = total.astype(out.dtype)


def row_call(kernel, order, rows, wide, dtypes, name):
    args = [value[None] if value.ndim == 1 else value for value in order]
    return pl.pallas_call(
        kernel,
        out_shape=[jax.ShapeDtypeStruct((rows, wide), d) for d in dtypes],
        in_specs=[pl.BlockSpec(memory_space=pltpu.VMEM)] * len(args),
        out_specs=[pl.BlockSpec(memory_space=pltpu.VMEM)] * len(dtypes),
        cost_estimate=pl.CostEstimate(
            flops=20 * rows * wide, bytes_accessed=16 * rows * wide, transcendentals=0
        ),
        name=name,
    )(*args)


def seen(pos_q, pos_k, lab_q, lab_k):
    return (pos_k <= pos_q) | ((lab_q == lab_k) & (lab_q > 0))


def both(own_ref, other_ref, low, high):
    own, other = own_ref[:, 0, :, low:high], other_ref[:, 0, :, low:high]
    chips, rows, width = own.shape
    return jnp.concatenate([own.reshape(chips * rows, width), other.reshape(chips * rows, width)], 0)


def put(own_ref, other_ref, low, high, value):
    chips, _, rows, _ = own_ref.shape
    half = chips * rows
    own_ref[:, 0, :, low:high] = value[:half].reshape(chips, rows, high - low)
    other_ref[:, 0, :, low:high] = value[half:].reshape(chips, rows, high - low)


def attend_kernel(pq, pk, lq, lk, own, other, out_own, out_other, lse_ref, *, heads, factor):
    allowed = seen(pq[...], pk[...], lq[0], lk[0])
    span = heads * HEAD
    for h in range(heads):
        low, high = h * HEAD, (h + 1) * HEAD
        q = both(own, other, low, high)
        k = both(own, other, span + low, span + high)
        v = both(own, other, 2 * span + low, 2 * span + high)
        scores = jnp.where(allowed, mm_t(q, k) * factor, MASKED)
        top = jnp.max(scores, axis=-1, keepdims=True)
        expo = jnp.exp(scores - top)
        total = jnp.sum(expo, axis=-1, keepdims=True)
        probs = (expo * (1.0 / total)).astype(BF16)
        put(out_own, out_other, low, high, mm(probs, v).astype(BF16))
        lse_ref[0, :, h : h + 1] = top + jnp.log(total)


def attend_specs(chips, count, rows, length):
    whole = pl.BlockSpec(memory_space=pltpu.VMEM)
    where = [
        pl.BlockSpec((length, 1), lambda s: (0, 0)),
        pl.BlockSpec((1, length), lambda s: (0, 0)),
        pl.BlockSpec((1, length, 1), lambda s: (s, 0, 0)),
        pl.BlockSpec((1, 1, length), lambda s: (s, 0, 0)),
    ]

    def of(width):
        return pl.BlockSpec((chips, 1, rows, width), lambda s: (0, s, 0, 0))

    return where, of


def attend(where, own, other, heads):
    chips, count, rows, _ = own.shape
    length = 2 * chips * rows
    span = heads * HEAD
    places, of = attend_specs(chips, count, rows, length)
    return pl.pallas_call(
        functools.partial(attend_kernel, heads=heads, factor=HEAD ** (-0.5)),
        out_shape=(
            jax.ShapeDtypeStruct((chips, count, rows, span), BF16),
            jax.ShapeDtypeStruct((chips, count, rows, span), BF16),
            jax.ShapeDtypeStruct((count, length, heads), F32),
        ),
        grid=(count,),
        in_specs=places + [of(3 * span), of(3 * span)],
        out_specs=(of(span), of(span), pl.BlockSpec((1, length, heads), lambda s: (s, 0, 0))),
        cost_estimate=pl.CostEstimate(
            flops=count * heads * length * length * HEAD * 4,
            bytes_accessed=count * length * heads * HEAD * 8,
            transcendentals=count * heads * length * length,
        ),
        name="attend",
    )(*where, own, other)


def attend_back_kernel(
    pq, pk, lq, lk, own, other, lse_ref, ga_own, ga_other, out_own, out_other, *, heads, factor
):
    allowed = seen(pq[...], pk[...], lq[0], lk[0])
    span = heads * HEAD
    for h in range(heads):
        low, high = h * HEAD, (h + 1) * HEAD
        q = both(own, other, low, high)
        k = both(own, other, span + low, span + high)
        v = both(own, other, 2 * span + low, 2 * span + high)
        ga = both(ga_own, ga_other, low, high)
        scores = jnp.where(allowed, mm_t(q, k) * factor, MASKED)
        probs = jnp.exp(scores - lse_ref[0, :, h : h + 1])
        grad_probs = mm_t(ga, v)
        inner = jnp.sum(probs * grad_probs, axis=-1, keepdims=True)
        grad_scores = (probs * (grad_probs - inner)).astype(BF16)
        put(out_own, out_other, low, high, (mm(grad_scores, k) * factor).astype(BF16))
        put(
            out_own,
            out_other,
            span + low,
            span + high,
            (t_mm(grad_scores, q) * factor).astype(BF16),
        )
        put(
            out_own,
            out_other,
            2 * span + low,
            2 * span + high,
            t_mm(probs.astype(BF16), ga).astype(BF16),
        )


def attend_back(where, own, other, lse, ga_own, ga_other, heads):
    chips, count, rows, _ = own.shape
    length = 2 * chips * rows
    span = heads * HEAD
    places, of = attend_specs(chips, count, rows, length)
    return pl.pallas_call(
        functools.partial(attend_back_kernel, heads=heads, factor=HEAD ** (-0.5)),
        out_shape=(jax.ShapeDtypeStruct((chips, count, rows, 3 * span), BF16),) * 2,
        grid=(count,),
        in_specs=places
        + [of(3 * span), of(3 * span)]
        + [pl.BlockSpec((1, length, heads), lambda s: (s, 0, 0)), of(span), of(span)],
        out_specs=(of(3 * span), of(3 * span)),
        cost_estimate=pl.CostEstimate(
            flops=count * heads * length * length * HEAD * 10,
            bytes_accessed=count * length * heads * HEAD * 14,
            transcendentals=count * heads * length * length,
        ),
        name="attend_back",
    )(*where, own, other, lse, ga_own, ga_other)


def on_device(
    inputs,
    ln1_gain,
    ln1_bias,
    w_query,
    b_query,
    w_key,
    w_value,
    b_value,
    w_out,
    b_out,
    ln2_gain,
    ln2_bias,
    w_up,
    b_up,
    w_down,
    b_down,
    in_query,
    out_query,
    in_key,
    out_key,
    in_value,
    out_value,
    in_attn,
    out_attn,
    in_expand,
    out_expand,
    in_reduce,
    out_reduce,
    adapter_pick,
    piece_start,
    cotangent,
):
    count, rows, wide = inputs.shape[1:]
    size = lax.axis_size("shard")
    chips = size // 2
    bits = bits_of(size)[1:]
    me = lax.axis_index("shard").astype(jnp.int32)
    me_arr = me[None]
    part = lax.axis_index("rep").astype(jnp.int32) & 1
    at = jnp.stack([me, part])
    heads = HEADS // size
    span = heads * HEAD
    slice_wide = wide // size
    ff_part = w_up.shape[1] // size
    rank = in_query.shape[1]
    block = count * rows
    chosen = adapter_pick[0]
    starts = piece_start[0]

    def keep_own(value, terms=1):
        of_row = lax.broadcasted_iota(jnp.int32, value.shape, 0) // rows % count
        of_col = lax.broadcasted_iota(jnp.int32, value.shape, 1) // (terms * rank)
        return jnp.where(of_row == of_col, value, 0.0).astype(BF16)

    chip = me // 2

    def exchange(pieces):
        return [pieces[0]] + [swap(p, "shard", 2 * i) for i, p in enumerate(pieces) if i]

    def halves_over_rep(pieces):
        return [swap(piece, "rep", 1) for piece in pieces]

    def both_cores(own):
        return list(own) + [swap(piece, "shard", 1) for piece in own]

    pieces_qkv = cut_pieces(at, [w_query, w_key, w_value], span, chips)
    turned = exchange(pieces_qkv)

    narrow = [out_query, out_key, out_value, in_attn, out_expand, in_reduce]
    edges = np.cumsum([0] + [n.shape[2] for n in narrow])
    mine, packed = pick_maps(
        after(chosen, *pieces_qkv),
        [in_query, in_key, in_value, in_expand, out_attn, out_reduce],
        narrow,
    )
    packed_other = swap(packed, "shard", 1)
    order = bits + [1]

    rows_in = after(inputs[0].reshape(block, wide), mine)
    features = rows_in.astype(F32)
    normed = layer_norm(features, ln1_gain.astype(F32), ln1_bias.astype(F32)).astype(BF16)
    starts, b_query, b_value, b_up, me_late, chosen, packed = after(
        (starts, b_query, b_value, b_up, me, chosen, packed), normed
    )
    hidden_block = after(normed, *turned[1:])
    hidden_one, one_first, one_last = gather_rows(hidden_block, bits)

    w_out, w_down, turned[0] = after((w_out, w_down, turned[0]), *one_first)
    w_qkv_mine, w_qkv_other = place_weights(
        at, both_cores(turned + halves_over_rep(turned[1:])), 3 * span, False
    )
    w_out_other = swap(w_out, "shard", 1)
    w_down_other = swap(w_down, "shard", 1)
    w_out_chip = jnp.concatenate([w_out, w_out_other], 0)
    w_down_chip = jnp.concatenate([w_down, w_down_other], 0)
    near_up = exchange(after(tuple(cut_pieces(at, [after(w_up, *one_first)], ff_part, chips)), one_last))
    hidden_one = after(hidden_one, w_out_chip, w_down_chip, near_up[0])
    near = gather_blocks(mine, "shard", bits, {bit: one_first for bit in bits[1:]})
    stacked = jnp.concatenate([near, swap(near, "shard", 1)], 0)

    owners = np.concatenate([np.arange(chips) * 2, np.arange(chips) * 2 + 1]).astype(np.int32)
    locs = np.tile(np.arange(rows, dtype=np.int32), 2 * chips)
    positions = (me_late ^ jnp.asarray(np.repeat(owners, rows))) * rows + jnp.asarray(locs)
    labels = jnp.stack([piece_labels(starts[s], positions) for s in range(count)])
    where = (positions[:, None], positions[None, :], labels[:, :, None], labels[:, None, :])

    whole = place_columns(me_arr, stacked, subsets(order)).reshape(6, count, rank, wide)
    in_qkv = jnp.swapaxes(whole[:3], 0, 1).reshape(count * 3 * rank, wide)
    in_exp, out_att, out_red = (whole[3 + i].reshape(count * rank, wide) for i in range(3))

    def unpack(table, i):
        return table[:, edges[i] : edges[i + 1]]

    def out_qkv_of(table):
        stacked = jnp.stack([unpack(table, t).reshape(count, rank, span) for t in range(3)], 1)
        spread = stacked[:, :, :, None, :] * jnp.eye(3, dtype=BF16)[None, :, None, :, None]
        return spread.reshape(count * 3 * rank, 3 * span)

    out_qkv_mine, out_qkv_other = out_qkv_of(packed), out_qkv_of(packed_other)
    in_att, out_exp, in_red = (
        jnp.concatenate([unpack(packed, i), unpack(packed_other, i)], 1) for i in (3, 4, 5)
    )

    def slice_of(bias, index, width):
        return lax.dynamic_slice_in_dim(bias, index * width, width).astype(F32)

    def b_qkv_of(index):
        return jnp.concatenate(
            [slice_of(b_query, index, span), jnp.zeros((span,), F32), slice_of(b_value, index, span)]
        )

    b_up_chip = jnp.concatenate([slice_of(b_up, me, ff_part), slice_of(b_up, me ^ 1, ff_part)])

    def by_chip(value):
        return value.reshape((chips, count, rows) + value.shape[1:])

    def flat(value):
        return value.reshape(chips * block, value.shape[-1])

    def block_products(products, low, table):
        parts = {}
        for i in reversed(range(chips)):
            at = slice(i * block, (i + 1) * block)
            total = mm(low[at], table)
            for value, weight, main in products:
                total = total + main(value[at], weight)
            parts[2 * i] = total.astype(BF16)
        return parts

    low_qkv = keep_own(mm_t(hidden_one, in_qkv), 3)
    qkv_away = (
        mm(hidden_one, w_qkv_other) + mm(low_qkv, out_qkv_other) + b_qkv_of(me ^ 1)
    ).astype(BF16)
    qkv_other = by_chip(swap(qkv_away, "shard", 1))
    qkv_own = by_chip(
        (mm(hidden_one, w_qkv_mine) + mm(low_qkv, out_qkv_mine) + b_qkv_of(me)).astype(BF16)
    )
    att_own, att_away, lse = attend(where, qkv_own, qkv_other, heads)
    cot_mine = cotangent[0].reshape(block, wide)
    attended = jnp.concatenate([flat(att_own), swap(flat(att_away), "shard", 1)], 1)
    low_att = keep_own(mm_t(attended, in_att))
    parts = block_products([(attended, w_out_chip, mm)], low_att, out_att)
    terms, relayed = scatter_rows(parts, bits)
    cot, _, _ = gather_rows(after(cot_mine, relayed), bits)

    rep_bits = bits_of(lax.axis_size("rep"))
    mark = (after(chosen, relayed)[:, None] == jnp.arange(ADAPTERS, dtype=jnp.int32)[None, :]).astype(BF16)
    marks = gather_blocks(jnp.pad(mark, ((0, 16 - count), (0, 128 - ADAPTERS))), "rep", rep_bits)
    groups = marks.shape[0]
    marks = marks[:, :count, :ADAPTERS].reshape(groups * count, 1, ADAPTERS, 1)
    place = (marks * jnp.eye(rank, dtype=BF16)[None, :, None, :]).reshape(
        groups * count * rank, ADAPTERS * rank
    )

    glow_red = keep_own(mm_t(cot, out_red))
    grad_act = (mm_t(cot, w_down_chip) + mm(glow_red, in_red)).astype(BF16)
    far_up = halves_over_rep(after(tuple(near_up[1:]), att_own))
    pieces_up = after(tuple(near_up + far_up), relayed)
    residual, hidden_block = row_call(
        norm_kernel, [rows_in, b_out, ln2_gain, ln2_bias] + terms, block, wide, [F32, BF16], "norm"
    )
    hidden_two, _, _ = gather_rows(hidden_block, bits)

    (w_up_chip,) = place_weights(at, both_cores(pieces_up), ff_part, True)
    hidden_two = after(hidden_two, grad_act)
    low_exp = keep_own(mm_t(hidden_two, in_exp))
    pre = mm(hidden_two, w_up_chip) + mm(low_exp, out_exp) + b_up_chip
    share = 0.5 * (1.0 + lax.erf(pre * np.float32(0.5**0.5)))
    act = (pre * share).astype(BF16)
    slope = share + pre * (jnp.exp(-0.5 * pre * pre) * np.float32((2 * np.pi) ** -0.5))
    grad_pre = (slope * grad_act.astype(F32)).astype(BF16)
    glow_exp = keep_own(mm_t(grad_pre, out_exp))
    terms, grad_sent = scatter_rows(block_products([(grad_pre, w_up_chip, mm_t)], glow_exp, in_exp), bits)
    grad_residual, grad_block = row_call(
        functools.partial(norm_back_kernel, outs=2),
        [residual, ln2_gain, cot_mine] + terms,
        block,
        wide,
        [F32, BF16],
        "norm_back",
    )
    grad_branch, _, branch_last = gather_rows(grad_block, bits)

    act_late = after(act, grad_block)
    low_red = keep_own(mm_t(act_late, in_red))
    down_parts = block_products([(act_late, w_down_chip, mm)], low_red, out_red)
    glow_att = keep_own(mm_t(grad_branch, out_att))
    grad_att = (mm_t(grad_branch, w_out_chip) + mm(glow_att, in_att)).astype(BF16)
    ga_own = by_chip(grad_att[:, :span])
    ga_other = by_chip(swap(grad_att[:, span:], "shard", 1))
    grad_own, grad_away = attend_back(where, qkv_own, qkv_other, lse, ga_own, ga_other, heads)
    grad_own = flat(grad_own)
    grad_other = swap(flat(grad_away), "shard", 1)
    glow_qkv = keep_own(mm_t(grad_own, out_qkv_mine) + mm_t(grad_other, out_qkv_other), 3)
    def sum_cores(own, away):
        return own + swap(away.astype(BF16), "shard", 1).astype(F32)

    def core_columns(value):
        width = value.shape[1] // size

        def side(which):
            return jnp.stack(
                [
                    lax.dynamic_slice_in_dim(value, (2 * k + which) * width, width, 1)
                    for k in range(chips)
                ]
            )

        core = me & 1
        return sum_cores(side(core), side(1 - core))

    def split_chips(current, bit):
        current = current.reshape((2, current.shape[0] // 2) + current.shape[1:])
        own = (me // bit) & 1
        away = lax.dynamic_index_in_dim(current, 1 - own, 0, False).astype(BF16)
        return lax.dynamic_index_in_dim(current, own, 0, False), away

    def sum_chips(current, gate):
        for i, bit in enumerate(bits[::-1]):
            current, away = split_chips(current, bit)
            there = swap(away, "shard", bit)
            current = current + (there if i else after(there, gate)).astype(F32)
        return current[0], away

    def over_groups(terms, gates=None):
        widths = [t.shape[1] for t in terms]
        data = jnp.concatenate([t.astype(BF16) for t in terms], 1)
        taken = gather_blocks(data, "rep", rep_bits, gates).reshape(groups * count * rank, -1)
        outs, start = [], 0
        for width in widths:
            out = t_mm(place, taken[:, start : start + width])
            outs.append(out.reshape(ADAPTERS, rank, width))
            start += width
        return outs

    def halves(value):
        middle = value.shape[1] // 2
        return value[:, :middle], value[:, middle:]

    glow_late, low_late = after((glow_exp, low_exp), grad_block)
    act_mid, grad_mid, low_mid, glow_mid = after((act, grad_pre, low_exp, glow_red), grad_sent)
    red_own, red_away = halves(t_mm(glow_mid, act_mid))
    exp_own, exp_away = halves(t_mm(low_mid, grad_mid))
    local = sum_cores(
        jnp.concatenate([red_own, exp_own], 1), jnp.concatenate([red_away, exp_away], 1)
    )
    s_in_red, s_out_exp = over_groups(
        [local[:, :ff_part], local[:, ff_part:]], {rep_bits[-1]: (grad_away,)}
    )

    near_first = core_columns(
        jnp.concatenate([t_mm(glow_late, hidden_two), t_mm(low_red, cot)], 0)
    ).astype(BF16)
    tall = near_first.shape[1]
    riders = {}
    for i in range(chips):
        rider = lax.dynamic_index_in_dim(near_first, chip ^ i, 0, False)
        rider = jnp.pad(rider, ((0, block - tall), (0, 0)))
        riders[2 * i] = after(jnp.concatenate([down_parts[2 * i], rider], 1), branch_last)
    att_side = sum_cores(*halves(t_mm(glow_att, attended)))

    glow_last = glow_qkv
    in_terms = jnp.concatenate([t_mm(glow_last, hidden_one), t_mm(low_att, grad_branch)], 0)

    def own_terms(full):
        full = full.reshape(count, 3, rank, 3, span)
        return jnp.concatenate(
            [full[:, t, :, t].reshape(count * rank, span) for t in range(3)], 1
        )

    near_second = core_columns(in_terms)
    products = [(grad_own, w_qkv_mine, mm_t), (grad_other, w_qkv_other, mm_t)]
    parts = block_products(products, after(glow_qkv, in_terms), in_qkv)
    far_part = parts[2 * (chips - 1)]
    aside = {}

    def hop(relayed):
        aside["second"], sent = sum_chips(after(near_second, far_part), relayed)
        return sent

    terms, relayed = scatter_rows(parts, bits, between=hop)
    second = aside["second"]
    down, _ = scatter_rows(riders, bits, (grad_away,))
    down[0] = after(down[0], relayed)
    first = sum(t[:tall, wide:].astype(F32) for t in down).reshape(2, count * rank, slice_wide)
    layer_rows = residual + b_down.astype(F32) + sum(t[:, :wide].astype(F32) for t in down)

    own_last, other_last = after((grad_own, grad_other), relayed)
    outer = sum_cores(own_terms(t_mm(low_qkv, own_last)), own_terms(t_mm(low_qkv, other_last)))
    (input_rows,) = row_call(
        functools.partial(norm_back_kernel, outs=1),
        [rows_in, ln1_gain, grad_residual] + terms,
        block,
        wide,
        [BF16],
        "norm_back",
    )
    out_att_sum = second[count * 3 * rank :]
    second = second[: count * 3 * rank].reshape(count, 3, rank, slice_wide)
    ends = {rep_bits[-1]: (input_rows,)}
    s_in_att, s_in_exp, s_out_red = over_groups([att_side, first[0], first[1]], ends)
    late = over_groups(
        [second[:, t].reshape(count * rank, slice_wide) for t in range(3)]
        + [outer[:, t * span : (t + 1) * span] for t in range(3)]
        + [out_att_sum],
        ends,
    )
    s_out_att = late.pop()
    shape = (1, count, rows, wide)
    return (
        layer_rows.astype(BF16).reshape(shape),
        input_rows.reshape(shape),
        late[0],
        late[3],
        late[1],
        late[4],
        late[2],
        late[5],
        s_in_att,
        s_out_att,
        s_in_exp,
        s_out_exp,
        s_in_red,
        s_out_red,
    )


def solution(mesh):
    row = P("shard", None)
    wide = P(None, None, "shard")
    acts = P("rep", None, "shard", None)
    in_specs = (
        (acts, P(), P(), row, P(), row, row, P(), row, P(), P(), P(), row, P(), row, P())
        + (wide,) * 12
        + (P("rep", None), P("rep", None, None), acts)
    )
    out_specs = (acts, acts) + (wide,) * 12
    return jax.shard_map(
        on_device, mesh=mesh, in_specs=in_specs, out_specs=out_specs, check_vma=False
    )
```

```python
import functools

import jax
import jax.numpy as jnp
import numpy as np
from jax import lax
from jax.experimental import pallas as pl
from jax.experimental.pallas import tpu as pltpu
from jax.sharding import PartitionSpec as P

HEADS = 16
HEAD = 128
ADAPTERS = 8
PIECE = 256

EPSILON = 1e-05
MASKED = -1e30
F32 = jnp.float32
BF16 = jnp.bfloat16


def layer_norm(values, gain_vec, shift_vec):
    centre = jnp.mean(values, axis=-1, keepdims=True)
    offset = values - centre
    spread = jnp.mean(offset * offset, axis=-1, keepdims=True)
    return offset * lax.rsqrt(spread + EPSILON) * gain_vec + shift_vec


def piece_labels(starts, positions):
    inside = (positions[:, None] >= starts[None, :]) & (
        positions[:, None] < starts[None, :] + PIECE
    )
    labels = jnp.arange(1, starts.shape[0] + 1, dtype=jnp.int32)
    return jnp.sum(jnp.where(inside, labels[None, :], 0), axis=1)


def mm(a, b):
    return lax.dot_general(a, b, (((1,), (0,)), ((), ())), preferred_element_type=F32)


def mm_t(a, b):
    return lax.dot_general(a, b, (((1,), (1,)), ((), ())), preferred_element_type=F32)


def t_mm(a, b):
    return lax.dot_general(a, b, (((0,), (0,)), ((), ())), preferred_element_type=F32)


def swap(value, axis, mask):
    size = lax.axis_size(axis)
    return lax.ppermute(value, axis, [(i, i ^ mask) for i in range(size)])


def after(value, *others):
    return lax.optimization_barrier((value,) + others)[0]


def bits_of(size):
    bits = []
    while (1 << len(bits)) < size:
        bits.append(1 << len(bits))
    return bits


def subsets(bits):
    masks = [0]
    for bit in bits:
        masks = masks + [m | bit for m in masks]
    return masks


def gather_rows(block, bits, gate=(), apart=False):
    half = block.shape[0] // 2
    got = {0: [block]}
    upper, lower = {}, {}
    for bit in bits:
        there = swap(block, "shard", bit)
        there = after(there, *gate) if gate else there
        got[bit] = [there]
        upper[bit], lower[bit] = there[:half], there[half:]
    for which, order in ((upper, bits), (lower, bits[::-1])):
        for k, bit in enumerate(order):
            for sub in subsets(order[:k])[1:]:
                which[sub | bit] = swap(which[sub], "shard", bit)
    pieces = []
    for mask in subsets(bits):
        pieces += got[mask] if mask in got else [upper[mask], lower[mask]]
    firsts = [got[bit][0] for bit in bits]
    if apart:
        return pieces, firsts, pieces[-1]
    return jnp.concatenate(pieces, 0), firsts, pieces[-1]


def scatter_rows(parts, bits, gate=(), between=None):
    half = parts[0].shape[0] // 2
    upper = {m: p[:half] for m, p in parts.items()}
    lower = {m: p[half:] for m, p in parts.items()}
    for which, order in ((upper, bits), (lower, bits[::-1])):
        for k in reversed(range(len(order))):
            for sub in subsets(order[:k])[1:]:
                other = swap(which[sub | order[k]], "shard", order[k])
                other = after(other, *gate) if gate else other
                which[sub] = (which[sub].astype(F32) + other.astype(F32)).astype(BF16)
    blocks = [jnp.concatenate([upper[bit], lower[bit]], 0) for bit in bits]
    if between:
        blocks = list(after(tuple(blocks), between(blocks)))
    return [parts[0]] + [swap(b, "shard", bit) for b, bit in zip(blocks, bits)], blocks


def gather_blocks(value, axis, bits, gates=None):
    current = value[None]
    for bit in bits:
        there = swap(current, axis, bit)
        if gates and bit in gates:
            there = after(there, *gates[bit])
        current = jnp.concatenate([current, there], 0)
    return current


def run_copies(copies):
    for copy in copies:
        copy.start()
    for copy in copies:
        copy.wait()


def cut_kernel(at_ref, *refs, count, terms, width):
    tables, outs, sems = refs[:terms], refs[terms:-1], refs[-1]
    me, part = at_ref[0], at_ref[1]
    copies = []
    for i in range(count):
        rows = outs[i].shape[0]
        first = pl.multiple_of(part * rows, rows) if rows < tables[0].shape[0] else 0
        for k in range(2):
            column = pl.multiple_of((((me // 2) ^ i) * 2 + k) * width, width)
            for t in range(terms):
                copies.append(
                    pltpu.make_async_copy(
                        tables[t].at[pl.ds(first, rows), pl.ds(column, width)],
                        outs[i].at[:, pl.ds((k * terms + t) * width, width)],
                        sems.at[len(copies)],
                    )
                )
    run_copies(copies)


def cut_pieces(at, tables, width, count, split):
    rows, terms = tables[0].shape[0], len(tables)
    shapes = [
        jax.ShapeDtypeStruct((rows // 2 if i and split else rows, 2 * terms * width), BF16)
        for i in range(count)
    ]
    return pl.pallas_call(
        functools.partial(cut_kernel, count=count, terms=terms, width=width),
        out_shape=shapes,
        in_specs=[pl.BlockSpec(memory_space=pltpu.SMEM)]
        + [pl.BlockSpec(memory_space=pl.ANY)] * terms,
        out_specs=[pl.BlockSpec(memory_space=pltpu.VMEM)] * count,
        scratch_shapes=[pltpu.SemaphoreType.DMA((2 * terms * count,))],
        cost_estimate=pl.CostEstimate(
            flops=0, bytes_accessed=4 * rows * count * terms * width, transcendentals=0
        ),
        name="cut_pieces",
    )(at, *tables)


def place_kernel(at_ref, *refs, count, width, rows, joined):
    each = (len(refs) - 1 - (1 if joined else 2)) // 2
    pieces, outs, sems = refs[: 2 * each], refs[2 * each : -1], refs[-1]
    me, part = at_ref[0], at_ref[1]

    def copies(core):
        made = []
        for side in range(2):
            for j in range(each):
                i, second = (j, 0) if j < count else (j - count + 1, 1)
                piece = pieces[side * each + j]
                height = piece.shape[0]
                row = (me ^ (2 * i) ^ side) * rows
                if height < rows:
                    row = row + (part ^ second) * height
                row = pl.multiple_of(row, height)
                for k in range(2):
                    own = k ^ core
                    source = piece.at[:, pl.ds(k * width, width)]
                    if joined:
                        target = outs[0].at[pl.ds(row, height), pl.ds(own * width, width)]
                    else:
                        target = outs[own].at[pl.ds(row, height)]
                    made.append(pltpu.make_async_copy(source, target, sems.at[len(made)]))
        return made

    @pl.when((me & 1) == 0)
    def _():
        run_copies(copies(0))

    @pl.when((me & 1) == 1)
    def _():
        run_copies(copies(1))


def place_weights(at, pieces, count, width, joined):
    rows = pieces[0].shape[0]
    if joined:
        shapes = [jax.ShapeDtypeStruct((rows * count * 2, 2 * width), BF16)]
    else:
        shapes = [jax.ShapeDtypeStruct((rows * count * 2, width), BF16)] * 2
    return pl.pallas_call(
        functools.partial(place_kernel, count=count, width=width, rows=rows, joined=joined),
        out_shape=shapes,
        in_specs=[pl.BlockSpec(memory_space=pltpu.SMEM)]
        + [pl.BlockSpec(memory_space=pl.ANY)] * len(pieces),
        out_specs=[pl.BlockSpec(memory_space=pltpu.VMEM)] * len(shapes),
        scratch_shapes=[pltpu.SemaphoreType.DMA((2 * len(pieces),))],
        cost_estimate=pl.CostEstimate(
            flops=0, bytes_accessed=16 * rows * count * width, transcendentals=0
        ),
        name="place_weights",
    )(at, *pieces)


def pick_kernel(chosen_ref, *refs, tall, rank):
    tables, (tall_ref, flat_ref, sems) = refs[:-3], refs[-3:]
    count = chosen_ref.shape[0]
    copies = []
    for s in range(count):
        column = 0
        for i, table in enumerate(tables):
            if i < tall:
                target = tall_ref.at[pl.ds((i * count + s) * rank, rank)]
            else:
                width = table.shape[2]
                target = flat_ref.at[pl.ds(s * rank, rank), pl.ds(column, width)]
                column += width
            copies.append(
                pltpu.make_async_copy(table.at[chosen_ref[s]], target, sems.at[len(copies)])
            )
    run_copies(copies)


def pick_maps(chosen, upright, flat):
    count, rank = chosen.shape[0], upright[0].shape[1]
    total = sum(t.shape[2] for t in flat)
    shapes = (
        jax.ShapeDtypeStruct((len(upright) * count * rank, upright[0].shape[2]), BF16),
        jax.ShapeDtypeStruct((count * rank, total), BF16),
    )
    tables = upright + flat
    return pl.pallas_call(
        functools.partial(pick_kernel, tall=len(upright), rank=rank),
        out_shape=shapes,
        in_specs=[pl.BlockSpec(memory_space=pltpu.SMEM)]
        + [pl.BlockSpec(memory_space=pl.ANY)] * len(tables),
        out_specs=[pl.BlockSpec(memory_space=pltpu.VMEM)] * 2,
        scratch_shapes=[pltpu.SemaphoreType.DMA((count * len(tables),))],
        cost_estimate=pl.CostEstimate(
            flops=0, bytes_accessed=8 * count * rank * total, transcendentals=0
        ),
        name="pick_maps",
    )(chosen, *tables)


def cols_kernel(me_ref, in_ref, out_ref, sems, *, masks):
    width = in_ref.shape[2]
    run_copies(
        [
            pltpu.make_async_copy(
                in_ref.at[i],
                out_ref.at[:, pl.ds(pl.multiple_of((me_ref[0] ^ mask) * width, width), width)],
                sems.at[i],
            )
            for i, mask in enumerate(masks)
        ]
    )


def place_columns(me, stacked, masks):
    count, rows, width = stacked.shape
    return pl.pallas_call(
        functools.partial(cols_kernel, masks=masks),
        out_shape=jax.ShapeDtypeStruct((rows, count * width), stacked.dtype),
        in_specs=[pl.BlockSpec(memory_space=pltpu.SMEM), pl.BlockSpec(memory_space=pltpu.VMEM)],
        out_specs=pl.BlockSpec(memory_space=pltpu.VMEM),
        scratch_shapes=[pltpu.SemaphoreType.DMA((count,))],
        cost_estimate=pl.CostEstimate(
            flops=0, bytes_accessed=4 * count * rows * width, transcendentals=0
        ),
        name="place_columns",
    )(me, stacked)


def normalised(values):
    centre = jnp.mean(values, axis=-1, keepdims=True)
    offset = values - centre
    scale = lax.rsqrt(jnp.mean(offset * offset, axis=-1, keepdims=True) + EPSILON)
    return offset * scale, scale


def total_of(refs, at):
    total = refs[0][at].astype(F32)
    for ref in refs[1:]:
        total = total + ref[at].astype(F32)
    return total


def tiles_of(rows):
    tile = 32 if rows % 32 == 0 else rows
    return [slice(i, i + tile) for i in range(0, rows, tile)]


def norm_kernel(base, vectors, *refs):
    terms, (res_ref, out_ref) = refs[:-2], refs[-2:]
    shift, gain, bias = vectors[0:1], vectors[1:2], vectors[2:3]
    for at in tiles_of(base.shape[0]):
        values = base[at].astype(F32) + (total_of(terms, at) + shift)
        res_ref[at] = values
        unit, _ = normalised(values)
        out_ref[at] = (unit * gain + bias).astype(BF16)


def norm_back_kernel(values, vectors, base, *refs, outs, row):
    gain = vectors[row : row + 1]
    terms, outputs = refs[: len(refs) - outs], refs[len(refs) - outs :]
    for at in tiles_of(values.shape[0]):
        unit, scale = normalised(values[at].astype(F32))
        grad = total_of(terms, at) * gain
        mean_one = jnp.mean(grad, axis=-1, keepdims=True)
        mean_two = jnp.mean(grad * unit, axis=-1, keepdims=True)
        total = base[at].astype(F32) + scale * (grad - mean_one - unit * mean_two)
        for out in outputs:
            out[at] = total.astype(out.dtype)


def row_call(kernel, order, rows, wide, dtypes, name):
    return pl.pallas_call(
        kernel,
        out_shape=[jax.ShapeDtypeStruct((rows, wide), d) for d in dtypes],
        in_specs=[pl.BlockSpec(memory_space=pltpu.VMEM)] * len(order),
        out_specs=[pl.BlockSpec(memory_space=pltpu.VMEM)] * len(dtypes),
        cost_estimate=pl.CostEstimate(
            flops=20 * rows * wide, bytes_accessed=16 * rows * wide, transcendentals=0
        ),
        name=name,
    )(*order)


def seen(pos_q, pos_k, lab_q, lab_k):
    return (pos_k <= pos_q) | ((lab_q == lab_k) & (lab_q > 0))


def both(own_ref, other_ref, low, high):
    own, other = own_ref[:, 0, :, low:high], other_ref[:, 0, :, low:high]
    chips, rows, width = own.shape
    return jnp.concatenate([own.reshape(chips * rows, width), other.reshape(chips * rows, width)], 0)


def put(own_ref, other_ref, low, high, value):
    chips, _, rows, _ = own_ref.shape
    half = chips * rows
    own_ref[:, 0, :, low:high] = value[:half].reshape(chips, rows, high - low)
    other_ref[:, 0, :, low:high] = value[half:].reshape(chips, rows, high - low)


def attend_kernel(pq, pk, lq, lk, own, other, out_own, out_other, lse_ref, *, heads, factor):
    allowed = seen(pq[...], pk[...], lq[0], lk[0])
    span = heads * HEAD
    for h in range(heads):
        low, high = h * HEAD, (h + 1) * HEAD
        q = both(own, other, low, high)
        k = both(own, other, span + low, span + high)
        v = both(own, other, 2 * span + low, 2 * span + high)
        scores = jnp.where(allowed, mm_t(q, k) * factor, MASKED)
        top = jnp.max(scores, axis=-1, keepdims=True)
        expo = jnp.exp(scores - top)
        total = jnp.sum(expo, axis=-1, keepdims=True)
        probs = (expo * (1.0 / total)).astype(BF16)
        put(out_own, out_other, low, high, mm(probs, v).astype(BF16))
        lse_ref[0, :, h : h + 1] = top + jnp.log(total)


def attend_specs(chips, count, rows, length):
    whole = pl.BlockSpec(memory_space=pltpu.VMEM)
    where = [
        pl.BlockSpec((length, 1), lambda s: (0, 0)),
        pl.BlockSpec((1, length), lambda s: (0, 0)),
        pl.BlockSpec((1, length, 1), lambda s: (s, 0, 0)),
        pl.BlockSpec((1, 1, length), lambda s: (s, 0, 0)),
    ]

    def of(width):
        return pl.BlockSpec((chips, 1, rows, width), lambda s: (0, s, 0, 0))

    return where, of


def attend(where, own, other, heads):
    chips, count, rows, _ = own.shape
    length = 2 * chips * rows
    span = heads * HEAD
    places, of = attend_specs(chips, count, rows, length)
    return pl.pallas_call(
        functools.partial(attend_kernel, heads=heads, factor=HEAD ** (-0.5)),
        out_shape=(
            jax.ShapeDtypeStruct((chips, count, rows, span), BF16),
            jax.ShapeDtypeStruct((chips, count, rows, span), BF16),
            jax.ShapeDtypeStruct((count, length, heads), F32),
        ),
        grid=(count,),
        in_specs=places + [of(3 * span), of(3 * span)],
        out_specs=(of(span), of(span), pl.BlockSpec((1, length, heads), lambda s: (s, 0, 0))),
        cost_estimate=pl.CostEstimate(
            flops=count * heads * length * length * HEAD * 4,
            bytes_accessed=count * length * heads * HEAD * 8,
            transcendentals=count * heads * length * length,
        ),
        name="attend",
    )(*where, own, other)


def attend_back_kernel(
    pq, pk, lq, lk, own, other, lse_ref, ga_own, ga_other, out_own, out_other, *, heads, factor
):
    allowed = seen(pq[...], pk[...], lq[0], lk[0])
    span = heads * HEAD
    for h in range(heads):
        low, high = h * HEAD, (h + 1) * HEAD
        q = both(own, other, low, high)
        k = both(own, other, span + low, span + high)
        v = both(own, other, 2 * span + low, 2 * span + high)
        ga = both(ga_own, ga_other, low, high)
        scores = jnp.where(allowed, mm_t(q, k) * factor, MASKED)
        probs = jnp.exp(scores - lse_ref[0, :, h : h + 1])
        grad_probs = mm_t(ga, v)
        inner = jnp.sum(probs * grad_probs, axis=-1, keepdims=True)
        grad_scores = (probs * (grad_probs - inner)).astype(BF16)
        put(out_own, out_other, low, high, (mm(grad_scores, k) * factor).astype(BF16))
        put(
            out_own,
            out_other,
            span + low,
            span + high,
            (t_mm(grad_scores, q) * factor).astype(BF16),
        )
        put(
            out_own,
            out_other,
            2 * span + low,
            2 * span + high,
            t_mm(probs.astype(BF16), ga).astype(BF16),
        )


def attend_back(where, own, other, lse, ga_own, ga_other, heads):
    chips, count, rows, _ = own.shape
    length = 2 * chips * rows
    span = heads * HEAD
    places, of = attend_specs(chips, count, rows, length)
    return pl.pallas_call(
        functools.partial(attend_back_kernel, heads=heads, factor=HEAD ** (-0.5)),
        out_shape=(jax.ShapeDtypeStruct((chips, count, rows, 3 * span), BF16),) * 2,
        grid=(count,),
        in_specs=places
        + [of(3 * span), of(3 * span)]
        + [pl.BlockSpec((1, length, heads), lambda s: (s, 0, 0)), of(span), of(span)],
        out_specs=(of(3 * span), of(3 * span)),
        cost_estimate=pl.CostEstimate(
            flops=count * heads * length * length * HEAD * 10,
            bytes_accessed=count * length * heads * HEAD * 14,
            transcendentals=count * heads * length * length,
        ),
        name="attend_back",
    )(*where, own, other, lse, ga_own, ga_other)


def on_device(
    inputs,
    ln1_gain,
    ln1_bias,
    w_query,
    b_query,
    w_key,
    w_value,
    b_value,
    w_out,
    b_out,
    ln2_gain,
    ln2_bias,
    w_up,
    b_up,
    w_down,
    b_down,
    in_query,
    out_query,
    in_key,
    out_key,
    in_value,
    out_value,
    in_attn,
    out_attn,
    in_expand,
    out_expand,
    in_reduce,
    out_reduce,
    adapter_pick,
    piece_start,
    cotangent,
):
    count, rows, wide = inputs.shape[1:]
    size = lax.axis_size("shard")
    chips = size // 2
    bits = bits_of(size)[1:]
    me = lax.axis_index("shard").astype(jnp.int32)
    me_arr = me[None]
    part = lax.axis_index("rep").astype(jnp.int32) & 1
    at = jnp.stack([me, part])
    heads = HEADS // size
    span = heads * HEAD
    slice_wide = wide // size
    ff_part = w_up.shape[1] // size
    rank = in_query.shape[1]
    block = count * rows
    chosen = adapter_pick[0]
    starts = piece_start[0]

    def keep_own(value, terms=1):
        of_row = lax.broadcasted_iota(jnp.int32, value.shape, 0) // rows % count
        of_col = lax.broadcasted_iota(jnp.int32, value.shape, 1) // (terms * rank)
        return jnp.where(of_row == of_col, value, 0.0).astype(BF16)

    chip = me // 2

    def exchange(pieces):
        return [pieces[0]] + [swap(p, "shard", 2 * i) for i, p in enumerate(pieces) if i]

    def halves_over_rep(pieces):
        return [swap(piece, "rep", 1) for piece in pieces]

    def both_cores(own):
        return list(own) + [swap(piece, "shard", 1) for piece in own]

    w_out_other = swap(w_out, "shard", 1)
    w_down_other = swap(w_down, "shard", 1)
    pieces_qkv = cut_pieces(at, [w_query, w_key, w_value], span, chips, True)
    turned = exchange(pieces_qkv)

    narrow = [out_query, out_key, out_value, in_attn, out_expand, in_reduce]
    edges = np.cumsum([0] + [n.shape[2] for n in narrow])
    mine, packed = pick_maps(
        after(chosen, w_out_other, w_down_other, *pieces_qkv),
        [in_query, in_key, in_value, in_expand, out_attn, out_reduce],
        narrow,
    )
    packed_other = swap(packed, "shard", 1)
    order = bits + [1]
    near_one = swap(mine[None], "shard", bits[0])

    rows_in = after(inputs[0].reshape(block, wide), mine)
    features = rows_in.astype(F32)
    normed = layer_norm(features, ln1_gain.astype(F32), ln1_bias.astype(F32)).astype(BF16)
    starts, b_query, b_value, b_up, me_late, chosen, packed = after(
        (starts, b_query, b_value, b_up, me, chosen, packed), normed
    )
    vectors = after(jnp.stack([b_out, ln2_gain, ln2_bias, ln1_gain]), normed).astype(F32)
    hidden_block = after(normed, packed_other, near_one, *turned[1:])
    hidden_one, one_first, one_last = gather_rows(hidden_block, bits)

    turned[0] = after(turned[0], *one_first)
    w_qkv_mine, w_qkv_other = place_weights(
        at, both_cores(turned + halves_over_rep(turned[1:])), chips, 3 * span, False
    )
    w_out_late, w_down_late = after((w_out, w_down), normed)
    w_out_chip = jnp.concatenate([w_out_late, w_out_other], 0)
    w_down_chip = jnp.concatenate([w_down_late, w_down_other], 0)
    hidden_one = after(hidden_one, w_out_chip, w_down_chip)
    cot_mine = cotangent[0].reshape(block, wide)
    cut_up = cut_pieces(at, [after(w_up, *one_first)], ff_part, chips, True)
    near_up = exchange(after(tuple(cut_up), one_last))
    near = after(jnp.concatenate([mine[None], near_one], 0), *one_first)
    for bit in bits[1:]:
        near = jnp.concatenate([near, swap(near, "shard", bit)], 0)
    stacked = jnp.concatenate([near, swap(near, "shard", 1)], 0)

    owners = np.concatenate([np.arange(chips) * 2, np.arange(chips) * 2 + 1]).astype(np.int32)
    locs = np.tile(np.arange(rows, dtype=np.int32), 2 * chips)
    positions = (me_late ^ jnp.asarray(np.repeat(owners, rows))) * rows + jnp.asarray(locs)
    labels = jnp.stack([piece_labels(starts[s], positions) for s in range(count)])
    where = (positions[:, None], positions[None, :], labels[:, :, None], labels[:, None, :])

    whole = place_columns(me_arr, stacked, subsets(order)).reshape(6, count, rank, wide)
    in_qkv = jnp.swapaxes(whole[:3], 0, 1).reshape(count * 3 * rank, wide)
    in_exp, out_att, out_red = (whole[3 + i].reshape(count * rank, wide) for i in range(3))

    def unpack(table, i):
        return table[:, edges[i] : edges[i + 1]]

    def out_qkv_of(table):
        stacked = jnp.stack([unpack(table, t).reshape(count, rank, span) for t in range(3)], 1)
        spread = stacked[:, :, :, None, :] * jnp.eye(3, dtype=BF16)[None, :, None, :, None]
        return spread.reshape(count * 3 * rank, 3 * span)

    out_qkv_mine, out_qkv_other = out_qkv_of(packed), out_qkv_of(packed_other)
    in_att, out_exp, in_red = (
        jnp.concatenate([unpack(packed, i), unpack(packed_other, i)], 1) for i in (3, 4, 5)
    )

    def slice_of(bias, index, width):
        return lax.dynamic_slice_in_dim(bias, index * width, width).astype(F32)

    def b_qkv_of(index):
        return jnp.concatenate(
            [slice_of(b_query, index, span), jnp.zeros((span,), F32), slice_of(b_value, index, span)]
        )

    b_up_chip = jnp.concatenate([slice_of(b_up, me, ff_part), slice_of(b_up, me ^ 1, ff_part)])

    def by_chip(value):
        return value.reshape((chips, count, rows) + value.shape[1:])

    def flat(value):
        return value.reshape(chips * block, value.shape[-1])

    def block_products(products, low, table):
        parts = {}
        for i in reversed(range(chips)):
            at = slice(i * block, (i + 1) * block)
            total = mm(low[at], table)
            for value, weight, main in products:
                total = total + main(value[at], weight)
            parts[2 * i] = total.astype(BF16)
            if i == chips - 1:
                low = after(low, parts[2 * i])
                products = [(after(v, parts[2 * i]), w, main) for v, w, main in products]
        return parts

    low_qkv = keep_own(mm_t(hidden_one, in_qkv), 3)
    qkv_away = (
        mm(hidden_one, w_qkv_other) + mm(low_qkv, out_qkv_other) + b_qkv_of(me ^ 1)
    ).astype(BF16)
    qkv_other = by_chip(swap(qkv_away, "shard", 1))
    qkv_own = by_chip(
        (mm(hidden_one, w_qkv_mine) + mm(low_qkv, out_qkv_mine) + b_qkv_of(me)).astype(BF16)
    )
    qkv_own = after(qkv_own, *near_up[1:])
    att_own, att_away, lse = attend(where, qkv_own, qkv_other, heads)
    cot_pieces, _, _ = gather_rows(after(cot_mine, att_own), bits, apart=True)
    attended = jnp.concatenate([flat(att_own), swap(flat(att_away), "shard", 1)], 1)
    low_att = keep_own(mm_t(attended, in_att))
    parts = block_products([(attended, w_out_chip, mm)], low_att, out_att)
    terms, relayed = scatter_rows(parts, bits)
    cot = jnp.concatenate(after(cot_pieces, *relayed), 0)
    glow_red = keep_own(mm_t(cot, out_red))
    grad_act = (mm_t(cot, w_down_chip) + mm(glow_red, in_red)).astype(BF16)
    terms[0] = after(terms[0], grad_act)
    residual, hidden_block = row_call(
        norm_kernel, [rows_in, vectors] + terms, block, wide, [F32, BF16], "norm"
    )
    far_up = halves_over_rep(after(tuple(near_up[1:]), parts[2 * (chips - 1)]))
    pieces_up = after((*near_up, *far_up), hidden_block)
    hidden_two, _, _ = gather_rows(hidden_block, bits)

    rep_bits = bits_of(lax.axis_size("rep"))
    mark = (after(chosen, hidden_block)[:, None] == jnp.arange(ADAPTERS, dtype=jnp.int32)[None, :]).astype(BF16)
    marks = gather_blocks(jnp.pad(mark, ((0, 16 - count), (0, 128 - ADAPTERS))), "rep", rep_bits)
    groups = marks.shape[0]
    marks = marks[:, :count, :ADAPTERS].reshape(groups * count, 1, ADAPTERS, 1)
    place = (marks * jnp.eye(rank, dtype=BF16)[None, :, None, :]).reshape(
        groups * count * rank, ADAPTERS * rank
    )


    (w_up_chip,) = place_weights(at, both_cores(pieces_up), chips, ff_part, True)
    hidden_two = after(hidden_two, grad_act)
    low_exp = keep_own(mm_t(hidden_two, in_exp))
    pre = mm(hidden_two, w_up_chip) + mm(low_exp, out_exp) + b_up_chip
    share = 0.5 * (1.0 + lax.erf(pre * np.float32(0.5**0.5)))
    act = (pre * share).astype(BF16)
    slope = share + pre * (jnp.exp(-0.5 * pre * pre) * np.float32((2 * np.pi) ** -0.5))
    grad_pre = (slope * grad_act.astype(F32)).astype(BF16)
    glow_exp = keep_own(mm_t(grad_pre, out_exp))
    terms, grad_sent = scatter_rows(block_products([(grad_pre, w_up_chip, mm_t)], glow_exp, in_exp), bits)
    grad_residual, grad_block = row_call(
        functools.partial(norm_back_kernel, outs=2, row=1),
        [residual, vectors, cot_mine] + terms,
        block,
        wide,
        [F32, BF16],
        "norm_back",
    )
    grad_branch, _, branch_last = gather_rows(grad_block, bits)

    act_late = after(act, grad_block)
    low_red = keep_own(mm_t(act_late, in_red))
    down_parts = block_products([(act_late, w_down_chip, mm)], low_red, out_red)
    glow_att = keep_own(mm_t(grad_branch, out_att))
    grad_att = (mm_t(grad_branch, w_out_chip) + mm(glow_att, in_att)).astype(BF16)
    ga_own = by_chip(grad_att[:, :span])
    ga_other = by_chip(swap(grad_att[:, span:], "shard", 1))
    grad_own, grad_away = attend_back(where, qkv_own, qkv_other, lse, ga_own, ga_other, heads)
    grad_own = flat(grad_own)
    grad_other = swap(flat(grad_away), "shard", 1)
    glow_qkv = keep_own(mm_t(grad_own, out_qkv_mine) + mm_t(grad_other, out_qkv_other), 3)
    def sum_cores(own, away):
        return own + swap(away.astype(BF16), "shard", 1).astype(F32)

    def core_columns(value):
        width = value.shape[1] // size

        def side(which):
            return jnp.stack(
                [
                    lax.dynamic_slice_in_dim(value, (2 * k + which) * width, width, 1)
                    for k in range(chips)
                ]
            )

        core = me & 1
        return sum_cores(side(core), side(1 - core))

    def split_chips(current, bit):
        current = current.reshape((2, current.shape[0] // 2) + current.shape[1:])
        own = (me // bit) & 1
        away = lax.dynamic_index_in_dim(current, 1 - own, 0, False).astype(BF16)
        return lax.dynamic_index_in_dim(current, own, 0, False), away

    def sum_chips(current, *gate):
        for i, bit in enumerate(bits[::-1]):
            current, away = split_chips(current, bit)
            there = swap(away, "shard", bit)
            current = current + (there if i else after(there, *gate)).astype(F32)
        return current[0], away

    def over_groups(terms, gates=None):
        widths = [t.shape[1] for t in terms]
        data = jnp.concatenate([t.astype(BF16) for t in terms], 1)
        taken = gather_blocks(data, "rep", rep_bits, gates).reshape(groups * count * rank, -1)
        outs, start = [], 0
        for width in widths:
            out = t_mm(place, taken[:, start : start + width])
            outs.append(out.reshape(ADAPTERS, rank, width))
            start += width
        return outs

    def halves(value):
        middle = value.shape[1] // 2
        return value[:, :middle], value[:, middle:]

    glow_late, low_late = after((glow_exp, low_exp), grad_block)
    act_mid, grad_mid, low_mid, glow_mid = after((act, grad_pre, low_exp, glow_red), *grad_sent)
    red_own, red_away = halves(t_mm(glow_mid, act_mid))
    exp_own, exp_away = halves(t_mm(low_mid, grad_mid))
    local = sum_cores(
        jnp.concatenate([red_own, exp_own], 1), jnp.concatenate([red_away, exp_away], 1)
    )
    s_in_red, s_out_exp = over_groups(
        [local[:, :ff_part], local[:, ff_part:]], {rep_bits[-1]: (grad_away,)}
    )

    near_first = core_columns(
        jnp.concatenate([t_mm(glow_late, hidden_two), t_mm(low_red, cot)], 0)
    ).astype(BF16)
    tall = near_first.shape[1]
    riders = {}
    for i in range(chips):
        rider = lax.dynamic_index_in_dim(near_first, chip ^ i, 0, False)
        rider = jnp.pad(rider, ((0, block - tall), (0, 0)))
        riders[2 * i] = after(jnp.concatenate([down_parts[2 * i], rider], 1), branch_last)
    att_side = sum_cores(*halves(t_mm(glow_att, attended)))

    glow_last = glow_qkv
    in_terms = jnp.concatenate([t_mm(glow_last, hidden_one), t_mm(low_att, grad_branch)], 0)

    def own_terms(full):
        full = full.reshape(count, 3, rank, 3, span)
        return jnp.concatenate(
            [full[:, t, :, t].reshape(count * rank, span) for t in range(3)], 1
        )

    near_second = core_columns(in_terms)
    products = [(grad_own, w_qkv_mine, mm_t), (grad_other, w_qkv_other, mm_t)]
    parts = block_products(products, after(glow_qkv, in_terms), in_qkv)
    far_part = parts[2 * (chips - 1)]
    aside = {}

    def hop(relayed):
        aside["second"], sent = sum_chips(after(near_second, far_part), *relayed)
        return sent

    terms, relayed = scatter_rows(parts, bits, between=hop)
    second = aside["second"]
    down, _ = scatter_rows(riders, bits, (grad_away,))
    down[0] = after(down[0], *relayed)
    first = sum(t[:tall, wide:].astype(F32) for t in down).reshape(2, count * rank, slice_wide)
    layer_rows = residual + b_down.astype(F32) + sum(t[:, :wide].astype(F32) for t in down)

    own_last, other_last = after((grad_own, grad_other), *relayed)
    outer = sum_cores(own_terms(t_mm(low_qkv, own_last)), own_terms(t_mm(low_qkv, other_last)))
    (input_rows,) = row_call(
        functools.partial(norm_back_kernel, outs=1, row=3),
        [rows_in, vectors, grad_residual] + terms,
        block,
        wide,
        [BF16],
        "norm_back",
    )
    out_att_sum = second[count * 3 * rank :]
    second = second[: count * 3 * rank].reshape(count, 3, rank, slice_wide)
    ends = {rep_bits[-1]: (input_rows,)}
    s_in_att, s_in_exp, s_out_red = over_groups([att_side, first[0], first[1]], ends)
    late = over_groups(
        [second[:, t].reshape(count * rank, slice_wide) for t in range(3)]
        + [outer[:, t * span : (t + 1) * span] for t in range(3)]
        + [out_att_sum],
        ends,
    )
    s_out_att = late.pop()
    shape = (1, count, rows, wide)
    return (
        layer_rows.astype(BF16).reshape(shape),
        input_rows.reshape(shape),
        late[0],
        late[3],
        late[1],
        late[4],
        late[2],
        late[5],
        s_in_att,
        s_out_att,
        s_in_exp,
        s_out_exp,
        s_in_red,
        s_out_red,
    )


def solution(mesh):
    row = P("shard", None)
    wide = P(None, None, "shard")
    acts = P("rep", None, "shard", None)
    in_specs = (
        (acts, P(), P(), row, P(), row, row, P(), row, P(), P(), P(), row, P(), row, P())
        + (wide,) * 12
        + (P("rep", None), P("rep", None, None), acts)
    )
    out_specs = (acts, acts) + (wide,) * 12
    return jax.shard_map(
        on_device, mesh=mesh, in_specs=in_specs, out_specs=out_specs, check_vma=False
    )
```

```python
import functools

import jax
import jax.numpy as jnp
import numpy as np
from jax import lax
from jax.experimental import pallas as pl
from jax.experimental.pallas import tpu as pltpu
from jax.sharding import PartitionSpec as P

HEADS = 16
HEAD = 128
ADAPTERS = 8
PIECE = 256

EPSILON = 1e-05
MASKED = -1e30
F32 = jnp.float32
BF16 = jnp.bfloat16


def layer_norm(values, gain_vec, shift_vec):
    centre = jnp.mean(values, axis=-1, keepdims=True)
    offset = values - centre
    spread = jnp.mean(offset * offset, axis=-1, keepdims=True)
    return offset * lax.rsqrt(spread + EPSILON) * gain_vec + shift_vec


def piece_labels(starts, positions):
    inside = (positions[:, None] >= starts[None, :]) & (
        positions[:, None] < starts[None, :] + PIECE
    )
    labels = jnp.arange(1, starts.shape[0] + 1, dtype=jnp.int32)
    return jnp.sum(jnp.where(inside, labels[None, :], 0), axis=1)


def mm(a, b):
    return lax.dot_general(a, b, (((1,), (0,)), ((), ())), preferred_element_type=F32)


def mm_t(a, b):
    return lax.dot_general(a, b, (((1,), (1,)), ((), ())), preferred_element_type=F32)


def t_mm(a, b):
    return lax.dot_general(a, b, (((0,), (0,)), ((), ())), preferred_element_type=F32)


def swap(value, axis, mask):
    size = lax.axis_size(axis)
    return lax.ppermute(value, axis, [(i, i ^ mask) for i in range(size)])


def after(value, *others):
    return lax.optimization_barrier((value,) + others)[0]


def bits_of(size):
    bits = []
    while (1 << len(bits)) < size:
        bits.append(1 << len(bits))
    return bits


def subsets(bits):
    masks = [0]
    for bit in bits:
        masks = masks + [m | bit for m in masks]
    return masks


def gather_rows(block, bits, gate=(), apart=False):
    half = block.shape[0] // 2
    got = {0: [block]}
    upper, lower = {}, {}
    for bit in bits:
        there = swap(block, "shard", bit)
        there = after(there, *gate) if gate else there
        got[bit] = [there]
        upper[bit], lower[bit] = there[:half], there[half:]
    for which, order in ((upper, bits), (lower, bits[::-1])):
        for k, bit in enumerate(order):
            for sub in subsets(order[:k])[1:]:
                which[sub | bit] = swap(which[sub], "shard", bit)
    pieces = []
    for mask in subsets(bits):
        pieces += got[mask] if mask in got else [upper[mask], lower[mask]]
    firsts = [got[bit][0] for bit in bits]
    if apart:
        return pieces, firsts, pieces[-1]
    return jnp.concatenate(pieces, 0), firsts, pieces[-1]


def scatter_rows(parts, bits, gate=(), between=None):
    half = parts[0].shape[0] // 2
    upper = {m: p[:half] for m, p in parts.items()}
    lower = {m: p[half:] for m, p in parts.items()}
    for which, order in ((upper, bits), (lower, bits[::-1])):
        for k in reversed(range(len(order))):
            for sub in subsets(order[:k])[1:]:
                other = swap(which[sub | order[k]], "shard", order[k])
                other = after(other, *gate) if gate else other
                which[sub] = (which[sub].astype(F32) + other.astype(F32)).astype(BF16)
    blocks = [jnp.concatenate([upper[bit], lower[bit]], 0) for bit in bits]
    if between:
        blocks = list(after(tuple(blocks), between(blocks)))
    return [parts[0]] + [swap(b, "shard", bit) for b, bit in zip(blocks, bits)], blocks


def gather_blocks(value, axis, bits):
    current = value[None]
    for bit in bits:
        current = jnp.concatenate([current, swap(current, axis, bit)], 0)
    return current


def run_copies(copies):
    for copy in copies:
        copy.start()
    for copy in copies:
        copy.wait()


def cut_kernel(at_ref, *refs, count, terms, width):
    tables, outs, sems = refs[:terms], refs[terms:-1], refs[-1]
    me, part = at_ref[0], at_ref[1]
    copies = []
    for i in range(count):
        rows = outs[i].shape[0]
        first = pl.multiple_of(part * rows, rows) if rows < tables[0].shape[0] else 0
        for k in range(2):
            column = pl.multiple_of((((me // 2) ^ i) * 2 + k) * width, width)
            for t in range(terms):
                copies.append(
                    pltpu.make_async_copy(
                        tables[t].at[pl.ds(first, rows), pl.ds(column, width)],
                        outs[i].at[:, pl.ds((k * terms + t) * width, width)],
                        sems.at[len(copies)],
                    )
                )
    run_copies(copies)


def cut_pieces(at, tables, width, count, split):
    rows, terms = tables[0].shape[0], len(tables)
    shapes = [
        jax.ShapeDtypeStruct((rows // 2 if i and split else rows, 2 * terms * width), BF16)
        for i in range(count)
    ]
    return pl.pallas_call(
        functools.partial(cut_kernel, count=count, terms=terms, width=width),
        out_shape=shapes,
        in_specs=[pl.BlockSpec(memory_space=pltpu.SMEM)]
        + [pl.BlockSpec(memory_space=pl.ANY)] * terms,
        out_specs=[pl.BlockSpec(memory_space=pltpu.VMEM)] * count,
        scratch_shapes=[pltpu.SemaphoreType.DMA((2 * terms * count,))],
        cost_estimate=pl.CostEstimate(
            flops=0, bytes_accessed=4 * rows * count * terms * width, transcendentals=0
        ),
        name="cut_pieces",
    )(at, *tables)


def place_kernel(at_ref, *refs, count, width, rows, joined):
    each = (len(refs) - 1 - (1 if joined else 2)) // 2
    pieces, outs, sems = refs[: 2 * each], refs[2 * each : -1], refs[-1]
    me, part = at_ref[0], at_ref[1]

    def copies(core):
        made = []
        for side in range(2):
            for j in range(each):
                i, second = (j, 0) if j < count else (j - count + 1, 1)
                piece = pieces[side * each + j]
                height = piece.shape[0]
                row = (me ^ (2 * i) ^ side) * rows
                if height < rows:
                    row = row + (part ^ second) * height
                row = pl.multiple_of(row, height)
                for k in range(2):
                    own = k ^ core
                    source = piece.at[:, pl.ds(k * width, width)]
                    if joined:
                        target = outs[0].at[pl.ds(row, height), pl.ds(own * width, width)]
                    else:
                        target = outs[own].at[pl.ds(row, height)]
                    made.append(pltpu.make_async_copy(source, target, sems.at[len(made)]))
        return made

    @pl.when((me & 1) == 0)
    def _():
        run_copies(copies(0))

    @pl.when((me & 1) == 1)
    def _():
        run_copies(copies(1))


def place_weights(at, pieces, count, width, joined):
    rows = pieces[0].shape[0]
    if joined:
        shapes = [jax.ShapeDtypeStruct((rows * count * 2, 2 * width), BF16)]
    else:
        shapes = [jax.ShapeDtypeStruct((rows * count * 2, width), BF16)] * 2
    return pl.pallas_call(
        functools.partial(place_kernel, count=count, width=width, rows=rows, joined=joined),
        out_shape=shapes,
        in_specs=[pl.BlockSpec(memory_space=pltpu.SMEM)]
        + [pl.BlockSpec(memory_space=pl.ANY)] * len(pieces),
        out_specs=[pl.BlockSpec(memory_space=pltpu.VMEM)] * len(shapes),
        scratch_shapes=[pltpu.SemaphoreType.DMA((2 * len(pieces),))],
        cost_estimate=pl.CostEstimate(
            flops=0, bytes_accessed=16 * rows * count * width, transcendentals=0
        ),
        name="place_weights",
    )(at, *pieces)


def pick_kernel(chosen_ref, *refs, tall, rank):
    tables, (tall_ref, flat_ref, sems) = refs[:-3], refs[-3:]
    count = chosen_ref.shape[0]
    copies = []
    for s in range(count):
        column = 0
        for i, table in enumerate(tables):
            if i < tall:
                target = tall_ref.at[pl.ds((i * count + s) * rank, rank)]
            else:
                width = table.shape[2]
                target = flat_ref.at[pl.ds(s * rank, rank), pl.ds(column, width)]
                column += width
            copies.append(
                pltpu.make_async_copy(table.at[chosen_ref[s]], target, sems.at[len(copies)])
            )
    run_copies(copies)


def pick_maps(chosen, upright, flat):
    count, rank = chosen.shape[0], upright[0].shape[1]
    total = sum(t.shape[2] for t in flat)
    shapes = (
        jax.ShapeDtypeStruct((len(upright) * count * rank, upright[0].shape[2]), BF16),
        jax.ShapeDtypeStruct((count * rank, total), BF16),
    )
    tables = upright + flat
    return pl.pallas_call(
        functools.partial(pick_kernel, tall=len(upright), rank=rank),
        out_shape=shapes,
        in_specs=[pl.BlockSpec(memory_space=pltpu.SMEM)]
        + [pl.BlockSpec(memory_space=pl.ANY)] * len(tables),
        out_specs=[pl.BlockSpec(memory_space=pltpu.VMEM)] * 2,
        scratch_shapes=[pltpu.SemaphoreType.DMA((count * len(tables),))],
        cost_estimate=pl.CostEstimate(
            flops=0, bytes_accessed=8 * count * rank * total, transcendentals=0
        ),
        name="pick_maps",
    )(chosen, *tables)


def cols_kernel(me_ref, in_ref, out_ref, sems, *, masks):
    width = in_ref.shape[2]
    run_copies(
        [
            pltpu.make_async_copy(
                in_ref.at[i],
                out_ref.at[:, pl.ds(pl.multiple_of((me_ref[0] ^ mask) * width, width), width)],
                sems.at[i],
            )
            for i, mask in enumerate(masks)
        ]
    )


def place_columns(me, stacked, masks):
    count, rows, width = stacked.shape
    return pl.pallas_call(
        functools.partial(cols_kernel, masks=masks),
        out_shape=jax.ShapeDtypeStruct((rows, count * width), stacked.dtype),
        in_specs=[pl.BlockSpec(memory_space=pltpu.SMEM), pl.BlockSpec(memory_space=pltpu.VMEM)],
        out_specs=pl.BlockSpec(memory_space=pltpu.VMEM),
        scratch_shapes=[pltpu.SemaphoreType.DMA((count,))],
        cost_estimate=pl.CostEstimate(
            flops=0, bytes_accessed=4 * count * rows * width, transcendentals=0
        ),
        name="place_columns",
    )(me, stacked)


def normalised(values):
    centre = jnp.mean(values, axis=-1, keepdims=True)
    offset = values - centre
    scale = lax.rsqrt(jnp.mean(offset * offset, axis=-1, keepdims=True) + EPSILON)
    return offset * scale, scale


def total_of(refs, at):
    total = refs[0][at].astype(F32)
    for ref in refs[1:]:
        total = total + ref[at].astype(F32)
    return total


def tiles_of(rows):
    tile = 32 if rows % 32 == 0 else rows
    return [slice(i, i + tile) for i in range(0, rows, tile)]


def norm_kernel(base, vectors, *refs):
    terms, (res_ref, out_ref) = refs[:-2], refs[-2:]
    shift, gain, bias = vectors[0:1], vectors[1:2], vectors[2:3]
    for at in tiles_of(base.shape[0]):
        values = base[at].astype(F32) + (total_of(terms, at) + shift)
        res_ref[at] = values
        unit, _ = normalised(values)
        out_ref[at] = (unit * gain + bias).astype(BF16)


def norm_back_kernel(values, vectors, base, *refs, outs, row):
    gain = vectors[row : row + 1]
    terms, outputs = refs[: len(refs) - outs], refs[len(refs) - outs :]
    for at in tiles_of(values.shape[0]):
        unit, scale = normalised(values[at].astype(F32))
        grad = total_of(terms, at) * gain
        mean_one = jnp.mean(grad, axis=-1, keepdims=True)
        mean_two = jnp.mean(grad * unit, axis=-1, keepdims=True)
        total = base[at].astype(F32) + scale * (grad - mean_one - unit * mean_two)
        for out in outputs:
            out[at] = total.astype(out.dtype)


def row_call(kernel, order, rows, wide, dtypes, name):
    return pl.pallas_call(
        kernel,
        out_shape=[jax.ShapeDtypeStruct((rows, wide), d) for d in dtypes],
        in_specs=[pl.BlockSpec(memory_space=pltpu.VMEM)] * len(order),
        out_specs=[pl.BlockSpec(memory_space=pltpu.VMEM)] * len(dtypes),
        cost_estimate=pl.CostEstimate(
            flops=20 * rows * wide, bytes_accessed=16 * rows * wide, transcendentals=0
        ),
        name=name,
    )(*order)


def sum_kernel(place, *refs, blocks):
    gathered, outs = refs[:blocks], refs[blocks:]
    start = 0
    for out in outs:
        width = out.shape[1]
        total, row = None, 0
        for ref in gathered:
            for g in range(ref.shape[0]):
                rows = ref.shape[1]
                term = t_mm(place[row : row + rows], ref[g, :, start : start + width])
                total = term if total is None else total + term
                row += rows
        out[...] = total
        start += width


def sum_blocks(place, gathered, widths):
    total = sum(widths)
    return pl.pallas_call(
        functools.partial(sum_kernel, blocks=len(gathered)),
        out_shape=[jax.ShapeDtypeStruct((place.shape[1], w), F32) for w in widths],
        in_specs=[pl.BlockSpec(memory_space=pltpu.VMEM)] * (1 + len(gathered)),
        out_specs=[pl.BlockSpec(memory_space=pltpu.VMEM)] * len(widths),
        cost_estimate=pl.CostEstimate(
            flops=2 * place.size * total, bytes_accessed=(2 * place.shape[0] + 4 * place.shape[1]) * total, transcendentals=0
        ),
        name="sum_blocks",
    )(place, *gathered)


def seen(pos_q, pos_k, lab_q, lab_k):
    return (pos_k <= pos_q) | ((lab_q == lab_k) & (lab_q > 0))


def both(own_ref, other_ref, low, high):
    own, other = own_ref[:, 0, :, low:high], other_ref[:, 0, :, low:high]
    chips, rows, width = own.shape
    return jnp.concatenate([own.reshape(chips * rows, width), other.reshape(chips * rows, width)], 0)


def put(own_ref, other_ref, low, high, value):
    chips, _, rows, _ = own_ref.shape
    half = chips * rows
    own_ref[:, 0, :, low:high] = value[:half].reshape(chips, rows, high - low)
    other_ref[:, 0, :, low:high] = value[half:].reshape(chips, rows, high - low)


def attend_kernel(pq, pk, lq, lk, own, other, out_own, out_other, lse_ref, *, heads, factor):
    allowed = seen(pq[...], pk[...], lq[0], lk[0])
    span = heads * HEAD
    for h in range(heads):
        low, high = h * HEAD, (h + 1) * HEAD
        q = both(own, other, low, high)
        k = both(own, other, span + low, span + high)
        v = both(own, other, 2 * span + low, 2 * span + high)
        scores = jnp.where(allowed, mm_t(q, k) * factor, MASKED)
        top = jnp.max(scores, axis=-1, keepdims=True)
        expo = jnp.exp(scores - top)
        total = jnp.sum(expo, axis=-1, keepdims=True)
        probs = (expo * (1.0 / total)).astype(BF16)
        put(out_own, out_other, low, high, mm(probs, v).astype(BF16))
        lse_ref[0, :, h : h + 1] = top + jnp.log(total)


def attend_specs(chips, count, rows, length):
    whole = pl.BlockSpec(memory_space=pltpu.VMEM)
    where = [
        pl.BlockSpec((length, 1), lambda s: (0, 0)),
        pl.BlockSpec((1, length), lambda s: (0, 0)),
        pl.BlockSpec((1, length, 1), lambda s: (s, 0, 0)),
        pl.BlockSpec((1, 1, length), lambda s: (s, 0, 0)),
    ]

    def of(width):
        return pl.BlockSpec((chips, 1, rows, width), lambda s: (0, s, 0, 0))

    return where, of


def attend(where, own, other, heads):
    chips, count, rows, _ = own.shape
    length = 2 * chips * rows
    span = heads * HEAD
    places, of = attend_specs(chips, count, rows, length)
    return pl.pallas_call(
        functools.partial(attend_kernel, heads=heads, factor=HEAD ** (-0.5)),
        out_shape=(
            jax.ShapeDtypeStruct((chips, count, rows, span), BF16),
            jax.ShapeDtypeStruct((chips, count, rows, span), BF16),
            jax.ShapeDtypeStruct((count, length, heads), F32),
        ),
        grid=(count,),
        in_specs=places + [of(3 * span), of(3 * span)],
        out_specs=(of(span), of(span), pl.BlockSpec((1, length, heads), lambda s: (s, 0, 0))),
        cost_estimate=pl.CostEstimate(
            flops=count * heads * length * length * HEAD * 4,
            bytes_accessed=count * length * heads * HEAD * 8,
            transcendentals=count * heads * length * length,
        ),
        name="attend",
    )(*where, own, other)


def attend_back_kernel(
    pq, pk, lq, lk, own, other, lse_ref, ga_own, ga_other, out_own, out_other, *, heads, factor
):
    allowed = seen(pq[...], pk[...], lq[0], lk[0])
    span = heads * HEAD
    for h in range(heads):
        low, high = h * HEAD, (h + 1) * HEAD
        q = both(own, other, low, high)
        k = both(own, other, span + low, span + high)
        v = both(own, other, 2 * span + low, 2 * span + high)
        ga = both(ga_own, ga_other, low, high)
        scores = jnp.where(allowed, mm_t(q, k) * factor, MASKED)
        probs = jnp.exp(scores - lse_ref[0, :, h : h + 1])
        grad_probs = mm_t(ga, v)
        inner = jnp.sum(probs * grad_probs, axis=-1, keepdims=True)
        grad_scores = (probs * (grad_probs - inner)).astype(BF16)
        put(out_own, out_other, low, high, (mm(grad_scores, k) * factor).astype(BF16))
        put(
            out_own,
            out_other,
            span + low,
            span + high,
            (t_mm(grad_scores, q) * factor).astype(BF16),
        )
        put(
            out_own,
            out_other,
            2 * span + low,
            2 * span + high,
            t_mm(probs.astype(BF16), ga).astype(BF16),
        )


def attend_back(where, own, other, lse, ga_own, ga_other, heads):
    chips, count, rows, _ = own.shape
    length = 2 * chips * rows
    span = heads * HEAD
    places, of = attend_specs(chips, count, rows, length)
    return pl.pallas_call(
        functools.partial(attend_back_kernel, heads=heads, factor=HEAD ** (-0.5)),
        out_shape=(jax.ShapeDtypeStruct((chips, count, rows, 3 * span), BF16),) * 2,
        grid=(count,),
        in_specs=places
        + [of(3 * span), of(3 * span)]
        + [pl.BlockSpec((1, length, heads), lambda s: (s, 0, 0)), of(span), of(span)],
        out_specs=(of(3 * span), of(3 * span)),
        cost_estimate=pl.CostEstimate(
            flops=count * heads * length * length * HEAD * 10,
            bytes_accessed=count * length * heads * HEAD * 14,
            transcendentals=count * heads * length * length,
        ),
        name="attend_back",
    )(*where, own, other, lse, ga_own, ga_other)


def on_device(
    inputs,
    ln1_gain,
    ln1_bias,
    w_query,
    b_query,
    w_key,
    w_value,
    b_value,
    w_out,
    b_out,
    ln2_gain,
    ln2_bias,
    w_up,
    b_up,
    w_down,
    b_down,
    in_query,
    out_query,
    in_key,
    out_key,
    in_value,
    out_value,
    in_attn,
    out_attn,
    in_expand,
    out_expand,
    in_reduce,
    out_reduce,
    adapter_pick,
    piece_start,
    cotangent,
):
    count, rows, wide = inputs.shape[1:]
    size = lax.axis_size("shard")
    chips = size // 2
    bits = bits_of(size)[1:]
    me = lax.axis_index("shard").astype(jnp.int32)
    me_arr = me[None]
    part = lax.axis_index("rep").astype(jnp.int32) & 1
    at = jnp.stack([me, part])
    heads = HEADS // size
    span = heads * HEAD
    slice_wide = wide // size
    ff_part = w_up.shape[1] // size
    rank = in_query.shape[1]
    block = count * rows
    chosen = adapter_pick[0]
    starts = piece_start[0]

    def keep_own(value, terms=1):
        of_row = lax.broadcasted_iota(jnp.int32, value.shape, 0) // rows % count
        of_col = lax.broadcasted_iota(jnp.int32, value.shape, 1) // (terms * rank)
        return jnp.where(of_row == of_col, value, 0.0).astype(BF16)

    chip = me // 2

    def exchange(pieces):
        return [pieces[0]] + [swap(p, "shard", 2 * i) for i, p in enumerate(pieces) if i]

    def halves_over_rep(pieces):
        return [swap(piece, "rep", 1) for piece in pieces]

    def both_cores(own):
        return list(own) + [swap(piece, "shard", 1) for piece in own]

    w_out_other = swap(w_out, "shard", 1)
    w_down_other = swap(w_down, "shard", 1)
    pieces_qkv = cut_pieces(at, [w_query, w_key, w_value], span, chips, True)
    turned = exchange(pieces_qkv)
    near_up = exchange(cut_pieces(at, [after(w_up, *pieces_qkv)], ff_part, chips, True))

    narrow = [out_query, out_key, out_value, in_attn, out_expand, in_reduce]
    edges = np.cumsum([0] + [n.shape[2] for n in narrow])
    mine, packed = pick_maps(
        after(chosen, w_out_other, w_down_other, *pieces_qkv),
        [in_query, in_key, in_value, in_expand, out_attn, out_reduce],
        narrow,
    )
    packed_other = swap(packed, "shard", 1)
    order = bits + [1]
    near_one = swap(mine[None], "shard", bits[0])

    rows_in = after(inputs[0].reshape(block, wide), mine)
    features = rows_in.astype(F32)
    normed = layer_norm(features, ln1_gain.astype(F32), ln1_bias.astype(F32)).astype(BF16)
    starts, b_query, b_value, b_up, me_late, chosen, packed = after(
        (starts, b_query, b_value, b_up, me, chosen, packed), normed
    )
    vectors = after(jnp.stack([b_out, ln2_gain, ln2_bias, ln1_gain]), normed).astype(F32)
    hidden_block = after(normed, packed_other, near_one, *turned[1:], *near_up[1:])
    hidden_one, one_first, one_last = gather_rows(hidden_block, bits)

    turned[0] = after(turned[0], *one_first)
    w_qkv_mine, w_qkv_other = place_weights(
        at, both_cores(turned + halves_over_rep(turned[1:])), chips, 3 * span, False
    )
    far_up = halves_over_rep(near_up[1:])
    w_out_late, w_down_late = after((w_out, w_down), normed)
    w_out_chip = jnp.concatenate([w_out_late, w_out_other], 0)
    w_down_chip = jnp.concatenate([w_down_late, w_down_other], 0)
    hidden_one = after(hidden_one, w_out_chip, w_down_chip, *far_up)
    cot_mine = cotangent[0].reshape(block, wide)
    near = after(jnp.concatenate([mine[None], near_one], 0), *one_first)
    for bit in bits[1:]:
        near = jnp.concatenate([near, swap(near, "shard", bit)], 0)
    stacked = jnp.concatenate([near, swap(near, "shard", 1)], 0)

    owners = np.concatenate([np.arange(chips) * 2, np.arange(chips) * 2 + 1]).astype(np.int32)
    locs = np.tile(np.arange(rows, dtype=np.int32), 2 * chips)
    positions = (me_late ^ jnp.asarray(np.repeat(owners, rows))) * rows + jnp.asarray(locs)
    labels = jnp.stack([piece_labels(starts[s], positions) for s in range(count)])
    where = (positions[:, None], positions[None, :], labels[:, :, None], labels[:, None, :])

    whole = place_columns(me_arr, stacked, subsets(order)).reshape(6, count, rank, wide)
    in_qkv = jnp.swapaxes(whole[:3], 0, 1).reshape(count * 3 * rank, wide)
    in_exp, out_att, out_red = (whole[3 + i].reshape(count * rank, wide) for i in range(3))

    def unpack(table, i):
        return table[:, edges[i] : edges[i + 1]]

    def out_qkv_of(table):
        stacked = jnp.stack([unpack(table, t).reshape(count, rank, span) for t in range(3)], 1)
        spread = stacked[:, :, :, None, :] * jnp.eye(3, dtype=BF16)[None, :, None, :, None]
        return spread.reshape(count * 3 * rank, 3 * span)

    out_qkv_mine, out_qkv_other = out_qkv_of(packed), out_qkv_of(packed_other)
    in_att, out_exp, in_red = (
        jnp.concatenate([unpack(packed, i), unpack(packed_other, i)], 1) for i in (3, 4, 5)
    )

    def slice_of(bias, index, width):
        return lax.dynamic_slice_in_dim(bias, index * width, width).astype(F32)

    def b_qkv_of(index):
        return jnp.concatenate(
            [slice_of(b_query, index, span), jnp.zeros((span,), F32), slice_of(b_value, index, span)]
        )

    b_up_chip = jnp.concatenate([slice_of(b_up, me, ff_part), slice_of(b_up, me ^ 1, ff_part)])

    def by_chip(value):
        return value.reshape((chips, count, rows) + value.shape[1:])

    def flat(value):
        return value.reshape(chips * block, value.shape[-1])

    def block_products(products, low, table):
        parts = {}
        for i in reversed(range(chips)):
            at = slice(i * block, (i + 1) * block)
            total = mm(low[at], table)
            for value, weight, main in products:
                total = total + main(value[at], weight)
            parts[2 * i] = total.astype(BF16)
            if i == chips - 1:
                low = after(low, parts[2 * i])
                products = [(after(v, parts[2 * i]), w, main) for v, w, main in products]
        return parts

    hidden_one = after(hidden_one, where, out_qkv_mine, out_qkv_other, in_att, out_exp, in_red)
    low_qkv = keep_own(mm_t(hidden_one, in_qkv), 3)
    qkv_away = (
        mm(hidden_one, w_qkv_other) + mm(low_qkv, out_qkv_other) + b_qkv_of(me ^ 1)
    ).astype(BF16)
    qkv_other = by_chip(swap(qkv_away, "shard", 1))
    qkv_own = by_chip(
        (mm(hidden_one, w_qkv_mine) + mm(low_qkv, out_qkv_mine) + b_qkv_of(me)).astype(BF16)
    )
    att_own, att_away, lse = attend(where, qkv_own, qkv_other, heads)
    attended = jnp.concatenate([flat(att_own), swap(flat(att_away), "shard", 1)], 1)
    low_att = keep_own(mm_t(attended, in_att))
    parts = block_products([(attended, w_out_chip, mm)], low_att, out_att)
    cot_pieces, _, _ = gather_rows(
        after(cot_mine, one_last), bits, (parts[2 * (chips - 1)],), apart=True
    )
    terms, relayed = scatter_rows(parts, bits)
    cot = jnp.concatenate(after(cot_pieces, *relayed), 0)
    glow_red = keep_own(mm_t(cot, out_red))
    grad_act = (mm_t(cot, w_down_chip) + mm(glow_red, in_red)).astype(BF16)
    terms[0] = after(terms[0], grad_act)
    residual, hidden_block = row_call(
        norm_kernel, [rows_in, vectors] + terms, block, wide, [F32, BF16], "norm"
    )
    pieces_up = after((*near_up, *far_up), hidden_block)
    hidden_two, _, _ = gather_rows(hidden_block, bits)

    (w_up_chip,) = place_weights(at, both_cores(pieces_up), chips, ff_part, True)
    hidden_two = after(hidden_two, grad_act)
    low_exp = keep_own(mm_t(hidden_two, in_exp))
    pre = mm(hidden_two, w_up_chip) + mm(low_exp, out_exp) + b_up_chip
    share = 0.5 * (1.0 + lax.erf(pre * np.float32(0.5**0.5)))
    act = (pre * share).astype(BF16)
    slope = share + pre * (jnp.exp(-0.5 * pre * pre) * np.float32((2 * np.pi) ** -0.5))
    grad_pre = (slope * grad_act.astype(F32)).astype(BF16)
    glow_exp = keep_own(mm_t(grad_pre, out_exp))
    terms, grad_sent = scatter_rows(block_products([(grad_pre, w_up_chip, mm_t)], glow_exp, in_exp), bits)
    grad_residual, grad_block = row_call(
        functools.partial(norm_back_kernel, outs=2, row=1),
        [residual, vectors, cot_mine] + terms,
        block,
        wide,
        [F32, BF16],
        "norm_back",
    )
    grad_branch, _, branch_last = gather_rows(grad_block, bits)

    rep_bits = bits_of(lax.axis_size("rep"))
    mark = (after(chosen, grad_block)[:, None] == jnp.arange(ADAPTERS, dtype=jnp.int32)[None, :]).astype(BF16)
    marks = gather_blocks(jnp.pad(mark, ((0, 16 - count), (0, 128 - ADAPTERS))), "rep", rep_bits)
    groups = marks.shape[0]
    marks = marks[:, :count, :ADAPTERS].reshape(groups * count, 1, ADAPTERS, 1)
    place = (marks * jnp.eye(rank, dtype=BF16)[None, :, None, :]).reshape(
        groups * count * rank, ADAPTERS * rank
    )


    act_late = after(act, grad_block)
    low_red = keep_own(mm_t(act_late, in_red))
    down_parts = block_products([(act_late, w_down_chip, mm)], low_red, out_red)
    glow_att = keep_own(mm_t(grad_branch, out_att))
    grad_att = (mm_t(grad_branch, w_out_chip) + mm(glow_att, in_att)).astype(BF16)
    ga_own = by_chip(grad_att[:, :span])
    ga_other = by_chip(swap(grad_att[:, span:], "shard", 1))
    grad_own, grad_away = attend_back(where, qkv_own, qkv_other, lse, ga_own, ga_other, heads)
    grad_own = flat(grad_own)
    grad_other = swap(flat(grad_away), "shard", 1)
    glow_qkv = keep_own(mm_t(grad_own, out_qkv_mine) + mm_t(grad_other, out_qkv_other), 3)
    def sum_cores(own, away):
        return own + swap(away.astype(BF16), "shard", 1).astype(F32)

    def core_columns(value):
        width = value.shape[1] // size

        def side(which):
            return jnp.stack(
                [
                    lax.dynamic_slice_in_dim(value, (2 * k + which) * width, width, 1)
                    for k in range(chips)
                ]
            )

        core = me & 1
        return sum_cores(side(core), side(1 - core))

    def split_chips(current, bit):
        current = current.reshape((2, current.shape[0] // 2) + current.shape[1:])
        own = (me // bit) & 1
        away = lax.dynamic_index_in_dim(current, 1 - own, 0, False).astype(BF16)
        return lax.dynamic_index_in_dim(current, own, 0, False), away

    def sum_chips(current, *gate):
        for i, bit in enumerate(bits[::-1]):
            current, away = split_chips(current, bit)
            there = swap(away, "shard", bit)
            current = current + (there if i else after(there, *gate)).astype(F32)
        return current[0], away

    def over_groups(terms, hold=()):
        widths = [t.shape[1] for t in terms]
        data = jnp.concatenate([t.astype(BF16) for t in terms], 1)
        gathered, current = [data[None]], data[None]
        for bit in rep_bits:
            if hold and bit == rep_bits[-1]:
                current = after(current, *hold)
            there = swap(current, "rep", bit)
            gathered.append(there)
            if bit != rep_bits[-1]:
                current = jnp.concatenate([current, there], 0)
        return [out.reshape(ADAPTERS, rank, -1) for out in sum_blocks(place, gathered, widths)]

    def halves(value):
        middle = value.shape[1] // 2
        return value[:, :middle], value[:, middle:]

    glow_late, low_late = after((glow_exp, low_exp), grad_block)
    act_mid, grad_mid, low_mid, glow_mid = after((act, grad_pre, low_exp, glow_red), grad_block)
    red_own, red_away = halves(t_mm(glow_mid, act_mid))
    exp_own, exp_away = halves(t_mm(low_mid, grad_mid))
    local = sum_cores(
        jnp.concatenate([red_own, exp_own], 1), jnp.concatenate([red_away, exp_away], 1)
    )
    s_in_red, s_out_exp = over_groups(
        [local[:, :ff_part], local[:, ff_part:]]
    )

    near_first = core_columns(
        jnp.concatenate([t_mm(glow_late, hidden_two), t_mm(low_red, cot)], 0)
    ).astype(BF16)
    tall = near_first.shape[1]
    riders = {}
    for i in range(chips):
        rider = lax.dynamic_index_in_dim(near_first, chip ^ i, 0, False)
        rider = jnp.pad(rider, ((0, block - tall), (0, 0)))
        riders[2 * i] = after(jnp.concatenate([down_parts[2 * i], rider], 1), branch_last)
    att_side = sum_cores(*halves(t_mm(glow_att, attended)))

    glow_last = glow_qkv
    in_terms = jnp.concatenate([t_mm(glow_last, hidden_one), t_mm(low_att, grad_branch)], 0)

    def own_terms(full):
        full = full.reshape(count, 3, rank, 3, span)
        return jnp.concatenate(
            [full[:, t, :, t].reshape(count * rank, span) for t in range(3)], 1
        )

    near_second = core_columns(in_terms)
    products = [(grad_own, w_qkv_mine, mm_t), (grad_other, w_qkv_other, mm_t)]
    parts = block_products(products, after(glow_qkv, in_terms), in_qkv)
    far_part = parts[2 * (chips - 1)]
    aside = {}

    def hop(relayed):
        aside["second"], sent = sum_chips(after(near_second, far_part), *relayed)
        return sent

    terms, relayed = scatter_rows(parts, bits, between=hop)
    second = aside["second"]
    riders[0] = after(riders[0], s_in_red, s_out_exp)
    down, _ = scatter_rows(riders, bits, (grad_away,))
    down[0] = after(down[0], *relayed)
    first = sum(t[:tall, wide:].astype(F32) for t in down).reshape(2, count * rank, slice_wide)
    layer_rows = residual + b_down.astype(F32) + sum(t[:, :wide].astype(F32) for t in down)

    own_last, other_last = after((grad_own, grad_other), *relayed)
    outer = sum_cores(own_terms(t_mm(low_qkv, own_last)), own_terms(t_mm(low_qkv, other_last)))
    (input_rows,) = row_call(
        functools.partial(norm_back_kernel, outs=1, row=3),
        [rows_in, vectors, grad_residual] + terms,
        block,
        wide,
        [BF16],
        "norm_back",
    )
    out_att_sum = second[count * 3 * rank :]
    second = second[: count * 3 * rank].reshape(count, 3, rank, slice_wide)
    s_in_att, s_in_exp, s_out_red = over_groups([att_side, first[0], first[1]])
    late = over_groups(
        [second[:, t].reshape(count * rank, slice_wide) for t in range(3)]
        + [outer[:, t * span : (t + 1) * span] for t in range(3)]
        + [out_att_sum],
        terms[1:],
    )
    s_out_att = late.pop()
    shape = (1, count, rows, wide)
    return (
        layer_rows.astype(BF16).reshape(shape),
        input_rows.reshape(shape),
        late[0],
        late[3],
        late[1],
        late[4],
        late[2],
        late[5],
        s_in_att,
        s_out_att,
        s_in_exp,
        s_out_exp,
        s_in_red,
        s_out_red,
    )


def solution(mesh):
    row = P("shard", None)
    wide = P(None, None, "shard")
    acts = P("rep", None, "shard", None)
    in_specs = (
        (acts, P(), P(), row, P(), row, row, P(), row, P(), P(), P(), row, P(), row, P())
        + (wide,) * 12
        + (P("rep", None), P("rep", None, None), acts)
    )
    out_specs = (acts, acts) + (wide,) * 12
    return jax.shard_map(
        on_device, mesh=mesh, in_specs=in_specs, out_specs=out_specs, check_vma=False
    )
```

```python
import functools

import jax
import jax.numpy as jnp
import numpy as np
from jax import lax
from jax.experimental import pallas as pl
from jax.experimental.pallas import tpu as pltpu
from jax.sharding import PartitionSpec as P

HEADS = 16
HEAD = 128
ADAPTERS = 8
PIECE = 256

EPSILON = 1e-05
MASKED = -1e30
F32 = jnp.float32
BF16 = jnp.bfloat16


def layer_norm(values, gain_vec, shift_vec):
    centre = jnp.mean(values, axis=-1, keepdims=True)
    offset = values - centre
    spread = jnp.mean(offset * offset, axis=-1, keepdims=True)
    return offset * lax.rsqrt(spread + EPSILON) * gain_vec + shift_vec


def piece_labels(starts, positions):
    inside = (positions[:, None] >= starts[None, :]) & (
        positions[:, None] < starts[None, :] + PIECE
    )
    labels = jnp.arange(1, starts.shape[0] + 1, dtype=jnp.int32)
    return jnp.sum(jnp.where(inside, labels[None, :], 0), axis=1)


def mm(a, b):
    return lax.dot_general(a, b, (((1,), (0,)), ((), ())), preferred_element_type=F32)


def mm_t(a, b):
    return lax.dot_general(a, b, (((1,), (1,)), ((), ())), preferred_element_type=F32)


def t_mm(a, b):
    return lax.dot_general(a, b, (((0,), (0,)), ((), ())), preferred_element_type=F32)


def swap(value, axis, mask):
    size = lax.axis_size(axis)
    return lax.ppermute(value, axis, [(i, i ^ mask) for i in range(size)])


def after(value, *others):
    return lax.optimization_barrier((value,) + others)[0]


def bits_of(size):
    bits = []
    while (1 << len(bits)) < size:
        bits.append(1 << len(bits))
    return bits


def subsets(bits):
    masks = [0]
    for bit in bits:
        masks = masks + [m | bit for m in masks]
    return masks


def gather_rows(block, bits, gate=(), apart=False):
    half = block.shape[0] // 2
    got = {0: [block]}
    upper, lower = {}, {}
    for bit in bits:
        there = swap(block, "shard", bit)
        there = after(there, *gate) if gate else there
        got[bit] = [there]
        upper[bit], lower[bit] = there[:half], there[half:]
    for which, order in ((upper, bits), (lower, bits[::-1])):
        for k, bit in enumerate(order):
            for sub in subsets(order[:k])[1:]:
                which[sub | bit] = swap(which[sub], "shard", bit)
    pieces = []
    for mask in subsets(bits):
        pieces += got[mask] if mask in got else [upper[mask], lower[mask]]
    firsts = [got[bit][0] for bit in bits]
    if apart:
        return pieces, firsts, pieces[-1]
    return jnp.concatenate(pieces, 0), firsts, pieces[-1]


def scatter_rows(parts, bits, gate=(), between=None):
    half = parts[0].shape[0] // 2
    upper = {m: p[:half] for m, p in parts.items()}
    lower = {m: p[half:] for m, p in parts.items()}
    for which, order in ((upper, bits), (lower, bits[::-1])):
        for k in reversed(range(len(order))):
            for sub in subsets(order[:k])[1:]:
                other = swap(which[sub | order[k]], "shard", order[k])
                other = after(other, *gate) if gate else other
                which[sub] = (which[sub].astype(F32) + other.astype(F32)).astype(BF16)
    blocks = [jnp.concatenate([upper[bit], lower[bit]], 0) for bit in bits]
    if between:
        blocks = list(after(tuple(blocks), between(blocks)))
    return [parts[0]] + [swap(b, "shard", bit) for b, bit in zip(blocks, bits)], blocks


def gather_blocks(value, axis, bits, gates=None):
    current = value[None]
    for bit in bits:
        there = swap(current, axis, bit)
        if gates and bit in gates:
            there = after(there, *gates[bit])
        current = jnp.concatenate([current, there], 0)
    return current


def run_copies(copies):
    for copy in copies:
        copy.start()
    for copy in copies:
        copy.wait()


def cut_kernel(at_ref, *refs, count, terms, width):
    tables, outs, sems = refs[:terms], refs[terms:-1], refs[-1]
    me, part = at_ref[0], at_ref[1]
    copies = []
    for i in range(count):
        rows = outs[i].shape[0]
        first = pl.multiple_of(part * rows, rows) if rows < tables[0].shape[0] else 0
        for k in range(2):
            column = pl.multiple_of((((me // 2) ^ i) * 2 + k) * width, width)
            for t in range(terms):
                copies.append(
                    pltpu.make_async_copy(
                        tables[t].at[pl.ds(first, rows), pl.ds(column, width)],
                        outs[i].at[:, pl.ds((k * terms + t) * width, width)],
                        sems.at[len(copies)],
                    )
                )
    run_copies(copies)


def cut_pieces(at, tables, width, count, split):
    rows, terms = tables[0].shape[0], len(tables)
    shapes = [
        jax.ShapeDtypeStruct((rows // 2 if i and split else rows, 2 * terms * width), BF16)
        for i in range(count)
    ]
    return pl.pallas_call(
        functools.partial(cut_kernel, count=count, terms=terms, width=width),
        out_shape=shapes,
        in_specs=[pl.BlockSpec(memory_space=pltpu.SMEM)]
        + [pl.BlockSpec(memory_space=pl.ANY)] * terms,
        out_specs=[pl.BlockSpec(memory_space=pltpu.VMEM)] * count,
        scratch_shapes=[pltpu.SemaphoreType.DMA((2 * terms * count,))],
        cost_estimate=pl.CostEstimate(
            flops=0, bytes_accessed=4 * rows * count * terms * width, transcendentals=0
        ),
        name="cut_pieces",
    )(at, *tables)


def place_kernel(at_ref, *refs, count, width, rows, joined):
    each = (len(refs) - 1 - (1 if joined else 2)) // 2
    pieces, outs, sems = refs[: 2 * each], refs[2 * each : -1], refs[-1]
    me, part = at_ref[0], at_ref[1]

    def copies(core):
        made = []
        for side in range(2):
            for j in range(each):
                i, second = (j, 0) if j < count else (j - count + 1, 1)
                piece = pieces[side * each + j]
                height = piece.shape[0]
                row = (me ^ (2 * i) ^ side) * rows
                if height < rows:
                    row = row + (part ^ second) * height
                row = pl.multiple_of(row, height)
                for k in range(2):
                    own = k ^ core
                    source = piece.at[:, pl.ds(k * width, width)]
                    if joined:
                        target = outs[0].at[pl.ds(row, height), pl.ds(own * width, width)]
                    else:
                        target = outs[own].at[pl.ds(row, height)]
                    made.append(pltpu.make_async_copy(source, target, sems.at[len(made)]))
        return made

    @pl.when((me & 1) == 0)
    def _():
        run_copies(copies(0))

    @pl.when((me & 1) == 1)
    def _():
        run_copies(copies(1))


def place_weights(at, pieces, count, width, joined):
    rows = pieces[0].shape[0]
    if joined:
        shapes = [jax.ShapeDtypeStruct((rows * count * 2, 2 * width), BF16)]
    else:
        shapes = [jax.ShapeDtypeStruct((rows * count * 2, width), BF16)] * 2
    return pl.pallas_call(
        functools.partial(place_kernel, count=count, width=width, rows=rows, joined=joined),
        out_shape=shapes,
        in_specs=[pl.BlockSpec(memory_space=pltpu.SMEM)]
        + [pl.BlockSpec(memory_space=pl.ANY)] * len(pieces),
        out_specs=[pl.BlockSpec(memory_space=pltpu.VMEM)] * len(shapes),
        scratch_shapes=[pltpu.SemaphoreType.DMA((2 * len(pieces),))],
        cost_estimate=pl.CostEstimate(
            flops=0, bytes_accessed=16 * rows * count * width, transcendentals=0
        ),
        name="place_weights",
    )(at, *pieces)


def pick_kernel(chosen_ref, *refs, tall, rank):
    tables, (tall_ref, flat_ref, sems) = refs[:-3], refs[-3:]
    count = chosen_ref.shape[0]
    copies = []
    for s in range(count):
        column = 0
        for i, table in enumerate(tables):
            if i < tall:
                target = tall_ref.at[pl.ds((i * count + s) * rank, rank)]
            else:
                width = table.shape[2]
                target = flat_ref.at[pl.ds(s * rank, rank), pl.ds(column, width)]
                column += width
            copies.append(
                pltpu.make_async_copy(table.at[chosen_ref[s]], target, sems.at[len(copies)])
            )
    run_copies(copies)


def pick_maps(chosen, upright, flat):
    count, rank = chosen.shape[0], upright[0].shape[1]
    total = sum(t.shape[2] for t in flat)
    shapes = (
        jax.ShapeDtypeStruct((len(upright) * count * rank, upright[0].shape[2]), BF16),
        jax.ShapeDtypeStruct((count * rank, total), BF16),
    )
    tables = upright + flat
    return pl.pallas_call(
        functools.partial(pick_kernel, tall=len(upright), rank=rank),
        out_shape=shapes,
        in_specs=[pl.BlockSpec(memory_space=pltpu.SMEM)]
        + [pl.BlockSpec(memory_space=pl.ANY)] * len(tables),
        out_specs=[pl.BlockSpec(memory_space=pltpu.VMEM)] * 2,
        scratch_shapes=[pltpu.SemaphoreType.DMA((count * len(tables),))],
        cost_estimate=pl.CostEstimate(
            flops=0, bytes_accessed=8 * count * rank * total, transcendentals=0
        ),
        name="pick_maps",
    )(chosen, *tables)


def cols_kernel(me_ref, in_ref, out_ref, sems, *, masks):
    width = in_ref.shape[2]
    run_copies(
        [
            pltpu.make_async_copy(
                in_ref.at[i],
                out_ref.at[:, pl.ds(pl.multiple_of((me_ref[0] ^ mask) * width, width), width)],
                sems.at[i],
            )
            for i, mask in enumerate(masks)
        ]
    )


def place_columns(me, stacked, masks):
    count, rows, width = stacked.shape
    return pl.pallas_call(
        functools.partial(cols_kernel, masks=masks),
        out_shape=jax.ShapeDtypeStruct((rows, count * width), stacked.dtype),
        in_specs=[pl.BlockSpec(memory_space=pltpu.SMEM), pl.BlockSpec(memory_space=pltpu.VMEM)],
        out_specs=pl.BlockSpec(memory_space=pltpu.VMEM),
        scratch_shapes=[pltpu.SemaphoreType.DMA((count,))],
        cost_estimate=pl.CostEstimate(
            flops=0, bytes_accessed=4 * count * rows * width, transcendentals=0
        ),
        name="place_columns",
    )(me, stacked)


def normalised(values):
    centre = jnp.mean(values, axis=-1, keepdims=True)
    offset = values - centre
    scale = lax.rsqrt(jnp.mean(offset * offset, axis=-1, keepdims=True) + EPSILON)
    return offset * scale, scale


def total_of(refs, at):
    total = refs[0][at].astype(F32)
    for ref in refs[1:]:
        total = total + ref[at].astype(F32)
    return total


def tiles_of(rows):
    tile = 32 if rows % 32 == 0 else rows
    return [slice(i, i + tile) for i in range(0, rows, tile)]


def norm_kernel(base, vectors, *refs):
    terms, (res_ref, out_ref) = refs[:-2], refs[-2:]
    shift, gain, bias = vectors[0:1], vectors[1:2], vectors[2:3]
    for at in tiles_of(base.shape[0]):
        values = base[at].astype(F32) + (total_of(terms, at) + shift)
        res_ref[at] = values
        unit, _ = normalised(values)
        out_ref[at] = (unit * gain + bias).astype(BF16)


def norm_back_kernel(values, vectors, base, *refs, outs, row):
    gain = vectors[row : row + 1]
    terms, outputs = refs[: len(refs) - outs], refs[len(refs) - outs :]
    for at in tiles_of(values.shape[0]):
        unit, scale = normalised(values[at].astype(F32))
        grad = total_of(terms, at) * gain
        mean_one = jnp.mean(grad, axis=-1, keepdims=True)
        mean_two = jnp.mean(grad * unit, axis=-1, keepdims=True)
        total = base[at].astype(F32) + scale * (grad - mean_one - unit * mean_two)
        for out in outputs:
            out[at] = total.astype(out.dtype)


def row_call(kernel, order, rows, wide, dtypes, name):
    return pl.pallas_call(
        kernel,
        out_shape=[jax.ShapeDtypeStruct((rows, wide), d) for d in dtypes],
        in_specs=[pl.BlockSpec(memory_space=pltpu.VMEM)] * len(order),
        out_specs=[pl.BlockSpec(memory_space=pltpu.VMEM)] * len(dtypes),
        cost_estimate=pl.CostEstimate(
            flops=20 * rows * wide, bytes_accessed=200 * rows * wide, transcendentals=0
        ),
        name=name,
    )(*order)


def sum_kernel(place, *refs, blocks, rows):
    gathered, outs = refs[:blocks], refs[blocks:]
    start = 0
    for out in outs:
        width = out.shape[1]
        total, row = None, 0
        for ref in gathered:
            for g in range(ref.shape[0]):
                term = t_mm(place[row : row + rows], ref[g, :rows, start : start + width])
                total = term if total is None else total + term
                row += rows
        out[...] = total
        start += width


def sum_blocks(place, gathered, rows, widths):
    total = sum(widths)
    return pl.pallas_call(
        functools.partial(sum_kernel, blocks=len(gathered), rows=rows),
        out_shape=[jax.ShapeDtypeStruct((place.shape[1], w), F32) for w in widths],
        in_specs=[pl.BlockSpec(memory_space=pltpu.VMEM)] * (1 + len(gathered)),
        out_specs=[pl.BlockSpec(memory_space=pltpu.VMEM)] * len(widths),
        cost_estimate=pl.CostEstimate(
            flops=2 * place.size * total, bytes_accessed=(2 * place.shape[0] + 4 * place.shape[1]) * total, transcendentals=0
        ),
        name="sum_blocks",
    )(place, *gathered)


def seen(pos_q, pos_k, lab_q, lab_k):
    return (pos_k <= pos_q) | ((lab_q == lab_k) & (lab_q > 0))


def both(own_ref, other_ref, low, high):
    own, other = own_ref[:, 0, :, low:high], other_ref[:, 0, :, low:high]
    chips, rows, width = own.shape
    return jnp.concatenate([own.reshape(chips * rows, width), other.reshape(chips * rows, width)], 0)


def put(own_ref, other_ref, low, high, value):
    chips, _, rows, _ = own_ref.shape
    half = chips * rows
    own_ref[:, 0, :, low:high] = value[:half].reshape(chips, rows, high - low)
    other_ref[:, 0, :, low:high] = value[half:].reshape(chips, rows, high - low)


def attend_kernel(pq, pk, lq, lk, own, other, out_own, out_other, lse_ref, *, heads, factor):
    allowed = seen(pq[...], pk[...], lq[0], lk[0])
    span = heads * HEAD
    for h in range(heads):
        low, high = h * HEAD, (h + 1) * HEAD
        q = both(own, other, low, high)
        k = both(own, other, span + low, span + high)
        v = both(own, other, 2 * span + low, 2 * span + high)
        scores = jnp.where(allowed, mm_t(q, k) * factor, MASKED)
        top = jnp.max(scores, axis=-1, keepdims=True)
        expo = jnp.exp(scores - top)
        total = jnp.sum(expo, axis=-1, keepdims=True)
        probs = (expo * (1.0 / total)).astype(BF16)
        put(out_own, out_other, low, high, mm(probs, v).astype(BF16))
        lse_ref[0, :, h : h + 1] = top + jnp.log(total)


def attend_specs(chips, count, rows, length):
    whole = pl.BlockSpec(memory_space=pltpu.VMEM)
    where = [
        pl.BlockSpec((length, 1), lambda s: (0, 0)),
        pl.BlockSpec((1, length), lambda s: (0, 0)),
        pl.BlockSpec((1, length, 1), lambda s: (s, 0, 0)),
        pl.BlockSpec((1, 1, length), lambda s: (s, 0, 0)),
    ]

    def of(width):
        return pl.BlockSpec((chips, 1, rows, width), lambda s: (0, s, 0, 0))

    return where, of


def attend(where, own, other, heads):
    chips, count, rows, _ = own.shape
    length = 2 * chips * rows
    span = heads * HEAD
    places, of = attend_specs(chips, count, rows, length)
    return pl.pallas_call(
        functools.partial(attend_kernel, heads=heads, factor=HEAD ** (-0.5)),
        out_shape=(
            jax.ShapeDtypeStruct((chips, count, rows, span), BF16),
            jax.ShapeDtypeStruct((chips, count, rows, span), BF16),
            jax.ShapeDtypeStruct((count, length, heads), F32),
        ),
        grid=(count,),
        in_specs=places + [of(3 * span), of(3 * span)],
        out_specs=(of(span), of(span), pl.BlockSpec((1, length, heads), lambda s: (s, 0, 0))),
        cost_estimate=pl.CostEstimate(
            flops=count * heads * length * length * HEAD * 4,
            bytes_accessed=count * length * heads * HEAD * 8,
            transcendentals=count * heads * length * length,
        ),
        name="attend",
    )(*where, own, other)


def attend_back_kernel(
    pq, pk, lq, lk, own, other, lse_ref, ga_own, ga_other, out_own, out_other, *, heads, factor
):
    allowed = seen(pq[...], pk[...], lq[0], lk[0])
    span = heads * HEAD
    for h in range(heads):
        low, high = h * HEAD, (h + 1) * HEAD
        q = both(own, other, low, high)
        k = both(own, other, span + low, span + high)
        v = both(own, other, 2 * span + low, 2 * span + high)
        ga = both(ga_own, ga_other, low, high)
        scores = jnp.where(allowed, mm_t(q, k) * factor, MASKED)
        probs = jnp.exp(scores - lse_ref[0, :, h : h + 1])
        grad_probs = mm_t(ga, v)
        inner = jnp.sum(probs * grad_probs, axis=-1, keepdims=True)
        grad_scores = (probs * (grad_probs - inner)).astype(BF16)
        put(out_own, out_other, low, high, (mm(grad_scores, k) * factor).astype(BF16))
        put(
            out_own,
            out_other,
            span + low,
            span + high,
            (t_mm(grad_scores, q) * factor).astype(BF16),
        )
        put(
            out_own,
            out_other,
            2 * span + low,
            2 * span + high,
            t_mm(probs.astype(BF16), ga).astype(BF16),
        )


def attend_back(where, own, other, lse, ga_own, ga_other, heads):
    chips, count, rows, _ = own.shape
    length = 2 * chips * rows
    span = heads * HEAD
    places, of = attend_specs(chips, count, rows, length)
    return pl.pallas_call(
        functools.partial(attend_back_kernel, heads=heads, factor=HEAD ** (-0.5)),
        out_shape=(jax.ShapeDtypeStruct((chips, count, rows, 3 * span), BF16),) * 2,
        grid=(count,),
        in_specs=places
        + [of(3 * span), of(3 * span)]
        + [pl.BlockSpec((1, length, heads), lambda s: (s, 0, 0)), of(span), of(span)],
        out_specs=(of(3 * span), of(3 * span)),
        cost_estimate=pl.CostEstimate(
            flops=count * heads * length * length * HEAD * 10,
            bytes_accessed=count * length * heads * HEAD * 14,
            transcendentals=count * heads * length * length,
        ),
        name="attend_back",
    )(*where, own, other, lse, ga_own, ga_other)


def on_device(
    inputs,
    ln1_gain,
    ln1_bias,
    w_query,
    b_query,
    w_key,
    w_value,
    b_value,
    w_out,
    b_out,
    ln2_gain,
    ln2_bias,
    w_up,
    b_up,
    w_down,
    b_down,
    in_query,
    out_query,
    in_key,
    out_key,
    in_value,
    out_value,
    in_attn,
    out_attn,
    in_expand,
    out_expand,
    in_reduce,
    out_reduce,
    adapter_pick,
    piece_start,
    cotangent,
):
    count, rows, wide = inputs.shape[1:]
    size = lax.axis_size("shard")
    chips = size // 2
    bits = bits_of(size)[1:]
    me = lax.axis_index("shard").astype(jnp.int32)
    me_arr = me[None]
    part = lax.axis_index("rep").astype(jnp.int32) & 1
    at = jnp.stack([me, part])
    heads = HEADS // size
    span = heads * HEAD
    slice_wide = wide // size
    ff_part = w_up.shape[1] // size
    rank = in_query.shape[1]
    block = count * rows
    chosen = adapter_pick[0]
    starts = piece_start[0]

    def keep_own(value):
        of_row = lax.broadcasted_iota(jnp.int32, value.shape, 0) // rows % count
        of_col = lax.broadcasted_iota(jnp.int32, value.shape, 1) // rank % count
        return jnp.where(of_row == of_col, value, 0.0).astype(BF16)

    chip = me // 2

    def exchange(pieces):
        return [pieces[0]] + [swap(p, "shard", 2 * i) for i, p in enumerate(pieces) if i]

    def halves_over_rep(pieces):
        return [swap(piece, "rep", 1) for piece in pieces]

    def both_cores(own):
        return list(own) + [swap(piece, "shard", 1) for piece in own]

    w_out_other = swap(w_out, "shard", 1)
    w_down_other = swap(w_down, "shard", 1)
    pieces_qkv = cut_pieces(at, [w_query, w_key, w_value], span, chips, True)
    turned = exchange(pieces_qkv)
    near_up = exchange(cut_pieces(at, [after(w_up, *pieces_qkv)], ff_part, chips, True))

    narrow = [out_query, out_key, out_value, in_attn, out_expand, in_reduce]
    edges = np.cumsum([0] + [n.shape[2] for n in narrow])
    mine, packed = pick_maps(
        after(chosen, w_out_other, w_down_other, *pieces_qkv),
        [in_query, in_key, in_value, in_expand, out_attn, out_reduce],
        narrow,
    )
    packed_other = swap(packed, "shard", 1)
    order = bits + [1]
    near_one = swap(mine[None], "shard", bits[0])

    rows_in = after(inputs[0].reshape(block, wide), mine)
    features = rows_in.astype(F32)
    normed = layer_norm(features, ln1_gain.astype(F32), ln1_bias.astype(F32)).astype(BF16)
    starts, b_query, b_value, b_up, me_late, chosen, packed = after(
        (starts, b_query, b_value, b_up, me, chosen, packed), normed
    )
    vectors = after(jnp.stack([b_out, ln2_gain, ln2_bias, ln1_gain]), normed).astype(F32)
    hidden_block = after(normed, packed_other, near_one, *turned[1:], *near_up[1:])
    hidden_one, one_first, one_last = gather_rows(hidden_block, bits)

    turned[0] = after(turned[0], *one_first)
    w_qkv_mine, w_qkv_other = place_weights(
        at, both_cores(turned + halves_over_rep(turned[1:])), chips, 3 * span, False
    )
    w_out_late, w_down_late = after((w_out, w_down), normed)
    w_out_chip = jnp.concatenate([w_out_late, w_out_other], 0)
    w_down_chip = jnp.concatenate([w_down_late, w_down_other], 0)
    hidden_one = after(hidden_one, w_out_chip, w_down_chip)
    cot_mine = cotangent[0].reshape(block, wide)
    near = after(jnp.concatenate([mine[None], near_one], 0), *one_first)
    for bit in bits[1:]:
        near = jnp.concatenate([near, swap(near, "shard", bit)], 0)
    stacked = jnp.concatenate([near, swap(near, "shard", 1)], 0)

    owners = np.concatenate([np.arange(chips) * 2, np.arange(chips) * 2 + 1]).astype(np.int32)
    locs = np.tile(np.arange(rows, dtype=np.int32), 2 * chips)
    positions = (me_late ^ jnp.asarray(np.repeat(owners, rows))) * rows + jnp.asarray(locs)
    labels = jnp.stack([piece_labels(starts[s], positions) for s in range(count)])
    where = (positions[:, None], positions[None, :], labels[:, :, None], labels[:, None, :])

    whole = place_columns(me_arr, stacked, subsets(order)).reshape(6, count, rank, wide)
    in_qkv = whole[:3].reshape(3 * count * rank, wide)
    in_exp, out_att, out_red = (whole[3 + i].reshape(count * rank, wide) for i in range(3))

    def unpack(table, i):
        return table[:, edges[i] : edges[i + 1]]

    def out_qkv_of(table):
        stacked = jnp.stack([unpack(table, t) for t in range(3)])
        spread = stacked[:, :, None, :] * jnp.eye(3, dtype=BF16)[:, None, :, None]
        return spread.reshape(count * 3 * rank, 3 * span)

    out_qkv_mine, out_qkv_other = out_qkv_of(packed), out_qkv_of(packed_other)
    in_att, out_exp, in_red = (
        jnp.concatenate([unpack(packed, i), unpack(packed_other, i)], 1) for i in (3, 4, 5)
    )

    def slice_of(bias, index, width):
        return lax.dynamic_slice_in_dim(bias, index * width, width).astype(F32)

    def b_qkv_of(index):
        return jnp.concatenate(
            [slice_of(b_query, index, span), jnp.zeros((span,), F32), slice_of(b_value, index, span)]
        )

    b_up_chip = jnp.concatenate([slice_of(b_up, me, ff_part), slice_of(b_up, me ^ 1, ff_part)])

    def by_chip(value):
        return value.reshape((chips, count, rows) + value.shape[1:])

    def flat(value):
        return value.reshape(chips * block, value.shape[-1])

    def block_products(products, low, table):
        parts = {}
        for i in reversed(range(chips)):
            at = slice(i * block, (i + 1) * block)
            total = mm(low[at], table)
            for value, weight, main in products:
                total = total + main(value[at], weight)
            parts[2 * i] = total.astype(BF16)
            if i == chips - 1:
                low = after(low, parts[2 * i])
                products = [(after(v, parts[2 * i]), w, main) for v, w, main in products]
        return parts

    low_qkv = keep_own(mm_t(hidden_one, in_qkv))
    qkv_away = (
        mm(hidden_one, w_qkv_other) + mm(low_qkv, out_qkv_other) + b_qkv_of(me ^ 1)
    ).astype(BF16)
    qkv_other = by_chip(swap(qkv_away, "shard", 1))
    qkv_own = by_chip(
        (mm(hidden_one, w_qkv_mine) + mm(low_qkv, out_qkv_mine) + b_qkv_of(me)).astype(BF16)
    )
    att_own, att_away, lse = attend(where, qkv_own, qkv_other, heads)
    cot_pieces, _, _ = gather_rows(after(cot_mine, att_own), bits, apart=True)
    attended = jnp.concatenate([flat(att_own), swap(flat(att_away), "shard", 1)], 1)
    low_att = keep_own(mm_t(attended, in_att))
    parts = block_products([(attended, w_out_chip, mm)], low_att, out_att)
    terms, relayed = scatter_rows(parts, bits)
    cot = jnp.concatenate(after(cot_pieces, *relayed), 0)
    glow_red = keep_own(mm_t(cot, out_red))
    grad_act = (mm_t(cot, w_down_chip) + mm(glow_red, in_red)).astype(BF16)
    terms[0] = after(terms[0], grad_act)
    residual, hidden_block = row_call(
        norm_kernel, [rows_in, vectors] + terms, block, wide, [F32, BF16], "norm"
    )
    far_up = halves_over_rep(after(tuple(near_up[1:]), *relayed))
    pieces_up = after((*near_up, *far_up), hidden_block)
    hidden_two, _, _ = gather_rows(hidden_block, bits)

    (w_up_chip,) = place_weights(at, both_cores(pieces_up), chips, ff_part, True)
    hidden_two = after(hidden_two, grad_act)
    low_exp = keep_own(mm_t(hidden_two, in_exp))
    pre = mm(hidden_two, w_up_chip) + mm(low_exp, out_exp) + b_up_chip
    share = 0.5 * (1.0 + lax.erf(pre * np.float32(0.5**0.5)))
    act = (pre * share).astype(BF16)
    slope = share + pre * (jnp.exp(-0.5 * pre * pre) * np.float32((2 * np.pi) ** -0.5))
    grad_pre = (slope * grad_act.astype(F32)).astype(BF16)
    glow_exp = keep_own(mm_t(grad_pre, out_exp))
    terms, grad_sent = scatter_rows(block_products([(grad_pre, w_up_chip, mm_t)], glow_exp, in_exp), bits)
    grad_residual, grad_block = row_call(
        functools.partial(norm_back_kernel, outs=2, row=1),
        [residual, vectors, cot_mine] + terms,
        block,
        wide,
        [F32, BF16],
        "norm_back",
    )
    grad_branch, _, branch_last = gather_rows(grad_block, bits)

    act_late = after(act, grad_block)
    low_red = keep_own(mm_t(act_late, in_red))
    down_parts = block_products([(act_late, w_down_chip, mm)], low_red, out_red)
    glow_att = keep_own(mm_t(grad_branch, out_att))
    grad_att = (mm_t(grad_branch, w_out_chip) + mm(glow_att, in_att)).astype(BF16)
    ga_own = by_chip(grad_att[:, :span])
    ga_other = by_chip(swap(grad_att[:, span:], "shard", 1))
    grad_own, grad_away = attend_back(where, qkv_own, qkv_other, lse, ga_own, ga_other, heads)
    grad_own = flat(grad_own)
    grad_other = swap(flat(grad_away), "shard", 1)
    glow_qkv = keep_own(mm_t(grad_own, out_qkv_mine) + mm_t(grad_other, out_qkv_other))
    def sum_cores(own, away):
        return own + swap(away.astype(BF16), "shard", 1).astype(F32)

    def core_columns(value):
        width = value.shape[1] // size

        def side(which):
            return jnp.stack(
                [
                    lax.dynamic_slice_in_dim(value, (2 * k + which) * width, width, 1)
                    for k in range(chips)
                ]
            )

        core = me & 1
        return sum_cores(side(core), side(1 - core))

    def split_chips(current, bit):
        current = current.reshape((2, current.shape[0] // 2) + current.shape[1:])
        own = (me // bit) & 1
        away = lax.dynamic_index_in_dim(current, 1 - own, 0, False).astype(BF16)
        return lax.dynamic_index_in_dim(current, own, 0, False), away

    def sum_chips(current, *gate):
        for i, bit in enumerate(bits[::-1]):
            current, away = split_chips(current, bit)
            there = swap(away, "shard", bit)
            current = current + (there if i else after(there, *gate)).astype(F32)
        return current[0], away

    rep_bits = bits_of(lax.axis_size("rep"))

    def over_rep(terms, extra=(), gates=None):
        current = jnp.concatenate([t.astype(BF16) for t in terms], 1)
        current = jnp.concatenate([current, *extra], 0)[None]
        gathered = [current]
        for bit in rep_bits:
            there = swap(current, "rep", bit)
            if gates and bit in gates:
                there = after(there, *gates[bit])
            gathered.append(there)
            if bit != rep_bits[-1]:
                current = jnp.concatenate([current, there], 0)
        return gathered

    def over_groups(terms, place, gathered):
        widths = [t.shape[1] for t in terms]
        outs = sum_blocks(place, gathered, count * rank, widths)
        return [out.reshape(ADAPTERS, rank, -1) for out in outs]

    def halves(value):
        middle = value.shape[1] // 2
        return value[:, :middle], value[:, middle:]

    glow_late, low_late = after((glow_exp, low_exp), grad_block)
    act_mid, grad_mid, low_mid, glow_mid = after((act, grad_pre, low_exp, glow_red), *grad_sent)
    red_own, red_away = halves(t_mm(glow_mid, act_mid))
    exp_own, exp_away = halves(t_mm(low_mid, grad_mid))
    local = sum_cores(
        jnp.concatenate([red_own, exp_own], 1), jnp.concatenate([red_away, exp_away], 1)
    )
    mark = (chosen[:, None] == jnp.arange(ADAPTERS, dtype=jnp.int32)[None, :]).astype(BF16)
    mark = jnp.pad(mark, ((0, 16 - count), (0, local.shape[1] - ADAPTERS)))
    sums = [local[:, :ff_part], local[:, ff_part:]]
    gathered = over_rep(sums, [mark], {rep_bits[-1]: (grad_away,)})
    marks = jnp.concatenate(
        [g[:, count * rank : count * rank + count, :ADAPTERS] for g in gathered], 0
    )
    place = marks.reshape(-1, 1, ADAPTERS, 1) * jnp.eye(rank, dtype=BF16)[None, :, None, :]
    place = place.reshape(-1, ADAPTERS * rank)
    s_in_red, s_out_exp = over_groups(sums, place, gathered)

    near_first = core_columns(
        jnp.concatenate([t_mm(glow_late, hidden_two), t_mm(low_red, cot)], 0)
    ).astype(BF16)
    tall = near_first.shape[1]
    riders = {}
    for i in range(chips):
        rider = lax.dynamic_index_in_dim(near_first, chip ^ i, 0, False)
        rider = jnp.pad(rider, ((0, block - tall), (0, 0)))
        riders[2 * i] = after(jnp.concatenate([down_parts[2 * i], rider], 1), branch_last)
    att_side = sum_cores(*halves(t_mm(glow_att, attended)))

    glow_last = glow_qkv
    in_terms = jnp.concatenate([t_mm(glow_last, hidden_one), t_mm(low_att, grad_branch)], 0)

    def own_terms(full):
        height = count * rank
        return jnp.concatenate(
            [full[t * height : (t + 1) * height, t * span : (t + 1) * span] for t in range(3)], 1
        )

    near_second = core_columns(in_terms)
    products = [(grad_own, w_qkv_mine, mm_t), (grad_other, w_qkv_other, mm_t)]
    parts = block_products(products, after(glow_qkv, in_terms), in_qkv)
    far_part = parts[2 * (chips - 1)]
    aside = {}

    def hop(relayed):
        aside["second"], sent = sum_chips(after(near_second, far_part), *relayed)
        return sent

    terms, relayed = scatter_rows(parts, bits, between=hop)
    second = aside["second"]
    down, _ = scatter_rows(riders, bits, (grad_away,))
    down[0] = after(down[0], *relayed)
    first = sum(t[:tall, wide:].astype(F32) for t in down).reshape(2, count * rank, slice_wide)
    layer_rows = residual + b_down.astype(F32) + sum(t[:, :wide].astype(F32) for t in down)

    own_last, other_last = after((grad_own, grad_other), *relayed)
    outer = sum_cores(own_terms(t_mm(low_qkv, own_last)), own_terms(t_mm(low_qkv, other_last)))
    (input_rows,) = row_call(
        functools.partial(norm_back_kernel, outs=1, row=3),
        [rows_in, vectors, grad_residual] + terms,
        block,
        wide,
        [BF16],
        "norm_back",
    )
    out_att_sum = second[count * 3 * rank :]
    second = second[: count * 3 * rank].reshape(3, count * rank, slice_wide)
    sums = [att_side, first[0], first[1]]
    ends = {rep_bits[-1]: (input_rows,)}
    s_in_att, s_in_exp, s_out_red = over_groups(sums, place, over_rep(sums, (), ends))
    sums = [second[t] for t in range(3)]
    sums += [outer[:, t * span : (t + 1) * span] for t in range(3)] + [out_att_sum]
    late = over_groups(sums, place, over_rep(sums, (), ends))
    s_out_att = late.pop()
    shape = (1, count, rows, wide)
    return (
        layer_rows.astype(BF16).reshape(shape),
        input_rows.reshape(shape),
        late[0],
        late[3],
        late[1],
        late[4],
        late[2],
        late[5],
        s_in_att,
        s_out_att,
        s_in_exp,
        s_out_exp,
        s_in_red,
        s_out_red,
    )


def solution(mesh):
    row = P("shard", None)
    wide = P(None, None, "shard")
    acts = P("rep", None, "shard", None)
    in_specs = (
        (acts, P(), P(), row, P(), row, row, P(), row, P(), P(), P(), row, P(), row, P())
        + (wide,) * 12
        + (P("rep", None), P("rep", None, None), acts)
    )
    out_specs = (acts, acts) + (wide,) * 12
    return jax.shard_map(
        on_device, mesh=mesh, in_specs=in_specs, out_specs=out_specs, check_vma=False
    )
```

```python
import functools

import jax
import jax.numpy as jnp
import numpy as np
from jax import lax
from jax.experimental import pallas as pl
from jax.experimental.pallas import tpu as pltpu
from jax.sharding import PartitionSpec as P

HEADS = 16
HEAD = 128
ADAPTERS = 8
PIECE = 256

EPSILON = 1e-05
MASKED = -1e30
F32 = jnp.float32
BF16 = jnp.bfloat16


def layer_norm(values, gain_vec, shift_vec):
    centre = jnp.mean(values, axis=-1, keepdims=True)
    offset = values - centre
    spread = jnp.mean(offset * offset, axis=-1, keepdims=True)
    return offset * lax.rsqrt(spread + EPSILON) * gain_vec + shift_vec


def piece_labels(starts, positions):
    inside = (positions[:, None] >= starts[None, :]) & (
        positions[:, None] < starts[None, :] + PIECE
    )
    labels = jnp.arange(1, starts.shape[0] + 1, dtype=jnp.int32)
    return jnp.sum(jnp.where(inside, labels[None, :], 0), axis=1)


def mm(a, b):
    return lax.dot_general(a, b, (((1,), (0,)), ((), ())), preferred_element_type=F32)


def mm_t(a, b):
    return lax.dot_general(a, b, (((1,), (1,)), ((), ())), preferred_element_type=F32)


def t_mm(a, b):
    return lax.dot_general(a, b, (((0,), (0,)), ((), ())), preferred_element_type=F32)


def swap(value, axis, mask):
    size = lax.axis_size(axis)
    return lax.ppermute(value, axis, [(i, i ^ mask) for i in range(size)])


def after(value, *others):
    return lax.optimization_barrier((value,) + others)[0]


def bits_of(size):
    bits = []
    while (1 << len(bits)) < size:
        bits.append(1 << len(bits))
    return bits


def subsets(bits):
    masks = [0]
    for bit in bits:
        masks = masks + [m | bit for m in masks]
    return masks


def gather_rows(block, bits, gate=(), apart=False):
    half = block.shape[0] // 2
    got = {0: [block]}
    upper, lower = {}, {}
    for bit in bits:
        there = swap(block, "shard", bit)
        there = after(there, *gate) if gate else there
        got[bit] = [there]
        upper[bit], lower[bit] = there[:half], there[half:]
    for which, order in ((upper, bits), (lower, bits[::-1])):
        for k, bit in enumerate(order):
            for sub in subsets(order[:k])[1:]:
                which[sub | bit] = swap(which[sub], "shard", bit)
    pieces = []
    for mask in subsets(bits):
        pieces += got[mask] if mask in got else [upper[mask], lower[mask]]
    firsts = [got[bit][0] for bit in bits]
    if apart:
        return pieces, firsts, pieces[-1]
    return jnp.concatenate(pieces, 0), firsts, pieces[-1]


def scatter_rows(parts, bits, gate=(), between=None):
    half = parts[0].shape[0] // 2
    upper = {m: p[:half] for m, p in parts.items()}
    lower = {m: p[half:] for m, p in parts.items()}
    for which, order in ((upper, bits), (lower, bits[::-1])):
        for k in reversed(range(len(order))):
            for sub in subsets(order[:k])[1:]:
                other = swap(which[sub | order[k]], "shard", order[k])
                other = after(other, *gate) if gate else other
                which[sub] = (which[sub].astype(F32) + other.astype(F32)).astype(BF16)
    blocks = [jnp.concatenate([upper[bit], lower[bit]], 0) for bit in bits]
    if between:
        blocks = list(after(tuple(blocks), between(blocks)))
    return [parts[0]] + [swap(b, "shard", bit) for b, bit in zip(blocks, bits)], blocks


def gather_blocks(value, axis, bits, gates=None):
    current = value[None]
    for bit in bits:
        there = swap(current, axis, bit)
        if gates and bit in gates:
            there = after(there, *gates[bit])
        current = jnp.concatenate([current, there], 0)
    return current


def run_copies(copies):
    for copy in copies:
        copy.start()
    for copy in copies:
        copy.wait()


def cut_kernel(at_ref, *refs, count, terms, width):
    tables, outs, sems = refs[:terms], refs[terms:-1], refs[-1]
    me, part = at_ref[0], at_ref[1]
    copies = []
    for i in range(count):
        rows = outs[i].shape[0]
        first = pl.multiple_of(part * rows, rows) if rows < tables[0].shape[0] else 0
        for k in range(2):
            column = pl.multiple_of((((me // 2) ^ i) * 2 + k) * width, width)
            for t in range(terms):
                copies.append(
                    pltpu.make_async_copy(
                        tables[t].at[pl.ds(first, rows), pl.ds(column, width)],
                        outs[i].at[:, pl.ds((k * terms + t) * width, width)],
                        sems.at[len(copies)],
                    )
                )
    run_copies(copies)


def cut_pieces(at, tables, width, count, split):
    rows, terms = tables[0].shape[0], len(tables)
    shapes = [
        jax.ShapeDtypeStruct((rows // 2 if i and split else rows, 2 * terms * width), BF16)
        for i in range(count)
    ]
    return pl.pallas_call(
        functools.partial(cut_kernel, count=count, terms=terms, width=width),
        out_shape=shapes,
        in_specs=[pl.BlockSpec(memory_space=pltpu.SMEM)]
        + [pl.BlockSpec(memory_space=pl.ANY)] * terms,
        out_specs=[pl.BlockSpec(memory_space=pltpu.VMEM)] * count,
        scratch_shapes=[pltpu.SemaphoreType.DMA((2 * terms * count,))],
        cost_estimate=pl.CostEstimate(
            flops=0, bytes_accessed=4 * rows * count * terms * width, transcendentals=0
        ),
        name="cut_pieces",
    )(at, *tables)


def place_kernel(at_ref, *refs, count, width, rows, joined):
    pieces, outs, sems = refs[:6], refs[6:-1], refs[-1]
    me, part = at_ref[0], at_ref[1]
    half = rows // 2

    def copies(core):
        made = []
        for side in range(2):
            parts = [(pieces[3 * side], 0, rows, 0, 0)]
            for second in range(2):
                parts += [
                    (pieces[3 * side + 1 + second], (i - 1) * half, half, i, part ^ second)
                    for i in range(1, count)
                ]
            for piece, first, height, i, which in parts:
                row = pl.multiple_of((me ^ (2 * i) ^ side) * rows + which * half, half)
                for k in range(2):
                    own = k ^ core
                    source = piece.at[pl.ds(first, height), pl.ds(k * width, width)]
                    if joined:
                        target = outs[0].at[pl.ds(row, height), pl.ds(own * width, width)]
                    else:
                        target = outs[own].at[pl.ds(row, height)]
                    made.append(pltpu.make_async_copy(source, target, sems.at[len(made)]))
        return made

    @pl.when((me & 1) == 0)
    def _():
        run_copies(copies(0))

    @pl.when((me & 1) == 1)
    def _():
        run_copies(copies(1))


def place_weights(at, pieces, count, width, joined):
    rows = pieces[0].shape[0]
    if joined:
        shapes = [jax.ShapeDtypeStruct((rows * count * 2, 2 * width), BF16)]
    else:
        shapes = [jax.ShapeDtypeStruct((rows * count * 2, width), BF16)] * 2
    return pl.pallas_call(
        functools.partial(place_kernel, count=count, width=width, rows=rows, joined=joined),
        out_shape=shapes,
        in_specs=[pl.BlockSpec(memory_space=pltpu.SMEM)]
        + [pl.BlockSpec(memory_space=pl.ANY)] * len(pieces),
        out_specs=[pl.BlockSpec(memory_space=pltpu.VMEM)] * len(shapes),
        scratch_shapes=[pltpu.SemaphoreType.DMA((8 * count - 4,))],
        cost_estimate=pl.CostEstimate(
            flops=0, bytes_accessed=16 * rows * count * width, transcendentals=0
        ),
        name="place_weights",
    )(at, *pieces)


def pick_kernel(chosen_ref, *refs, tall, rank):
    tables, (tall_ref, flat_ref, sems) = refs[:-3], refs[-3:]
    count = chosen_ref.shape[0]
    copies = []
    for s in range(count):
        column = 0
        for i, table in enumerate(tables):
            if i < tall:
                target = tall_ref.at[pl.ds((i * count + s) * rank, rank)]
            else:
                width = table.shape[2]
                target = flat_ref.at[pl.ds(s * rank, rank), pl.ds(column, width)]
                column += width
            copies.append(
                pltpu.make_async_copy(table.at[chosen_ref[s]], target, sems.at[len(copies)])
            )
    run_copies(copies)


def pick_maps(chosen, upright, flat):
    count, rank = chosen.shape[0], upright[0].shape[1]
    total = sum(t.shape[2] for t in flat)
    shapes = (
        jax.ShapeDtypeStruct((len(upright) * count * rank, upright[0].shape[2]), BF16),
        jax.ShapeDtypeStruct((count * rank, total), BF16),
    )
    tables = upright + flat
    return pl.pallas_call(
        functools.partial(pick_kernel, tall=len(upright), rank=rank),
        out_shape=shapes,
        in_specs=[pl.BlockSpec(memory_space=pltpu.SMEM)]
        + [pl.BlockSpec(memory_space=pl.ANY)] * len(tables),
        out_specs=[pl.BlockSpec(memory_space=pltpu.VMEM)] * 2,
        scratch_shapes=[pltpu.SemaphoreType.DMA((count * len(tables),))],
        cost_estimate=pl.CostEstimate(
            flops=0, bytes_accessed=8 * count * rank * total, transcendentals=0
        ),
        name="pick_maps",
    )(chosen, *tables)


def cols_kernel(me_ref, in_ref, out_ref, sems, *, masks):
    width = in_ref.shape[2]
    run_copies(
        [
            pltpu.make_async_copy(
                in_ref.at[i],
                out_ref.at[:, pl.ds(pl.multiple_of((me_ref[0] ^ mask) * width, width), width)],
                sems.at[i],
            )
            for i, mask in enumerate(masks)
        ]
    )


def place_columns(me, stacked, masks):
    count, rows, width = stacked.shape
    return pl.pallas_call(
        functools.partial(cols_kernel, masks=masks),
        out_shape=jax.ShapeDtypeStruct((rows, count * width), stacked.dtype),
        in_specs=[pl.BlockSpec(memory_space=pltpu.SMEM), pl.BlockSpec(memory_space=pltpu.VMEM)],
        out_specs=pl.BlockSpec(memory_space=pltpu.VMEM),
        scratch_shapes=[pltpu.SemaphoreType.DMA((count,))],
        cost_estimate=pl.CostEstimate(
            flops=0, bytes_accessed=4 * count * rows * width, transcendentals=0
        ),
        name="place_columns",
    )(me, stacked)


def normalised(values):
    centre = jnp.mean(values, axis=-1, keepdims=True)
    offset = values - centre
    scale = lax.rsqrt(jnp.mean(offset * offset, axis=-1, keepdims=True) + EPSILON)
    return offset * scale, scale


def total_of(refs, at):
    total = refs[0][at].astype(F32)
    for ref in refs[1:]:
        total = total + ref[at].astype(F32)
    return total


def tiles_of(rows):
    tile = 32 if rows % 32 == 0 else rows
    return [slice(i, i + tile) for i in range(0, rows, tile)]


def norm_kernel(base, vectors, *refs):
    terms, (res_ref, out_ref) = refs[:-2], refs[-2:]
    shift, gain, bias = vectors[0:1], vectors[1:2], vectors[2:3]
    for at in tiles_of(base.shape[0]):
        values = base[at].astype(F32) + (total_of(terms, at) + shift)
        res_ref[at] = values
        unit, _ = normalised(values)
        out_ref[at] = (unit * gain + bias).astype(BF16)


def norm_back_kernel(values, vectors, base, *refs, outs, row):
    gain = vectors[row : row + 1]
    terms, outputs = refs[: len(refs) - outs], refs[len(refs) - outs :]
    for at in tiles_of(values.shape[0]):
        unit, scale = normalised(values[at].astype(F32))
        grad = total_of(terms, at) * gain
        mean_one = jnp.mean(grad, axis=-1, keepdims=True)
        mean_two = jnp.mean(grad * unit, axis=-1, keepdims=True)
        total = base[at].astype(F32) + scale * (grad - mean_one - unit * mean_two)
        for out in outputs:
            out[at] = total.astype(out.dtype)


def row_call(kernel, order, rows, wide, dtypes, name):
    return pl.pallas_call(
        kernel,
        out_shape=[jax.ShapeDtypeStruct((rows, wide), d) for d in dtypes],
        in_specs=[pl.BlockSpec(memory_space=pltpu.VMEM)] * len(order),
        out_specs=[pl.BlockSpec(memory_space=pltpu.VMEM)] * len(dtypes),
        cost_estimate=pl.CostEstimate(
            flops=20 * rows * wide, bytes_accessed=200 * rows * wide, transcendentals=0
        ),
        name=name,
    )(*order)


def sum_kernel(place, *refs, blocks, rows):
    gathered, outs = refs[:blocks], refs[blocks:]
    start = 0
    for out in outs:
        width = out.shape[1]
        total, row = None, 0
        for ref in gathered:
            for g in range(ref.shape[0]):
                term = t_mm(place[row : row + rows], ref[g, :rows, start : start + width])
                total = term if total is None else total + term
                row += rows
        out[...] = total
        start += width


def sum_blocks(place, gathered, rows, widths):
    total = sum(widths)
    return pl.pallas_call(
        functools.partial(sum_kernel, blocks=len(gathered), rows=rows),
        out_shape=[jax.ShapeDtypeStruct((place.shape[1], w), F32) for w in widths],
        in_specs=[pl.BlockSpec(memory_space=pltpu.VMEM)] * (1 + len(gathered)),
        out_specs=[pl.BlockSpec(memory_space=pltpu.VMEM)] * len(widths),
        cost_estimate=pl.CostEstimate(
            flops=2 * place.size * total, bytes_accessed=(2 * place.shape[0] + 4 * place.shape[1]) * total, transcendentals=0
        ),
        name="sum_blocks",
    )(place, *gathered)


def seen(pos_q, pos_k, lab_q, lab_k):
    return (pos_k <= pos_q) | ((lab_q == lab_k) & (lab_q > 0))


def both(own_ref, other_ref, low, high):
    own, other = own_ref[:, 0, :, low:high], other_ref[:, 0, :, low:high]
    chips, rows, width = own.shape
    return jnp.concatenate([own.reshape(chips * rows, width), other.reshape(chips * rows, width)], 0)


def put(own_ref, other_ref, low, high, value):
    chips, _, rows, _ = own_ref.shape
    half = chips * rows
    own_ref[:, 0, :, low:high] = value[:half].reshape(chips, rows, high - low)
    other_ref[:, 0, :, low:high] = value[half:].reshape(chips, rows, high - low)


def attend_kernel(pq, pk, lq, lk, own, other, out_own, out_other, lse_ref, *, heads, factor):
    allowed = seen(pq[...], pk[...], lq[0], lk[0])
    span = heads * HEAD
    for h in range(heads):
        low, high = h * HEAD, (h + 1) * HEAD
        q = both(own, other, low, high)
        k = both(own, other, span + low, span + high)
        v = both(own, other, 2 * span + low, 2 * span + high)
        scores = jnp.where(allowed, mm_t(q, k) * factor, MASKED)
        top = jnp.max(scores, axis=-1, keepdims=True)
        expo = jnp.exp(scores - top)
        total = jnp.sum(expo, axis=-1, keepdims=True)
        probs = (expo * (1.0 / total)).astype(BF16)
        put(out_own, out_other, low, high, mm(probs, v).astype(BF16))
        lse_ref[0, :, h : h + 1] = top + jnp.log(total)


def attend_specs(chips, count, rows, length):
    whole = pl.BlockSpec(memory_space=pltpu.VMEM)
    where = [
        pl.BlockSpec((length, 1), lambda s: (0, 0)),
        pl.BlockSpec((1, length), lambda s: (0, 0)),
        pl.BlockSpec((1, length, 1), lambda s: (s, 0, 0)),
        pl.BlockSpec((1, 1, length), lambda s: (s, 0, 0)),
    ]

    def of(width):
        return pl.BlockSpec((chips, 1, rows, width), lambda s: (0, s, 0, 0))

    return where, of


def attend(where, own, other, heads):
    chips, count, rows, _ = own.shape
    length = 2 * chips * rows
    span = heads * HEAD
    places, of = attend_specs(chips, count, rows, length)
    return pl.pallas_call(
        functools.partial(attend_kernel, heads=heads, factor=HEAD ** (-0.5)),
        out_shape=(
            jax.ShapeDtypeStruct((chips, count, rows, span), BF16),
            jax.ShapeDtypeStruct((chips, count, rows, span), BF16),
            jax.ShapeDtypeStruct((count, length, heads), F32),
        ),
        grid=(count,),
        in_specs=places + [of(3 * span), of(3 * span)],
        out_specs=(of(span), of(span), pl.BlockSpec((1, length, heads), lambda s: (s, 0, 0))),
        cost_estimate=pl.CostEstimate(
            flops=count * heads * length * length * HEAD * 4,
            bytes_accessed=count * length * heads * HEAD * 8,
            transcendentals=count * heads * length * length,
        ),
        name="attend",
    )(*where, own, other)


def attend_back_kernel(
    pq, pk, lq, lk, own, other, lse_ref, ga_own, ga_other, out_own, out_other, *, heads, factor
):
    allowed = seen(pq[...], pk[...], lq[0], lk[0])
    span = heads * HEAD
    for h in range(heads):
        low, high = h * HEAD, (h + 1) * HEAD
        q = both(own, other, low, high)
        k = both(own, other, span + low, span + high)
        v = both(own, other, 2 * span + low, 2 * span + high)
        ga = both(ga_own, ga_other, low, high)
        scores = jnp.where(allowed, mm_t(q, k) * factor, MASKED)
        probs = jnp.exp(scores - lse_ref[0, :, h : h + 1])
        grad_probs = mm_t(ga, v)
        inner = jnp.sum(probs * grad_probs, axis=-1, keepdims=True)
        grad_scores = (probs * (grad_probs - inner)).astype(BF16)
        put(out_own, out_other, low, high, (mm(grad_scores, k) * factor).astype(BF16))
        put(
            out_own,
            out_other,
            span + low,
            span + high,
            (t_mm(grad_scores, q) * factor).astype(BF16),
        )
        put(
            out_own,
            out_other,
            2 * span + low,
            2 * span + high,
            t_mm(probs.astype(BF16), ga).astype(BF16),
        )


def attend_back(where, own, other, lse, ga_own, ga_other, heads):
    chips, count, rows, _ = own.shape
    length = 2 * chips * rows
    span = heads * HEAD
    places, of = attend_specs(chips, count, rows, length)
    return pl.pallas_call(
        functools.partial(attend_back_kernel, heads=heads, factor=HEAD ** (-0.5)),
        out_shape=(jax.ShapeDtypeStruct((chips, count, rows, 3 * span), BF16),) * 2,
        grid=(count,),
        in_specs=places
        + [of(3 * span), of(3 * span)]
        + [pl.BlockSpec((1, length, heads), lambda s: (s, 0, 0)), of(span), of(span)],
        out_specs=(of(3 * span), of(3 * span)),
        cost_estimate=pl.CostEstimate(
            flops=count * heads * length * length * HEAD * 10,
            bytes_accessed=count * length * heads * HEAD * 14,
            transcendentals=count * heads * length * length,
        ),
        name="attend_back",
    )(*where, own, other, lse, ga_own, ga_other)


def on_device(
    inputs,
    ln1_gain,
    ln1_bias,
    w_query,
    b_query,
    w_key,
    w_value,
    b_value,
    w_out,
    b_out,
    ln2_gain,
    ln2_bias,
    w_up,
    b_up,
    w_down,
    b_down,
    in_query,
    out_query,
    in_key,
    out_key,
    in_value,
    out_value,
    in_attn,
    out_attn,
    in_expand,
    out_expand,
    in_reduce,
    out_reduce,
    adapter_pick,
    piece_start,
    cotangent,
):
    count, rows, wide = inputs.shape[1:]
    size = lax.axis_size("shard")
    chips = size // 2
    bits = bits_of(size)[1:]
    me = lax.axis_index("shard").astype(jnp.int32)
    me_arr = me[None]
    part = lax.axis_index("rep").astype(jnp.int32) & 1
    at = jnp.stack([me, part])
    heads = HEADS // size
    span = heads * HEAD
    slice_wide = wide // size
    ff_part = w_up.shape[1] // size
    rank = in_query.shape[1]
    block = count * rows
    chosen = adapter_pick[0]
    starts = piece_start[0]

    def keep_own(value):
        of_row = lax.broadcasted_iota(jnp.int32, value.shape, 0) // rows % count
        of_col = lax.broadcasted_iota(jnp.int32, value.shape, 1) // rank % count
        return jnp.where(of_row == of_col, value, 0.0).astype(BF16)

    chip = me // 2

    def exchange(pieces):
        return [pieces[0]] + [swap(p, "shard", 2 * i) for i, p in enumerate(pieces) if i]

    def with_halves(pieces):
        near = jnp.concatenate(pieces[1:], 0)
        return [pieces[0], near, swap(near, "rep", 1)]

    def both_cores(own):
        return list(own) + [swap(piece, "shard", 1) for piece in own]

    w_out_other = swap(w_out, "shard", 1)
    w_down_other = swap(w_down, "shard", 1)
    pieces_qkv = cut_pieces(at, [w_query, w_key, w_value], span, chips, True)
    turned = exchange(pieces_qkv)
    near_up = exchange(cut_pieces(at, [after(w_up, *pieces_qkv)], ff_part, chips, True))

    narrow = [out_query, out_key, out_value, in_attn, out_expand, in_reduce]
    edges = np.cumsum([0] + [n.shape[2] for n in narrow])
    mine, packed = pick_maps(
        after(chosen, w_out_other, w_down_other, *pieces_qkv),
        [in_query, in_key, in_value, in_expand, out_attn, out_reduce],
        narrow,
    )
    packed_other = swap(packed, "shard", 1)
    order = bits + [1]
    near_one = swap(mine[None], "shard", bits[0])

    rows_in = after(inputs[0].reshape(block, wide), mine)
    features = rows_in.astype(F32)
    normed = layer_norm(features, ln1_gain.astype(F32), ln1_bias.astype(F32)).astype(BF16)
    starts, b_query, b_value, b_up, me_late, chosen, packed = after(
        (starts, b_query, b_value, b_up, me, chosen, packed), normed
    )
    vectors = after(jnp.stack([b_out, ln2_gain, ln2_bias, ln1_gain]), normed).astype(F32)
    hidden_block = after(normed, packed_other, near_one, *turned[1:], *near_up[1:])
    hidden_one, one_first, one_last = gather_rows(hidden_block, bits)

    turned[0] = after(turned[0], *one_first)
    w_qkv_mine, w_qkv_other = place_weights(
        at, both_cores(with_halves(turned)), chips, 3 * span, False
    )
    w_out_late, w_down_late = after((w_out, w_down), normed)
    w_out_chip = jnp.concatenate([w_out_late, w_out_other], 0)
    w_down_chip = jnp.concatenate([w_down_late, w_down_other], 0)
    hidden_one = after(hidden_one, w_out_chip, w_down_chip)
    cot_mine = cotangent[0].reshape(block, wide)
    near = after(jnp.concatenate([mine[None], near_one], 0), *one_first)
    for bit in bits[1:]:
        near = jnp.concatenate([near, swap(near, "shard", bit)], 0)
    stacked = jnp.concatenate([near, swap(near, "shard", 1)], 0)

    owners = np.concatenate([np.arange(chips) * 2, np.arange(chips) * 2 + 1]).astype(np.int32)
    locs = np.tile(np.arange(rows, dtype=np.int32), 2 * chips)
    positions = (me_late ^ jnp.asarray(np.repeat(owners, rows))) * rows + jnp.asarray(locs)
    labels = jnp.stack([piece_labels(starts[s], positions) for s in range(count)])
    where = (positions[:, None], positions[None, :], labels[:, :, None], labels[:, None, :])

    whole = place_columns(me_arr, stacked, subsets(order)).reshape(6, count, rank, wide)
    in_qkv = whole[:3].reshape(3 * count * rank, wide)
    in_exp, out_att, out_red = (whole[3 + i].reshape(count * rank, wide) for i in range(3))

    def unpack(table, i):
        return table[:, edges[i] : edges[i + 1]]

    def out_qkv_of(table):
        stacked = jnp.stack([unpack(table, t) for t in range(3)])
        spread = stacked[:, :, None, :] * jnp.eye(3, dtype=BF16)[:, None, :, None]
        return spread.reshape(count * 3 * rank, 3 * span)

    out_qkv_mine, out_qkv_other = out_qkv_of(packed), out_qkv_of(packed_other)
    in_att, out_exp, in_red = (
        jnp.concatenate([unpack(packed, i), unpack(packed_other, i)], 1) for i in (3, 4, 5)
    )

    def slice_of(bias, index, width):
        return lax.dynamic_slice_in_dim(bias, index * width, width).astype(F32)

    def b_qkv_of(index):
        return jnp.concatenate(
            [slice_of(b_query, index, span), jnp.zeros((span,), F32), slice_of(b_value, index, span)]
        )

    b_up_chip = jnp.concatenate([slice_of(b_up, me, ff_part), slice_of(b_up, me ^ 1, ff_part)])

    def by_chip(value):
        return value.reshape((chips, count, rows) + value.shape[1:])

    def flat(value):
        return value.reshape(chips * block, value.shape[-1])

    def block_products(products, low, table):
        parts = {}
        for i in reversed(range(chips)):
            at = slice(i * block, (i + 1) * block)
            total = mm(low[at], table)
            for value, weight, main in products:
                total = total + main(value[at], weight)
            parts[2 * i] = total.astype(BF16)
            if i == chips - 1:
                low = after(low, parts[2 * i])
                products = [(after(v, parts[2 * i]), w, main) for v, w, main in products]
        return parts

    low_qkv = keep_own(mm_t(hidden_one, in_qkv))
    qkv_away = (
        mm(hidden_one, w_qkv_other) + mm(low_qkv, out_qkv_other) + b_qkv_of(me ^ 1)
    ).astype(BF16)
    qkv_other = by_chip(swap(qkv_away, "shard", 1))
    qkv_own = by_chip(
        (mm(hidden_one, w_qkv_mine) + mm(low_qkv, out_qkv_mine) + b_qkv_of(me)).astype(BF16)
    )
    att_own, att_away, lse = attend(where, qkv_own, qkv_other, heads)
    near_up[1:] = after(tuple(near_up[1:]), att_own)
    halves_up = with_halves(near_up)
    cot_pieces, _, _ = gather_rows(after(cot_mine, att_own), bits, apart=True)
    attended = jnp.concatenate([flat(att_own), swap(flat(att_away), "shard", 1)], 1)
    low_att = keep_own(mm_t(attended, in_att))
    parts = block_products([(attended, w_out_chip, mm)], low_att, out_att)
    terms, relayed = scatter_rows(parts, bits)
    cot = jnp.concatenate(after(cot_pieces, *relayed), 0)
    glow_red = keep_own(mm_t(cot, out_red))
    grad_act = (mm_t(cot, w_down_chip) + mm(glow_red, in_red)).astype(BF16)
    terms[0] = after(terms[0], grad_act)
    residual, hidden_block = row_call(
        norm_kernel, [rows_in, vectors] + terms, block, wide, [F32, BF16], "norm"
    )
    pieces_up = after(tuple(halves_up), hidden_block)
    hidden_two, _, _ = gather_rows(hidden_block, bits)

    (w_up_chip,) = place_weights(at, both_cores(pieces_up), chips, ff_part, True)
    hidden_two = after(hidden_two, grad_act)
    low_exp = keep_own(mm_t(hidden_two, in_exp))
    pre = mm(hidden_two, w_up_chip) + mm(low_exp, out_exp) + b_up_chip
    share = 0.5 * (1.0 + lax.erf(pre * np.float32(0.5**0.5)))
    act = (pre * share).astype(BF16)
    slope = share + pre * (jnp.exp(-0.5 * pre * pre) * np.float32((2 * np.pi) ** -0.5))
    grad_pre = (slope * grad_act.astype(F32)).astype(BF16)
    glow_exp = keep_own(mm_t(grad_pre, out_exp))
    parts = block_products([(grad_pre, w_up_chip, mm_t)], glow_exp, in_exp)
    far = 2 * (chips - 1)

    def halves(value):
        middle = value.shape[1] // 2
        return value[:, :middle], value[:, middle:]

    act_mid, grad_mid, low_mid, glow_mid = after((act, grad_pre, low_exp, glow_red), parts[far])
    red_own, red_away = halves(t_mm(glow_mid, act_mid))
    exp_own, exp_away = halves(t_mm(low_mid, grad_mid))
    terms, _ = scatter_rows(parts, bits, (parts[0], red_own, exp_own))
    grad_residual, grad_block = row_call(
        functools.partial(norm_back_kernel, outs=2, row=1),
        [residual, vectors, cot_mine] + terms,
        block,
        wide,
        [F32, BF16],
        "norm_back",
    )
    grad_branch, branch_first, branch_last = gather_rows(grad_block, bits)

    act_late = after(act, grad_block)
    low_red = keep_own(mm_t(act_late, in_red))
    down_parts = block_products([(act_late, w_down_chip, mm)], low_red, out_red)
    glow_att = keep_own(mm_t(grad_branch, out_att))
    grad_att = (mm_t(grad_branch, w_out_chip) + mm(glow_att, in_att)).astype(BF16)
    ga_own = by_chip(grad_att[:, :span])
    ga_other = by_chip(swap(grad_att[:, span:], "shard", 1))
    grad_own, grad_away = attend_back(where, qkv_own, qkv_other, lse, ga_own, ga_other, heads)
    grad_own = flat(grad_own)
    grad_other = swap(flat(grad_away), "shard", 1)
    glow_qkv = keep_own(mm_t(grad_own, out_qkv_mine) + mm_t(grad_other, out_qkv_other))
    def sum_cores(own, away):
        return own + swap(away.astype(BF16), "shard", 1).astype(F32)

    def core_columns(value):
        width = value.shape[1] // size

        def side(which):
            return jnp.stack(
                [
                    lax.dynamic_slice_in_dim(value, (2 * k + which) * width, width, 1)
                    for k in range(chips)
                ]
            )

        core = me & 1
        return sum_cores(side(core), side(1 - core))

    def split_chips(current, bit):
        current = current.reshape((2, current.shape[0] // 2) + current.shape[1:])
        own = (me // bit) & 1
        away = lax.dynamic_index_in_dim(current, 1 - own, 0, False).astype(BF16)
        return lax.dynamic_index_in_dim(current, own, 0, False), away

    def sum_chips(current, *gate):
        for i, bit in enumerate(bits[::-1]):
            current, away = split_chips(current, bit)
            there = swap(away, "shard", bit)
            current = current + (there if i else after(there, *gate)).astype(F32)
        return current[0], away

    rep_bits = bits_of(lax.axis_size("rep"))

    def over_rep(terms, extra=(), gates=None):
        current = jnp.concatenate([t.astype(BF16) for t in terms], 1)
        current = jnp.concatenate([current, *extra], 0)[None]
        gathered = [current]
        for bit in rep_bits:
            there = swap(current, "rep", bit)
            if gates and bit in gates:
                there = after(there, *gates[bit])
            gathered.append(there)
            if bit != rep_bits[-1]:
                current = jnp.concatenate([current, there], 0)
        return gathered

    def over_groups(terms, place, gathered):
        widths = [t.shape[1] for t in terms]
        outs = sum_blocks(place, gathered, count * rank, widths)
        return [out.reshape(ADAPTERS, rank, -1) for out in outs]

    local = sum_cores(
        jnp.concatenate([red_own, exp_own], 1), jnp.concatenate([red_away, exp_away], 1)
    )
    glow_late, low_late = after((glow_exp, low_red), *branch_first)
    near_first = core_columns(
        jnp.concatenate([t_mm(glow_late, hidden_two), t_mm(low_late, cot)], 0)
    ).astype(BF16)
    tall = near_first.shape[1]
    riders = {}
    for i in range(chips):
        rider = lax.dynamic_index_in_dim(near_first, chip ^ i, 0, False)
        rider = jnp.pad(rider, ((0, block - tall), (0, 0)))
        riders[2 * i] = after(jnp.concatenate([down_parts[2 * i], rider], 1), branch_last)
    att_side = sum_cores(*halves(t_mm(glow_att, attended)))

    glow_last = glow_qkv
    in_terms = jnp.concatenate([t_mm(glow_last, hidden_one), t_mm(low_att, grad_branch)], 0)

    def own_terms(full):
        height = count * rank
        return jnp.concatenate(
            [full[t * height : (t + 1) * height, t * span : (t + 1) * span] for t in range(3)], 1
        )

    near_second = core_columns(in_terms)
    products = [(grad_own, w_qkv_mine, mm_t), (grad_other, w_qkv_other, mm_t)]
    parts = block_products(products, after(glow_qkv, in_terms), in_qkv)
    far_part = parts[2 * (chips - 1)]
    mark = (chosen[:, None] == jnp.arange(ADAPTERS, dtype=jnp.int32)[None, :]).astype(BF16)
    mark = jnp.pad(mark, ((0, 16 - count), (0, local.shape[1] - ADAPTERS)))
    sums = [local[:, :ff_part], local[:, ff_part:]]
    gathered = over_rep(sums, [mark], {rep_bits[-1]: (far_part,)})
    marks = jnp.concatenate(
        [g[:, count * rank : count * rank + count, :ADAPTERS] for g in gathered], 0
    )
    place = marks.reshape(-1, 1, ADAPTERS, 1) * jnp.eye(rank, dtype=BF16)[None, :, None, :]
    place = place.reshape(-1, ADAPTERS * rank)
    s_in_red, s_out_exp = over_groups(sums, place, gathered)

    own_last, other_last = after((grad_own, grad_other), far_part)
    outer_own = own_terms(t_mm(low_qkv, own_last))
    outer_away = own_terms(t_mm(low_qkv, other_last))
    aside = {}

    def hop(relayed):
        aside["second"], sent = sum_chips(after(near_second, far_part), *relayed)
        return sent

    terms, relayed = scatter_rows(parts, bits, (parts[0], outer_own, outer_away), hop)
    outer = sum_cores(outer_own, after(outer_away, *relayed))
    second = aside["second"]
    down, _ = scatter_rows(riders, bits, (grad_away,))
    down[0] = after(down[0], *relayed)
    first = sum(t[:tall, wide:].astype(F32) for t in down).reshape(2, count * rank, slice_wide)
    layer_rows = residual + b_down.astype(F32) + sum(t[:, :wide].astype(F32) for t in down)

    (input_rows,) = row_call(
        functools.partial(norm_back_kernel, outs=1, row=3),
        [rows_in, vectors, grad_residual] + terms,
        block,
        wide,
        [BF16],
        "norm_back",
    )
    out_att_sum = second[count * 3 * rank :]
    second = second[: count * 3 * rank].reshape(3, count * rank, slice_wide)
    sums = [att_side, first[0], first[1]]
    ends = {rep_bits[-1]: (input_rows,)}
    s_in_att, s_in_exp, s_out_red = over_groups(sums, place, over_rep(sums, (), ends))
    sums = [second[t] for t in range(3)]
    sums += [outer[:, t * span : (t + 1) * span] for t in range(3)] + [out_att_sum]
    late = over_groups(sums, place, over_rep(sums, (), ends))
    s_out_att = late.pop()
    shape = (1, count, rows, wide)
    return (
        layer_rows.astype(BF16).reshape(shape),
        input_rows.reshape(shape),
        late[0],
        late[3],
        late[1],
        late[4],
        late[2],
        late[5],
        s_in_att,
        s_out_att,
        s_in_exp,
        s_out_exp,
        s_in_red,
        s_out_red,
    )


def solution(mesh):
    row = P("shard", None)
    wide = P(None, None, "shard")
    acts = P("rep", None, "shard", None)
    in_specs = (
        (acts, P(), P(), row, P(), row, row, P(), row, P(), P(), P(), row, P(), row, P())
        + (wide,) * 12
        + (P("rep", None), P("rep", None, None), acts)
    )
    out_specs = (acts, acts) + (wide,) * 12
    return jax.shard_map(
        on_device, mesh=mesh, in_specs=in_specs, out_specs=out_specs, check_vma=False
    )
```

```python
import functools

import jax
import jax.numpy as jnp
import numpy as np
from jax import lax
from jax.experimental import pallas as pl
from jax.experimental.pallas import tpu as pltpu
from jax.sharding import PartitionSpec as P

HEADS = 16
HEAD = 128
ADAPTERS = 8
PIECE = 256

EPSILON = 1e-05
MASKED = -1e30
F32 = jnp.float32
BF16 = jnp.bfloat16


def layer_norm(values, gain_vec, shift_vec):
    centre = jnp.mean(values, axis=-1, keepdims=True)
    offset = values - centre
    spread = jnp.mean(offset * offset, axis=-1, keepdims=True)
    return offset * lax.rsqrt(spread + EPSILON) * gain_vec + shift_vec


def piece_labels(starts, positions):
    inside = (positions[:, None] >= starts[None, :]) & (
        positions[:, None] < starts[None, :] + PIECE
    )
    labels = jnp.arange(1, starts.shape[0] + 1, dtype=jnp.int32)
    return jnp.sum(jnp.where(inside, labels[None, :], 0), axis=1)


def mm(a, b):
    return lax.dot_general(a, b, (((1,), (0,)), ((), ())), preferred_element_type=F32)


def mm_t(a, b):
    return lax.dot_general(a, b, (((1,), (1,)), ((), ())), preferred_element_type=F32)


def t_mm(a, b):
    return lax.dot_general(a, b, (((0,), (0,)), ((), ())), preferred_element_type=F32)


def swap(value, axis, mask):
    size = lax.axis_size(axis)
    return lax.ppermute(value, axis, [(i, i ^ mask) for i in range(size)])


def after(value, *others):
    return lax.optimization_barrier((value,) + others)[0]


def bits_of(size):
    bits = []
    while (1 << len(bits)) < size:
        bits.append(1 << len(bits))
    return bits


def subsets(bits):
    masks = [0]
    for bit in bits:
        masks = masks + [m | bit for m in masks]
    return masks


def gather_rows(block, bits, gate=(), apart=False):
    half = block.shape[0] // 2
    got = {0: [block]}
    upper, lower = {}, {}
    for bit in bits:
        there = swap(block, "shard", bit)
        there = after(there, *gate) if gate else there
        got[bit] = [there]
        upper[bit], lower[bit] = there[:half], there[half:]
    for which, order in ((upper, bits), (lower, bits[::-1])):
        for k, bit in enumerate(order):
            for sub in subsets(order[:k])[1:]:
                which[sub | bit] = swap(which[sub], "shard", bit)
    pieces = []
    for mask in subsets(bits):
        pieces += got[mask] if mask in got else [upper[mask], lower[mask]]
    firsts = [got[bit][0] for bit in bits]
    if apart:
        return pieces, firsts, pieces[-1]
    return jnp.concatenate(pieces, 0), firsts, pieces[-1]


def scatter_rows(parts, bits, gate=(), between=None):
    half = parts[0].shape[0] // 2
    upper = {m: p[:half] for m, p in parts.items()}
    lower = {m: p[half:] for m, p in parts.items()}
    for which, order in ((upper, bits), (lower, bits[::-1])):
        for k in reversed(range(len(order))):
            for sub in subsets(order[:k])[1:]:
                other = swap(which[sub | order[k]], "shard", order[k])
                other = after(other, *gate) if gate else other
                which[sub] = (which[sub].astype(F32) + other.astype(F32)).astype(BF16)
    blocks = [jnp.concatenate([upper[bit], lower[bit]], 0) for bit in bits]
    if between:
        blocks = list(after(tuple(blocks), between(blocks)))
    return [parts[0]] + [swap(b, "shard", bit) for b, bit in zip(blocks, bits)], blocks


def gather_blocks(value, axis, bits, gates=None):
    current = value[None]
    for bit in bits:
        there = swap(current, axis, bit)
        if gates and bit in gates:
            there = after(there, *gates[bit])
        current = jnp.concatenate([current, there], 0)
    return current


def run_copies(copies):
    for copy in copies:
        copy.start()
    for copy in copies:
        copy.wait()


def cut_kernel(at_ref, *refs, count, terms, width):
    tables, outs, sems = refs[:terms], refs[terms:-1], refs[-1]
    me, part = at_ref[0], at_ref[1]
    copies = []
    for i in range(count):
        rows = outs[i].shape[0]
        first = pl.multiple_of(part * rows, rows) if rows < tables[0].shape[0] else 0
        for k in range(2):
            column = pl.multiple_of((((me // 2) ^ i) * 2 + k) * width, width)
            for t in range(terms):
                copies.append(
                    pltpu.make_async_copy(
                        tables[t].at[pl.ds(first, rows), pl.ds(column, width)],
                        outs[i].at[:, pl.ds((k * terms + t) * width, width)],
                        sems.at[len(copies)],
                    )
                )
    run_copies(copies)


def cut_pieces(at, tables, width, count, split):
    rows, terms = tables[0].shape[0], len(tables)
    shapes = [
        jax.ShapeDtypeStruct((rows // 2 if i and split else rows, 2 * terms * width), BF16)
        for i in range(count)
    ]
    return pl.pallas_call(
        functools.partial(cut_kernel, count=count, terms=terms, width=width),
        out_shape=shapes,
        in_specs=[pl.BlockSpec(memory_space=pltpu.SMEM)]
        + [pl.BlockSpec(memory_space=pl.ANY)] * terms,
        out_specs=[pl.BlockSpec(memory_space=pltpu.VMEM)] * count,
        scratch_shapes=[pltpu.SemaphoreType.DMA((2 * terms * count,))],
        cost_estimate=pl.CostEstimate(
            flops=0, bytes_accessed=4 * rows * count * terms * width, transcendentals=0
        ),
        name="cut_pieces",
    )(at, *tables)


def place_kernel(at_ref, *refs, count, width, rows, joined):
    pieces, outs, sems = refs[:6], refs[6:-1], refs[-1]
    me, part = at_ref[0], at_ref[1]
    half = rows // 2

    def copies(core):
        made = []
        for side in range(2):
            parts = [(pieces[3 * side], 0, rows, 0, 0)]
            for second in range(2):
                parts += [
                    (pieces[3 * side + 1 + second], (i - 1) * half, half, i, part ^ second)
                    for i in range(1, count)
                ]
            for piece, first, height, i, which in parts:
                row = pl.multiple_of((me ^ (2 * i) ^ side) * rows + which * half, half)
                for k in range(2):
                    own = k ^ core
                    source = piece.at[pl.ds(first, height), pl.ds(k * width, width)]
                    if joined:
                        target = outs[0].at[pl.ds(row, height), pl.ds(own * width, width)]
                    else:
                        target = outs[own].at[pl.ds(row, height)]
                    made.append(pltpu.make_async_copy(source, target, sems.at[len(made)]))
        return made

    @pl.when((me & 1) == 0)
    def _():
        run_copies(copies(0))

    @pl.when((me & 1) == 1)
    def _():
        run_copies(copies(1))


def place_weights(at, pieces, count, width, joined):
    rows = pieces[0].shape[0]
    if joined:
        shapes = [jax.ShapeDtypeStruct((rows * count * 2, 2 * width), BF16)]
    else:
        shapes = [jax.ShapeDtypeStruct((rows * count * 2, width), BF16)] * 2
    return pl.pallas_call(
        functools.partial(place_kernel, count=count, width=width, rows=rows, joined=joined),
        out_shape=shapes,
        in_specs=[pl.BlockSpec(memory_space=pltpu.SMEM)]
        + [pl.BlockSpec(memory_space=pl.ANY)] * len(pieces),
        out_specs=[pl.BlockSpec(memory_space=pltpu.VMEM)] * len(shapes),
        scratch_shapes=[pltpu.SemaphoreType.DMA((8 * count - 4,))],
        cost_estimate=pl.CostEstimate(
            flops=0, bytes_accessed=16 * rows * count * width, transcendentals=0
        ),
        name="place_weights",
    )(at, *pieces)


def pick_kernel(chosen_ref, *refs, tall, rank):
    tables, (tall_ref, flat_ref, sems) = refs[:-3], refs[-3:]
    count = chosen_ref.shape[0]
    copies = []
    for s in range(count):
        column = 0
        for i, table in enumerate(tables):
            if i < tall:
                target = tall_ref.at[pl.ds((i * count + s) * rank, rank)]
            else:
                width = table.shape[2]
                target = flat_ref.at[pl.ds(s * rank, rank), pl.ds(column, width)]
                column += width
            copies.append(
                pltpu.make_async_copy(table.at[chosen_ref[s]], target, sems.at[len(copies)])
            )
    run_copies(copies)


def pick_maps(chosen, upright, flat):
    count, rank = chosen.shape[0], upright[0].shape[1]
    total = sum(t.shape[2] for t in flat)
    shapes = (
        jax.ShapeDtypeStruct((len(upright) * count * rank, upright[0].shape[2]), BF16),
        jax.ShapeDtypeStruct((count * rank, total), BF16),
    )
    tables = upright + flat
    return pl.pallas_call(
        functools.partial(pick_kernel, tall=len(upright), rank=rank),
        out_shape=shapes,
        in_specs=[pl.BlockSpec(memory_space=pltpu.SMEM)]
        + [pl.BlockSpec(memory_space=pl.ANY)] * len(tables),
        out_specs=[pl.BlockSpec(memory_space=pltpu.VMEM)] * 2,
        scratch_shapes=[pltpu.SemaphoreType.DMA((count * len(tables),))],
        cost_estimate=pl.CostEstimate(
            flops=0, bytes_accessed=8 * count * rank * total, transcendentals=0
        ),
        name="pick_maps",
    )(chosen, *tables)


def cols_kernel(me_ref, in_ref, out_ref, sems, *, masks):
    width = in_ref.shape[2]
    run_copies(
        [
            pltpu.make_async_copy(
                in_ref.at[i],
                out_ref.at[:, pl.ds(pl.multiple_of((me_ref[0] ^ mask) * width, width), width)],
                sems.at[i],
            )
            for i, mask in enumerate(masks)
        ]
    )


def place_columns(me, stacked, masks):
    count, rows, width = stacked.shape
    return pl.pallas_call(
        functools.partial(cols_kernel, masks=masks),
        out_shape=jax.ShapeDtypeStruct((rows, count * width), stacked.dtype),
        in_specs=[pl.BlockSpec(memory_space=pltpu.SMEM), pl.BlockSpec(memory_space=pltpu.VMEM)],
        out_specs=pl.BlockSpec(memory_space=pltpu.VMEM),
        scratch_shapes=[pltpu.SemaphoreType.DMA((count,))],
        cost_estimate=pl.CostEstimate(
            flops=0, bytes_accessed=4 * count * rows * width, transcendentals=0
        ),
        name="place_columns",
    )(me, stacked)


def normalised(values):
    centre = jnp.mean(values, axis=-1, keepdims=True)
    offset = values - centre
    scale = lax.rsqrt(jnp.mean(offset * offset, axis=-1, keepdims=True) + EPSILON)
    return offset * scale, scale


def total_of(refs, at):
    total = refs[0][at].astype(F32)
    for ref in refs[1:]:
        total = total + ref[at].astype(F32)
    return total


def tiles_of(rows):
    tile = 32 if rows % 32 == 0 else rows
    return [slice(i, i + tile) for i in range(0, rows, tile)]


def norm_kernel(base, vectors, *refs):
    terms, (res_ref, out_ref) = refs[:-2], refs[-2:]
    shift, gain, bias = vectors[0:1], vectors[1:2], vectors[2:3]
    for at in tiles_of(base.shape[0]):
        values = base[at].astype(F32) + (total_of(terms, at) + shift)
        res_ref[at] = values
        unit, _ = normalised(values)
        out_ref[at] = (unit * gain + bias).astype(BF16)


def norm_back_kernel(values, vectors, base, *refs, outs, row):
    gain = vectors[row : row + 1]
    terms, outputs = refs[: len(refs) - outs], refs[len(refs) - outs :]
    for at in tiles_of(values.shape[0]):
        unit, scale = normalised(values[at].astype(F32))
        grad = total_of(terms, at) * gain
        mean_one = jnp.mean(grad, axis=-1, keepdims=True)
        mean_two = jnp.mean(grad * unit, axis=-1, keepdims=True)
        total = base[at].astype(F32) + scale * (grad - mean_one - unit * mean_two)
        for out in outputs:
            out[at] = total.astype(out.dtype)


def row_call(kernel, order, rows, wide, dtypes, name):
    return pl.pallas_call(
        kernel,
        out_shape=[jax.ShapeDtypeStruct((rows, wide), d) for d in dtypes],
        in_specs=[pl.BlockSpec(memory_space=pltpu.VMEM)] * len(order),
        out_specs=[pl.BlockSpec(memory_space=pltpu.VMEM)] * len(dtypes),
        cost_estimate=pl.CostEstimate(
            flops=20 * rows * wide, bytes_accessed=200 * rows * wide, transcendentals=0
        ),
        name=name,
    )(*order)


def sum_kernel(place, *refs, blocks, rows):
    gathered, outs = refs[:blocks], refs[blocks:]
    start = 0
    for out in outs:
        width = out.shape[1]
        total, row = None, 0
        for ref in gathered:
            for g in range(ref.shape[0]):
                term = t_mm(place[row : row + rows], ref[g, :rows, start : start + width])
                total = term if total is None else total + term
                row += rows
        out[...] = total
        start += width


def sum_blocks(place, gathered, rows, widths):
    total = sum(widths)
    return pl.pallas_call(
        functools.partial(sum_kernel, blocks=len(gathered), rows=rows),
        out_shape=[jax.ShapeDtypeStruct((place.shape[1], w), F32) for w in widths],
        in_specs=[pl.BlockSpec(memory_space=pltpu.VMEM)] * (1 + len(gathered)),
        out_specs=[pl.BlockSpec(memory_space=pltpu.VMEM)] * len(widths),
        cost_estimate=pl.CostEstimate(
            flops=2 * place.size * total, bytes_accessed=(2 * place.shape[0] + 4 * place.shape[1]) * total, transcendentals=0
        ),
        name="sum_blocks",
    )(place, *gathered)


def seen(pos_q, pos_k, lab_q, lab_k):
    return (pos_k <= pos_q) | ((lab_q == lab_k) & (lab_q > 0))


def both(own_ref, other_ref, low, high):
    own, other = own_ref[:, 0, :, low:high], other_ref[:, 0, :, low:high]
    chips, rows, width = own.shape
    return jnp.concatenate([own.reshape(chips * rows, width), other.reshape(chips * rows, width)], 0)


def put(own_ref, other_ref, low, high, value):
    chips, _, rows, _ = own_ref.shape
    half = chips * rows
    own_ref[:, 0, :, low:high] = value[:half].reshape(chips, rows, high - low)
    other_ref[:, 0, :, low:high] = value[half:].reshape(chips, rows, high - low)


def attend_kernel(pq, pk, lq, lk, own, other, out_own, out_other, lse_ref, *, heads, factor):
    allowed = seen(pq[...], pk[...], lq[0], lk[0])
    span = heads * HEAD
    for h in range(heads):
        low, high = h * HEAD, (h + 1) * HEAD
        q = both(own, other, low, high)
        k = both(own, other, span + low, span + high)
        v = both(own, other, 2 * span + low, 2 * span + high)
        scores = jnp.where(allowed, mm_t(q, k) * factor, MASKED)
        top = jnp.max(scores, axis=-1, keepdims=True)
        expo = jnp.exp(scores - top)
        total = jnp.sum(expo, axis=-1, keepdims=True)
        probs = (expo * (1.0 / total)).astype(BF16)
        put(out_own, out_other, low, high, mm(probs, v).astype(BF16))
        lse_ref[0, :, h : h + 1] = top + jnp.log(total)


def attend_specs(chips, count, rows, length):
    whole = pl.BlockSpec(memory_space=pltpu.VMEM)
    where = [
        pl.BlockSpec((length, 1), lambda s: (0, 0)),
        pl.BlockSpec((1, length), lambda s: (0, 0)),
        pl.BlockSpec((1, length, 1), lambda s: (s, 0, 0)),
        pl.BlockSpec((1, 1, length), lambda s: (s, 0, 0)),
    ]

    def of(width):
        return pl.BlockSpec((chips, 1, rows, width), lambda s: (0, s, 0, 0))

    return where, of


def attend(where, own, other, heads):
    chips, count, rows, _ = own.shape
    length = 2 * chips * rows
    span = heads * HEAD
    places, of = attend_specs(chips, count, rows, length)
    return pl.pallas_call(
        functools.partial(attend_kernel, heads=heads, factor=HEAD ** (-0.5)),
        out_shape=(
            jax.ShapeDtypeStruct((chips, count, rows, span), BF16),
            jax.ShapeDtypeStruct((chips, count, rows, span), BF16),
            jax.ShapeDtypeStruct((count, length, heads), F32),
        ),
        grid=(count,),
        in_specs=places + [of(3 * span), of(3 * span)],
        out_specs=(of(span), of(span), pl.BlockSpec((1, length, heads), lambda s: (s, 0, 0))),
        cost_estimate=pl.CostEstimate(
            flops=count * heads * length * length * HEAD * 4,
            bytes_accessed=count * length * heads * HEAD * 8,
            transcendentals=count * heads * length * length,
        ),
        name="attend",
    )(*where, own, other)


def attend_back_kernel(
    pq, pk, lq, lk, own, other, lse_ref, ga_own, ga_other, out_own, out_other, *, heads, factor
):
    allowed = seen(pq[...], pk[...], lq[0], lk[0])
    span = heads * HEAD
    for h in range(heads):
        low, high = h * HEAD, (h + 1) * HEAD
        q = both(own, other, low, high)
        k = both(own, other, span + low, span + high)
        v = both(own, other, 2 * span + low, 2 * span + high)
        ga = both(ga_own, ga_other, low, high)
        scores = jnp.where(allowed, mm_t(q, k) * factor, MASKED)
        probs = jnp.exp(scores - lse_ref[0, :, h : h + 1])
        grad_probs = mm_t(ga, v)
        inner = jnp.sum(probs * grad_probs, axis=-1, keepdims=True)
        grad_scores = (probs * (grad_probs - inner)).astype(BF16)
        put(out_own, out_other, low, high, (mm(grad_scores, k) * factor).astype(BF16))
        put(
            out_own,
            out_other,
            span + low,
            span + high,
            (t_mm(grad_scores, q) * factor).astype(BF16),
        )
        put(
            out_own,
            out_other,
            2 * span + low,
            2 * span + high,
            t_mm(probs.astype(BF16), ga).astype(BF16),
        )


def attend_back(where, own, other, lse, ga_own, ga_other, heads):
    chips, count, rows, _ = own.shape
    length = 2 * chips * rows
    span = heads * HEAD
    places, of = attend_specs(chips, count, rows, length)
    return pl.pallas_call(
        functools.partial(attend_back_kernel, heads=heads, factor=HEAD ** (-0.5)),
        out_shape=(jax.ShapeDtypeStruct((chips, count, rows, 3 * span), BF16),) * 2,
        grid=(count,),
        in_specs=places
        + [of(3 * span), of(3 * span)]
        + [pl.BlockSpec((1, length, heads), lambda s: (s, 0, 0)), of(span), of(span)],
        out_specs=(of(3 * span), of(3 * span)),
        cost_estimate=pl.CostEstimate(
            flops=count * heads * length * length * HEAD * 10,
            bytes_accessed=count * length * heads * HEAD * 14,
            transcendentals=count * heads * length * length,
        ),
        name="attend_back",
    )(*where, own, other, lse, ga_own, ga_other)


def on_device(
    inputs,
    ln1_gain,
    ln1_bias,
    w_query,
    b_query,
    w_key,
    w_value,
    b_value,
    w_out,
    b_out,
    ln2_gain,
    ln2_bias,
    w_up,
    b_up,
    w_down,
    b_down,
    in_query,
    out_query,
    in_key,
    out_key,
    in_value,
    out_value,
    in_attn,
    out_attn,
    in_expand,
    out_expand,
    in_reduce,
    out_reduce,
    adapter_pick,
    piece_start,
    cotangent,
):
    count, rows, wide = inputs.shape[1:]
    size = lax.axis_size("shard")
    chips = size // 2
    bits = bits_of(size)[1:]
    me = lax.axis_index("shard").astype(jnp.int32)
    me_arr = me[None]
    part = lax.axis_index("rep").astype(jnp.int32) & 1
    at = jnp.stack([me, part])
    heads = HEADS // size
    span = heads * HEAD
    slice_wide = wide // size
    ff_part = w_up.shape[1] // size
    rank = in_query.shape[1]
    block = count * rows
    chosen = adapter_pick[0]
    starts = piece_start[0]

    def keep_own(value):
        of_row = lax.broadcasted_iota(jnp.int32, value.shape, 0) // rows % count
        of_col = lax.broadcasted_iota(jnp.int32, value.shape, 1) // rank % count
        return jnp.where(of_row == of_col, value, 0.0).astype(BF16)

    chip = me // 2

    def exchange(pieces):
        return [pieces[0]] + [swap(p, "shard", 2 * i) for i, p in enumerate(pieces) if i]

    def with_halves(pieces):
        near = jnp.concatenate(pieces[1:], 0)
        return [pieces[0], near, swap(near, "rep", 1)]

    def both_cores(own):
        return list(own) + [swap(piece, "shard", 1) for piece in own]

    w_out_other = swap(w_out, "shard", 1)
    w_down_other = swap(w_down, "shard", 1)
    pieces_qkv = cut_pieces(at, [w_query, w_key, w_value], span, chips, True)
    turned = exchange(pieces_qkv)
    near_up = exchange(cut_pieces(at, [after(w_up, *pieces_qkv)], ff_part, chips, True))

    narrow = [out_query, out_key, out_value, in_attn, out_expand, in_reduce]
    edges = np.cumsum([0] + [n.shape[2] for n in narrow])
    mine, packed = pick_maps(
        after(chosen, w_out_other, w_down_other, *pieces_qkv),
        [in_query, in_key, in_value, in_expand, out_attn, out_reduce],
        narrow,
    )
    packed_other = swap(packed, "shard", 1)
    order = bits + [1]
    near_one = swap(mine[None], "shard", bits[0])

    rows_in = after(inputs[0].reshape(block, wide), mine)
    features = rows_in.astype(F32)
    normed = layer_norm(features, ln1_gain.astype(F32), ln1_bias.astype(F32)).astype(BF16)
    vectors = after(jnp.stack([b_out, ln2_gain, ln2_bias, ln1_gain]), normed).astype(F32)
    hidden_block = after(normed, packed_other, near_one, *turned[1:], *near_up[1:])
    starts, b_query, b_value, b_up, me_late, chosen, packed = after(
        (starts, b_query, b_value, b_up, me, chosen, packed), hidden_block
    )
    hidden_one, one_first, one_last = gather_rows(hidden_block, bits)

    turned[0] = after(turned[0], *one_first)
    w_qkv_mine, w_qkv_other = place_weights(
        at, both_cores(with_halves(turned)), chips, 3 * span, False
    )
    w_out_late, w_down_late, *near_up = after((w_out, w_down, *near_up), hidden_block)
    merged_up = jnp.concatenate(near_up[1:], 0)
    w_out_chip = jnp.concatenate([w_out_late, w_out_other], 0)
    w_down_chip = jnp.concatenate([w_down_late, w_down_other], 0)
    hidden_one = after(hidden_one, merged_up, w_out_chip, w_down_chip)
    cot_mine = cotangent[0].reshape(block, wide)
    near = after(jnp.concatenate([mine[None], near_one], 0), *one_first)
    for bit in bits[1:]:
        near = jnp.concatenate([near, swap(near, "shard", bit)], 0)
    stacked = jnp.concatenate([near, swap(near, "shard", 1)], 0)

    owners = np.concatenate([np.arange(chips) * 2, np.arange(chips) * 2 + 1]).astype(np.int32)
    locs = np.tile(np.arange(rows, dtype=np.int32), 2 * chips)
    positions = (me_late ^ jnp.asarray(np.repeat(owners, rows))) * rows + jnp.asarray(locs)
    labels = jnp.stack([piece_labels(starts[s], positions) for s in range(count)])
    where = (positions[:, None], positions[None, :], labels[:, :, None], labels[:, None, :])

    whole = place_columns(me_arr, stacked, subsets(order)).reshape(6, count, rank, wide)
    in_qkv = whole[:3].reshape(3 * count * rank, wide)
    in_exp, out_att, out_red = (whole[3 + i].reshape(count * rank, wide) for i in range(3))

    def unpack(table, i):
        return table[:, edges[i] : edges[i + 1]]

    def out_qkv_of(table):
        stacked = jnp.stack([unpack(table, t) for t in range(3)])
        spread = stacked[:, :, None, :] * jnp.eye(3, dtype=BF16)[:, None, :, None]
        return spread.reshape(count * 3 * rank, 3 * span)

    out_qkv_mine, out_qkv_other = out_qkv_of(packed), out_qkv_of(packed_other)
    in_att, out_exp, in_red = (
        jnp.concatenate([unpack(packed, i), unpack(packed_other, i)], 1) for i in (3, 4, 5)
    )

    def slice_of(bias, index, width):
        return lax.dynamic_slice_in_dim(bias, index * width, width).astype(F32)

    def b_qkv_of(index):
        return jnp.concatenate(
            [slice_of(b_query, index, span), jnp.zeros((span,), F32), slice_of(b_value, index, span)]
        )

    b_up_chip = jnp.concatenate([slice_of(b_up, me, ff_part), slice_of(b_up, me ^ 1, ff_part)])

    def by_chip(value):
        return value.reshape((chips, count, rows) + value.shape[1:])

    def flat(value):
        return value.reshape(chips * block, value.shape[-1])

    def block_products(products, low, table):
        parts = {}
        for i in reversed(range(chips)):
            at = slice(i * block, (i + 1) * block)
            total = mm(low[at], table)
            for value, weight, main in products:
                total = total + main(value[at], weight)
            parts[2 * i] = total.astype(BF16)
            if i == chips - 1:
                low = after(low, parts[2 * i])
                products = [(after(v, parts[2 * i]), w, main) for v, w, main in products]
        return parts

    low_qkv = keep_own(mm_t(hidden_one, in_qkv))
    qkv_away = (
        mm(hidden_one, w_qkv_other) + mm(low_qkv, out_qkv_other) + b_qkv_of(me ^ 1)
    ).astype(BF16)
    qkv_other = by_chip(swap(qkv_away, "shard", 1))
    qkv_own = by_chip(
        (mm(hidden_one, w_qkv_mine) + mm(low_qkv, out_qkv_mine) + b_qkv_of(me)).astype(BF16)
    )
    att_own, att_away, lse = attend(where, qkv_own, qkv_other, heads)
    halves_up = [near_up[0], merged_up, swap(after(merged_up, att_own), "rep", 1)]
    cot_pieces, _, _ = gather_rows(after(cot_mine, att_own), bits, apart=True)
    attended = jnp.concatenate([flat(att_own), swap(flat(att_away), "shard", 1)], 1)
    low_att = keep_own(mm_t(attended, in_att))
    parts = block_products([(attended, w_out_chip, mm)], low_att, out_att)
    terms, relayed = scatter_rows(parts, bits)
    cot = jnp.concatenate(after(cot_pieces, *relayed), 0)
    glow_red = keep_own(mm_t(cot, out_red))
    grad_act = (mm_t(cot, w_down_chip) + mm(glow_red, in_red)).astype(BF16)
    terms[0] = after(terms[0], grad_act)
    residual, hidden_block = row_call(
        norm_kernel, [rows_in, vectors] + terms, block, wide, [F32, BF16], "norm"
    )
    pieces_up = after(tuple(halves_up), hidden_block)
    two_pieces, _, _ = gather_rows(hidden_block, bits, apart=True)

    (w_up_chip,) = place_weights(at, both_cores(pieces_up), chips, ff_part, True)
    two_pieces[-2:] = after(tuple(two_pieces[-2:]), w_up_chip)
    hidden_two = jnp.concatenate(two_pieces, 0)
    low_exp = keep_own(mm_t(hidden_two, in_exp))
    pre = mm(hidden_two, w_up_chip) + mm(low_exp, out_exp) + b_up_chip
    share = 0.5 * (1.0 + lax.erf(pre * np.float32(0.5**0.5)))
    act = (pre * share).astype(BF16)
    slope = share + pre * (jnp.exp(-0.5 * pre * pre) * np.float32((2 * np.pi) ** -0.5))
    grad_pre = (slope * grad_act.astype(F32)).astype(BF16)
    glow_exp = keep_own(mm_t(grad_pre, out_exp))
    parts = block_products([(grad_pre, w_up_chip, mm_t)], glow_exp, in_exp)
    far = 2 * (chips - 1)

    def halves(value):
        middle = value.shape[1] // 2
        return value[:, :middle], value[:, middle:]

    act_mid, grad_mid, low_mid, glow_mid = after((act, grad_pre, low_exp, glow_red), parts[far])
    red_own, red_away = halves(t_mm(glow_mid, act_mid))
    exp_own, exp_away = halves(t_mm(low_mid, grad_mid))
    terms, _ = scatter_rows(parts, bits, (parts[0], red_own, exp_own))
    grad_residual, grad_block = row_call(
        functools.partial(norm_back_kernel, outs=2, row=1),
        [residual, vectors, cot_mine] + terms,
        block,
        wide,
        [F32, BF16],
        "norm_back",
    )
    grad_branch, branch_first, branch_last = gather_rows(grad_block, bits)

    act_late = after(act, grad_block)
    low_red = keep_own(mm_t(act_late, in_red))
    down = (mm(act_late, w_down_chip) + mm(low_red, out_red)).astype(BF16)
    down_parts = {2 * i: down[i * block : (i + 1) * block] for i in range(chips)}
    glow_att = keep_own(mm_t(grad_branch, out_att))
    grad_att = (mm_t(grad_branch, w_out_chip) + mm(glow_att, in_att)).astype(BF16)
    ga_own = by_chip(grad_att[:, :span])
    ga_other = by_chip(swap(grad_att[:, span:], "shard", 1))
    grad_own, grad_away = attend_back(where, qkv_own, qkv_other, lse, ga_own, ga_other, heads)
    grad_own = flat(grad_own)
    grad_other = swap(flat(grad_away), "shard", 1)
    glow_qkv = keep_own(mm_t(grad_own, out_qkv_mine) + mm_t(grad_other, out_qkv_other))
    def sum_cores(own, away):
        return own + swap(away.astype(BF16), "shard", 1).astype(F32)

    def core_columns(value):
        width = value.shape[1] // size

        def side(which):
            return jnp.stack(
                [
                    lax.dynamic_slice_in_dim(value, (2 * k + which) * width, width, 1)
                    for k in range(chips)
                ]
            )

        core = me & 1
        return sum_cores(side(core), side(1 - core))

    def split_chips(current, bit):
        current = current.reshape((2, current.shape[0] // 2) + current.shape[1:])
        own = (me // bit) & 1
        away = lax.dynamic_index_in_dim(current, 1 - own, 0, False).astype(BF16)
        return lax.dynamic_index_in_dim(current, own, 0, False), away

    def sum_chips(current, *gate):
        for i, bit in enumerate(bits[::-1]):
            current, away = split_chips(current, bit)
            there = swap(away, "shard", bit)
            current = current + (there if i else after(there, *gate)).astype(F32)
        return current[0], away

    rep_bits = bits_of(lax.axis_size("rep"))

    def over_rep(terms, extra=(), gates=None):
        current = jnp.concatenate([t.astype(BF16) for t in terms], 1)
        current = jnp.concatenate([current, *extra], 0)[None]
        gathered = [current]
        for bit in rep_bits:
            there = swap(current, "rep", bit)
            if gates and bit in gates:
                there = after(there, *gates[bit])
            gathered.append(there)
            if bit != rep_bits[-1]:
                current = jnp.concatenate([current, there], 0)
        return gathered

    def over_groups(terms, place, gathered):
        widths = [t.shape[1] for t in terms]
        outs = sum_blocks(place, gathered, count * rank, widths)
        return [out.reshape(ADAPTERS, rank, -1) for out in outs]

    local = sum_cores(
        jnp.concatenate([red_own, exp_own], 1), jnp.concatenate([red_away, exp_away], 1)
    )
    glow_late, low_late = after((glow_exp, low_red), *branch_first)
    near_first = core_columns(
        jnp.concatenate([t_mm(glow_late, hidden_two), t_mm(low_late, cot)], 0)
    ).astype(BF16)
    tall = near_first.shape[1]
    riders = {}
    for i in range(chips):
        rider = lax.dynamic_index_in_dim(near_first, chip ^ i, 0, False)
        rider = jnp.pad(rider, ((0, block - tall), (0, 0)))
        riders[2 * i] = after(jnp.concatenate([down_parts[2 * i], rider], 1), branch_last)
    att_side = sum_cores(*halves(t_mm(glow_att, attended)))

    glow_last = glow_qkv
    in_terms = jnp.concatenate([t_mm(glow_last, hidden_one), t_mm(low_att, grad_branch)], 0)

    def own_terms(full):
        height = count * rank
        return jnp.concatenate(
            [full[t * height : (t + 1) * height, t * span : (t + 1) * span] for t in range(3)], 1
        )

    near_second = core_columns(in_terms)
    products = [(grad_own, w_qkv_mine, mm_t), (grad_other, w_qkv_other, mm_t)]
    parts = block_products(products, after(glow_qkv, in_terms), in_qkv)
    far_part = parts[2 * (chips - 1)]
    mark = (chosen[:, None] == jnp.arange(ADAPTERS, dtype=jnp.int32)[None, :]).astype(BF16)
    mark = jnp.pad(mark, ((0, 16 - count), (0, local.shape[1] - ADAPTERS)))
    sums = [local[:, :ff_part], local[:, ff_part:]]
    gathered = over_rep(sums, [mark], {rep_bits[-1]: (far_part,)})
    marks = jnp.concatenate(
        [g[:, count * rank : count * rank + count, :ADAPTERS] for g in gathered], 0
    )
    place = marks.reshape(-1, 1, ADAPTERS, 1) * jnp.eye(rank, dtype=BF16)[None, :, None, :]
    place = place.reshape(-1, ADAPTERS * rank)
    s_in_red, s_out_exp = over_groups(sums, place, gathered)

    own_last, other_last = after((grad_own, grad_other), far_part)
    outer_own = own_terms(t_mm(low_qkv, own_last))
    outer_away = own_terms(t_mm(low_qkv, other_last))
    aside = {}

    def hop(relayed):
        aside["second"], sent = sum_chips(after(near_second, far_part), *relayed)
        return sent

    terms, relayed = scatter_rows(parts, bits, (parts[0], outer_own, outer_away), hop)
    outer = sum_cores(outer_own, after(outer_away, *relayed))
    second = aside["second"]
    down, _ = scatter_rows(riders, bits, (grad_away,))
    down[0] = after(down[0], *relayed)
    first = sum(t[:tall, wide:].astype(F32) for t in down).reshape(2, count * rank, slice_wide)
    layer_rows = residual + b_down.astype(F32) + sum(t[:, :wide].astype(F32) for t in down)

    (input_rows,) = row_call(
        functools.partial(norm_back_kernel, outs=1, row=3),
        [rows_in, vectors, grad_residual] + terms,
        block,
        wide,
        [BF16],
        "norm_back",
    )
    out_att_sum = second[count * 3 * rank :]
    second = second[: count * 3 * rank].reshape(3, count * rank, slice_wide)
    sums = [att_side, first[0], first[1]]
    ends = {rep_bits[-1]: (input_rows,)}
    s_in_att, s_in_exp, s_out_red = over_groups(sums, place, over_rep(sums, (), ends))
    sums = [second[t] for t in range(3)]
    sums += [outer[:, t * span : (t + 1) * span] for t in range(3)] + [out_att_sum]
    late = over_groups(sums, place, over_rep(sums, (), ends))
    s_out_att = late.pop()
    shape = (1, count, rows, wide)
    return (
        layer_rows.astype(BF16).reshape(shape),
        input_rows.reshape(shape),
        late[0],
        late[3],
        late[1],
        late[4],
        late[2],
        late[5],
        s_in_att,
        s_out_att,
        s_in_exp,
        s_out_exp,
        s_in_red,
        s_out_red,
    )


def solution(mesh):
    row = P("shard", None)
    wide = P(None, None, "shard")
    acts = P("rep", None, "shard", None)
    in_specs = (
        (acts, P(), P(), row, P(), row, row, P(), row, P(), P(), P(), row, P(), row, P())
        + (wide,) * 12
        + (P("rep", None), P("rep", None, None), acts)
    )
    out_specs = (acts, acts) + (wide,) * 12
    return jax.shard_map(
        on_device, mesh=mesh, in_specs=in_specs, out_specs=out_specs, check_vma=False
    )
```

```python
import functools

import jax
import jax.numpy as jnp
import numpy as np
from jax import lax
from jax.experimental import pallas as pl
from jax.experimental.pallas import tpu as pltpu
from jax.sharding import PartitionSpec as P

HEADS = 16
HEAD = 128
ADAPTERS = 8
PIECE = 256

EPSILON = 1e-05
MASKED = -1e30
F32 = jnp.float32
BF16 = jnp.bfloat16


def layer_norm(values, gain_vec, shift_vec):
    centre = jnp.mean(values, axis=-1, keepdims=True)
    offset = values - centre
    spread = jnp.mean(offset * offset, axis=-1, keepdims=True)
    return offset * lax.rsqrt(spread + EPSILON) * gain_vec + shift_vec


def piece_labels(starts, positions):
    inside = (positions[:, None] >= starts[None, :]) & (
        positions[:, None] < starts[None, :] + PIECE
    )
    labels = jnp.arange(1, starts.shape[0] + 1, dtype=jnp.int32)
    return jnp.sum(jnp.where(inside, labels[None, :], 0), axis=1)


def mm(a, b):
    return lax.dot_general(a, b, (((1,), (0,)), ((), ())), preferred_element_type=F32)


def mm_t(a, b):
    return lax.dot_general(a, b, (((1,), (1,)), ((), ())), preferred_element_type=F32)


def t_mm(a, b):
    return lax.dot_general(a, b, (((0,), (0,)), ((), ())), preferred_element_type=F32)


def swap(value, axis, mask):
    size = lax.axis_size(axis)
    return lax.ppermute(value, axis, [(i, i ^ mask) for i in range(size)])


def after(value, *others):
    return lax.optimization_barrier((value,) + others)[0]


def bits_of(size):
    bits = []
    while (1 << len(bits)) < size:
        bits.append(1 << len(bits))
    return bits


def subsets(bits):
    masks = [0]
    for bit in bits:
        masks = masks + [m | bit for m in masks]
    return masks


def gather_rows(block, bits, gate=(), apart=False):
    half = block.shape[0] // 2
    got = {0: [block]}
    upper, lower = {}, {}
    for bit in bits:
        there = swap(block, "shard", bit)
        there = after(there, *gate) if gate else there
        got[bit] = [there]
        upper[bit], lower[bit] = there[:half], there[half:]
    for which, order in ((upper, bits), (lower, bits[::-1])):
        for k, bit in enumerate(order):
            for sub in subsets(order[:k])[1:]:
                which[sub | bit] = swap(which[sub], "shard", bit)
    pieces = []
    for mask in subsets(bits):
        pieces += got[mask] if mask in got else [upper[mask], lower[mask]]
    firsts = [got[bit][0] for bit in bits]
    if apart:
        return pieces, firsts, pieces[-1]
    return jnp.concatenate(pieces, 0), firsts, pieces[-1]


def scatter_rows(parts, bits, gate=(), between=None):
    half = parts[0].shape[0] // 2
    upper = {m: p[:half] for m, p in parts.items()}
    lower = {m: p[half:] for m, p in parts.items()}
    for which, order in ((upper, bits), (lower, bits[::-1])):
        for k in reversed(range(len(order))):
            for sub in subsets(order[:k])[1:]:
                other = swap(which[sub | order[k]], "shard", order[k])
                other = after(other, *gate) if gate else other
                which[sub] = (which[sub].astype(F32) + other.astype(F32)).astype(BF16)
    blocks = [jnp.concatenate([upper[bit], lower[bit]], 0) for bit in bits]
    if between:
        blocks = list(after(tuple(blocks), between(blocks)))
    return [parts[0]] + [swap(b, "shard", bit) for b, bit in zip(blocks, bits)], blocks


def gather_blocks(value, axis, bits, gates=None):
    current = value[None]
    for bit in bits:
        there = swap(current, axis, bit)
        if gates and bit in gates:
            there = after(there, *gates[bit])
        current = jnp.concatenate([current, there], 0)
    return current


def run_copies(copies):
    for copy in copies:
        copy.start()
    for copy in copies:
        copy.wait()


def cut_kernel(at_ref, *refs, count, terms, width):
    tables, outs, sems = refs[:terms], refs[terms:-1], refs[-1]
    me, part = at_ref[0], at_ref[1]
    copies = []
    for i in range(count):
        rows = outs[i].shape[0]
        first = pl.multiple_of(part * rows, rows) if rows < tables[0].shape[0] else 0
        for k in range(2):
            column = pl.multiple_of((((me // 2) ^ i) * 2 + k) * width, width)
            for t in range(terms):
                copies.append(
                    pltpu.make_async_copy(
                        tables[t].at[pl.ds(first, rows), pl.ds(column, width)],
                        outs[i].at[:, pl.ds((k * terms + t) * width, width)],
                        sems.at[len(copies)],
                    )
                )
    run_copies(copies)


def cut_pieces(at, tables, width, count, split):
    rows, terms = tables[0].shape[0], len(tables)
    shapes = [
        jax.ShapeDtypeStruct((rows // 2 if i and split else rows, 2 * terms * width), BF16)
        for i in range(count)
    ]
    return pl.pallas_call(
        functools.partial(cut_kernel, count=count, terms=terms, width=width),
        out_shape=shapes,
        in_specs=[pl.BlockSpec(memory_space=pltpu.SMEM)]
        + [pl.BlockSpec(memory_space=pl.ANY)] * terms,
        out_specs=[pl.BlockSpec(memory_space=pltpu.VMEM)] * count,
        scratch_shapes=[pltpu.SemaphoreType.DMA((2 * terms * count,))],
        cost_estimate=pl.CostEstimate(
            flops=0, bytes_accessed=4 * rows * count * terms * width, transcendentals=0
        ),
        name="cut_pieces",
    )(at, *tables)


def place_kernel(at_ref, *refs, count, width, rows, joined):
    pieces, outs, sems = refs[:6], refs[6:-1], refs[-1]
    me, part = at_ref[0], at_ref[1]
    half = rows // 2

    def copies(core):
        made = []
        for side in range(2):
            parts = [(pieces[3 * side], 0, rows, 0, 0)]
            for second in range(2):
                parts += [
                    (pieces[3 * side + 1 + second], (i - 1) * half, half, i, part ^ second)
                    for i in range(1, count)
                ]
            for piece, first, height, i, which in parts:
                row = pl.multiple_of((me ^ (2 * i) ^ side) * rows + which * half, half)
                for k in range(2):
                    own = k ^ core
                    source = piece.at[pl.ds(first, height), pl.ds(k * width, width)]
                    if joined:
                        target = outs[0].at[pl.ds(row, height), pl.ds(own * width, width)]
                    else:
                        target = outs[own].at[pl.ds(row, height)]
                    made.append(pltpu.make_async_copy(source, target, sems.at[len(made)]))
        return made

    @pl.when((me & 1) == 0)
    def _():
        run_copies(copies(0))

    @pl.when((me & 1) == 1)
    def _():
        run_copies(copies(1))


def place_weights(at, pieces, count, width, joined):
    rows = pieces[0].shape[0]
    if joined:
        shapes = [jax.ShapeDtypeStruct((rows * count * 2, 2 * width), BF16)]
    else:
        shapes = [jax.ShapeDtypeStruct((rows * count * 2, width), BF16)] * 2
    return pl.pallas_call(
        functools.partial(place_kernel, count=count, width=width, rows=rows, joined=joined),
        out_shape=shapes,
        in_specs=[pl.BlockSpec(memory_space=pltpu.SMEM)]
        + [pl.BlockSpec(memory_space=pl.ANY)] * len(pieces),
        out_specs=[pl.BlockSpec(memory_space=pltpu.VMEM)] * len(shapes),
        scratch_shapes=[pltpu.SemaphoreType.DMA((8 * count - 4,))],
        cost_estimate=pl.CostEstimate(
            flops=0, bytes_accessed=16 * rows * count * width, transcendentals=0
        ),
        name="place_weights",
    )(at, *pieces)


def pick_kernel(chosen_ref, *refs, tall, rank):
    tables, (tall_ref, flat_ref, sems) = refs[:-3], refs[-3:]
    count = chosen_ref.shape[0]
    copies = []
    for s in range(count):
        column = 0
        for i, table in enumerate(tables):
            if i < tall:
                target = tall_ref.at[pl.ds((i * count + s) * rank, rank)]
            else:
                width = table.shape[2]
                target = flat_ref.at[pl.ds(s * rank, rank), pl.ds(column, width)]
                column += width
            copies.append(
                pltpu.make_async_copy(table.at[chosen_ref[s]], target, sems.at[len(copies)])
            )
    run_copies(copies)


def pick_maps(chosen, upright, flat):
    count, rank = chosen.shape[0], upright[0].shape[1]
    total = sum(t.shape[2] for t in flat)
    shapes = (
        jax.ShapeDtypeStruct((len(upright) * count * rank, upright[0].shape[2]), BF16),
        jax.ShapeDtypeStruct((count * rank, total), BF16),
    )
    tables = upright + flat
    return pl.pallas_call(
        functools.partial(pick_kernel, tall=len(upright), rank=rank),
        out_shape=shapes,
        in_specs=[pl.BlockSpec(memory_space=pltpu.SMEM)]
        + [pl.BlockSpec(memory_space=pl.ANY)] * len(tables),
        out_specs=[pl.BlockSpec(memory_space=pltpu.VMEM)] * 2,
        scratch_shapes=[pltpu.SemaphoreType.DMA((count * len(tables),))],
        cost_estimate=pl.CostEstimate(
            flops=0, bytes_accessed=8 * count * rank * total, transcendentals=0
        ),
        name="pick_maps",
    )(chosen, *tables)


def cols_kernel(me_ref, in_ref, out_ref, sems, *, masks):
    width = in_ref.shape[2]
    run_copies(
        [
            pltpu.make_async_copy(
                in_ref.at[i],
                out_ref.at[:, pl.ds(pl.multiple_of((me_ref[0] ^ mask) * width, width), width)],
                sems.at[i],
            )
            for i, mask in enumerate(masks)
        ]
    )


def place_columns(me, stacked, masks):
    count, rows, width = stacked.shape
    return pl.pallas_call(
        functools.partial(cols_kernel, masks=masks),
        out_shape=jax.ShapeDtypeStruct((rows, count * width), stacked.dtype),
        in_specs=[pl.BlockSpec(memory_space=pltpu.SMEM), pl.BlockSpec(memory_space=pltpu.VMEM)],
        out_specs=pl.BlockSpec(memory_space=pltpu.VMEM),
        scratch_shapes=[pltpu.SemaphoreType.DMA((count,))],
        cost_estimate=pl.CostEstimate(
            flops=0, bytes_accessed=4 * count * rows * width, transcendentals=0
        ),
        name="place_columns",
    )(me, stacked)


def normalised(values):
    centre = jnp.mean(values, axis=-1, keepdims=True)
    offset = values - centre
    scale = lax.rsqrt(jnp.mean(offset * offset, axis=-1, keepdims=True) + EPSILON)
    return offset * scale, scale


def total_of(refs, at):
    total = refs[0][at].astype(F32)
    for ref in refs[1:]:
        total = total + ref[at].astype(F32)
    return total


def tiles_of(rows):
    tile = 32 if rows % 32 == 0 else rows
    return [slice(i, i + tile) for i in range(0, rows, tile)]


def norm_kernel(base, vectors, *refs):
    terms, (res_ref, out_ref) = refs[:-2], refs[-2:]
    shift, gain, bias = vectors[0:1], vectors[1:2], vectors[2:3]
    for at in tiles_of(base.shape[0]):
        values = base[at].astype(F32) + (total_of(terms, at) + shift)
        res_ref[at] = values
        unit, _ = normalised(values)
        out_ref[at] = (unit * gain + bias).astype(BF16)


def norm_back_kernel(values, vectors, base, *refs, outs, row):
    gain = vectors[row : row + 1]
    terms, outputs = refs[: len(refs) - outs], refs[len(refs) - outs :]
    for at in tiles_of(values.shape[0]):
        unit, scale = normalised(values[at].astype(F32))
        grad = total_of(terms, at) * gain
        mean_one = jnp.mean(grad, axis=-1, keepdims=True)
        mean_two = jnp.mean(grad * unit, axis=-1, keepdims=True)
        total = base[at].astype(F32) + scale * (grad - mean_one - unit * mean_two)
        for out in outputs:
            out[at] = total.astype(out.dtype)


def row_call(kernel, order, rows, wide, dtypes, name):
    return pl.pallas_call(
        kernel,
        out_shape=[jax.ShapeDtypeStruct((rows, wide), d) for d in dtypes],
        in_specs=[pl.BlockSpec(memory_space=pltpu.VMEM)] * len(order),
        out_specs=[pl.BlockSpec(memory_space=pltpu.VMEM)] * len(dtypes),
        cost_estimate=pl.CostEstimate(
            flops=20 * rows * wide, bytes_accessed=200 * rows * wide, transcendentals=0
        ),
        name=name,
    )(*order)


def sum_kernel(place, *refs, blocks, rows):
    gathered, outs = refs[:blocks], refs[blocks:]
    start = 0
    for out in outs:
        width = out.shape[1]
        total, row = None, 0
        for ref in gathered:
            for g in range(ref.shape[0]):
                term = t_mm(place[row : row + rows], ref[g, :rows, start : start + width])
                total = term if total is None else total + term
                row += rows
        out[...] = total
        start += width


def sum_blocks(place, gathered, rows, widths):
    total = sum(widths)
    return pl.pallas_call(
        functools.partial(sum_kernel, blocks=len(gathered), rows=rows),
        out_shape=[jax.ShapeDtypeStruct((place.shape[1], w), F32) for w in widths],
        in_specs=[pl.BlockSpec(memory_space=pltpu.VMEM)] * (1 + len(gathered)),
        out_specs=[pl.BlockSpec(memory_space=pltpu.VMEM)] * len(widths),
        cost_estimate=pl.CostEstimate(
            flops=2 * place.size * total, bytes_accessed=(2 * place.shape[0] + 4 * place.shape[1]) * total, transcendentals=0
        ),
        name="sum_blocks",
    )(place, *gathered)


def seen(pos_q, pos_k, lab_q, lab_k):
    return (pos_k <= pos_q) | ((lab_q == lab_k) & (lab_q > 0))


def both(own_ref, other_ref, low, high):
    own, other = own_ref[:, 0, :, low:high], other_ref[:, 0, :, low:high]
    chips, rows, width = own.shape
    return jnp.concatenate([own.reshape(chips * rows, width), other.reshape(chips * rows, width)], 0)


def put(own_ref, other_ref, low, high, value):
    chips, _, rows, _ = own_ref.shape
    half = chips * rows
    own_ref[:, 0, :, low:high] = value[:half].reshape(chips, rows, high - low)
    other_ref[:, 0, :, low:high] = value[half:].reshape(chips, rows, high - low)


def attend_kernel(pq, pk, lq, lk, own, other, out_own, out_other, lse_ref, *, heads, factor):
    allowed = seen(pq[...], pk[...], lq[0], lk[0])
    span = heads * HEAD
    for h in range(heads):
        low, high = h * HEAD, (h + 1) * HEAD
        q = both(own, other, low, high)
        k = both(own, other, span + low, span + high)
        v = both(own, other, 2 * span + low, 2 * span + high)
        scores = jnp.where(allowed, mm_t(q, k) * factor, MASKED)
        top = jnp.max(scores, axis=-1, keepdims=True)
        expo = jnp.exp(scores - top)
        total = jnp.sum(expo, axis=-1, keepdims=True)
        probs = (expo * (1.0 / total)).astype(BF16)
        put(out_own, out_other, low, high, mm(probs, v).astype(BF16))
        lse_ref[0, :, h : h + 1] = top + jnp.log(total)


def attend_specs(chips, count, rows, length):
    whole = pl.BlockSpec(memory_space=pltpu.VMEM)
    where = [
        pl.BlockSpec((length, 1), lambda s: (0, 0)),
        pl.BlockSpec((1, length), lambda s: (0, 0)),
        pl.BlockSpec((1, length, 1), lambda s: (s, 0, 0)),
        pl.BlockSpec((1, 1, length), lambda s: (s, 0, 0)),
    ]

    def of(width):
        return pl.BlockSpec((chips, 1, rows, width), lambda s: (0, s, 0, 0))

    return where, of


def attend(where, own, other, heads):
    chips, count, rows, _ = own.shape
    length = 2 * chips * rows
    span = heads * HEAD
    places, of = attend_specs(chips, count, rows, length)
    return pl.pallas_call(
        functools.partial(attend_kernel, heads=heads, factor=HEAD ** (-0.5)),
        out_shape=(
            jax.ShapeDtypeStruct((chips, count, rows, span), BF16),
            jax.ShapeDtypeStruct((chips, count, rows, span), BF16),
            jax.ShapeDtypeStruct((count, length, heads), F32),
        ),
        grid=(count,),
        in_specs=places + [of(3 * span), of(3 * span)],
        out_specs=(of(span), of(span), pl.BlockSpec((1, length, heads), lambda s: (s, 0, 0))),
        cost_estimate=pl.CostEstimate(
            flops=count * heads * length * length * HEAD * 4,
            bytes_accessed=count * length * heads * HEAD * 8,
            transcendentals=count * heads * length * length,
        ),
        name="attend",
    )(*where, own, other)


def attend_back_kernel(
    pq, pk, lq, lk, own, other, lse_ref, ga_own, ga_other, out_own, out_other, *, heads, factor
):
    allowed = seen(pq[...], pk[...], lq[0], lk[0])
    span = heads * HEAD
    for h in range(heads):
        low, high = h * HEAD, (h + 1) * HEAD
        q = both(own, other, low, high)
        k = both(own, other, span + low, span + high)
        v = both(own, other, 2 * span + low, 2 * span + high)
        ga = both(ga_own, ga_other, low, high)
        scores = jnp.where(allowed, mm_t(q, k) * factor, MASKED)
        probs = jnp.exp(scores - lse_ref[0, :, h : h + 1])
        grad_probs = mm_t(ga, v)
        inner = jnp.sum(probs * grad_probs, axis=-1, keepdims=True)
        grad_scores = (probs * (grad_probs - inner)).astype(BF16)
        put(out_own, out_other, low, high, (mm(grad_scores, k) * factor).astype(BF16))
        put(
            out_own,
            out_other,
            span + low,
            span + high,
            (t_mm(grad_scores, q) * factor).astype(BF16),
        )
        put(
            out_own,
            out_other,
            2 * span + low,
            2 * span + high,
            t_mm(probs.astype(BF16), ga).astype(BF16),
        )


def attend_back(where, own, other, lse, ga_own, ga_other, heads):
    chips, count, rows, _ = own.shape
    length = 2 * chips * rows
    span = heads * HEAD
    places, of = attend_specs(chips, count, rows, length)
    return pl.pallas_call(
        functools.partial(attend_back_kernel, heads=heads, factor=HEAD ** (-0.5)),
        out_shape=(jax.ShapeDtypeStruct((chips, count, rows, 3 * span), BF16),) * 2,
        grid=(count,),
        in_specs=places
        + [of(3 * span), of(3 * span)]
        + [pl.BlockSpec((1, length, heads), lambda s: (s, 0, 0)), of(span), of(span)],
        out_specs=(of(3 * span), of(3 * span)),
        cost_estimate=pl.CostEstimate(
            flops=count * heads * length * length * HEAD * 10,
            bytes_accessed=count * length * heads * HEAD * 14,
            transcendentals=count * heads * length * length,
        ),
        name="attend_back",
    )(*where, own, other, lse, ga_own, ga_other)


def on_device(
    inputs,
    ln1_gain,
    ln1_bias,
    w_query,
    b_query,
    w_key,
    w_value,
    b_value,
    w_out,
    b_out,
    ln2_gain,
    ln2_bias,
    w_up,
    b_up,
    w_down,
    b_down,
    in_query,
    out_query,
    in_key,
    out_key,
    in_value,
    out_value,
    in_attn,
    out_attn,
    in_expand,
    out_expand,
    in_reduce,
    out_reduce,
    adapter_pick,
    piece_start,
    cotangent,
):
    count, rows, wide = inputs.shape[1:]
    size = lax.axis_size("shard")
    chips = size // 2
    bits = bits_of(size)[1:]
    me = lax.axis_index("shard").astype(jnp.int32)
    me_arr = me[None]
    part = lax.axis_index("rep").astype(jnp.int32) & 1
    at = jnp.stack([me, part])
    heads = HEADS // size
    span = heads * HEAD
    slice_wide = wide // size
    ff_part = w_up.shape[1] // size
    rank = in_query.shape[1]
    block = count * rows
    chosen = adapter_pick[0]
    starts = piece_start[0]

    def keep_own(value):
        of_row = lax.broadcasted_iota(jnp.int32, value.shape, 0) // rows % count
        of_col = lax.broadcasted_iota(jnp.int32, value.shape, 1) // rank % count
        return jnp.where(of_row == of_col, value, 0.0).astype(BF16)

    chip = me // 2

    def exchange(pieces):
        return [pieces[0]] + [swap(p, "shard", 2 * i) for i, p in enumerate(pieces) if i]

    def with_halves(pieces):
        near = jnp.concatenate(pieces[1:], 0)
        return [pieces[0], near, swap(near, "rep", 1)]

    def both_cores(own):
        return list(own) + [swap(piece, "shard", 1) for piece in own]

    w_out_other = swap(w_out, "shard", 1)
    w_down_other = swap(w_down, "shard", 1)
    pieces_qkv = cut_pieces(at, [w_query, w_key, w_value], span, chips, True)
    turned = exchange(pieces_qkv)
    near_up = exchange(cut_pieces(at, [after(w_up, *pieces_qkv)], ff_part, chips, True))

    narrow = [out_query, out_key, out_value, in_attn, out_expand, in_reduce]
    edges = np.cumsum([0] + [n.shape[2] for n in narrow])
    mine, packed = pick_maps(
        after(chosen, w_out_other, w_down_other, *pieces_qkv),
        [in_query, in_key, in_value, in_expand, out_attn, out_reduce],
        narrow,
    )
    packed_other = swap(packed, "shard", 1)
    order = bits + [1]
    near_one = swap(mine[None], "shard", bits[0])

    rows_in = after(inputs[0].reshape(block, wide), mine)
    features = rows_in.astype(F32)
    normed = layer_norm(features, ln1_gain.astype(F32), ln1_bias.astype(F32)).astype(BF16)
    vectors = after(jnp.stack([b_out, ln2_gain, ln2_bias, ln1_gain]), normed).astype(F32)
    hidden_block = after(normed, packed_other, near_one, *turned[1:], *near_up[1:])
    starts, b_query, b_value, b_up, me_late, chosen, packed = after(
        (starts, b_query, b_value, b_up, me, chosen, packed), hidden_block
    )
    hidden_one, one_first, one_last = gather_rows(hidden_block, bits)

    halves_qkv = after(tuple(with_halves(turned)), *one_first)
    w_qkv_mine, w_qkv_other = place_weights(at, both_cores(halves_qkv), chips, 3 * span, False)
    w_out_late, w_down_late, *near_up = after((w_out, w_down, *near_up), hidden_block)
    merged_up = jnp.concatenate(near_up[1:], 0)
    w_out_chip = jnp.concatenate([w_out_late, w_out_other], 0)
    w_down_chip = jnp.concatenate([w_down_late, w_down_other], 0)
    hidden_one = after(hidden_one, merged_up, w_out_chip, w_down_chip)
    cot_mine = cotangent[0].reshape(block, wide)
    near = after(jnp.concatenate([mine[None], near_one], 0), hidden_block)
    for bit in bits[1:]:
        near = jnp.concatenate([near, swap(near, "shard", bit)], 0)
    stacked = jnp.concatenate([near, swap(near, "shard", 1)], 0)

    owners = np.concatenate([np.arange(chips) * 2, np.arange(chips) * 2 + 1]).astype(np.int32)
    locs = np.tile(np.arange(rows, dtype=np.int32), 2 * chips)
    positions = (me_late ^ jnp.asarray(np.repeat(owners, rows))) * rows + jnp.asarray(locs)
    labels = jnp.stack([piece_labels(starts[s], positions) for s in range(count)])
    where = (positions[:, None], positions[None, :], labels[:, :, None], labels[:, None, :])

    whole = place_columns(me_arr, stacked, subsets(order)).reshape(6, count, rank, wide)
    in_qkv = whole[:3].reshape(3 * count * rank, wide)
    in_exp, out_att, out_red = (whole[3 + i].reshape(count * rank, wide) for i in range(3))

    def unpack(table, i):
        return table[:, edges[i] : edges[i + 1]]

    def out_qkv_of(table):
        stacked = jnp.stack([unpack(table, t) for t in range(3)])
        spread = stacked[:, :, None, :] * jnp.eye(3, dtype=BF16)[:, None, :, None]
        return spread.reshape(count * 3 * rank, 3 * span)

    out_qkv_mine, out_qkv_other = out_qkv_of(packed), out_qkv_of(packed_other)
    in_att, out_exp, in_red = (
        jnp.concatenate([unpack(packed, i), unpack(packed_other, i)], 1) for i in (3, 4, 5)
    )

    def slice_of(bias, index, width):
        return lax.dynamic_slice_in_dim(bias, index * width, width).astype(F32)

    def b_qkv_of(index):
        return jnp.concatenate(
            [slice_of(b_query, index, span), jnp.zeros((span,), F32), slice_of(b_value, index, span)]
        )

    b_up_chip = jnp.concatenate([slice_of(b_up, me, ff_part), slice_of(b_up, me ^ 1, ff_part)])

    def by_chip(value):
        return value.reshape((chips, count, rows) + value.shape[1:])

    def flat(value):
        return value.reshape(chips * block, value.shape[-1])

    def block_products(products, low, table):
        parts = {}
        for i in reversed(range(chips)):
            at = slice(i * block, (i + 1) * block)
            total = mm(low[at], table)
            for value, weight, main in products:
                total = total + main(value[at], weight)
            parts[2 * i] = total.astype(BF16)
            if i == chips - 1:
                low = after(low, parts[2 * i])
                products = [(after(v, parts[2 * i]), w, main) for v, w, main in products]
        return parts

    low_qkv = keep_own(mm_t(hidden_one, in_qkv))
    qkv_away = (
        mm(hidden_one, w_qkv_other) + mm(low_qkv, out_qkv_other) + b_qkv_of(me ^ 1)
    ).astype(BF16)
    qkv_other = by_chip(swap(qkv_away, "shard", 1))
    qkv_own = by_chip(
        (mm(hidden_one, w_qkv_mine) + mm(low_qkv, out_qkv_mine) + b_qkv_of(me)).astype(BF16)
    )
    att_own, att_away, lse = attend(where, qkv_own, qkv_other, heads)
    halves_up = [near_up[0], merged_up, swap(after(merged_up, att_own), "rep", 1)]
    cot_pieces, _, _ = gather_rows(after(cot_mine, att_own), bits, apart=True)
    attended = jnp.concatenate([flat(att_own), swap(flat(att_away), "shard", 1)], 1)
    low_att = keep_own(mm_t(attended, in_att))
    parts = block_products([(attended, w_out_chip, mm)], low_att, out_att)
    terms, relayed = scatter_rows(parts, bits)
    cot = jnp.concatenate(after(cot_pieces, *relayed), 0)
    glow_red = keep_own(mm_t(cot, out_red))
    grad_act = (mm_t(cot, w_down_chip) + mm(glow_red, in_red)).astype(BF16)
    terms[0] = after(terms[0], grad_act)
    residual, hidden_block = row_call(
        norm_kernel, [rows_in, vectors] + terms, block, wide, [F32, BF16], "norm"
    )
    pieces_up = after(tuple(halves_up), hidden_block)
    two_pieces, _, _ = gather_rows(hidden_block, bits, apart=True)

    (w_up_chip,) = place_weights(at, both_cores(pieces_up), chips, ff_part, True)
    two_pieces[-2:] = after(tuple(two_pieces[-2:]), w_up_chip)
    hidden_two = jnp.concatenate(two_pieces, 0)
    low_exp = keep_own(mm_t(hidden_two, in_exp))
    pre = mm(hidden_two, w_up_chip) + mm(low_exp, out_exp) + b_up_chip
    share = 0.5 * (1.0 + lax.erf(pre * np.float32(0.5**0.5)))
    act = (pre * share).astype(BF16)
    slope = share + pre * (jnp.exp(-0.5 * pre * pre) * np.float32((2 * np.pi) ** -0.5))
    grad_pre = (slope * grad_act.astype(F32)).astype(BF16)
    glow_exp = keep_own(mm_t(grad_pre, out_exp))
    parts = block_products([(grad_pre, w_up_chip, mm_t)], glow_exp, in_exp)
    far = 2 * (chips - 1)

    def halves(value):
        middle = value.shape[1] // 2
        return value[:, :middle], value[:, middle:]

    act_mid, grad_mid, low_mid, glow_mid = after((act, grad_pre, low_exp, glow_red), parts[far])
    red_own, red_away = halves(t_mm(glow_mid, act_mid))
    exp_own, exp_away = halves(t_mm(low_mid, grad_mid))
    terms, _ = scatter_rows(parts, bits, (parts[0], red_own, exp_own))
    grad_residual, grad_block = row_call(
        functools.partial(norm_back_kernel, outs=2, row=1),
        [residual, vectors, cot_mine] + terms,
        block,
        wide,
        [F32, BF16],
        "norm_back",
    )
    grad_branch, branch_first, branch_last = gather_rows(grad_block, bits)

    act_late = after(act, grad_block)
    low_red = keep_own(mm_t(act_late, in_red))
    down = (mm(act_late, w_down_chip) + mm(low_red, out_red)).astype(BF16)
    down_parts = {2 * i: down[i * block : (i + 1) * block] for i in range(chips)}
    glow_att = keep_own(mm_t(grad_branch, out_att))
    grad_att = (mm_t(grad_branch, w_out_chip) + mm(glow_att, in_att)).astype(BF16)
    ga_own = by_chip(grad_att[:, :span])
    ga_other = by_chip(swap(grad_att[:, span:], "shard", 1))
    grad_own, grad_away = attend_back(where, qkv_own, qkv_other, lse, ga_own, ga_other, heads)
    grad_own = flat(grad_own)
    grad_other = swap(flat(grad_away), "shard", 1)
    glow_qkv = keep_own(mm_t(grad_own, out_qkv_mine) + mm_t(grad_other, out_qkv_other))
    def sum_cores(own, away):
        return own + swap(away.astype(BF16), "shard", 1).astype(F32)

    def core_columns(value):
        width = value.shape[1] // size

        def side(which):
            return jnp.stack(
                [
                    lax.dynamic_slice_in_dim(value, (2 * k + which) * width, width, 1)
                    for k in range(chips)
                ]
            )

        core = me & 1
        return sum_cores(side(core), side(1 - core))

    def split_chips(current, bit):
        current = current.reshape((2, current.shape[0] // 2) + current.shape[1:])
        own = (me // bit) & 1
        away = lax.dynamic_index_in_dim(current, 1 - own, 0, False).astype(BF16)
        return lax.dynamic_index_in_dim(current, own, 0, False), away

    def sum_chips(current, *gate):
        for i, bit in enumerate(bits[::-1]):
            current, away = split_chips(current, bit)
            there = swap(away, "shard", bit)
            current = current + (there if i else after(there, *gate)).astype(F32)
        return current[0], away

    rep_bits = bits_of(lax.axis_size("rep"))

    def over_rep(terms, extra=(), gates=None):
        current = jnp.concatenate([t.astype(BF16) for t in terms], 1)
        current = jnp.concatenate([current, *extra], 0)[None]
        gathered = [current]
        for bit in rep_bits:
            there = swap(current, "rep", bit)
            if gates and bit in gates:
                there = after(there, *gates[bit])
            gathered.append(there)
            if bit != rep_bits[-1]:
                current = jnp.concatenate([current, there], 0)
        return gathered

    def over_groups(terms, place, gathered):
        widths = [t.shape[1] for t in terms]
        outs = sum_blocks(place, gathered, count * rank, widths)
        return [out.reshape(ADAPTERS, rank, -1) for out in outs]

    local = sum_cores(
        jnp.concatenate([red_own, exp_own], 1), jnp.concatenate([red_away, exp_away], 1)
    )
    glow_late, low_late = after((glow_exp, low_red), *branch_first)
    near_first = core_columns(
        jnp.concatenate([t_mm(glow_late, hidden_two), t_mm(low_late, cot)], 0)
    ).astype(BF16)
    tall = near_first.shape[1]
    riders = {}
    for i in range(chips):
        rider = lax.dynamic_index_in_dim(near_first, chip ^ i, 0, False)
        rider = jnp.pad(rider, ((0, block - tall), (0, 0)))
        riders[2 * i] = after(jnp.concatenate([down_parts[2 * i], rider], 1), branch_last)
    att_side = sum_cores(*halves(t_mm(glow_att, attended)))

    glow_last = glow_qkv
    in_terms = jnp.concatenate([t_mm(glow_last, hidden_one), t_mm(low_att, grad_branch)], 0)

    def own_terms(full):
        height = count * rank
        return jnp.concatenate(
            [full[t * height : (t + 1) * height, t * span : (t + 1) * span] for t in range(3)], 1
        )

    near_second = core_columns(in_terms)
    products = [(grad_own, w_qkv_mine, mm_t), (grad_other, w_qkv_other, mm_t)]
    parts = block_products(products, after(glow_qkv, in_terms), in_qkv)
    far_part = parts[2 * (chips - 1)]
    mark = (chosen[:, None] == jnp.arange(ADAPTERS, dtype=jnp.int32)[None, :]).astype(BF16)
    mark = jnp.pad(mark, ((0, 16 - count), (0, local.shape[1] - ADAPTERS)))
    sums = [local[:, :ff_part], local[:, ff_part:]]
    gathered = over_rep(sums, [mark], {rep_bits[-1]: (far_part,)})
    marks = jnp.concatenate(
        [g[:, count * rank : count * rank + count, :ADAPTERS] for g in gathered], 0
    )
    place = marks.reshape(-1, 1, ADAPTERS, 1) * jnp.eye(rank, dtype=BF16)[None, :, None, :]
    place = place.reshape(-1, ADAPTERS * rank)
    s_in_red, s_out_exp = over_groups(sums, place, gathered)

    own_last, other_last = after((grad_own, grad_other), far_part)
    outer_own = own_terms(t_mm(low_qkv, own_last))
    outer_away = own_terms(t_mm(low_qkv, other_last))
    aside = {}

    def hop(relayed):
        aside["second"], sent = sum_chips(after(near_second, far_part), *relayed)
        return sent

    terms, relayed = scatter_rows(parts, bits, (parts[0], outer_own, outer_away), hop)
    outer = sum_cores(outer_own, after(outer_away, *relayed))
    second = aside["second"]
    down, _ = scatter_rows(riders, bits, (grad_away,))
    down[0] = after(down[0], *relayed)
    first = sum(t[:tall, wide:].astype(F32) for t in down).reshape(2, count * rank, slice_wide)
    layer_rows = residual + b_down.astype(F32) + sum(t[:, :wide].astype(F32) for t in down)

    (input_rows,) = row_call(
        functools.partial(norm_back_kernel, outs=1, row=3),
        [rows_in, vectors, grad_residual] + terms,
        block,
        wide,
        [BF16],
        "norm_back",
    )
    out_att_sum = second[count * 3 * rank :]
    second = second[: count * 3 * rank].reshape(3, count * rank, slice_wide)
    sums = [att_side, first[0], first[1]]
    ends = {rep_bits[-1]: (input_rows,)}
    s_in_att, s_in_exp, s_out_red = over_groups(sums, place, over_rep(sums, (), ends))
    sums = [second[t] for t in range(3)]
    sums += [outer[:, t * span : (t + 1) * span] for t in range(3)] + [out_att_sum]
    late = over_groups(sums, place, over_rep(sums, (), ends))
    s_out_att = late.pop()
    shape = (1, count, rows, wide)
    return (
        layer_rows.astype(BF16).reshape(shape),
        input_rows.reshape(shape),
        late[0],
        late[3],
        late[1],
        late[4],
        late[2],
        late[5],
        s_in_att,
        s_out_att,
        s_in_exp,
        s_out_exp,
        s_in_red,
        s_out_red,
    )


def solution(mesh):
    row = P("shard", None)
    wide = P(None, None, "shard")
    acts = P("rep", None, "shard", None)
    in_specs = (
        (acts, P(), P(), row, P(), row, row, P(), row, P(), P(), P(), row, P(), row, P())
        + (wide,) * 12
        + (P("rep", None), P("rep", None, None), acts)
    )
    out_specs = (acts, acts) + (wide,) * 12
    return jax.shard_map(
        on_device, mesh=mesh, in_specs=in_specs, out_specs=out_specs, check_vma=False
    )
```

```python
import functools

import jax
import jax.numpy as jnp
import numpy as np
from jax import lax
from jax.experimental import pallas as pl
from jax.experimental.pallas import tpu as pltpu
from jax.sharding import PartitionSpec as P

HEADS = 16
HEAD = 128
ADAPTERS = 8
PIECE = 256

EPSILON = 1e-05
MASKED = -1e30
F32 = jnp.float32
BF16 = jnp.bfloat16


def layer_norm(values, gain_vec, shift_vec):
    centre = jnp.mean(values, axis=-1, keepdims=True)
    offset = values - centre
    spread = jnp.mean(offset * offset, axis=-1, keepdims=True)
    return offset * lax.rsqrt(spread + EPSILON) * gain_vec + shift_vec


def piece_labels(starts, positions):
    inside = (positions[:, None] >= starts[None, :]) & (
        positions[:, None] < starts[None, :] + PIECE
    )
    labels = jnp.arange(1, starts.shape[0] + 1, dtype=jnp.int32)
    return jnp.sum(jnp.where(inside, labels[None, :], 0), axis=1)


def mm(a, b):
    return lax.dot_general(a, b, (((1,), (0,)), ((), ())), preferred_element_type=F32)


def mm_t(a, b):
    return lax.dot_general(a, b, (((1,), (1,)), ((), ())), preferred_element_type=F32)


def t_mm(a, b):
    return lax.dot_general(a, b, (((0,), (0,)), ((), ())), preferred_element_type=F32)


def swap(value, axis, mask):
    size = lax.axis_size(axis)
    return lax.ppermute(value, axis, [(i, i ^ mask) for i in range(size)])


def after(value, *others):
    return lax.optimization_barrier((value,) + others)[0]


def bits_of(size):
    bits = []
    while (1 << len(bits)) < size:
        bits.append(1 << len(bits))
    return bits


def subsets(bits):
    masks = [0]
    for bit in bits:
        masks = masks + [m | bit for m in masks]
    return masks


def gather_rows(block, bits, gate=(), apart=False):
    half = block.shape[0] // 2
    got = {0: [block]}
    upper, lower = {}, {}
    for bit in bits:
        there = swap(block, "shard", bit)
        there = after(there, *gate) if gate else there
        got[bit] = [there]
        upper[bit], lower[bit] = there[:half], there[half:]
    for which, order in ((upper, bits), (lower, bits[::-1])):
        for k, bit in enumerate(order):
            for sub in subsets(order[:k])[1:]:
                which[sub | bit] = swap(which[sub], "shard", bit)
    pieces = []
    for mask in subsets(bits):
        pieces += got[mask] if mask in got else [upper[mask], lower[mask]]
    firsts = [got[bit][0] for bit in bits]
    if apart:
        return pieces, firsts, pieces[-1]
    return jnp.concatenate(pieces, 0), firsts, pieces[-1]


def scatter_rows(parts, bits, gate=(), between=None):
    half = parts[0].shape[0] // 2
    upper = {m: p[:half] for m, p in parts.items()}
    lower = {m: p[half:] for m, p in parts.items()}
    for which, order in ((upper, bits), (lower, bits[::-1])):
        for k in reversed(range(len(order))):
            for sub in subsets(order[:k])[1:]:
                other = swap(which[sub | order[k]], "shard", order[k])
                other = after(other, *gate) if gate else other
                which[sub] = (which[sub].astype(F32) + other.astype(F32)).astype(BF16)
    blocks = [jnp.concatenate([upper[bit], lower[bit]], 0) for bit in bits]
    if between:
        blocks = list(after(tuple(blocks), between(blocks)))
    return [parts[0]] + [swap(b, "shard", bit) for b, bit in zip(blocks, bits)], blocks


def gather_blocks(value, axis, bits, gates=None):
    current = value[None]
    for bit in bits:
        there = swap(current, axis, bit)
        if gates and bit in gates:
            there = after(there, *gates[bit])
        current = jnp.concatenate([current, there], 0)
    return current


def run_copies(copies):
    for copy in copies:
        copy.start()
    for copy in copies:
        copy.wait()


def cut_kernel(at_ref, *refs, count, terms, width):
    tables, outs, sems = refs[:terms], refs[terms:-1], refs[-1]
    me, part = at_ref[0], at_ref[1]
    copies = []
    for i in range(count):
        rows = outs[i].shape[0]
        first = pl.multiple_of(part * rows, rows) if rows < tables[0].shape[0] else 0
        for k in range(2):
            column = pl.multiple_of((((me // 2) ^ i) * 2 + k) * width, width)
            for t in range(terms):
                copies.append(
                    pltpu.make_async_copy(
                        tables[t].at[pl.ds(first, rows), pl.ds(column, width)],
                        outs[i].at[:, pl.ds((k * terms + t) * width, width)],
                        sems.at[len(copies)],
                    )
                )
    run_copies(copies)


def cut_pieces(at, tables, width, count, split):
    rows, terms = tables[0].shape[0], len(tables)
    shapes = [
        jax.ShapeDtypeStruct((rows // 2 if i and split else rows, 2 * terms * width), BF16)
        for i in range(count)
    ]
    return pl.pallas_call(
        functools.partial(cut_kernel, count=count, terms=terms, width=width),
        out_shape=shapes,
        in_specs=[pl.BlockSpec(memory_space=pltpu.SMEM)]
        + [pl.BlockSpec(memory_space=pl.ANY)] * terms,
        out_specs=[pl.BlockSpec(memory_space=pltpu.VMEM)] * count,
        scratch_shapes=[pltpu.SemaphoreType.DMA((2 * terms * count,))],
        cost_estimate=pl.CostEstimate(
            flops=0, bytes_accessed=4 * rows * count * terms * width, transcendentals=0
        ),
        name="cut_pieces",
    )(at, *tables)


def place_kernel(at_ref, *refs, count, width, rows, joined):
    pieces, outs, sems = refs[:6], refs[6:-1], refs[-1]
    me, part = at_ref[0], at_ref[1]
    half = rows // 2

    def copies(core):
        made = []
        for side in range(2):
            parts = [(pieces[3 * side], 0, rows, 0, 0)]
            for second in range(2):
                parts += [
                    (pieces[3 * side + 1 + second], (i - 1) * half, half, i, part ^ second)
                    for i in range(1, count)
                ]
            for piece, first, height, i, which in parts:
                row = pl.multiple_of((me ^ (2 * i) ^ side) * rows + which * half, half)
                for k in range(2):
                    own = k ^ core
                    source = piece.at[pl.ds(first, height), pl.ds(k * width, width)]
                    if joined:
                        target = outs[0].at[pl.ds(row, height), pl.ds(own * width, width)]
                    else:
                        target = outs[own].at[pl.ds(row, height)]
                    made.append(pltpu.make_async_copy(source, target, sems.at[len(made)]))
        return made

    @pl.when((me & 1) == 0)
    def _():
        run_copies(copies(0))

    @pl.when((me & 1) == 1)
    def _():
        run_copies(copies(1))


def place_weights(at, pieces, count, width, joined):
    rows = pieces[0].shape[0]
    if joined:
        shapes = [jax.ShapeDtypeStruct((rows * count * 2, 2 * width), BF16)]
    else:
        shapes = [jax.ShapeDtypeStruct((rows * count * 2, width), BF16)] * 2
    return pl.pallas_call(
        functools.partial(place_kernel, count=count, width=width, rows=rows, joined=joined),
        out_shape=shapes,
        in_specs=[pl.BlockSpec(memory_space=pltpu.SMEM)]
        + [pl.BlockSpec(memory_space=pl.ANY)] * len(pieces),
        out_specs=[pl.BlockSpec(memory_space=pltpu.VMEM)] * len(shapes),
        scratch_shapes=[pltpu.SemaphoreType.DMA((8 * count - 4,))],
        cost_estimate=pl.CostEstimate(
            flops=0, bytes_accessed=16 * rows * count * width, transcendentals=0
        ),
        name="place_weights",
    )(at, *pieces)


def pick_kernel(chosen_ref, *refs, tall, rank):
    tables, (tall_ref, flat_ref, sems) = refs[:-3], refs[-3:]
    count = chosen_ref.shape[0]
    copies = []
    for s in range(count):
        column = 0
        for i, table in enumerate(tables):
            if i < tall:
                target = tall_ref.at[pl.ds((i * count + s) * rank, rank)]
            else:
                width = table.shape[2]
                target = flat_ref.at[pl.ds(s * rank, rank), pl.ds(column, width)]
                column += width
            copies.append(
                pltpu.make_async_copy(table.at[chosen_ref[s]], target, sems.at[len(copies)])
            )
    run_copies(copies)


def pick_maps(chosen, upright, flat):
    count, rank = chosen.shape[0], upright[0].shape[1]
    total = sum(t.shape[2] for t in flat)
    shapes = (
        jax.ShapeDtypeStruct((len(upright) * count * rank, upright[0].shape[2]), BF16),
        jax.ShapeDtypeStruct((count * rank, total), BF16),
    )
    tables = upright + flat
    return pl.pallas_call(
        functools.partial(pick_kernel, tall=len(upright), rank=rank),
        out_shape=shapes,
        in_specs=[pl.BlockSpec(memory_space=pltpu.SMEM)]
        + [pl.BlockSpec(memory_space=pl.ANY)] * len(tables),
        out_specs=[pl.BlockSpec(memory_space=pltpu.VMEM)] * 2,
        scratch_shapes=[pltpu.SemaphoreType.DMA((count * len(tables),))],
        cost_estimate=pl.CostEstimate(
            flops=0, bytes_accessed=8 * count * rank * total, transcendentals=0
        ),
        name="pick_maps",
    )(chosen, *tables)


def cols_kernel(me_ref, in_ref, out_ref, sems, *, masks):
    width = in_ref.shape[2]
    run_copies(
        [
            pltpu.make_async_copy(
                in_ref.at[i],
                out_ref.at[:, pl.ds(pl.multiple_of((me_ref[0] ^ mask) * width, width), width)],
                sems.at[i],
            )
            for i, mask in enumerate(masks)
        ]
    )


def place_columns(me, stacked, masks):
    count, rows, width = stacked.shape
    return pl.pallas_call(
        functools.partial(cols_kernel, masks=masks),
        out_shape=jax.ShapeDtypeStruct((rows, count * width), stacked.dtype),
        in_specs=[pl.BlockSpec(memory_space=pltpu.SMEM), pl.BlockSpec(memory_space=pltpu.VMEM)],
        out_specs=pl.BlockSpec(memory_space=pltpu.VMEM),
        scratch_shapes=[pltpu.SemaphoreType.DMA((count,))],
        cost_estimate=pl.CostEstimate(
            flops=0, bytes_accessed=4 * count * rows * width, transcendentals=0
        ),
        name="place_columns",
    )(me, stacked)


def normalised(values):
    centre = jnp.mean(values, axis=-1, keepdims=True)
    offset = values - centre
    scale = lax.rsqrt(jnp.mean(offset * offset, axis=-1, keepdims=True) + EPSILON)
    return offset * scale, scale


def total_of(refs, at):
    total = refs[0][at].astype(F32)
    for ref in refs[1:]:
        total = total + ref[at].astype(F32)
    return total


def tiles_of(rows):
    tile = 32 if rows % 32 == 0 else rows
    return [slice(i, i + tile) for i in range(0, rows, tile)]


def norm_kernel(base, vectors, *refs):
    terms, (res_ref, out_ref) = refs[:-2], refs[-2:]
    shift, gain, bias = vectors[0:1], vectors[1:2], vectors[2:3]
    for at in tiles_of(base.shape[0]):
        values = base[at].astype(F32) + (total_of(terms, at) + shift)
        res_ref[at] = values
        unit, _ = normalised(values)
        out_ref[at] = (unit * gain + bias).astype(BF16)


def norm_back_kernel(values, vectors, base, *refs, outs, row):
    gain = vectors[row : row + 1]
    terms, outputs = refs[: len(refs) - outs], refs[len(refs) - outs :]
    for at in tiles_of(values.shape[0]):
        unit, scale = normalised(values[at].astype(F32))
        grad = total_of(terms, at) * gain
        mean_one = jnp.mean(grad, axis=-1, keepdims=True)
        mean_two = jnp.mean(grad * unit, axis=-1, keepdims=True)
        total = base[at].astype(F32) + scale * (grad - mean_one - unit * mean_two)
        for out in outputs:
            out[at] = total.astype(out.dtype)


def row_call(kernel, order, rows, wide, dtypes, name):
    return pl.pallas_call(
        kernel,
        out_shape=[jax.ShapeDtypeStruct((rows, wide), d) for d in dtypes],
        in_specs=[pl.BlockSpec(memory_space=pltpu.VMEM)] * len(order),
        out_specs=[pl.BlockSpec(memory_space=pltpu.VMEM)] * len(dtypes),
        cost_estimate=pl.CostEstimate(
            flops=20 * rows * wide, bytes_accessed=200 * rows * wide, transcendentals=0
        ),
        name=name,
    )(*order)


def sum_kernel(place, *refs, blocks, rows):
    gathered, outs = refs[:blocks], refs[blocks:]
    start = 0
    for out in outs:
        width = out.shape[1]
        total, row = None, 0
        for ref in gathered:
            for g in range(ref.shape[0]):
                term = t_mm(place[row : row + rows], ref[g, :rows, start : start + width])
                total = term if total is None else total + term
                row += rows
        out[...] = total
        start += width


def sum_blocks(place, gathered, rows, widths):
    total = sum(widths)
    return pl.pallas_call(
        functools.partial(sum_kernel, blocks=len(gathered), rows=rows),
        out_shape=[jax.ShapeDtypeStruct((place.shape[1], w), F32) for w in widths],
        in_specs=[pl.BlockSpec(memory_space=pltpu.VMEM)] * (1 + len(gathered)),
        out_specs=[pl.BlockSpec(memory_space=pltpu.VMEM)] * len(widths),
        cost_estimate=pl.CostEstimate(
            flops=2 * place.size * total, bytes_accessed=(2 * place.shape[0] + 4 * place.shape[1]) * total, transcendentals=0
        ),
        name="sum_blocks",
    )(place, *gathered)


def seen(pos_q, pos_k, lab_q, lab_k):
    return (pos_k <= pos_q) | ((lab_q == lab_k) & (lab_q > 0))


def both(own_ref, other_ref, low, high):
    own, other = own_ref[:, 0, :, low:high], other_ref[:, 0, :, low:high]
    chips, rows, width = own.shape
    return jnp.concatenate([own.reshape(chips * rows, width), other.reshape(chips * rows, width)], 0)


def put(own_ref, other_ref, low, high, value):
    chips, _, rows, _ = own_ref.shape
    half = chips * rows
    own_ref[:, 0, :, low:high] = value[:half].reshape(chips, rows, high - low)
    other_ref[:, 0, :, low:high] = value[half:].reshape(chips, rows, high - low)


def attend_kernel(pq, pk, lq, lk, own, other, out_own, out_other, lse_ref, *, heads, factor):
    allowed = seen(pq[...], pk[...], lq[0], lk[0])
    span = heads * HEAD
    for h in range(heads):
        low, high = h * HEAD, (h + 1) * HEAD
        q = both(own, other, low, high)
        k = both(own, other, span + low, span + high)
        v = both(own, other, 2 * span + low, 2 * span + high)
        scores = jnp.where(allowed, mm_t(q, k) * factor, MASKED)
        top = jnp.max(scores, axis=-1, keepdims=True)
        expo = jnp.exp(scores - top)
        total = jnp.sum(expo, axis=-1, keepdims=True)
        probs = (expo * (1.0 / total)).astype(BF16)
        put(out_own, out_other, low, high, mm(probs, v).astype(BF16))
        lse_ref[0, :, h : h + 1] = top + jnp.log(total)


def attend_specs(chips, count, rows, length):
    whole = pl.BlockSpec(memory_space=pltpu.VMEM)
    where = [
        pl.BlockSpec((length, 1), lambda s: (0, 0)),
        pl.BlockSpec((1, length), lambda s: (0, 0)),
        pl.BlockSpec((1, length, 1), lambda s: (s, 0, 0)),
        pl.BlockSpec((1, 1, length), lambda s: (s, 0, 0)),
    ]

    def of(width):
        return pl.BlockSpec((chips, 1, rows, width), lambda s: (0, s, 0, 0))

    return where, of


def attend(where, own, other, heads):
    chips, count, rows, _ = own.shape
    length = 2 * chips * rows
    span = heads * HEAD
    places, of = attend_specs(chips, count, rows, length)
    return pl.pallas_call(
        functools.partial(attend_kernel, heads=heads, factor=HEAD ** (-0.5)),
        out_shape=(
            jax.ShapeDtypeStruct((chips, count, rows, span), BF16),
            jax.ShapeDtypeStruct((chips, count, rows, span), BF16),
            jax.ShapeDtypeStruct((count, length, heads), F32),
        ),
        grid=(count,),
        in_specs=places + [of(3 * span), of(3 * span)],
        out_specs=(of(span), of(span), pl.BlockSpec((1, length, heads), lambda s: (s, 0, 0))),
        cost_estimate=pl.CostEstimate(
            flops=count * heads * length * length * HEAD * 4,
            bytes_accessed=count * length * heads * HEAD * 8,
            transcendentals=count * heads * length * length,
        ),
        name="attend",
    )(*where, own, other)


def attend_back_kernel(
    pq, pk, lq, lk, own, other, lse_ref, ga_own, ga_other, out_own, out_other, *, heads, factor
):
    allowed = seen(pq[...], pk[...], lq[0], lk[0])
    span = heads * HEAD
    for h in range(heads):
        low, high = h * HEAD, (h + 1) * HEAD
        q = both(own, other, low, high)
        k = both(own, other, span + low, span + high)
        v = both(own, other, 2 * span + low, 2 * span + high)
        ga = both(ga_own, ga_other, low, high)
        scores = jnp.where(allowed, mm_t(q, k) * factor, MASKED)
        probs = jnp.exp(scores - lse_ref[0, :, h : h + 1])
        grad_probs = mm_t(ga, v)
        inner = jnp.sum(probs * grad_probs, axis=-1, keepdims=True)
        grad_scores = (probs * (grad_probs - inner)).astype(BF16)
        put(out_own, out_other, low, high, (mm(grad_scores, k) * factor).astype(BF16))
        put(
            out_own,
            out_other,
            span + low,
            span + high,
            (t_mm(grad_scores, q) * factor).astype(BF16),
        )
        put(
            out_own,
            out_other,
            2 * span + low,
            2 * span + high,
            t_mm(probs.astype(BF16), ga).astype(BF16),
        )


def attend_back(where, own, other, lse, ga_own, ga_other, heads):
    chips, count, rows, _ = own.shape
    length = 2 * chips * rows
    span = heads * HEAD
    places, of = attend_specs(chips, count, rows, length)
    return pl.pallas_call(
        functools.partial(attend_back_kernel, heads=heads, factor=HEAD ** (-0.5)),
        out_shape=(jax.ShapeDtypeStruct((chips, count, rows, 3 * span), BF16),) * 2,
        grid=(count,),
        in_specs=places
        + [of(3 * span), of(3 * span)]
        + [pl.BlockSpec((1, length, heads), lambda s: (s, 0, 0)), of(span), of(span)],
        out_specs=(of(3 * span), of(3 * span)),
        cost_estimate=pl.CostEstimate(
            flops=count * heads * length * length * HEAD * 10,
            bytes_accessed=count * length * heads * HEAD * 14,
            transcendentals=count * heads * length * length,
        ),
        name="attend_back",
    )(*where, own, other, lse, ga_own, ga_other)


def on_device(
    inputs,
    ln1_gain,
    ln1_bias,
    w_query,
    b_query,
    w_key,
    w_value,
    b_value,
    w_out,
    b_out,
    ln2_gain,
    ln2_bias,
    w_up,
    b_up,
    w_down,
    b_down,
    in_query,
    out_query,
    in_key,
    out_key,
    in_value,
    out_value,
    in_attn,
    out_attn,
    in_expand,
    out_expand,
    in_reduce,
    out_reduce,
    adapter_pick,
    piece_start,
    cotangent,
):
    count, rows, wide = inputs.shape[1:]
    size = lax.axis_size("shard")
    chips = size // 2
    bits = bits_of(size)[1:]
    me = lax.axis_index("shard").astype(jnp.int32)
    me_arr = me[None]
    part = lax.axis_index("rep").astype(jnp.int32) & 1
    at = jnp.stack([me, part])
    heads = HEADS // size
    span = heads * HEAD
    slice_wide = wide // size
    ff_part = w_up.shape[1] // size
    rank = in_query.shape[1]
    block = count * rows
    chosen = adapter_pick[0]
    starts = piece_start[0]

    def keep_own(value):
        of_row = lax.broadcasted_iota(jnp.int32, value.shape, 0) // rows % count
        of_col = lax.broadcasted_iota(jnp.int32, value.shape, 1) // rank % count
        return jnp.where(of_row == of_col, value, 0.0).astype(BF16)

    chip = me // 2

    def exchange(pieces):
        return [pieces[0]] + [swap(p, "shard", 2 * i) for i, p in enumerate(pieces) if i]

    def with_halves(pieces):
        near = jnp.concatenate(pieces[1:], 0)
        return [pieces[0], near, swap(near, "rep", 1)]

    def both_cores(own):
        return list(own) + [swap(piece, "shard", 1) for piece in own]

    w_out_other = swap(w_out, "shard", 1)
    w_down_other = swap(w_down, "shard", 1)
    pieces_qkv = cut_pieces(at, [w_query, w_key, w_value], span, chips, True)
    turned = exchange(pieces_qkv)
    near_up = exchange(cut_pieces(at, [after(w_up, *pieces_qkv)], ff_part, chips, True))

    narrow = [out_query, out_key, out_value, in_attn, out_expand, in_reduce]
    edges = np.cumsum([0] + [n.shape[2] for n in narrow])
    mine, packed = pick_maps(
        after(chosen, w_out_other, w_down_other, *pieces_qkv),
        [in_query, in_key, in_value, in_expand, out_attn, out_reduce],
        narrow,
    )
    packed_other = swap(packed, "shard", 1)
    order = bits + [1]
    near_one = swap(mine[None], "shard", bits[0])

    rows_in = after(inputs[0].reshape(block, wide), mine)
    features = rows_in.astype(F32)
    normed = layer_norm(features, ln1_gain.astype(F32), ln1_bias.astype(F32)).astype(BF16)
    vectors = after(jnp.stack([b_out, ln2_gain, ln2_bias, ln1_gain]), normed).astype(F32)
    hidden_block = after(normed, packed_other, near_one, *turned[1:], *near_up[1:])
    starts, b_query, b_value, b_up, me_late, chosen, packed = after(
        (starts, b_query, b_value, b_up, me, chosen, packed), hidden_block
    )
    hidden_one, one_first, one_last = gather_rows(hidden_block, bits)

    halves_qkv = after(tuple(with_halves(turned)), *one_first)
    w_qkv_mine, w_qkv_other = place_weights(at, both_cores(halves_qkv), chips, 3 * span, False)
    w_out_late, w_down_late, *near_up = after((w_out, w_down, *near_up), hidden_block)
    merged_up = jnp.concatenate(near_up[1:], 0)
    w_out_chip = jnp.concatenate([w_out_late, w_out_other], 0)
    w_down_chip = jnp.concatenate([w_down_late, w_down_other], 0)
    hidden_one = after(hidden_one, merged_up, w_out_chip, w_down_chip)
    cot_mine = cotangent[0].reshape(block, wide)
    near = after(jnp.concatenate([mine[None], near_one], 0), hidden_block)
    for bit in bits[1:]:
        near = jnp.concatenate([near, swap(near, "shard", bit)], 0)
    stacked = jnp.concatenate([near, swap(near, "shard", 1)], 0)

    owners = np.concatenate([np.arange(chips) * 2, np.arange(chips) * 2 + 1]).astype(np.int32)
    locs = np.tile(np.arange(rows, dtype=np.int32), 2 * chips)
    positions = (me_late ^ jnp.asarray(np.repeat(owners, rows))) * rows + jnp.asarray(locs)
    labels = jnp.stack([piece_labels(starts[s], positions) for s in range(count)])
    where = (positions[:, None], positions[None, :], labels[:, :, None], labels[:, None, :])

    whole = place_columns(me_arr, stacked, subsets(order)).reshape(6, count, rank, wide)
    in_qkv = whole[:3].reshape(3 * count * rank, wide)
    in_exp, out_att, out_red = (whole[3 + i].reshape(count * rank, wide) for i in range(3))

    def unpack(table, i):
        return table[:, edges[i] : edges[i + 1]]

    def out_qkv_of(table):
        stacked = jnp.stack([unpack(table, t) for t in range(3)])
        spread = stacked[:, :, None, :] * jnp.eye(3, dtype=BF16)[:, None, :, None]
        return spread.reshape(count * 3 * rank, 3 * span)

    out_qkv_mine, out_qkv_other = out_qkv_of(packed), out_qkv_of(packed_other)
    in_att, out_exp, in_red = (
        jnp.concatenate([unpack(packed, i), unpack(packed_other, i)], 1) for i in (3, 4, 5)
    )

    def slice_of(bias, index, width):
        return lax.dynamic_slice_in_dim(bias, index * width, width).astype(F32)

    def b_qkv_of(index):
        return jnp.concatenate(
            [slice_of(b_query, index, span), jnp.zeros((span,), F32), slice_of(b_value, index, span)]
        )

    b_up_chip = jnp.concatenate([slice_of(b_up, me, ff_part), slice_of(b_up, me ^ 1, ff_part)])

    def by_chip(value):
        return value.reshape((chips, count, rows) + value.shape[1:])

    def flat(value):
        return value.reshape(chips * block, value.shape[-1])

    def block_products(products, low, table):
        total = mm(low, table)
        for value, weight, main in products:
            total = total + main(value, weight)
        total = total.astype(BF16)
        return {2 * i: total[i * block : (i + 1) * block] for i in range(chips)}

    low_qkv = keep_own(mm_t(hidden_one, in_qkv))
    qkv_away = (
        mm(hidden_one, w_qkv_other) + mm(low_qkv, out_qkv_other) + b_qkv_of(me ^ 1)
    ).astype(BF16)
    qkv_other = by_chip(swap(qkv_away, "shard", 1))
    qkv_own = by_chip(
        (mm(hidden_one, w_qkv_mine) + mm(low_qkv, out_qkv_mine) + b_qkv_of(me)).astype(BF16)
    )
    att_own, att_away, lse = attend(where, qkv_own, qkv_other, heads)
    halves_up = [near_up[0], merged_up, swap(after(merged_up, att_own), "rep", 1)]
    cot_pieces, _, _ = gather_rows(after(cot_mine, att_own), bits, apart=True)
    attended = jnp.concatenate([flat(att_own), swap(flat(att_away), "shard", 1)], 1)
    low_att = keep_own(mm_t(attended, in_att))
    parts = block_products([(attended, w_out_chip, mm)], low_att, out_att)
    terms, relayed = scatter_rows(parts, bits)
    cot = jnp.concatenate(after(cot_pieces, *relayed), 0)
    glow_red = keep_own(mm_t(cot, out_red))
    grad_act = (mm_t(cot, w_down_chip) + mm(glow_red, in_red)).astype(BF16)
    terms[0] = after(terms[0], grad_act)
    residual, hidden_block = row_call(
        norm_kernel, [rows_in, vectors] + terms, block, wide, [F32, BF16], "norm"
    )
    pieces_up = after(tuple(halves_up), hidden_block)
    two_pieces, _, _ = gather_rows(hidden_block, bits, apart=True)

    (w_up_chip,) = place_weights(at, both_cores(pieces_up), chips, ff_part, True)
    two_pieces[-2:] = after(tuple(two_pieces[-2:]), w_up_chip)
    hidden_two = jnp.concatenate(two_pieces, 0)
    low_exp = keep_own(mm_t(hidden_two, in_exp))
    pre = mm(hidden_two, w_up_chip) + mm(low_exp, out_exp) + b_up_chip
    share = 0.5 * (1.0 + lax.erf(pre * np.float32(0.5**0.5)))
    act = (pre * share).astype(BF16)
    slope = share + pre * (jnp.exp(-0.5 * pre * pre) * np.float32((2 * np.pi) ** -0.5))
    grad_pre = (slope * grad_act.astype(F32)).astype(BF16)
    glow_exp = keep_own(mm_t(grad_pre, out_exp))
    parts = block_products([(grad_pre, w_up_chip, mm_t)], glow_exp, in_exp)
    far = 2 * (chips - 1)

    def halves(value):
        middle = value.shape[1] // 2
        return value[:, :middle], value[:, middle:]

    act_mid, grad_mid, low_mid, glow_mid = after((act, grad_pre, low_exp, glow_red), parts[far])
    red_own, red_away = halves(t_mm(glow_mid, act_mid))
    exp_own, exp_away = halves(t_mm(low_mid, grad_mid))
    terms, _ = scatter_rows(parts, bits, (parts[0], red_own, exp_own))
    grad_residual, grad_block = row_call(
        functools.partial(norm_back_kernel, outs=2, row=1),
        [residual, vectors, cot_mine] + terms,
        block,
        wide,
        [F32, BF16],
        "norm_back",
    )
    grad_branch, branch_first, branch_last = gather_rows(grad_block, bits)

    act_late = after(act, grad_block)
    low_red = keep_own(mm_t(act_late, in_red))
    down_parts = block_products([(act_late, w_down_chip, mm)], low_red, out_red)
    glow_att = keep_own(mm_t(grad_branch, out_att))
    grad_att = (mm_t(grad_branch, w_out_chip) + mm(glow_att, in_att)).astype(BF16)
    ga_own = by_chip(grad_att[:, :span])
    ga_other = by_chip(swap(grad_att[:, span:], "shard", 1))
    grad_own, grad_away = attend_back(where, qkv_own, qkv_other, lse, ga_own, ga_other, heads)
    grad_own = flat(grad_own)
    grad_other = swap(flat(grad_away), "shard", 1)
    glow_qkv = keep_own(mm_t(grad_own, out_qkv_mine) + mm_t(grad_other, out_qkv_other))
    def sum_cores(own, away):
        return own + swap(away.astype(BF16), "shard", 1).astype(F32)

    def core_columns(value):
        width = value.shape[1] // size

        def side(which):
            return jnp.stack(
                [
                    lax.dynamic_slice_in_dim(value, (2 * k + which) * width, width, 1)
                    for k in range(chips)
                ]
            )

        core = me & 1
        return sum_cores(side(core), side(1 - core))

    def split_chips(current, bit):
        current = current.reshape((2, current.shape[0] // 2) + current.shape[1:])
        own = (me // bit) & 1
        away = lax.dynamic_index_in_dim(current, 1 - own, 0, False).astype(BF16)
        return lax.dynamic_index_in_dim(current, own, 0, False), away

    def sum_chips(current, *gate):
        for i, bit in enumerate(bits[::-1]):
            current, away = split_chips(current, bit)
            there = swap(away, "shard", bit)
            current = current + (there if i else after(there, *gate)).astype(F32)
        return current[0], away

    rep_bits = bits_of(lax.axis_size("rep"))

    def over_rep(terms, extra=(), gates=None):
        current = jnp.concatenate([t.astype(BF16) for t in terms], 1)
        current = jnp.concatenate([current, *extra], 0)[None]
        gathered = [current]
        for bit in rep_bits:
            there = swap(current, "rep", bit)
            if gates and bit in gates:
                there = after(there, *gates[bit])
            gathered.append(there)
            if bit != rep_bits[-1]:
                current = jnp.concatenate([current, there], 0)
        return gathered

    def over_groups(terms, place, gathered):
        widths = [t.shape[1] for t in terms]
        outs = sum_blocks(place, gathered, count * rank, widths)
        return [out.reshape(ADAPTERS, rank, -1) for out in outs]

    local = sum_cores(
        jnp.concatenate([red_own, exp_own], 1), jnp.concatenate([red_away, exp_away], 1)
    )
    glow_late, low_late = after((glow_exp, low_red), *branch_first)
    near_first = core_columns(
        jnp.concatenate([t_mm(glow_late, hidden_two), t_mm(low_late, cot)], 0)
    ).astype(BF16)
    tall = near_first.shape[1]
    riders = {}
    for i in range(chips):
        rider = lax.dynamic_index_in_dim(near_first, chip ^ i, 0, False)
        rider = jnp.pad(rider, ((0, block - tall), (0, 0)))
        riders[2 * i] = after(jnp.concatenate([down_parts[2 * i], rider], 1), branch_last)
    att_side = sum_cores(*halves(t_mm(glow_att, attended)))

    glow_last = glow_qkv
    in_terms = jnp.concatenate([t_mm(glow_last, hidden_one), t_mm(low_att, grad_branch)], 0)

    def own_terms(full):
        height = count * rank
        return jnp.concatenate(
            [full[t * height : (t + 1) * height, t * span : (t + 1) * span] for t in range(3)], 1
        )

    near_second = core_columns(in_terms)
    products = [(grad_own, w_qkv_mine, mm_t), (grad_other, w_qkv_other, mm_t)]
    parts = block_products(products, after(glow_qkv, in_terms), in_qkv)
    far_part = parts[2 * (chips - 1)]
    mark = (chosen[:, None] == jnp.arange(ADAPTERS, dtype=jnp.int32)[None, :]).astype(BF16)
    mark = jnp.pad(mark, ((0, 16 - count), (0, local.shape[1] - ADAPTERS)))
    sums = [local[:, :ff_part], local[:, ff_part:]]
    gathered = over_rep(sums, [mark], {rep_bits[-1]: (far_part,)})
    marks = jnp.concatenate(
        [g[:, count * rank : count * rank + count, :ADAPTERS] for g in gathered], 0
    )
    place = marks.reshape(-1, 1, ADAPTERS, 1) * jnp.eye(rank, dtype=BF16)[None, :, None, :]
    place = place.reshape(-1, ADAPTERS * rank)
    s_in_red, s_out_exp = over_groups(sums, place, gathered)

    own_last, other_last = after((grad_own, grad_other), far_part)
    outer_own = own_terms(t_mm(low_qkv, own_last))
    outer_away = own_terms(t_mm(low_qkv, other_last))
    aside = {}

    def hop(relayed):
        aside["second"], sent = sum_chips(after(near_second, far_part), *relayed)
        return sent

    terms, relayed = scatter_rows(parts, bits, (parts[0], outer_own, outer_away), hop)
    outer = sum_cores(outer_own, after(outer_away, *relayed))
    second = aside["second"]
    down, _ = scatter_rows(riders, bits, (grad_away,))
    down[0] = after(down[0], *relayed)
    first = sum(t[:tall, wide:].astype(F32) for t in down).reshape(2, count * rank, slice_wide)
    layer_rows = residual + b_down.astype(F32) + sum(t[:, :wide].astype(F32) for t in down)

    (input_rows,) = row_call(
        functools.partial(norm_back_kernel, outs=1, row=3),
        [rows_in, vectors, grad_residual] + terms,
        block,
        wide,
        [BF16],
        "norm_back",
    )
    out_att_sum = second[count * 3 * rank :]
    second = second[: count * 3 * rank].reshape(3, count * rank, slice_wide)
    sums = [att_side, first[0], first[1]]
    ends = {rep_bits[-1]: (input_rows,)}
    s_in_att, s_in_exp, s_out_red = over_groups(sums, place, over_rep(sums, (), ends))
    sums = [second[t] for t in range(3)]
    sums += [outer[:, t * span : (t + 1) * span] for t in range(3)] + [out_att_sum]
    late = over_groups(sums, place, over_rep(sums, (), ends))
    s_out_att = late.pop()
    shape = (1, count, rows, wide)
    return (
        layer_rows.astype(BF16).reshape(shape),
        input_rows.reshape(shape),
        late[0],
        late[3],
        late[1],
        late[4],
        late[2],
        late[5],
        s_in_att,
        s_out_att,
        s_in_exp,
        s_out_exp,
        s_in_red,
        s_out_red,
    )


def solution(mesh):
    row = P("shard", None)
    wide = P(None, None, "shard")
    acts = P("rep", None, "shard", None)
    in_specs = (
        (acts, P(), P(), row, P(), row, row, P(), row, P(), P(), P(), row, P(), row, P())
        + (wide,) * 12
        + (P("rep", None), P("rep", None, None), acts)
    )
    out_specs = (acts, acts) + (wide,) * 12
    return jax.shard_map(
        on_device, mesh=mesh, in_specs=in_specs, out_specs=out_specs, check_vma=False
    )
```
